32 devices in a mesh: dp: 8 (over y, x, core), expert: 4 (over z).
Axes of the slice: x: 2, y: 2, z: 4, core: 2. Of those that a mesh axis runs over, the one named last changes fastest.
Arguments:
- tokens: bfloat16 [4096, 2048], P(('dp', 'expert')), may hold values from -6 to 6
- w_qkv: bfloat16 [3, 2048, 2048], P(None, 'dp', 'expert'), may hold values from -0.125 to 0.125
- w_out: bfloat16 [2048, 2048], P('expert', 'dp'), may hold values from -0.5 to 0.5
- attention_norm_gain: bfloat16 [2048], P('dp'), may hold values from 0.5 to 1.5
- gain_ffn: bfloat16 [2048], P('dp'), may hold values from 0.5 to 1.5
- w_router: bfloat16 [2048, 4], P('dp'), may hold values from -0.09375 to 0.09375
- w_gate_up: bfloat16 [4, 2048, 11264], P('expert', 'dp'), may hold values from -0.125 to 0.125
- w_down: bfloat16 [4, 5632, 2048], P('expert', 'dp'), may hold values from -0.15625 to 0.15625
- lengths: int32 [8], P('dp'), may hold values from 128 to 512, as said below
- routes: int32 [4096, 2], P(('dp', 'expert')), may hold values from 0 to 3, all different within a row
- order: int32 [4096], P(('dp', 'expert')), may hold values from 0 to 127, as said below
- cotangent: bfloat16 [4096, 2048], P(('dp', 'expert')), may hold values from -6 to 6
Outputs:
- output: bfloat16 [4096, 2048], P(('dp', 'expert'))
- grad_tokens: bfloat16 [4096, 2048], P(('dp', 'expert'))
- grad_qkv: float32 [3, 2048, 2048], P(None, 'dp', 'expert')
- grad_out: float32 [2048, 2048], P('expert', 'dp')
- grad_gain_attn: float32 [2048], P('dp')
- grad_gain_ffn: float32 [2048], P('dp')
- grad_router: float32 [2048, 4], P('dp')
- grad_gate_up: float32 [4, 2048, 11264], P('expert', 'dp')
- grad_down: float32 [4, 5632, 2048], P('expert', 'dp')
The draws below stay inside these ranges and needn't reach their ends.
Inputs may be any that keep to these rules, and one draw needn't show every extreme that they name: `lengths`: one sequence of every draw has exactly 512 live tokens. `routes`: each token slot names 2 different experts, and every expert is named somewhere. `order`: each aligned block of 128 entries holds every number of 0 to 127 once.
All inputs are finite; a program needn't handle non-finite values.
Results may differ from the reference program's by a relative error of at most 0.023.
Values may be sent and summed in bfloat16 or wider, within the bound.
A program may use at most 384 MiB of HBM per device.

```python
import jax
import jax.numpy as jnp
from jax import lax

D = 2048
HEADS = 16
HEAD_DIM = 128
FF = 5632
TOP = 2
LEN = 512
EXPERTS = 4
SEQS = 8
TOKENS = 4096
TOK_DEV = 128
CAP = 64
N_EXPERT = 4


def draw_lengths(key, part):
    values = jax.random.randint(key, (SEQS,), LEN // 4, LEN + 1)
    longest = jax.random.randint(jax.random.fold_in(key, 7), (), 0, SEQS)
    return values.at[longest].set(LEN).astype(jnp.int32)


def draw_order(key, part):
    block_keys = jax.random.split(key, TOKENS // TOK_DEV)
    ranks = jax.vmap(lambda k: jax.random.permutation(k, TOK_DEV))(block_keys)
    return ranks.reshape(TOKENS).astype(jnp.int32)


def with_spikes(entries, key, source, target, parts, factor):
    def block_of(axis_at):
        return (jnp.arange(entries.shape[axis_at]) // (entries.shape[axis_at] // parts)).reshape((-1,) + (1,) * (entries.ndim - 1 - axis_at))

    first = jax.random.permutation(key, parts)[block_of(target)]
    other_side = (block_of(target) + parts // 2) % parts
    return jnp.where((block_of(source) == first) | (block_of(source) == other_side), factor * entries, entries)


def shard_levels(own_key, shape, shards, least, largest):
    loudness, own = 1.0, jax.random.fold_in(own_key, 6)
    for dim, blocks in shards:
        steps = jnp.exp(jax.random.uniform(jax.random.fold_in(own, dim), (blocks,), jnp.float32, least / len(shards), largest / len(shards)))
        loudness = loudness * jnp.repeat(steps, shape[dim] // blocks).reshape([-1 if axis == dim else 1 for axis in range(len(shape))])
    return loudness


def choose_distinct(rng, rows, count, top, lift):
    order = jax.random.permutation(jax.random.fold_in(rng, 1), count)
    boost = order
    for power in range(3):
        boost = boost * boost // count
    boost = boost * lift // count
    tickets = jax.random.randint(jax.random.fold_in(rng, 2), (rows, count), 0, 4096) + boost
    sure = jax.random.permutation(jax.random.fold_in(rng, 3), rows)[jnp.arange(count) % rows]
    tickets = jnp.where(jnp.arange(rows)[:, None] == sure[None, :], 1 << 14, tickets)
    priority = tickets * count + jnp.arange(count)
    return lax.top_k(priority.astype(jnp.int32), top)[1].astype(jnp.int32)


def normal_values(key, extent, scale, limit, cuts=(), kind=jnp.bfloat16):
    level = shard_levels(key, extent, cuts, -0.22, 0.18) if cuts else 1.0
    drawn = jax.random.normal(key, extent, jnp.float32) * scale * level
    return jnp.minimum(jnp.maximum(drawn, -limit), limit).astype(kind)


def gaussian_with(own_key, dims, width, bound, cuts, heavy, kind=jnp.bfloat16):
    entries = width * jax.random.normal(own_key, dims, jnp.float32)
    if cuts:
        entries = entries * shard_levels(own_key, dims, cuts, -0.22, 0.18)
    return jnp.clip(with_spikes(entries, jax.random.fold_in(own_key, 3), *heavy), -bound, bound).astype(kind)


def setup_inputs(seed: int = 0) -> dict:
    key_list = jax.random.split(jax.random.key(seed), 13)
    tokens = normal_values(key_list[0], (TOKENS, D), 1.0, 6.0, ((0, 32),))
    w_qkv = normal_values(key_list[1], (3, D, D), D ** -0.5, 0.125, ((1, 8), (2, 4)))
    w_out = normal_values(key_list[2], (D, D), (D // 16) ** -0.5, 0.5, ((0, 4), (1, 8)))
    attention_norm_gain = jnp.clip(1.0 + 0.1 * jax.random.normal(key_list[3], (D,), jnp.float32), 0.5, 1.5).astype(jnp.bfloat16)
    gain_ffn = jnp.clip(1.0 + 0.1 * jax.random.normal(key_list[4], (D,), jnp.float32), 0.5, 1.5).astype(jnp.bfloat16)
    w_router = normal_values(key_list[5], (D, EXPERTS), (2 * D) ** -0.5, 0.09375, ((0, 8),))
    w_gate_up = normal_values(key_list[6], (EXPERTS, D, 2 * FF), D ** -0.5, 0.125, ((0, 4), (1, 8)))
    w_down = normal_values(key_list[7], (EXPERTS, FF, D), (FF // 4) ** -0.5, 0.15625, ((0, 4), (1, 8)))
    lengths = draw_lengths(jax.random.fold_in(key_list[12], 71), 0)
    routes = choose_distinct(key_list[9], TOKENS, EXPERTS, TOP, 4096)
    order = draw_order(jax.random.fold_in(key_list[12], 71), 0)
    cotangent = gaussian_with(key_list[11], (TOKENS, D), 1.0, 6.0, ((0, 32),), (0, 1, 32, 2.75))
    return dict(tokens=tokens, w_qkv=w_qkv, w_out=w_out, attention_norm_gain=attention_norm_gain, gain_ffn=gain_ffn, w_router=w_router, w_gate_up=w_gate_up, w_down=w_down, lengths=lengths, routes=routes, order=order, cotangent=cotangent)


NORM_EPSILON = 1e-05
NEGATIVE = -1e+30
THETA = 10000.0
HIGH = lax.Precision.HIGHEST

@jax.custom_vjp
def reduced_precision(v):
    return lax.optimization_barrier(v.astype(jnp.bfloat16)).astype(jnp.float32)

@jax.custom_vjp
def low_back(v):
    return v

def low_keep(v):
    return (reduced_precision(v), None)

def low_pass(kept, grad):
    return (grad,)

def back_keep(v):
    return (v, None)

def back_low(kept, grad):
    return (reduced_precision(grad),)
reduced_precision.defvjp(low_keep, low_pass)
low_back.defvjp(back_keep, back_low)

def product(left, right):
    return jnp.dot(left, right, precision=HIGH, preferred_element_type=jnp.float32)

def rotary_tables(length_total, head_size):
    position = jnp.arange(length_total, dtype=jnp.float32)
    frequency = THETA ** (-(jnp.arange(head_size // 2, dtype=jnp.float32) * 2.0 / head_size))
    angles = position[:, None] * frequency[None, :]
    return (jnp.cos(angles)[:, None, :], jnp.sin(angles)[:, None, :])

def rotate(values, cosine, sine):
    half_size = values.shape[-1] // 2
    first = values[..., :half_size]
    second = values[..., half_size:]
    return jnp.concatenate([first * cosine - second * sine, second * cosine + first * sine], axis=-1)

def slot_table(routes, order, valid, experts, capacity):
    row_count = routes.shape[0]
    top_count = routes.shape[1]
    pair_rank = order[:, None] + row_count * jnp.arange(top_count, dtype=jnp.int32)[None, :]
    flat_rank = pair_rank.reshape(-1)
    flat_expert = routes.reshape(-1)
    flat_valid = jnp.broadcast_to(valid[:, None], routes.shape).reshape(-1)
    earlier = (flat_rank[None, :] < flat_rank[:, None]) & (flat_expert[None, :] == flat_expert[:, None]) & flat_valid[None, :]
    slot_index = lax.optimization_barrier(jnp.sum(earlier.astype(jnp.int32), axis=1)).reshape(row_count, top_count)
    kept_pair = valid[:, None] & (slot_index < capacity)
    target = routes * capacity + jnp.minimum(slot_index, capacity - 1)
    return (target.astype(jnp.int32), kept_pair)

def group_layer(params, inputs):
    w_qkv, w_out, attention_norm_gain, gain_ffn, w_router, w_gate_up, w_down = params
    tokens, length, routes, order = inputs
    blocks = N_EXPERT
    position = jnp.arange(LEN, dtype=jnp.int32)
    valid = position < length
    valid_rows = valid.astype(jnp.float32)[:, None]
    input_normalized_hat = tokens * lax.rsqrt(lax.optimization_barrier(jnp.mean(tokens * tokens, axis=-1, keepdims=True)) + NORM_EPSILON)
    normalized_input = reduced_precision(input_normalized_hat * attention_norm_gain)
    cosine, sine = rotary_tables(LEN, HEAD_DIM)
    query = reduced_precision(rotate(low_back(product(normalized_input, w_qkv[0])).reshape(LEN, HEADS, HEAD_DIM), cosine, sine))
    key_rows = reduced_precision(rotate(low_back(product(normalized_input, w_qkv[1])).reshape(LEN, HEADS, HEAD_DIM), cosine, sine))
    value = reduced_precision(low_back(product(normalized_input, w_qkv[2]))).reshape(LEN, HEADS, HEAD_DIM)
    raw = jnp.einsum('qhd,khd->hqk', query, key_rows, precision=HIGH)
    scores = low_back(raw * HEAD_DIM ** (-0.5))
    allowed = (position[None, :] <= position[:, None]) & valid[None, :]
    scores = jnp.where(allowed[None], scores, NEGATIVE)
    probs = reduced_precision(jax.nn.softmax(scores, axis=-1))
    heads_out = jnp.einsum('hqk,khd->qhd', probs, value, precision=HIGH).reshape(LEN, D)
    attended = reduced_precision(low_back(heads_out))
    resid = tokens + low_back(product(attended, w_out))
    hhat = resid * lax.rsqrt(lax.optimization_barrier(jnp.mean(resid * resid, axis=-1, keepdims=True)) + NORM_EPSILON)
    hidden_in = reduced_precision(hhat * gain_ffn)
    logits = product(hidden_in, w_router)
    chosen = jnp.take_along_axis(logits, routes, axis=1)
    gates = jax.nn.softmax(chosen, axis=1)
    target, kept_pair = jax.vmap(lambda r, o, v: slot_table(r, o, v, EXPERTS, CAP))(routes.reshape(blocks, TOK_DEV, TOP), order.reshape(blocks, TOK_DEV), valid.reshape(blocks, TOK_DEV))
    slot_ids = jnp.arange(EXPERTS * CAP, dtype=jnp.int32)
    pair_hits = ((slot_ids[None, :, None, None] == target[:, None]) & kept_pair[:, None]).astype(jnp.float32)
    select = lax.optimization_barrier(jnp.sum(pair_hits, axis=3))
    sent = jnp.einsum('bst,btd->bsd', select, hidden_in.reshape(blocks, TOK_DEV, D), precision=HIGH)
    expert_rows = low_back(sent.reshape(blocks, EXPERTS, CAP, D).transpose(1, 0, 2, 3).reshape(EXPERTS, blocks * CAP, D))
    outs = []
    for index in range(EXPERTS):
        gate_up = low_back(product(expert_rows[index], w_gate_up[index]))
        activated = reduced_precision(jax.nn.silu(gate_up[:, :FF]) * gate_up[:, FF:])
        outs.append(reduced_precision(low_back(product(activated, w_down[index]))))
    expert_out = jnp.stack(outs)
    returned = expert_out.reshape(EXPERTS, blocks, CAP, D).transpose(1, 0, 2, 3).reshape(blocks, EXPERTS * CAP, D)
    picked = jnp.einsum('bstk,bsd->btkd', pair_hits, returned, precision=HIGH)
    moe = lax.optimization_barrier(jnp.sum(gates.reshape(blocks, TOK_DEV, TOP)[..., None] * picked, axis=2)).reshape(LEN, D)
    return valid_rows * (resid + moe)

def reference(tokens, w_qkv, w_out, attention_norm_gain, gain_ffn, w_router, w_gate_up, w_down, lengths, routes, order, cotangent):
    params = tuple((p.astype(jnp.float32) for p in (w_qkv, w_out, attention_norm_gain, gain_ffn, w_router, w_gate_up, w_down)))
    tokens_f = tokens.astype(jnp.float32)
    routes_seq = routes.reshape(SEQS, LEN, TOP)
    order_seq = order.reshape(SEQS, LEN)

    def forward(tokens_in, weights):

        def step(carry, inputs):
            return (carry, jax.checkpoint(group_layer)(weights, inputs))
        _, outs = lax.scan(step, jnp.zeros((), jnp.float32), (tokens_in.reshape(SEQS, LEN, D), lengths, routes_seq, order_seq))
        return outs.reshape(TOKENS, D)
    output, pullback = jax.vjp(forward, tokens_f, params)
    grad_tokens, grads = pullback(cotangent.astype(jnp.float32))
    return (output.astype(jnp.bfloat16), grad_tokens.astype(jnp.bfloat16), grads[0], grads[1], grads[2], grads[3], grads[4], grads[5], grads[6])
```

```python
import jax
import jax.numpy as jnp
from jax import lax
from jax.sharding import PartitionSpec as P

HEAD_DIM = 128
FF = 5632


NORM_EPSILON = 1e-05
NEGATIVE = -1e30
THETA = 10000.0
HIGH = lax.Precision.HIGHEST


def rotary_tables(length_total, head_size):
    position = jnp.arange(length_total, dtype=jnp.float32)
    frequency = THETA ** (-(jnp.arange(head_size // 2, dtype=jnp.float32) * 2.0 / head_size))
    angles = position[:, None] * frequency[None, :]
    return (jnp.cos(angles)[:, None, :], jnp.sin(angles)[:, None, :])


def rotate(values, cosine, sine):
    half_size = values.shape[-1] // 2
    first = values[..., :half_size]
    second = values[..., half_size:]
    return jnp.concatenate(
        [first * cosine - second * sine, second * cosine + first * sine], axis=-1
    )


def rotate_back(grad_rows, cosine, sine):
    half_size = grad_rows.shape[-1] // 2
    first = grad_rows[..., :half_size]
    second = grad_rows[..., half_size:]
    return jnp.concatenate(
        [first * cosine + second * sine, second * cosine - first * sine], axis=-1
    )


def slot_table(routes, order, valid, capacity):
    row_count = routes.shape[0]
    top_count = routes.shape[1]
    pair_rank = order[:, None] + row_count * jnp.arange(top_count, dtype=jnp.int32)[None, :]
    flat_rank = pair_rank.reshape(-1)
    flat_expert = routes.reshape(-1)
    flat_valid = jnp.broadcast_to(valid[:, None], routes.shape).reshape(-1)
    earlier = (
        (flat_rank[None, :] < flat_rank[:, None])
        & (flat_expert[None, :] == flat_expert[:, None])
        & flat_valid[None, :]
    )
    slot_index = jnp.sum(earlier.astype(jnp.int32), axis=1).reshape(row_count, top_count)
    kept_pair = valid[:, None] & (slot_index < capacity)
    target = routes * capacity + jnp.minimum(slot_index, capacity - 1)
    return (target, kept_pair)


def masked_scores(query, key_rows, allowed):
    scale = query.shape[-1] ** (-0.5)
    raw = jnp.einsum("qhd,khd->hqk", query, key_rows, preferred_element_type=jnp.float32) * scale
    return jnp.where(allowed[None], raw, NEGATIVE)


def contract_first(left, right):
    return lax.dot_general(
        left, right, (((0,), (0,)), ((), ())), preferred_element_type=jnp.float32
    )


def contract_last(left, right):
    return lax.dot_general(
        left, right, (((1,), (1,)), ((), ())), preferred_element_type=jnp.float32
    )


def normalize(rows):
    inverse = lax.rsqrt(jnp.mean(rows * rows, axis=-1, keepdims=True) + NORM_EPSILON)
    return rows * inverse, inverse


def exchange_experts(blocks):
    return lax.all_to_all(blocks, "expert", split_axis=0, concat_axis=0, tiled=True)


def by_hidden(w_gate_up):
    parts = lax.axis_size("dp")
    rows = w_gate_up.shape[1]
    ff_part = w_gate_up.shape[2] // 2 // parts
    pieces = w_gate_up[0].reshape(rows, 2, parts, ff_part).transpose(2, 0, 1, 3)
    pieces = pieces.reshape(parts, rows, 2 * ff_part)
    got = lax.all_to_all(pieces, "dp", split_axis=0, concat_axis=0, tiled=True)
    return got.reshape(parts * rows, 2 * ff_part)


def by_rows(grad):
    parts = lax.axis_size("dp")
    rows = grad.shape[0] // parts
    ff_part = grad.shape[1] // 2
    pieces = grad.astype(jnp.bfloat16).reshape(parts, rows, 2 * ff_part)
    got = lax.all_to_all(pieces, "dp", split_axis=0, concat_axis=0, tiled=True)
    got = got.reshape(parts, rows, 2, ff_part).transpose(1, 2, 0, 3)
    return got.reshape(1, rows, 2 * parts * ff_part).astype(jnp.float32)


def expert_step(gate_up_w, down_w, rows, d_rows_out):
    ff = down_w.shape[0]
    gate_up = jnp.dot(rows, gate_up_w, preferred_element_type=jnp.float32)
    gate = gate_up[:, :ff]
    upward = gate_up[:, ff:]
    sigmoid = jax.nn.sigmoid(gate)
    activated = (gate * sigmoid * upward).astype(jnp.bfloat16)
    out = jnp.dot(activated, down_w, preferred_element_type=jnp.float32).astype(jnp.bfloat16)
    d_activated = contract_last(d_rows_out, down_w)
    grad_down = contract_first(activated, d_rows_out)
    d_gate = d_activated * upward * sigmoid * (1.0 + gate * (1.0 - sigmoid))
    d_up = d_activated * gate * sigmoid
    d_gate_up = jnp.concatenate([d_gate, d_up], axis=1).astype(jnp.bfloat16)
    d_rows = contract_last(d_gate_up, gate_up_w).astype(jnp.bfloat16)
    grad_gate_up = contract_first(rows, d_gate_up)
    return out, d_rows, grad_gate_up, grad_down


def experts_split_hidden(w_gate_up, w_down, rows, d_rows_out):
    gate_up_w = by_hidden(w_gate_up)
    all_rows = lax.all_gather(rows, "dp", axis=0, tiled=True)
    all_d_out = lax.all_gather(d_rows_out, "dp", axis=0, tiled=True)
    out, d_rows, grad_gate_up, grad_down = expert_step(
        gate_up_w, w_down[0], all_rows, all_d_out
    )
    out = lax.psum_scatter(out, "dp", scatter_dimension=0, tiled=True)
    d_rows = lax.psum_scatter(d_rows, "dp", scatter_dimension=0, tiled=True)
    return out, d_rows, by_rows(grad_gate_up), grad_down[None]


def experts_gather_weights(w_gate_up, w_down, rows, d_rows_out):
    gate_up_w = lax.all_gather(w_gate_up, "dp", axis=1, tiled=True)[0]
    down_w = lax.all_gather(w_down, "dp", axis=1, tiled=True)[0]
    out, d_rows, grad_gate_up, grad_down = expert_step(gate_up_w, down_w, rows, d_rows_out)
    grad_gate_up = lax.psum_scatter(
        grad_gate_up.astype(jnp.bfloat16), "dp", scatter_dimension=0, tiled=True
    )
    grad_down = lax.psum_scatter(
        grad_down.astype(jnp.bfloat16), "dp", scatter_dimension=0, tiled=True
    )
    return (
        out,
        d_rows,
        grad_gate_up.astype(jnp.float32)[None],
        grad_down.astype(jnp.float32)[None],
    )


def on_device(
    tokens,
    w_qkv,
    w_out,
    attention_norm_gain,
    gain_ffn,
    w_router,
    w_gate_up,
    w_down,
    lengths,
    routes,
    order,
    cotangent,
):
    group_size = lax.axis_size("expert")
    dp_size = lax.axis_size("dp")
    tok_dev = tokens.shape[0]
    seq_len = tok_dev * group_size
    width = tokens.shape[1]
    top_count = routes.shape[1]
    capacity = tok_dev * top_count // group_size
    slots = group_size * capacity
    head_size = HEAD_DIM
    local_width = w_qkv.shape[2]
    heads_local = local_width // head_size
    tokens_all = lax.all_gather(tokens, "expert", axis=0, tiled=True)
    small = jnp.concatenate(
        [attention_norm_gain[:, None], gain_ffn[:, None], w_router], axis=1
    )
    small_full = lax.all_gather(small, "dp", axis=0, tiled=True)
    qkv_full = lax.all_gather(w_qkv, "dp", axis=1, tiled=True)
    out_full = lax.all_gather(w_out, "dp", axis=1, tiled=True)
    first_norm_gain = small_full[:, 0].astype(jnp.float32)
    gain_two = small_full[:, 1].astype(jnp.float32)
    router_full = small_full[:, 2:]

    own_start = lax.axis_index("expert") * tok_dev
    own_position = own_start + jnp.arange(tok_dev, dtype=jnp.int32)
    live_own = own_position < lengths[0]
    live_rows = live_own.astype(jnp.float32)[:, None]
    target, kept_pair = slot_table(routes, order, live_own, capacity)
    slot_ids = jnp.arange(slots, dtype=jnp.int32)
    pair_hits = (slot_ids[:, None, None] == target[None]) & kept_pair[None]
    select = jnp.sum(pair_hits.astype(jnp.float32), axis=2).astype(jnp.bfloat16)

    inputs_float = tokens.astype(jnp.float32)
    input_normalized_hat, first_inverse_rms = normalize(inputs_float)
    hat_all, _ = normalize(tokens_all.astype(jnp.float32))
    whole = (hat_all * first_norm_gain).astype(jnp.bfloat16)
    cosine, sine = rotary_tables(seq_len, head_size)
    projected = jnp.einsum("td,cde->cte", whole, qkv_full, preferred_element_type=jnp.float32)
    query = rotate(projected[0].reshape(seq_len, heads_local, head_size), cosine, sine).astype(
        jnp.bfloat16
    )
    key_rows = rotate(projected[1].reshape(seq_len, heads_local, head_size), cosine, sine).astype(
        jnp.bfloat16
    )
    value = projected[2].astype(jnp.bfloat16).reshape(seq_len, heads_local, head_size)
    position = jnp.arange(seq_len, dtype=jnp.int32)
    live_all = position < lengths[0]
    allowed = (position[None, :] <= position[:, None]) & live_all[None, :]
    scores = masked_scores(query, key_rows, allowed)
    top_score = jnp.max(scores, axis=-1, keepdims=True)
    exponent = jnp.exp(scores - top_score)
    row_total = jnp.sum(exponent, axis=-1, keepdims=True)
    probs = exponent / row_total
    log_total = top_score + jnp.log(row_total)
    probs_low = probs.astype(jnp.bfloat16)
    attended = jnp.einsum("hqk,khd->qhd", probs_low, value, preferred_element_type=jnp.float32)
    attended = attended.reshape(seq_len, local_width).astype(jnp.bfloat16)
    attn_part = jnp.dot(attended, out_full, preferred_element_type=jnp.float32)
    attn_own = lax.psum_scatter(
        attn_part.astype(jnp.bfloat16), "expert", scatter_dimension=0, tiled=True
    ).astype(jnp.float32)
    resid = inputs_float + attn_own
    hhat, inverse_two = normalize(resid)
    hidden_in = (hhat * gain_two).astype(jnp.bfloat16)
    sent = jnp.dot(select, hidden_in, preferred_element_type=jnp.float32).astype(jnp.bfloat16)
    dispatched = exchange_experts(sent.reshape(group_size, capacity, width)).reshape(slots, width)

    logits = jnp.dot(hidden_in, router_full, preferred_element_type=jnp.float32)
    chosen = jnp.take_along_axis(logits, routes, axis=1)
    gates = jax.nn.softmax(chosen, axis=1)
    d_out = live_rows * cotangent.astype(jnp.float32)
    d_back = jnp.zeros((slots, width), jnp.float32)
    for index in range(top_count):
        weighted = (gates[:, index : index + 1] * d_out).astype(jnp.bfloat16)
        d_back = d_back + jnp.dot(
            pair_hits[:, :, index].astype(jnp.bfloat16),
            weighted,
            preferred_element_type=jnp.float32,
        )
    d_back = d_back.astype(jnp.bfloat16)
    d_out_rows = exchange_experts(d_back.reshape(group_size, capacity, width)).reshape(
        slots, width
    )

    split_cost = 4 * dp_size * slots * width + 2 * 2 * FF * width // dp_size
    gather_cost = 2 * 3 * FF * width
    experts = experts_split_hidden if split_cost < gather_cost else experts_gather_weights
    expert_out, d_rows, grad_gate_up, grad_down = experts(
        w_gate_up, w_down, dispatched, d_out_rows
    )
    d_sent = exchange_experts(d_rows.reshape(group_size, capacity, width)).reshape(slots, width)
    returned = exchange_experts(expert_out.reshape(group_size, capacity, width)).reshape(
        slots, width
    )

    moe = jnp.zeros_like(resid)
    d_gates_list = []
    for index in range(top_count):
        one_hot = pair_hits[:, :, index].astype(jnp.bfloat16)
        picked = contract_first(one_hot, returned)
        d_gates_list.append(jnp.sum(d_out * picked, axis=-1))
        moe = moe + gates[:, index : index + 1] * picked
    output = (live_rows * (resid + moe)).astype(jnp.bfloat16)
    d_gates = jnp.stack(d_gates_list, axis=1)
    d_hidden = contract_first(select, d_sent)
    d_chosen = gates * (d_gates - jnp.sum(gates * d_gates, axis=1, keepdims=True))
    expert_ids = jnp.arange(group_size, dtype=jnp.int32)
    route_hits = (routes[:, :, None] == expert_ids[None, None, :]).astype(jnp.float32)
    d_logits = jnp.sum(route_hits * d_chosen[:, :, None], axis=1)
    router_f = router_full.astype(jnp.float32)
    d_hidden = d_hidden + jnp.dot(
        d_logits, router_f.T, precision=HIGH, preferred_element_type=jnp.float32
    )
    router_part = jnp.dot(
        hidden_in.astype(jnp.float32).T,
        d_logits,
        precision=HIGH,
        preferred_element_type=jnp.float32,
    )
    gain_two_part = jnp.sum(d_hidden * hhat, axis=0)
    scaled_two = d_hidden * gain_two
    d_resid = d_out + inverse_two * (
        scaled_two - hhat * jnp.mean(scaled_two * hhat, axis=-1, keepdims=True)
    )
    d_attn = d_resid.astype(jnp.bfloat16)
    whole_grad = lax.all_gather(d_attn, "expert", axis=0, tiled=True)
    d_attended = contract_last(whole_grad, out_full).astype(jnp.bfloat16)
    out_part = contract_first(attended, whole_grad)
    grad_out = lax.psum_scatter(
        out_part.astype(jnp.bfloat16), "dp", scatter_dimension=1, tiled=True
    ).astype(jnp.float32)
    d_heads = d_attended.reshape(seq_len, heads_local, head_size)
    probs = jnp.exp(masked_scores(query, key_rows, allowed) - log_total)
    probs_low = probs.astype(jnp.bfloat16)
    d_value = jnp.einsum(
        "hqk,qhd->khd", probs_low, d_heads, preferred_element_type=jnp.float32
    ).astype(jnp.bfloat16)
    d_probs = jnp.einsum("qhd,khd->hqk", d_heads, value, preferred_element_type=jnp.float32)
    row_delta = jnp.sum(probs * d_probs, axis=-1, keepdims=True)
    d_scores = (probs * (d_probs - row_delta)).astype(jnp.bfloat16)
    scale = head_size ** (-0.5)
    d_query = (
        jnp.einsum("hqk,khd->qhd", d_scores, key_rows, preferred_element_type=jnp.float32) * scale
    )
    d_key = jnp.einsum("hqk,qhd->khd", d_scores, query, preferred_element_type=jnp.float32) * scale
    d_query_pre = (
        rotate_back(d_query, cosine, sine).reshape(seq_len, local_width).astype(jnp.bfloat16)
    )
    d_key_pre = rotate_back(d_key, cosine, sine).reshape(seq_len, local_width).astype(jnp.bfloat16)
    d_projected = jnp.stack([d_query_pre, d_key_pre, d_value.reshape(seq_len, local_width)])
    d_normed_part = jnp.einsum(
        "cte,cde->td", d_projected, qkv_full, preferred_element_type=jnp.float32
    )
    grad_normalized = lax.psum_scatter(
        d_normed_part.astype(jnp.bfloat16), "expert", scatter_dimension=0, tiled=True
    ).astype(jnp.float32)
    qkv_part = jnp.einsum("td,cte->cde", whole, d_projected, preferred_element_type=jnp.float32)
    grad_qkv = lax.psum_scatter(
        qkv_part.astype(jnp.bfloat16), "dp", scatter_dimension=1, tiled=True
    ).astype(jnp.float32)
    first_gain_part = jnp.sum(d_normed_part * hat_all, axis=0)
    first_scaled_input = grad_normalized * first_norm_gain
    grad_tokens = d_resid + first_inverse_rms * (
        first_scaled_input
        - input_normalized_hat
        * jnp.mean(first_scaled_input * input_normalized_hat, axis=-1, keepdims=True)
    )
    small_part = jnp.concatenate(
        [first_gain_part[None], gain_two_part[None], router_part.T], axis=0
    )
    small_sum = lax.psum(small_part, ("dp", "expert"))
    own_rows = width // dp_size
    small_own = lax.dynamic_slice_in_dim(
        small_sum, lax.axis_index("dp") * own_rows, own_rows, axis=1
    )
    return (
        output,
        grad_tokens.astype(jnp.bfloat16),
        grad_qkv,
        grad_out,
        small_own[0],
        small_own[1],
        small_own[2:].T,
        grad_gate_up,
        grad_down,
    )


def solution(mesh):
    placed = (
        P(("dp", "expert"), None),
        P(None, "dp", "expert"),
        P("expert", "dp"),
        P("dp"),
        P("dp"),
        P("dp", None),
        P("expert", "dp", None),
        P("expert", "dp", None),
        P("dp"),
        P(("dp", "expert"), None),
        P(("dp", "expert")),
        P(("dp", "expert"), None),
    )
    return jax.shard_map(
        on_device,
        mesh=mesh,
        in_specs=placed,
        out_specs=(
            P(("dp", "expert"), None),
            P(("dp", "expert"), None),
            P(None, "dp", "expert"),
            P("expert", "dp"),
            P("dp"),
            P("dp"),
            P("dp", None),
            P("expert", "dp", None),
            P("expert", "dp", None),
        ),
        check_vma=False,
    )
```

```python
import functools

import jax
import jax.numpy as jnp
from jax import lax
from jax.experimental import pallas as pl
from jax.experimental.pallas import tpu as pltpu
from jax.sharding import PartitionSpec as P

HEAD_DIM = 128
FF = 5632


NORM_EPSILON = 1e-05
NEGATIVE = -1e30
THETA = 10000.0
HIGH = lax.Precision.HIGHEST
MESH_ID = pl.DeviceIdType.MESH
LANES = 128


def remote(src, dst, send_sem, recv_sem, peer):
    return pltpu.make_async_remote_copy(
        src_ref=src,
        dst_ref=dst,
        send_sem=send_sem,
        recv_sem=recv_sem,
        device_id=peer,
        device_id_type=MESH_ID,
    )


def greet(peers):
    barrier = pltpu.get_barrier_semaphore()
    for peer in peers:
        pl.semaphore_signal(barrier, inc=1, device_id=peer, device_id_type=MESH_ID)
    pl.semaphore_wait(barrier, len(peers))


def dot_nn(left, right):
    return jnp.dot(left, right, preferred_element_type=jnp.float32)


def dot_nt(left, right):
    return lax.dot_general(
        left, right, (((1,), (1,)), ((), ())), preferred_element_type=jnp.float32
    )


def experts_kernel(
    group,
    sent,
    d_back,
    w_own,
    w_x,
    w_y,
    w_diag,
    down_own,
    ret,
    d_ret,
    grad_gate_up,
    grad_down,
    w_buf,
    down_buf,
    rows_buf,
    gate_buf,
    act_buf,
    part_buf,
    half_x,
    half_y,
    full_x,
    full_y,
    other_gate,
    other_down,
    stage,
    ag_sems,
    rs_sems,
    weight_sems,
    local_sems,
    grad_sems,
):
    cap, width = sent.shape[1], sent.shape[2]
    half = cap // 2
    piece = w_own.shape[0]
    hidden2 = w_own.shape[1]
    hidden = hidden2 // 2
    down_rows = down_own.shape[0]
    chunk = 4 * cap
    total = group * chunk

    index = lax.axis_index("dp")
    place = lax.axis_index("expert")
    core = index % 2
    at_x = (index // 2) % 2
    at_y = index // 4
    partner = {"dp": at_y * 4 + at_x * 2 + (1 - core)}
    along_x = {"dp": at_y * 4 + (1 - at_x) * 2 + core}
    along_y = {"dp": (1 - at_y) * 4 + at_x * 2 + core}
    chips = [
        at_y * 2 + at_x,
        at_y * 2 + (1 - at_x),
        (1 - at_y) * 2 + at_x,
        (1 - at_y) * 2 + (1 - at_x),
    ]

    def ahead(k):
        return {"expert": (place + k) % group}

    def behind(k):
        return {"expert": (place + group - k) % group}

    greet([partner, along_x, along_y] + [ahead(k) for k in range(1, group)])

    def block(t, k, r, start=0, size=None):
        size = cap if size is None else size
        return rows_buf.at[t, pl.ds((k * 4 + r) * cap + start, size), :]

    def part(t, k, r, start=0, size=None):
        size = cap if size is None else size
        return part_buf.at[t, pl.ds((k * 4 + r) * cap + start, size), :]

    def ag(kind, t, k):
        return ag_sems.at[0, kind, t, k], ag_sems.at[1, kind, t, k]

    def rs(kind, t, k):
        return rs_sems.at[0, kind, t, k], rs_sems.at[1, kind, t, k]

    sources = (sent, d_back)
    results = (ret, d_ret)

    def z_copy(t, k):
        return remote(sources[t].at[k], block(t, k, 0), *ag(0, t, k), ahead(k))

    def own_copy(t):
        return pltpu.make_async_copy(sources[t].at[0], block(t, 0, 0), local_sems.at[t])

    def x_copy(t, k):
        return remote(block(t, k, 0), block(t, k, 1), *ag(1, t, k), along_x)

    def y_copy(t, k):
        return remote(block(t, k, 0), block(t, k, 2), *ag(2, t, k), along_y)

    def a_copy(t, k):
        return remote(block(t, k, 2, 0, half), block(t, k, 3, 0, half), *ag(3, t, k), along_x)

    def b_copy(t, k):
        return remote(
            block(t, k, 1, half, half), block(t, k, 3, half, half), *ag(4, t, k), along_y
        )

    def spread(t, k):
        if k == 0:
            own_copy(t).wait()
        else:
            z_copy(t, k).wait_recv()
        x_copy(t, k).start()
        y_copy(t, k).start()

    def relay(t, k):
        y_copy(t, k).wait_recv()
        a_copy(t, k).start()
        x_copy(t, k).wait_recv()
        b_copy(t, k).start()

    def arrived(t, k):
        a_copy(t, k).wait_recv()
        b_copy(t, k).wait_recv()

    def half_x_copy(t, k):
        return remote(part(t, k, 3, 0, half), half_x.at[t, k], *rs(0, t, k), along_x)

    def half_y_copy(t, k):
        return remote(part(t, k, 3, half, half), half_y.at[t, k], *rs(1, t, k), along_y)

    def full_x_copy(t, k):
        return remote(part(t, k, 1), full_x.at[t, k], *rs(2, t, k), along_x)

    def full_y_copy(t, k):
        return remote(part(t, k, 2), full_y.at[t, k], *rs(3, t, k), along_y)

    def back_copy(t, k):
        return remote(part(t, k, 0), results[t].at[k], *rs(4, t, k), behind(k))

    def keep_copy(t):
        return pltpu.make_async_copy(part(t, 0, 0), results[t].at[0], local_sems.at[2 + t])

    def halves_out(t, k):
        half_x_copy(t, k).start()
        half_y_copy(t, k).start()

    def add_into(target, *others):
        value = target[...].astype(jnp.float32)
        for other in others:
            value = value + other[...].astype(jnp.float32)
        target[...] = value.astype(jnp.bfloat16)

    def fulls_out(t, k):
        half_x_copy(t, k).wait_recv()
        add_into(part(t, k, 2, 0, half), half_x.at[t, k])
        full_y_copy(t, k).start()
        half_y_copy(t, k).wait_recv()
        add_into(part(t, k, 1, half, half), half_y.at[t, k])
        full_x_copy(t, k).start()

    def home(t, k):
        full_x_copy(t, k).wait_recv()
        full_y_copy(t, k).wait_recv()
        add_into(part(t, k, 0), full_x.at[t, k], full_y.at[t, k])
        if k == 0:
            keep_copy(t).start()
        else:
            back_copy(t, k).start()

    pieces = (w_own, w_x, w_y, w_diag)

    def w_rows(r, which):
        return w_buf.at[pl.ds(pl.multiple_of((chips[r] * 2 + which) * piece, piece), piece), :]

    def w_share(r):
        return remote(
            pieces[r], w_rows(r, core), weight_sems.at[0, r], weight_sems.at[1, r], partner
        )

    def w_share_in(r):
        return remote(
            pieces[r], w_rows(r, 1 - core), weight_sems.at[0, r], weight_sems.at[1, r], partner
        )

    def w_keep(r):
        return pltpu.make_async_copy(pieces[r], w_rows(r, core), local_sems.at[4 + r])

    def down_at(which):
        return down_buf.at[pl.ds(pl.multiple_of(which * down_rows, down_rows), down_rows), :]

    def down_share():
        return remote(
            down_own, down_at(core), weight_sems.at[0, 4], weight_sems.at[1, 4], partner
        )

    down_keep = pltpu.make_async_copy(down_own, down_at(core), local_sems.at[8])

    def forward(k):
        base = k * chunk

        def tile(j, carry):
            cols = pl.ds(pl.multiple_of(j * 2 * LANES, 2 * LANES), 2 * LANES)
            both = dot_nn(rows_buf[0, base : base + chunk, :], w_buf[:, cols])
            gate = both[:, :LANES]
            sigmoid = 1.0 / (1.0 + jnp.exp(-gate))
            act = gate * sigmoid * both[:, LANES:]
            gate_buf[base : base + chunk, cols] = both.astype(jnp.bfloat16)
            narrow = pl.ds(pl.multiple_of(j * LANES, LANES), LANES)
            act_buf[base : base + chunk, narrow] = act.astype(jnp.bfloat16)
            return carry

        lax.fori_loop(0, hidden // LANES, tile, 0)

        def out_tile(j, carry):
            cols = pl.ds(pl.multiple_of(j * 2 * LANES, 2 * LANES), 2 * LANES)
            out = dot_nn(act_buf[base : base + chunk, :], down_buf[:, cols])
            part_buf[0, base : base + chunk, cols] = out.astype(jnp.bfloat16)
            return carry

        lax.fori_loop(0, width // (2 * LANES), out_tile, 0)

    def backward(k):
        base = k * chunk

        def tile(first, count):
            rows = pl.ds(pl.multiple_of(first * LANES, LANES), count * LANES)
            d_act = dot_nt(rows_buf[1, base : base + chunk, :], down_buf[rows, :])
            for i in range(count):
                cols = pl.ds(pl.multiple_of((first + i) * 2 * LANES, 2 * LANES), 2 * LANES)
                both = gate_buf[base : base + chunk, cols].astype(jnp.float32)
                gate = both[:, :LANES]
                up = both[:, LANES:]
                sigmoid = 1.0 / (1.0 + jnp.exp(-gate))
                scaled = d_act[:, i * LANES : (i + 1) * LANES] * sigmoid
                d_gate = scaled * up * (1.0 + gate * (1.0 - sigmoid))
                d_up = scaled * gate
                gate_buf[base : base + chunk, cols] = jnp.concatenate(
                    [d_gate, d_up], axis=1
                ).astype(jnp.bfloat16)

        def pair(j, carry):
            tile(2 * j, 2)
            return carry

        blocks = hidden // LANES
        lax.fori_loop(0, blocks // 2, pair, 0)
        if blocks % 2:
            tile(blocks - 1, 1)

        def out_tile(j, carry):
            cols = pl.ds(pl.multiple_of(j * 2 * LANES, 2 * LANES), 2 * LANES)
            out = dot_nt(gate_buf[base : base + chunk, :], w_buf[cols, :])
            part_buf[1, base : base + chunk, cols] = out.astype(jnp.bfloat16)
            return carry

        lax.fori_loop(0, width // (2 * LANES), out_tile, 0)

    w_share(0).start()
    w_keep(0).start()
    own_copy(0).start()
    for k in range(1, group):
        z_copy(0, k).start()
    for r in range(1, 4):
        w_share(r).start()
        w_keep(r).start()
    down_share().start()
    down_keep.start()
    own_copy(1).start()

    spread(0, 0)
    spread(0, 1)
    relay(0, 0)
    for k in range(1, group):
        z_copy(1, k).start()
    spread(0, 2)
    relay(0, 1)
    arrived(0, 0)
    for r in range(4):
        w_keep(r).wait()
        w_share_in(r).wait_recv()
    down_keep.wait()
    down_share().wait_recv()
    forward(0)
    spread(0, 3)
    relay(0, 2)
    arrived(0, 1)
    forward(1)
    spread(1, 0)
    relay(0, 3)
    arrived(0, 2)
    forward(2)
    spread(1, 1)
    relay(1, 0)
    arrived(0, 3)
    forward(3)
    spread(1, 2)
    relay(1, 1)
    arrived(1, 0)
    backward(0)
    spread(1, 3)
    relay(1, 2)
    arrived(1, 1)
    halves_out(0, 0)
    halves_out(0, 1)
    backward(1)
    relay(1, 3)
    arrived(1, 2)
    halves_out(0, 2)
    halves_out(0, 3)
    fulls_out(0, 0)
    fulls_out(0, 1)
    halves_out(1, 0)
    backward(2)
    arrived(1, 3)
    fulls_out(0, 2)
    fulls_out(0, 3)
    halves_out(1, 1)
    home(0, 0)
    home(0, 1)
    backward(3)
    halves_out(1, 2)
    halves_out(1, 3)
    fulls_out(1, 0)
    fulls_out(1, 1)

    act_t = down_buf.at[:, pl.ds(0, total)]
    rows_t = down_buf.at[pl.ds(0, piece), pl.ds(total, total)]
    send_down = w_buf.at[pl.ds(4 * piece, down_rows), pl.ds(0, width)]

    def send_gate(r):
        return w_buf.at[pl.ds(r * piece, piece), :]

    def turn(j, carry):
        cols = pl.ds(pl.multiple_of(j * LANES, LANES), LANES)
        act_t[cols, :] = act_buf[:, cols].T
        return carry

    lax.fori_loop(0, hidden // LANES, turn, 0)

    def down_grad(which, j):
        cols = pl.ds(pl.multiple_of(j * 2 * LANES, 2 * LANES), 2 * LANES)
        rows = pl.ds(pl.multiple_of(which * down_rows, down_rows), down_rows)
        return cols, dot_nn(act_t[rows, :], rows_buf[1, :, cols])

    def down_for_partner(j, carry):
        cols, value = down_grad(1 - core, j)
        send_down[:, cols] = value.astype(jnp.bfloat16)
        return carry

    tiles = width // (2 * LANES)
    lax.fori_loop(0, tiles, down_for_partner, 0)
    down_send = remote(
        send_down, other_down, grad_sems.at[0, 4], grad_sems.at[1, 4], partner
    )
    down_send.start()
    home(0, 2)
    home(0, 3)
    fulls_out(1, 2)
    fulls_out(1, 3)

    def gate_grad(r, which, store):
        start = pl.multiple_of((chips[r] * 2 + which) * piece, piece)
        rows_t[...] = rows_buf[0, :, pl.ds(start, piece)].T

        def tile(j, carry):
            cols = pl.ds(pl.multiple_of(j * 2 * LANES, 2 * LANES), 2 * LANES)
            store(cols, dot_nn(rows_t[...], gate_buf[:, cols]))
            return carry

        lax.fori_loop(0, hidden2 // (2 * LANES), tile, 0)

    def gate_send(r):
        return remote(
            send_gate(r), other_gate.at[r], grad_sems.at[0, r], grad_sems.at[1, r], partner
        )

    for r in range(4):
        target = send_gate(r)

        def store(cols, value, target=target):
            target[:, cols] = value.astype(jnp.bfloat16)

        gate_grad(r, 1 - core, store)
        gate_send(r).start()
        if r == 0:
            home(1, 0)
            home(1, 1)
        if r == 1:
            home(1, 2)
        if r == 2:
            home(1, 3)

    down_send.wait_recv()

    def stage_copy(j):
        cols = pl.ds(pl.multiple_of(j * 2 * LANES, 2 * LANES), 2 * LANES)
        return pltpu.make_async_copy(
            stage.at[j % 2], grad_down.at[:, cols], grad_sems.at[2, j % 2]
        )

    def down_for_self(j, carry):
        cols, value = down_grad(core, j)

        @pl.when(j >= 2)
        def _():
            stage_copy(j - 2).wait()

        stage[j % 2] = value + other_down[:, cols].astype(jnp.float32)
        stage_copy(j).start()
        return carry

    lax.fori_loop(0, tiles, down_for_self, 0)

    def gate_out(r):
        return pltpu.make_async_copy(other_gate.at[r], grad_gate_up.at[r], grad_sems.at[2, 2 + r])

    for r in range(4):
        gate_send(r).wait_recv()
        target = other_gate.at[r]

        def store(cols, value, target=target):
            target[:, cols] = (value + target[:, cols].astype(jnp.float32)).astype(jnp.bfloat16)

        gate_grad(r, core, store)
        gate_out(r).start()

    stage_copy(tiles - 2).wait()
    stage_copy(tiles - 1).wait()
    for r in range(4):
        gate_out(r).wait()
        gate_send(r).wait_send()
        w_share(r).wait_send()
    down_share().wait_send()
    down_send.wait_send()
    for t in range(2):
        keep_copy(t).wait()
        for k in range(group):
            x_copy(t, k).wait_send()
            y_copy(t, k).wait_send()
            a_copy(t, k).wait_send()
            b_copy(t, k).wait_send()
            half_x_copy(t, k).wait_send()
            half_y_copy(t, k).wait_send()
            full_x_copy(t, k).wait_send()
            full_y_copy(t, k).wait_send()
            if k > 0:
                z_copy(t, k).wait_send()
                back_copy(t, k).wait_send()
                back_copy(t, k).wait_recv()


def experts_call(sent, d_back, pieces, down_own):
    group, cap, width = sent.shape
    piece, hidden2 = pieces[0].shape
    hidden = hidden2 // 2
    down_rows = down_own.shape[0]
    chunk = 4 * cap
    total = group * chunk
    low = jnp.bfloat16
    anywhere = pl.BlockSpec(memory_space=pl.ANY)
    flops = 2 * total * width * hidden * 9
    moved = 2 * (4 * piece * hidden2 * 2 + down_rows * width * 3)
    return pl.pallas_call(
        functools.partial(experts_kernel, group),
        out_shape=(
            jax.ShapeDtypeStruct((group, cap, width), low),
            jax.ShapeDtypeStruct((group, cap, width), low),
            jax.ShapeDtypeStruct((4, piece, hidden2), low),
            jax.ShapeDtypeStruct((down_rows, width), jnp.float32),
        ),
        in_specs=[anywhere] * 7,
        out_specs=(anywhere,) * 4,
        scratch_shapes=[
            pltpu.VMEM((width, hidden2), low),
            pltpu.VMEM((hidden, width), low),
            pltpu.VMEM((2, total, width), low),
            pltpu.VMEM((total, hidden2), low),
            pltpu.VMEM((total, hidden), low),
            pltpu.VMEM((2, total, width), low),
            pltpu.VMEM((2, group, cap // 2, width), low),
            pltpu.VMEM((2, group, cap // 2, width), low),
            pltpu.VMEM((2, group, cap, width), low),
            pltpu.VMEM((2, group, cap, width), low),
            pltpu.VMEM((4, piece, hidden2), low),
            pltpu.VMEM((down_rows, width), low),
            pltpu.VMEM((2, down_rows, 2 * LANES), jnp.float32),
            pltpu.SemaphoreType.DMA((2, 5, 2, group)),
            pltpu.SemaphoreType.DMA((2, 5, 2, group)),
            pltpu.SemaphoreType.DMA((2, 5)),
            pltpu.SemaphoreType.DMA((9,)),
            pltpu.SemaphoreType.DMA((3, 6)),
        ],
        compiler_params=pltpu.CompilerParams(
            collective_id=1, has_side_effects=True, vmem_limit_bytes=67043328
        ),
        cost_estimate=pl.CostEstimate(flops=flops, bytes_accessed=moved, transcendentals=0),
        name="experts",
    )(sent, d_back, *pieces, down_own)


def rotary_tables(length_total, head_size):
    position = jnp.arange(length_total, dtype=jnp.float32)
    frequency = THETA ** (-(jnp.arange(head_size // 2, dtype=jnp.float32) * 2.0 / head_size))
    angles = position[:, None] * frequency[None, :]
    return (jnp.cos(angles)[:, None, :], jnp.sin(angles)[:, None, :])


def rotate(values, cosine, sine):
    half_size = values.shape[-1] // 2
    first = values[..., :half_size]
    second = values[..., half_size:]
    return jnp.concatenate(
        [first * cosine - second * sine, second * cosine + first * sine], axis=-1
    )


def rotate_back(grad_rows, cosine, sine):
    half_size = grad_rows.shape[-1] // 2
    first = grad_rows[..., :half_size]
    second = grad_rows[..., half_size:]
    return jnp.concatenate(
        [first * cosine + second * sine, second * cosine - first * sine], axis=-1
    )


def slot_table(routes, order, valid, capacity, first_expert, experts):
    row_count = routes.shape[0]
    top_count = routes.shape[1]
    pair_rank = order[:, None] + row_count * jnp.arange(top_count, dtype=jnp.int32)[None, :]
    flat_rank = pair_rank.reshape(-1)
    flat_expert = routes.reshape(-1)
    flat_valid = jnp.broadcast_to(valid[:, None], routes.shape).reshape(-1)
    earlier = (
        (flat_rank[None, :] < flat_rank[:, None])
        & (flat_expert[None, :] == flat_expert[:, None])
        & flat_valid[None, :]
    )
    slot_index = jnp.sum(earlier.astype(jnp.int32), axis=1).reshape(row_count, top_count)
    kept_pair = valid[:, None] & (slot_index < capacity)
    place = (routes + experts - first_expert) % experts
    target = place * capacity + jnp.minimum(slot_index, capacity - 1)
    return (target, kept_pair)


def masked_scores(query, key_rows, allowed):
    scale = query.shape[-1] ** (-0.5)
    raw = jnp.einsum("qhd,khd->hqk", query, key_rows, preferred_element_type=jnp.float32) * scale
    return jnp.where(allowed[None], raw, NEGATIVE)


def contract_first(left, right):
    return lax.dot_general(
        left, right, (((0,), (0,)), ((), ())), preferred_element_type=jnp.float32
    )


def contract_last(left, right):
    return lax.dot_general(
        left, right, (((1,), (1,)), ((), ())), preferred_element_type=jnp.float32
    )


def normalize(rows):
    inverse = lax.rsqrt(jnp.mean(rows * rows, axis=-1, keepdims=True) + NORM_EPSILON)
    return rows * inverse, inverse


def exchange_experts(blocks):
    return lax.all_to_all(blocks, "expert", split_axis=0, concat_axis=0, tiled=True)


def across(index, step):
    return ((index // 2) ^ step) * 2 + index % 2


def swap_chips(pieces):
    parts = lax.axis_size("dp")
    got = [pieces[0]]
    for step in (1, 2, 3):
        pairs = [(index, across(index, step)) for index in range(parts)]
        got.append(lax.ppermute(pieces[step], "dp", pairs))
    return got


def chip_slices(w_gate_up):
    rows, ff2 = w_gate_up.shape[1:]
    chips = lax.axis_size("dp") // 2
    blocks = ff2 // 2 // chips // LANES
    own = lax.axis_index("dp") // 2
    slices = w_gate_up[0].reshape(rows, 2, chips, blocks, LANES).transpose(2, 0, 3, 1, 4)
    slices = slices.reshape(chips, rows, ff2 // chips)
    return swap_chips(
        [lax.dynamic_index_in_dim(slices, own ^ step, 0, keepdims=False) for step in range(chips)]
    )


def chip_slices_back(grads):
    chips, rows, hidden2 = grads.shape
    own = lax.axis_index("dp") // 2
    got = swap_chips([grads[step] for step in range(chips)])
    whole = jnp.zeros((chips, rows, hidden2), jnp.bfloat16)
    for step in range(chips):
        whole = lax.dynamic_update_index_in_dim(whole, got[step], own ^ step, 0)
    blocks = hidden2 // 2 // LANES
    whole = whole.reshape(chips, rows, blocks, 2, LANES).transpose(1, 3, 0, 2, 4)
    return whole.reshape(1, rows, chips * hidden2).astype(jnp.float32)


def expert_step(gate_up_w, down_w, rows, d_rows_out):
    ff = down_w.shape[0]
    gate_up = jnp.dot(rows, gate_up_w, preferred_element_type=jnp.float32)
    gate = gate_up[:, :ff]
    upward = gate_up[:, ff:]
    sigmoid = jax.nn.sigmoid(gate)
    activated = (gate * sigmoid * upward).astype(jnp.bfloat16)
    out = jnp.dot(activated, down_w, preferred_element_type=jnp.float32).astype(jnp.bfloat16)
    d_activated = contract_last(d_rows_out, down_w)
    grad_down = contract_first(activated, d_rows_out)
    d_gate = d_activated * upward * sigmoid * (1.0 + gate * (1.0 - sigmoid))
    d_up = d_activated * gate * sigmoid
    d_gate_up = jnp.concatenate([d_gate, d_up], axis=1).astype(jnp.bfloat16)
    d_rows = contract_last(d_gate_up, gate_up_w).astype(jnp.bfloat16)
    grad_gate_up = contract_first(rows, d_gate_up)
    return out, d_rows, grad_gate_up, grad_down


def experts_split_hidden(w_gate_up, w_down, rows, d_rows_out):
    out, d_rows, grad_gate_up, grad_down = experts_call(
        rows, d_rows_out, chip_slices(w_gate_up), w_down[0]
    )
    return out, d_rows, chip_slices_back(grad_gate_up), grad_down[None]


def experts_gather_weights(w_gate_up, w_down, rows, d_rows_out):
    gate_up_w = lax.all_gather(w_gate_up, "dp", axis=1, tiled=True)[0]
    down_w = lax.all_gather(w_down, "dp", axis=1, tiled=True)[0]
    shape = rows.shape
    flat = (-1, shape[2])
    rows = exchange_experts(rows).reshape(flat)
    d_rows_out = exchange_experts(d_rows_out).reshape(flat)
    out, d_rows, grad_gate_up, grad_down = expert_step(gate_up_w, down_w, rows, d_rows_out)
    out = exchange_experts(out.reshape(shape))
    d_rows = exchange_experts(d_rows.reshape(shape))
    grad_gate_up = lax.psum_scatter(
        grad_gate_up.astype(jnp.bfloat16), "dp", scatter_dimension=0, tiled=True
    )
    grad_down = lax.psum_scatter(
        grad_down.astype(jnp.bfloat16), "dp", scatter_dimension=0, tiled=True
    )
    return (
        out,
        d_rows,
        grad_gate_up.astype(jnp.float32)[None],
        grad_down.astype(jnp.float32)[None],
    )


def on_device(
    tokens,
    w_qkv,
    w_out,
    attention_norm_gain,
    gain_ffn,
    w_router,
    w_gate_up,
    w_down,
    lengths,
    routes,
    order,
    cotangent,
):
    group_size = lax.axis_size("expert")
    dp_size = lax.axis_size("dp")
    tok_dev = tokens.shape[0]
    seq_len = tok_dev * group_size
    width = tokens.shape[1]
    top_count = routes.shape[1]
    capacity = tok_dev * top_count // group_size
    slots = group_size * capacity
    head_size = HEAD_DIM
    local_width = w_qkv.shape[2]
    heads_local = local_width // head_size
    tokens_all = lax.all_gather(tokens, "expert", axis=0, tiled=True)
    small = jnp.concatenate(
        [attention_norm_gain[:, None], gain_ffn[:, None], w_router], axis=1
    )
    small_full = lax.all_gather(small, "dp", axis=0, tiled=True)
    qkv_full = lax.all_gather(w_qkv, "dp", axis=1, tiled=True)
    out_full = lax.all_gather(w_out, "dp", axis=1, tiled=True)
    first_norm_gain = small_full[:, 0].astype(jnp.float32)
    gain_two = small_full[:, 1].astype(jnp.float32)
    router_full = small_full[:, 2:]

    own_start = lax.axis_index("expert") * tok_dev
    own_position = own_start + jnp.arange(tok_dev, dtype=jnp.int32)
    live_own = own_position < lengths[0]
    live_rows = live_own.astype(jnp.float32)[:, None]
    split = dp_size == 8 and group_size == 4
    first_expert = lax.axis_index("expert") if split else 0
    target, kept_pair = slot_table(routes, order, live_own, capacity, first_expert, group_size)
    slot_ids = jnp.arange(slots, dtype=jnp.int32)
    pair_hits = (slot_ids[:, None, None] == target[None]) & kept_pair[None]
    select = jnp.sum(pair_hits.astype(jnp.float32), axis=2).astype(jnp.bfloat16)

    inputs_float = tokens.astype(jnp.float32)
    input_normalized_hat, first_inverse_rms = normalize(inputs_float)
    hat_all, _ = normalize(tokens_all.astype(jnp.float32))
    whole = (hat_all * first_norm_gain).astype(jnp.bfloat16)
    cosine, sine = rotary_tables(seq_len, head_size)
    projected = jnp.einsum("td,cde->cte", whole, qkv_full, preferred_element_type=jnp.float32)
    query = rotate(projected[0].reshape(seq_len, heads_local, head_size), cosine, sine).astype(
        jnp.bfloat16
    )
    key_rows = rotate(projected[1].reshape(seq_len, heads_local, head_size), cosine, sine).astype(
        jnp.bfloat16
    )
    value = projected[2].astype(jnp.bfloat16).reshape(seq_len, heads_local, head_size)
    position = jnp.arange(seq_len, dtype=jnp.int32)
    live_all = position < lengths[0]
    allowed = (position[None, :] <= position[:, None]) & live_all[None, :]
    scores = masked_scores(query, key_rows, allowed)
    top_score = jnp.max(scores, axis=-1, keepdims=True)
    exponent = jnp.exp(scores - top_score)
    row_total = jnp.sum(exponent, axis=-1, keepdims=True)
    probs = exponent / row_total
    log_total = top_score + jnp.log(row_total)
    probs_low = probs.astype(jnp.bfloat16)
    attended = jnp.einsum("hqk,khd->qhd", probs_low, value, preferred_element_type=jnp.float32)
    attended = attended.reshape(seq_len, local_width).astype(jnp.bfloat16)
    attn_part = jnp.dot(attended, out_full, preferred_element_type=jnp.float32)
    attn_own = lax.psum_scatter(
        attn_part.astype(jnp.bfloat16), "expert", scatter_dimension=0, tiled=True
    ).astype(jnp.float32)
    resid = inputs_float + attn_own
    hhat, inverse_two = normalize(resid)
    hidden_in = (hhat * gain_two).astype(jnp.bfloat16)
    sent = jnp.dot(select, hidden_in, preferred_element_type=jnp.float32).astype(jnp.bfloat16)

    logits = jnp.dot(hidden_in, router_full, preferred_element_type=jnp.float32)
    chosen = jnp.take_along_axis(logits, routes, axis=1)
    gates = jax.nn.softmax(chosen, axis=1)
    d_out = live_rows * cotangent.astype(jnp.float32)
    d_back = jnp.zeros((slots, width), jnp.float32)
    for index in range(top_count):
        weighted = (gates[:, index : index + 1] * d_out).astype(jnp.bfloat16)
        d_back = d_back + jnp.dot(
            pair_hits[:, :, index].astype(jnp.bfloat16),
            weighted,
            preferred_element_type=jnp.float32,
        )
    d_back = d_back.astype(jnp.bfloat16)
    experts = experts_split_hidden if split else experts_gather_weights
    blocked = (group_size, capacity, width)
    returned, d_sent, grad_gate_up, grad_down = experts(
        w_gate_up, w_down, sent.reshape(blocked), d_back.reshape(blocked)
    )
    returned = returned.reshape(slots, width)
    d_sent = d_sent.reshape(slots, width)

    moe = jnp.zeros_like(resid)
    d_gates_list = []
    for index in range(top_count):
        one_hot = pair_hits[:, :, index].astype(jnp.bfloat16)
        picked = contract_first(one_hot, returned)
        d_gates_list.append(jnp.sum(d_out * picked, axis=-1))
        moe = moe + gates[:, index : index + 1] * picked
    output = (live_rows * (resid + moe)).astype(jnp.bfloat16)
    d_gates = jnp.stack(d_gates_list, axis=1)
    d_hidden = contract_first(select, d_sent)
    d_chosen = gates * (d_gates - jnp.sum(gates * d_gates, axis=1, keepdims=True))
    expert_ids = jnp.arange(group_size, dtype=jnp.int32)
    route_hits = (routes[:, :, None] == expert_ids[None, None, :]).astype(jnp.float32)
    d_logits = jnp.sum(route_hits * d_chosen[:, :, None], axis=1)
    router_f = router_full.astype(jnp.float32)
    d_hidden = d_hidden + jnp.dot(
        d_logits, router_f.T, precision=HIGH, preferred_element_type=jnp.float32
    )
    router_part = jnp.dot(
        hidden_in.astype(jnp.float32).T,
        d_logits,
        precision=HIGH,
        preferred_element_type=jnp.float32,
    )
    gain_two_part = jnp.sum(d_hidden * hhat, axis=0)
    scaled_two = d_hidden * gain_two
    d_resid = d_out + inverse_two * (
        scaled_two - hhat * jnp.mean(scaled_two * hhat, axis=-1, keepdims=True)
    )
    d_attn = d_resid.astype(jnp.bfloat16)
    whole_grad = lax.all_gather(d_attn, "expert", axis=0, tiled=True)
    d_attended = contract_last(whole_grad, out_full).astype(jnp.bfloat16)
    out_part = contract_first(attended, whole_grad)
    grad_out = lax.psum_scatter(
        out_part.astype(jnp.bfloat16), "dp", scatter_dimension=1, tiled=True
    ).astype(jnp.float32)
    d_heads = d_attended.reshape(seq_len, heads_local, head_size)
    probs = jnp.exp(masked_scores(query, key_rows, allowed) - log_total)
    probs_low = probs.astype(jnp.bfloat16)
    d_value = jnp.einsum(
        "hqk,qhd->khd", probs_low, d_heads, preferred_element_type=jnp.float32
    ).astype(jnp.bfloat16)
    d_probs = jnp.einsum("qhd,khd->hqk", d_heads, value, preferred_element_type=jnp.float32)
    row_delta = jnp.sum(probs * d_probs, axis=-1, keepdims=True)
    d_scores = (probs * (d_probs - row_delta)).astype(jnp.bfloat16)
    scale = head_size ** (-0.5)
    d_query = (
        jnp.einsum("hqk,khd->qhd", d_scores, key_rows, preferred_element_type=jnp.float32) * scale
    )
    d_key = jnp.einsum("hqk,qhd->khd", d_scores, query, preferred_element_type=jnp.float32) * scale
    d_query_pre = (
        rotate_back(d_query, cosine, sine).reshape(seq_len, local_width).astype(jnp.bfloat16)
    )
    d_key_pre = rotate_back(d_key, cosine, sine).reshape(seq_len, local_width).astype(jnp.bfloat16)
    d_projected = jnp.stack([d_query_pre, d_key_pre, d_value.reshape(seq_len, local_width)])
    d_normed_part = jnp.einsum(
        "cte,cde->td", d_projected, qkv_full, preferred_element_type=jnp.float32
    )
    grad_normalized = lax.psum_scatter(
        d_normed_part.astype(jnp.bfloat16), "expert", scatter_dimension=0, tiled=True
    ).astype(jnp.float32)
    qkv_part = jnp.einsum("td,cte->cde", whole, d_projected, preferred_element_type=jnp.float32)
    grad_qkv = lax.psum_scatter(
        qkv_part.astype(jnp.bfloat16), "dp", scatter_dimension=1, tiled=True
    ).astype(jnp.float32)
    first_gain_part = jnp.sum(d_normed_part * hat_all, axis=0)
    first_scaled_input = grad_normalized * first_norm_gain
    grad_tokens = d_resid + first_inverse_rms * (
        first_scaled_input
        - input_normalized_hat
        * jnp.mean(first_scaled_input * input_normalized_hat, axis=-1, keepdims=True)
    )
    small_part = jnp.concatenate(
        [first_gain_part[None], gain_two_part[None], router_part.T], axis=0
    )
    small_sum = lax.psum(small_part, ("dp", "expert"))
    own_rows = width // dp_size
    small_own = lax.dynamic_slice_in_dim(
        small_sum, lax.axis_index("dp") * own_rows, own_rows, axis=1
    )
    return (
        output,
        grad_tokens.astype(jnp.bfloat16),
        grad_qkv,
        grad_out,
        small_own[0],
        small_own[1],
        small_own[2:].T,
        grad_gate_up,
        grad_down,
    )


def solution(mesh):
    placed = (
        P(("dp", "expert"), None),
        P(None, "dp", "expert"),
        P("expert", "dp"),
        P("dp"),
        P("dp"),
        P("dp", None),
        P("expert", "dp", None),
        P("expert", "dp", None),
        P("dp"),
        P(("dp", "expert"), None),
        P(("dp", "expert")),
        P(("dp", "expert"), None),
    )
    return jax.shard_map(
        on_device,
        mesh=mesh,
        in_specs=placed,
        out_specs=(
            P(("dp", "expert"), None),
            P(("dp", "expert"), None),
            P(None, "dp", "expert"),
            P("expert", "dp"),
            P("dp"),
            P("dp"),
            P("dp", None),
            P("expert", "dp", None),
            P("expert", "dp", None),
        ),
        check_vma=False,
    )
```

```python
import functools

import jax
import jax.numpy as jnp
from jax import lax
from jax.experimental import pallas as pl
from jax.experimental.pallas import tpu as pltpu
from jax.sharding import PartitionSpec as P

HEAD_DIM = 128
FF = 5632


NORM_EPSILON = 1e-05
NEGATIVE = -1e30
THETA = 10000.0
HIGH = lax.Precision.HIGHEST
MESH_ID = pl.DeviceIdType.MESH
LANES = 128


def remote(src, dst, send_sem, recv_sem, peer):
    return pltpu.make_async_remote_copy(
        src_ref=src,
        dst_ref=dst,
        send_sem=send_sem,
        recv_sem=recv_sem,
        device_id=peer,
        device_id_type=MESH_ID,
    )


def greet(peers):
    barrier = pltpu.get_barrier_semaphore()
    for peer in peers:
        pl.semaphore_signal(barrier, inc=1, device_id=peer, device_id_type=MESH_ID)
    pl.semaphore_wait(barrier, len(peers))


def dot_nn(left, right):
    return jnp.dot(left, right, preferred_element_type=jnp.float32)


def dot_nt(left, right):
    return lax.dot_general(
        left, right, (((1,), (1,)), ((), ())), preferred_element_type=jnp.float32
    )


def experts_kernel(
    group,
    sent,
    d_back,
    w_own,
    w_x,
    w_y,
    w_diag,
    down_own,
    ret,
    d_ret,
    grad_gate_up,
    grad_down,
    w_buf,
    down_buf,
    rows_buf,
    gate_buf,
    act_buf,
    part_buf,
    half_x,
    half_y,
    full_x,
    full_y,
    other_gate,
    other_down,
    stage,
    ag_sems,
    rs_sems,
    weight_sems,
    local_sems,
    grad_sems,
):
    cap, width = sent.shape[1], sent.shape[2]
    half = cap // 2
    piece = w_own.shape[0]
    hidden2 = w_own.shape[1]
    hidden = hidden2 // 2
    down_rows = down_own.shape[0]
    chunk = 4 * cap
    total = group * chunk

    index = lax.axis_index("dp")
    place = lax.axis_index("expert")
    core = index % 2
    at_x = (index // 2) % 2
    at_y = index // 4
    partner = {"dp": at_y * 4 + at_x * 2 + (1 - core)}
    along_x = {"dp": at_y * 4 + (1 - at_x) * 2 + core}
    along_y = {"dp": (1 - at_y) * 4 + at_x * 2 + core}
    chips = [
        at_y * 2 + at_x,
        at_y * 2 + (1 - at_x),
        (1 - at_y) * 2 + at_x,
        (1 - at_y) * 2 + (1 - at_x),
    ]

    def ahead(k):
        return {"expert": (place + k) % group}

    def behind(k):
        return {"expert": (place + group - k) % group}

    greet([partner, along_x, along_y] + [ahead(k) for k in range(1, group)])

    def block(t, k, r, start=0, size=None):
        size = cap if size is None else size
        return rows_buf.at[t, pl.ds((k * 4 + r) * cap + start, size), :]

    def part(t, k, r, start=0, size=None):
        size = cap if size is None else size
        return part_buf.at[t, pl.ds((k * 4 + r) * cap + start, size), :]

    def ag(kind, t, k):
        return ag_sems.at[0, kind, t, k], ag_sems.at[1, kind, t, k]

    def rs(kind, t, k):
        return rs_sems.at[0, kind, t, k], rs_sems.at[1, kind, t, k]

    sources = (sent, d_back)
    results = (ret, d_ret)

    def z_copy(t, k):
        return remote(sources[t].at[k], block(t, k, 0), *ag(0, t, k), ahead(k))

    def own_copy(t):
        return pltpu.make_async_copy(sources[t].at[0], block(t, 0, 0), local_sems.at[t])

    def x_copy(t, k):
        return remote(block(t, k, 0), block(t, k, 1), *ag(1, t, k), along_x)

    def y_copy(t, k):
        return remote(block(t, k, 0), block(t, k, 2), *ag(2, t, k), along_y)

    def a_copy(t, k):
        return remote(block(t, k, 2, 0, half), block(t, k, 3, 0, half), *ag(3, t, k), along_x)

    def b_copy(t, k):
        return remote(
            block(t, k, 1, half, half), block(t, k, 3, half, half), *ag(4, t, k), along_y
        )

    def spread(t, k):
        if k == 0:
            own_copy(t).wait()
        else:
            z_copy(t, k).wait_recv()
        x_copy(t, k).start()
        y_copy(t, k).start()

    def relay(t, k):
        y_copy(t, k).wait_recv()
        a_copy(t, k).start()
        x_copy(t, k).wait_recv()
        b_copy(t, k).start()

    def arrived(t, k):
        a_copy(t, k).wait_recv()
        b_copy(t, k).wait_recv()

    def half_x_copy(t, k):
        return remote(part(t, k, 3, 0, half), half_x.at[t, k], *rs(0, t, k), along_x)

    def half_y_copy(t, k):
        return remote(part(t, k, 3, half, half), half_y.at[t, k], *rs(1, t, k), along_y)

    def full_x_copy(t, k):
        return remote(part(t, k, 1), full_x.at[t, k], *rs(2, t, k), along_x)

    def full_y_copy(t, k):
        return remote(part(t, k, 2), full_y.at[t, k], *rs(3, t, k), along_y)

    def back_copy(t, k):
        return remote(part(t, k, 0), results[t].at[k], *rs(4, t, k), behind(k))

    def keep_copy(t):
        return pltpu.make_async_copy(part(t, 0, 0), results[t].at[0], local_sems.at[2 + t])

    def halves_out(t, k):
        half_x_copy(t, k).start()
        half_y_copy(t, k).start()

    def add_into(target, *others):
        value = target[...].astype(jnp.float32)
        for other in others:
            value = value + other[...].astype(jnp.float32)
        target[...] = value.astype(jnp.bfloat16)

    def fulls_out(t, k):
        half_x_copy(t, k).wait_recv()
        add_into(part(t, k, 2, 0, half), half_x.at[t, k])
        full_y_copy(t, k).start()
        half_y_copy(t, k).wait_recv()
        add_into(part(t, k, 1, half, half), half_y.at[t, k])
        full_x_copy(t, k).start()

    def home(t, k):
        full_x_copy(t, k).wait_recv()
        full_y_copy(t, k).wait_recv()
        add_into(part(t, k, 0), full_x.at[t, k], full_y.at[t, k])
        if k == 0:
            keep_copy(t).start()
        else:
            back_copy(t, k).start()

    pieces = (w_own, w_x, w_y, w_diag)

    def w_rows(r, which):
        return w_buf.at[pl.ds(pl.multiple_of((chips[r] * 2 + which) * piece, piece), piece), :]

    def w_share(r):
        return remote(
            pieces[r], w_rows(r, core), weight_sems.at[0, r], weight_sems.at[1, r], partner
        )

    def w_share_in(r):
        return remote(
            pieces[r], w_rows(r, 1 - core), weight_sems.at[0, r], weight_sems.at[1, r], partner
        )

    def w_keep(r):
        return pltpu.make_async_copy(pieces[r], w_rows(r, core), local_sems.at[4 + r])

    def down_at(which):
        return down_buf.at[pl.ds(pl.multiple_of(which * down_rows, down_rows), down_rows), :]

    def down_share():
        return remote(
            down_own, down_at(core), weight_sems.at[0, 4], weight_sems.at[1, 4], partner
        )

    down_keep = pltpu.make_async_copy(down_own, down_at(core), local_sems.at[8])

    def forward(k):
        base = k * chunk

        def tile(first, count):
            gate_cols = pl.ds(pl.multiple_of(first * LANES, LANES), count * LANES)
            up_cols = pl.ds(pl.multiple_of(hidden + first * LANES, LANES), count * LANES)
            rows = rows_buf[0, base : base + chunk, :]
            if count == 1:
                weights = jnp.concatenate([w_buf[:, gate_cols], w_buf[:, up_cols]], axis=1)
                both = dot_nn(rows, weights)
                gate = both[:, :LANES]
                up = both[:, LANES:]
            else:
                gate = dot_nn(rows, w_buf[:, gate_cols])
                up = dot_nn(rows, w_buf[:, up_cols])
            sigmoid = 1.0 / (1.0 + jnp.exp(-gate))
            gate_buf[base : base + chunk, gate_cols] = gate.astype(jnp.bfloat16)
            gate_buf[base : base + chunk, up_cols] = up.astype(jnp.bfloat16)
            act_buf[base : base + chunk, gate_cols] = (gate * sigmoid * up).astype(jnp.bfloat16)

        def pair(j, carry):
            tile(2 * j, 2)
            return carry

        blocks = hidden // LANES
        lax.fori_loop(0, blocks // 2, pair, 0)
        if blocks % 2:
            tile(blocks - 1, 1)

        def out_tile(j, carry):
            cols = pl.ds(pl.multiple_of(j * 2 * LANES, 2 * LANES), 2 * LANES)
            out = dot_nn(act_buf[base : base + chunk, :], down_buf[:, cols])
            part_buf[0, base : base + chunk, cols] = out.astype(jnp.bfloat16)
            return carry

        lax.fori_loop(0, width // (2 * LANES), out_tile, 0)

    def backward(k):
        base = k * chunk

        def tile(first, count):
            rows = pl.ds(pl.multiple_of(first * LANES, LANES), count * LANES)
            d_act = dot_nt(rows_buf[1, base : base + chunk, :], down_buf[rows, :])
            up_rows = pl.ds(pl.multiple_of(hidden + first * LANES, LANES), count * LANES)
            gate = gate_buf[base : base + chunk, rows].astype(jnp.float32)
            up = gate_buf[base : base + chunk, up_rows].astype(jnp.float32)
            sigmoid = 1.0 / (1.0 + jnp.exp(-gate))
            scaled = d_act * sigmoid
            d_gate = scaled * up * (1.0 + gate * (1.0 - sigmoid))
            gate_buf[base : base + chunk, rows] = d_gate.astype(jnp.bfloat16)
            gate_buf[base : base + chunk, up_rows] = (scaled * gate).astype(jnp.bfloat16)

        def pair(j, carry):
            tile(2 * j, 2)
            return carry

        blocks = hidden // LANES
        lax.fori_loop(0, blocks // 2, pair, 0)
        if blocks % 2:
            tile(blocks - 1, 1)

        def out_tile(j, carry):
            cols = pl.ds(pl.multiple_of(j * 2 * LANES, 2 * LANES), 2 * LANES)
            out = dot_nt(gate_buf[base : base + chunk, :], w_buf[cols, :])
            part_buf[1, base : base + chunk, cols] = out.astype(jnp.bfloat16)
            return carry

        lax.fori_loop(0, width // (2 * LANES), out_tile, 0)

    w_share(0).start()
    w_keep(0).start()
    own_copy(0).start()
    for k in range(1, group):
        z_copy(0, k).start()
    for r in range(1, 4):
        w_share(r).start()
        w_keep(r).start()
    down_share().start()
    down_keep.start()
    own_copy(1).start()

    spread(0, 0)
    spread(0, 1)
    relay(0, 0)
    for k in range(1, group):
        z_copy(1, k).start()
    spread(0, 2)
    relay(0, 1)
    arrived(0, 0)
    for r in range(4):
        w_keep(r).wait()
        w_share_in(r).wait_recv()
    down_keep.wait()
    down_share().wait_recv()
    forward(0)
    spread(0, 3)
    relay(0, 2)
    arrived(0, 1)
    forward(1)
    spread(1, 0)
    relay(0, 3)
    arrived(0, 2)
    forward(2)
    spread(1, 1)
    relay(1, 0)
    arrived(0, 3)
    forward(3)
    spread(1, 2)
    relay(1, 1)
    arrived(1, 0)
    backward(0)
    spread(1, 3)
    relay(1, 2)
    arrived(1, 1)
    halves_out(0, 0)
    halves_out(0, 1)
    backward(1)
    relay(1, 3)
    arrived(1, 2)
    halves_out(0, 2)
    halves_out(0, 3)
    fulls_out(0, 0)
    fulls_out(0, 1)
    halves_out(1, 0)
    backward(2)
    arrived(1, 3)
    fulls_out(0, 2)
    fulls_out(0, 3)
    halves_out(1, 1)
    home(0, 0)
    home(0, 1)
    backward(3)
    halves_out(1, 2)
    halves_out(1, 3)
    fulls_out(1, 0)
    fulls_out(1, 1)

    act_t = down_buf.at[:, pl.ds(0, total)]
    rows_t = down_buf.at[pl.ds(0, piece), pl.ds(total, total)]
    send_down = w_buf.at[pl.ds(4 * piece, down_rows), pl.ds(0, width)]

    def send_gate(r):
        return w_buf.at[pl.ds(r * piece, piece), :]

    def turn(j, carry):
        cols = pl.ds(pl.multiple_of(j * LANES, LANES), LANES)
        act_t[cols, :] = act_buf[:, cols].T
        return carry

    lax.fori_loop(0, hidden // LANES, turn, 0)

    def down_grad(which, j):
        cols = pl.ds(pl.multiple_of(j * 2 * LANES, 2 * LANES), 2 * LANES)
        rows = pl.ds(pl.multiple_of(which * down_rows, down_rows), down_rows)
        return cols, dot_nn(act_t[rows, :], rows_buf[1, :, cols])

    def down_for_partner(j, carry):
        cols, value = down_grad(1 - core, j)
        send_down[:, cols] = value.astype(jnp.bfloat16)
        return carry

    tiles = width // (2 * LANES)
    lax.fori_loop(0, tiles, down_for_partner, 0)
    down_send = remote(
        send_down, other_down, grad_sems.at[0, 4], grad_sems.at[1, 4], partner
    )
    down_send.start()
    home(0, 2)
    home(0, 3)
    fulls_out(1, 2)
    fulls_out(1, 3)

    def gate_grad(r, which, store):
        start = pl.multiple_of((chips[r] * 2 + which) * piece, piece)
        rows_t[...] = rows_buf[0, :, pl.ds(start, piece)].T

        def tile(j, carry):
            cols = pl.ds(pl.multiple_of(j * 2 * LANES, 2 * LANES), 2 * LANES)
            store(cols, dot_nn(rows_t[...], gate_buf[:, cols]))
            return carry

        lax.fori_loop(0, hidden2 // (2 * LANES), tile, 0)

    def gate_send(r):
        return remote(
            send_gate(r), other_gate.at[r], grad_sems.at[0, r], grad_sems.at[1, r], partner
        )

    for r in range(4):
        target = send_gate(r)

        def store(cols, value, target=target):
            target[:, cols] = value.astype(jnp.bfloat16)

        gate_grad(r, 1 - core, store)
        gate_send(r).start()
        if r == 0:
            home(1, 0)
            home(1, 1)
        if r == 1:
            home(1, 2)
        if r == 2:
            home(1, 3)

    down_send.wait_recv()

    def stage_copy(j):
        cols = pl.ds(pl.multiple_of(j * 2 * LANES, 2 * LANES), 2 * LANES)
        return pltpu.make_async_copy(
            stage.at[j % 2], grad_down.at[:, cols], grad_sems.at[2, j % 2]
        )

    def down_for_self(j, carry):
        cols, value = down_grad(core, j)

        @pl.when(j >= 2)
        def _():
            stage_copy(j - 2).wait()

        stage[j % 2] = value + other_down[:, cols].astype(jnp.float32)
        stage_copy(j).start()
        return carry

    lax.fori_loop(0, tiles, down_for_self, 0)

    def gate_out(r):
        return pltpu.make_async_copy(other_gate.at[r], grad_gate_up.at[r], grad_sems.at[2, 2 + r])

    for r in range(4):
        gate_send(r).wait_recv()
        target = other_gate.at[r]

        def store(cols, value, target=target):
            target[:, cols] = (value + target[:, cols].astype(jnp.float32)).astype(jnp.bfloat16)

        gate_grad(r, core, store)
        gate_out(r).start()

    stage_copy(tiles - 2).wait()
    stage_copy(tiles - 1).wait()
    for r in range(4):
        gate_out(r).wait()
        gate_send(r).wait_send()
        w_share(r).wait_send()
    down_share().wait_send()
    down_send.wait_send()
    for t in range(2):
        keep_copy(t).wait()
        for k in range(group):
            x_copy(t, k).wait_send()
            y_copy(t, k).wait_send()
            a_copy(t, k).wait_send()
            b_copy(t, k).wait_send()
            half_x_copy(t, k).wait_send()
            half_y_copy(t, k).wait_send()
            full_x_copy(t, k).wait_send()
            full_y_copy(t, k).wait_send()
            if k > 0:
                z_copy(t, k).wait_send()
                back_copy(t, k).wait_send()
                back_copy(t, k).wait_recv()


def experts_call(sent, d_back, pieces, down_own):
    group, cap, width = sent.shape
    piece, hidden2 = pieces[0].shape
    hidden = hidden2 // 2
    down_rows = down_own.shape[0]
    chunk = 4 * cap
    total = group * chunk
    low = jnp.bfloat16
    anywhere = pl.BlockSpec(memory_space=pl.ANY)
    flops = 2 * total * width * hidden * 9
    moved = 2 * (4 * piece * hidden2 * 2 + down_rows * width * 3)
    return pl.pallas_call(
        functools.partial(experts_kernel, group),
        out_shape=(
            jax.ShapeDtypeStruct((group, cap, width), low),
            jax.ShapeDtypeStruct((group, cap, width), low),
            jax.ShapeDtypeStruct((4, piece, hidden2), low),
            jax.ShapeDtypeStruct((down_rows, width), jnp.float32),
        ),
        in_specs=[anywhere] * 7,
        out_specs=(anywhere,) * 4,
        scratch_shapes=[
            pltpu.VMEM((width, hidden2), low),
            pltpu.VMEM((hidden, width), low),
            pltpu.VMEM((2, total, width), low),
            pltpu.VMEM((total, hidden2), low),
            pltpu.VMEM((total, hidden), low),
            pltpu.VMEM((2, total, width), low),
            pltpu.VMEM((2, group, cap // 2, width), low),
            pltpu.VMEM((2, group, cap // 2, width), low),
            pltpu.VMEM((2, group, cap, width), low),
            pltpu.VMEM((2, group, cap, width), low),
            pltpu.VMEM((4, piece, hidden2), low),
            pltpu.VMEM((down_rows, width), low),
            pltpu.VMEM((2, down_rows, 2 * LANES), jnp.float32),
            pltpu.SemaphoreType.DMA((2, 5, 2, group)),
            pltpu.SemaphoreType.DMA((2, 5, 2, group)),
            pltpu.SemaphoreType.DMA((2, 5)),
            pltpu.SemaphoreType.DMA((9,)),
            pltpu.SemaphoreType.DMA((3, 6)),
        ],
        compiler_params=pltpu.CompilerParams(
            collective_id=1, has_side_effects=True, vmem_limit_bytes=67043328
        ),
        cost_estimate=pl.CostEstimate(flops=flops, bytes_accessed=moved, transcendentals=0),
        name="experts",
    )(sent, d_back, *pieces, down_own)


def rotary_tables(length_total, head_size):
    position = jnp.arange(length_total, dtype=jnp.float32)
    frequency = THETA ** (-(jnp.arange(head_size // 2, dtype=jnp.float32) * 2.0 / head_size))
    angles = position[:, None] * frequency[None, :]
    return (jnp.cos(angles)[:, None, :], jnp.sin(angles)[:, None, :])


def rotate(values, cosine, sine):
    half_size = values.shape[-1] // 2
    first = values[..., :half_size]
    second = values[..., half_size:]
    return jnp.concatenate(
        [first * cosine - second * sine, second * cosine + first * sine], axis=-1
    )


def rotate_back(grad_rows, cosine, sine):
    half_size = grad_rows.shape[-1] // 2
    first = grad_rows[..., :half_size]
    second = grad_rows[..., half_size:]
    return jnp.concatenate(
        [first * cosine + second * sine, second * cosine - first * sine], axis=-1
    )


def slot_table(routes, order, valid, capacity, first_expert, experts):
    row_count = routes.shape[0]
    top_count = routes.shape[1]
    pair_rank = order[:, None] + row_count * jnp.arange(top_count, dtype=jnp.int32)[None, :]
    flat_rank = pair_rank.reshape(-1)
    flat_expert = routes.reshape(-1)
    flat_valid = jnp.broadcast_to(valid[:, None], routes.shape).reshape(-1)
    earlier = (
        (flat_rank[None, :] < flat_rank[:, None])
        & (flat_expert[None, :] == flat_expert[:, None])
        & flat_valid[None, :]
    )
    slot_index = jnp.sum(earlier.astype(jnp.int32), axis=1).reshape(row_count, top_count)
    kept_pair = valid[:, None] & (slot_index < capacity)
    place = (routes + experts - first_expert) % experts
    target = place * capacity + jnp.minimum(slot_index, capacity - 1)
    return (target, kept_pair)


def masked_scores(query, key_rows, allowed):
    scale = query.shape[-1] ** (-0.5)
    raw = jnp.einsum("qhd,khd->hqk", query, key_rows, preferred_element_type=jnp.float32) * scale
    return jnp.where(allowed[None], raw, NEGATIVE)


def contract_first(left, right):
    return lax.dot_general(
        left, right, (((0,), (0,)), ((), ())), preferred_element_type=jnp.float32
    )


def contract_last(left, right):
    return lax.dot_general(
        left, right, (((1,), (1,)), ((), ())), preferred_element_type=jnp.float32
    )


def normalize(rows):
    inverse = lax.rsqrt(jnp.mean(rows * rows, axis=-1, keepdims=True) + NORM_EPSILON)
    return rows * inverse, inverse


def exchange_experts(blocks):
    return lax.all_to_all(blocks, "expert", split_axis=0, concat_axis=0, tiled=True)


def line_order(place, step):
    upper = place // 2
    low = place * (1 - upper) + (3 - place) * upper
    first = 1 - (step + 1) // 2
    block = step + first * (1 - low) + (1 - first)
    return block * (1 - upper) + (3 - block) * upper


def rotated(grad, cosine, sine):
    return grad * cosine + pltpu.roll(grad, grad.shape[1] // 2, 1) * sine


def attention_back_kernel(
    heads,
    length,
    d_attn,
    tokens_all,
    inverse_all,
    whole,
    w_out,
    w_qkv,
    query,
    key_rows,
    value,
    attended,
    log_total,
    cosine,
    sine,
    small_part,
    gate_grads,
    grad_normed,
    grad_weights,
    small_out,
    gate_got,
    da_buf,
    tokens_buf,
    inverse_buf,
    whole_buf,
    w_out_buf,
    w_qkv_buf,
    query_buf,
    key_buf,
    value_buf,
    attended_buf,
    log_buf,
    cosine_buf,
    sine_buf,
    d_key_acc,
    d_value_acc,
    d_proj,
    normed_part,
    from_left,
    from_right,
    send_pair,
    recv_pair,
    own_part,
    half_x,
    half_y,
    full_x,
    full_y,
    small_buf,
    small_recv,
    small_z,
    keep_buf,
    load_sems,
    line_sems,
    sum_sems,
    pair_sems,
    ring_sems,
    small_sems,
    gate_sems,
):
    tok, width = d_attn.shape
    seq_len = tokens_all.shape[0]
    group = seq_len // tok
    local_width = w_out.shape[0]
    head_size = local_width // heads
    piece = own_part.shape[1]
    half = piece // 2
    scale = head_size**-0.5

    index = lax.axis_index("dp")
    place = lax.axis_index("expert")
    core = index % 2
    at_x = (index // 2) % 2
    at_y = index // 4
    partner = {"dp": at_y * 4 + at_x * 2 + (1 - core)}
    along_x = {"dp": at_y * 4 + (1 - at_x) * 2 + core}
    along_y = {"dp": (1 - at_y) * 4 + at_x * 2 + core}
    over = {"dp": (1 - at_y) * 4 + (1 - at_x) * 2 + core}
    parts = width // piece

    def chip(r):
        step_y = r // 2
        step_x = r % 2
        return (at_y + step_y - 2 * at_y * step_y) * 2 + (at_x + step_x - 2 * at_x * step_x)

    def ring_peer(k):
        return {"dp": (index + k) % parts}

    def line_peer(k):
        return {"expert": (place + k) % group}

    right = {"expert": (place + 1) % group}
    left = {"expert": (place + group - 1) % group}

    loads = [
        pltpu.make_async_copy(source, target, load_sems.at[number])
        for number, (source, target) in enumerate(
            [
                (w_out, w_out_buf),
                (query, query_buf),
                (key_rows, key_buf),
                (value, value_buf),
                (log_total, log_buf),
                (cosine, cosine_buf),
                (sine, sine_buf),
                (w_qkv, w_qkv_buf),
                (tokens_all, tokens_buf),
                (inverse_all, inverse_buf),
                (whole, whole_buf),
                (attended, attended_buf),
                (small_part, small_buf),
                (gate_grads.at[0], keep_buf),
            ]
        )
    ]
    early = 7
    for load in loads[:early]:
        load.start()

    greet([ring_peer(k) for k in range(1, parts)] + [line_peer(k) for k in range(1, group)])

    def rows_of(block):
        return pl.ds(pl.multiple_of(block * tok, tok), tok)

    own_load = pltpu.make_async_copy(d_attn, da_buf.at[rows_of(place)], load_sems.at[14])
    own_load.start()

    def own_right():
        return remote(
            d_attn, da_buf.at[rows_of(place)], line_sems.at[0, place], line_sems.at[2, place], right
        )

    def own_left():
        return remote(
            d_attn, da_buf.at[rows_of(place)], line_sems.at[1, place], line_sems.at[2, place], left
        )

    def pass_right(block):
        spot = da_buf.at[rows_of(block)]
        return remote(spot, spot, line_sems.at[0, block], line_sems.at[2, block], right)

    def pass_left(block):
        spot = da_buf.at[rows_of(block)]
        return remote(spot, spot, line_sems.at[1, block], line_sems.at[2, block], left)

    @pl.when(place < group - 1)
    def _():
        own_right().start()

    @pl.when(place > 0)
    def _():
        own_left().start()

    def gate_copy(r, peer):
        return remote(
            gate_grads.at[r], gate_got.at[r], gate_sems.at[0, r], gate_sems.at[1, r], peer
        )

    peers = (None, along_x, along_y, over)
    for r in (3, 1, 2):
        gate_copy(r, peers[r]).start()
    for load in loads[early:]:
        load.start()
    d_key_acc[...] = jnp.zeros_like(d_key_acc)
    d_value_acc[...] = jnp.zeros_like(d_value_acc)

    def attend_back(block):
        rows = rows_of(block)
        d_heads = dot_nt(da_buf[rows, :], w_out_buf[...]).astype(jnp.bfloat16)
        shape = (tok, seq_len)
        at_query = block * tok + lax.broadcasted_iota(jnp.int32, shape, 0)
        at_key = lax.broadcasted_iota(jnp.int32, shape, 1)
        allowed = (at_key <= at_query) & (at_key < length[0])
        for head in range(heads):
            cols = slice(head * head_size, (head + 1) * head_size)
            one_query = query_buf[rows, cols]
            one_key = key_buf[:, cols]
            d_head = d_heads[:, cols]
            scores = jnp.where(allowed, dot_nt(one_query, one_key) * scale, NEGATIVE)
            probs = jnp.exp(scores - log_buf[rows, head : head + 1])
            d_probs = dot_nt(d_head, value_buf[:, cols])
            delta = jnp.sum(probs * d_probs, axis=-1, keepdims=True)
            d_scores = (probs * (d_probs - delta)).astype(jnp.bfloat16)
            d_query = dot_nn(d_scores, one_key) * scale
            d_key_acc[:, cols] += dot_nn(d_scores.T, one_query) * scale
            d_value_acc[:, cols] += dot_nn(probs.astype(jnp.bfloat16).T, d_head)
            d_proj[rows, cols] = rotated(d_query, cosine_buf[rows, :], sine_buf[rows, :]).astype(
                jnp.bfloat16
            )

    for load in loads[:early]:
        load.wait()
    own_load.wait()
    attend_back(place)

    def arrive(step, carry):
        block = line_order(place, step)
        pass_right(block).wait_recv()

        @pl.when((block < place) & (place < group - 1))
        def _():
            pass_right(block).start()

        @pl.when((block > place) & (place > 0))
        def _():
            pass_left(block).start()

        attend_back(block)
        return carry

    lax.fori_loop(0, group - 1, arrive, 0)
    for load in loads[early:]:
        load.wait()
    keep = pltpu.make_async_copy(keep_buf, gate_got.at[0], load_sems.at[15])
    keep.start()

    for head in range(heads):
        cols = slice(head * head_size, (head + 1) * head_size)
        key_cols = slice(local_width + head * head_size, local_width + (head + 1) * head_size)
        d_proj[:, key_cols] = rotated(d_key_acc[:, cols], cosine_buf[...], sine_buf[...]).astype(
            jnp.bfloat16
        )
    d_proj[:, 2 * local_width :] = d_value_acc[...].astype(jnp.bfloat16)

    def normed_tile(j, carry):
        cols = pl.ds(pl.multiple_of(j * piece, piece), piece)
        d_normed = jnp.zeros((seq_len, piece), jnp.float32)
        for c in range(3):
            d_normed += dot_nt(
                d_proj[:, c * local_width : (c + 1) * local_width], w_qkv_buf[c, cols, :]
            )
        hat = tokens_buf[:, cols].astype(jnp.float32) * inverse_buf[...]
        small_buf[0:1, cols] = jnp.sum(d_normed * hat, axis=0, keepdims=True)
        normed_part[:, cols] = d_normed.astype(jnp.bfloat16)
        return carry

    lax.fori_loop(0, parts, normed_tile, 0)

    def go_right(block):
        return remote(
            normed_part.at[pl.ds(block * tok, tok)],
            from_left.at[block],
            sum_sems.at[0, block],
            sum_sems.at[1, block],
            right,
        )

    def go_left(block):
        return remote(
            normed_part.at[pl.ds(block * tok, tok)],
            from_right.at[block],
            sum_sems.at[0, block],
            sum_sems.at[2, block],
            left,
        )

    def add_into(target, other):
        value = target[...].astype(jnp.float32) + other[...].astype(jnp.float32)
        target[...] = value.astype(jnp.bfloat16)

    def on_right(block):
        go_right(block).wait_recv()
        add_into(normed_part.at[pl.ds(block * tok, tok)], from_left.at[block])
        go_right(block).start()

    def on_left(block):
        go_left(block).wait_recv()
        add_into(normed_part.at[pl.ds(block * tok, tok)], from_right.at[block])
        go_left(block).start()

    @pl.when(place == 0)
    def _():
        for block in (3, 2, 1):
            go_right(block).start()

    @pl.when(place == 3)
    def _():
        for block in (0, 1, 2):
            go_left(block).start()

    def small_copy(k):
        to = (index + k) % parts
        cols = pl.ds(pl.multiple_of(to * piece, piece), piece)
        return remote(
            small_buf.at[:, cols],
            small_recv.at[k],
            small_sems.at[0, k],
            small_sems.at[1, k],
            ring_peer(k),
        )

    for k in range(1, parts):
        small_copy(k).start()

    def weight_grad(which, r):
        cols = pl.ds(pl.multiple_of((chip(r) * 2 + which) * piece, piece), piece)
        left_side = whole_buf[:, cols].T
        first = dot_nn(left_side, d_proj[...])
        second = dot_nn(da_buf[:, cols].T, attended_buf[...])
        return jnp.concatenate([first, second], axis=1)

    def pair_copy(r):
        return remote(
            send_pair.at[r], recv_pair.at[r], pair_sems.at[0, r], pair_sems.at[1, r], partner
        )

    def for_partner(i, carry):
        r = 3 - i
        send_pair[r] = weight_grad(1 - core, r).astype(jnp.bfloat16)
        pair_copy(r).start()
        return carry

    lax.fori_loop(0, 4, for_partner, 0)

    @pl.when(place == 1)
    def _():
        on_right(3)

    @pl.when(place == 2)
    def _():
        on_left(0)

    def half_x_copy():
        return remote(
            own_part.at[3, pl.ds(0, half)], half_x, ring_sems.at[0, 0], ring_sems.at[1, 0], along_x
        )

    def half_y_copy():
        return remote(
            own_part.at[3, pl.ds(half, half)],
            half_y,
            ring_sems.at[0, 1],
            ring_sems.at[1, 1],
            along_y,
        )

    def full_x_copy():
        return remote(own_part.at[1], full_x, ring_sems.at[0, 2], ring_sems.at[1, 2], along_x)

    def full_y_copy():
        return remote(own_part.at[2], full_y, ring_sems.at[0, 3], ring_sems.at[1, 3], along_y)

    def for_self(i, carry):
        r = 3 - i
        pair_copy(r).wait_recv()
        own_part[r] = (weight_grad(core, r) + recv_pair[r].astype(jnp.float32)).astype(
            jnp.bfloat16
        )

        @pl.when(i == 0)
        def _():
            half_x_copy().start()
            half_y_copy().start()

        return carry

    lax.fori_loop(0, 4, for_self, 0)

    total = small_buf[:, pl.ds(pl.multiple_of(index * piece, piece), piece)]
    for k in range(1, parts):
        small_copy(k).wait_recv()
        total = total + small_recv[k]
    small_z[0] = total

    @pl.when(place == 1)
    def _():
        on_right(2)

    @pl.when(place == 2)
    def _():
        on_left(1)

    def small_line_copy(k):
        return remote(
            small_z.at[0],
            small_z.at[k],
            small_sems.at[0, parts + k],
            small_sems.at[1, parts + k],
            line_peer(k),
        )

    for k in range(1, group):
        small_line_copy(k).start()

    half_x_copy().wait_recv()
    add_into(own_part.at[2, pl.ds(0, half)], half_x)
    full_y_copy().start()
    half_y_copy().wait_recv()
    add_into(own_part.at[1, pl.ds(half, half)], half_y)
    full_x_copy().start()

    @pl.when(place == 1)
    def _():
        on_left(0)

    @pl.when(place == 2)
    def _():
        on_right(3)

    total = small_z[0]
    for k in range(1, group):
        small_line_copy(k).wait_recv()
        total = total + small_z[k]
    small_out[...] = total

    grad_normed[...] = normed_part[rows_of(place), :].astype(jnp.float32)

    @pl.when(place > 0)
    def _():
        go_right(place).wait_recv()
        grad_normed[...] += from_left[place].astype(jnp.float32)

    @pl.when(place < group - 1)
    def _():
        go_left(place).wait_recv()
        grad_normed[...] += from_right[place].astype(jnp.float32)

    full_x_copy().wait_recv()
    full_y_copy().wait_recv()
    grad_weights[...] = (
        own_part[0].astype(jnp.float32)
        + full_x[...].astype(jnp.float32)
        + full_y[...].astype(jnp.float32)
    )

    for r in (1, 2, 3):
        gate_copy(r, peers[r]).wait()
    keep.wait()
    half_x_copy().wait_send()
    half_y_copy().wait_send()
    full_x_copy().wait_send()
    full_y_copy().wait_send()
    for r in range(4):
        pair_copy(r).wait_send()
    for k in range(1, parts):
        small_copy(k).wait_send()
    for k in range(1, group):
        small_line_copy(k).wait_send()
    for block in range(group):

        @pl.when(block > place)
        def _():
            go_right(block).wait_send()

        @pl.when(block < place)
        def _():
            go_left(block).wait_send()

        @pl.when((block <= place) & (place < group - 1))
        def _():
            pass_right(block).wait_send()

        @pl.when((block >= place) & (place > 0))
        def _():
            pass_left(block).wait_send()


def attention_back_call(
    lengths,
    d_attn,
    tokens_all,
    inverse_all,
    whole,
    w_out,
    w_qkv,
    query,
    key_rows,
    value,
    attended,
    log_total,
    cosine,
    sine,
    small_part,
    gate_grads,
):
    tok, width = d_attn.shape
    seq_len = tokens_all.shape[0]
    group = seq_len // tok
    local_width = w_out.shape[0]
    heads = log_total.shape[1]
    piece = gate_grads.shape[1]
    half = piece // 2
    parts = width // piece
    small_rows = small_part.shape[0]
    low, full = jnp.bfloat16, jnp.float32
    anywhere = pl.BlockSpec(memory_space=pl.ANY)
    inside = pl.BlockSpec(memory_space=pltpu.VMEM)

    def like(array):
        return pltpu.VMEM(array.shape, array.dtype)

    flops = 2 * seq_len * width * local_width * 8 + 10 * seq_len * seq_len * local_width
    return pl.pallas_call(
        functools.partial(attention_back_kernel, heads),
        out_shape=(
            jax.ShapeDtypeStruct((tok, width), full),
            jax.ShapeDtypeStruct((piece, 4 * local_width), full),
            jax.ShapeDtypeStruct((small_rows, piece), full),
            jax.ShapeDtypeStruct(gate_grads.shape, low),
        ),
        in_specs=[pl.BlockSpec(memory_space=pltpu.SMEM)] + [anywhere] * 15,
        out_specs=(inside, inside, inside, anywhere),
        scratch_shapes=[
            pltpu.VMEM((seq_len, width), low),
            like(tokens_all),
            like(inverse_all),
            like(whole),
            like(w_out),
            like(w_qkv),
            like(query),
            like(key_rows),
            like(value),
            like(attended),
            like(log_total),
            like(cosine),
            like(sine),
            pltpu.VMEM((seq_len, local_width), full),
            pltpu.VMEM((seq_len, local_width), full),
            pltpu.VMEM((seq_len, 3 * local_width), low),
            pltpu.VMEM((seq_len, width), low),
            pltpu.VMEM((group, tok, width), low),
            pltpu.VMEM((group, tok, width), low),
            pltpu.VMEM((4, piece, 4 * local_width), low),
            pltpu.VMEM((4, piece, 4 * local_width), low),
            pltpu.VMEM((4, piece, 4 * local_width), low),
            pltpu.VMEM((half, 4 * local_width), low),
            pltpu.VMEM((half, 4 * local_width), low),
            pltpu.VMEM((piece, 4 * local_width), low),
            pltpu.VMEM((piece, 4 * local_width), low),
            like(small_part),
            pltpu.VMEM((parts, small_rows, piece), full),
            pltpu.VMEM((group, small_rows, piece), full),
            pltpu.VMEM(gate_grads.shape[1:], low),
            pltpu.SemaphoreType.DMA((16,)),
            pltpu.SemaphoreType.DMA((3, group)),
            pltpu.SemaphoreType.DMA((3, group)),
            pltpu.SemaphoreType.DMA((2, 4)),
            pltpu.SemaphoreType.DMA((2, 4)),
            pltpu.SemaphoreType.DMA((2, parts + group)),
            pltpu.SemaphoreType.DMA((2, 4)),
        ],
        compiler_params=pltpu.CompilerParams(
            collective_id=2, has_side_effects=True, vmem_limit_bytes=67043328
        ),
        cost_estimate=pl.CostEstimate(flops=flops, bytes_accessed=40000000, transcendentals=0),
        name="attention_back",
    )(
        lengths,
        d_attn,
        tokens_all,
        inverse_all,
        whole,
        w_out,
        w_qkv,
        query,
        key_rows,
        value,
        attended,
        log_total,
        cosine,
        sine,
        small_part,
        gate_grads,
    )


def widen_slices(grads):
    chips, rows, hidden2 = grads.shape
    own = (lax.axis_index("dp") // 2).astype(jnp.int32).reshape(1)
    size = hidden2 // 2

    def body(own_ref, source, target):
        target[...] = source[0].astype(jnp.float32)

    wide = pl.pallas_call(
        body,
        out_shape=jax.ShapeDtypeStruct((rows, chips * hidden2), jnp.float32),
        grid_spec=pltpu.PrefetchScalarGridSpec(
            num_scalar_prefetch=1,
            grid=(2, chips),
            in_specs=[
                pl.BlockSpec((1, rows, size), lambda part, at, own_ref: (at ^ own_ref[0], 0, part))
            ],
            out_specs=pl.BlockSpec((rows, size), lambda part, at, own_ref: (0, part * chips + at)),
        ),
        name="widen",
    )(own, grads)
    return wide[None]


def across(index, step):
    return ((index // 2) ^ step) * 2 + index % 2


def swap_chips(pieces):
    parts = lax.axis_size("dp")
    got = [pieces[0]]
    for step in (1, 2, 3):
        pairs = [(index, across(index, step)) for index in range(parts)]
        got.append(lax.ppermute(pieces[step], "dp", pairs))
    return got


def chip_slices(w_gate_up):
    rows, ff2 = w_gate_up.shape[1:]
    chips = lax.axis_size("dp") // 2
    size = ff2 // 2 // chips
    own = lax.axis_index("dp") // 2

    def of_chip(chip):
        gate = lax.dynamic_slice(w_gate_up[0], (0, chip * size), (rows, size))
        up = lax.dynamic_slice(w_gate_up[0], (0, ff2 // 2 + chip * size), (rows, size))
        return jnp.concatenate([gate, up], axis=1)

    return swap_chips([of_chip(own ^ step) for step in range(chips)])


def expert_step(gate_up_w, down_w, rows, d_rows_out):
    ff = down_w.shape[0]
    gate_up = jnp.dot(rows, gate_up_w, preferred_element_type=jnp.float32)
    gate = gate_up[:, :ff]
    upward = gate_up[:, ff:]
    sigmoid = jax.nn.sigmoid(gate)
    activated = (gate * sigmoid * upward).astype(jnp.bfloat16)
    out = jnp.dot(activated, down_w, preferred_element_type=jnp.float32).astype(jnp.bfloat16)
    d_activated = contract_last(d_rows_out, down_w)
    grad_down = contract_first(activated, d_rows_out)
    d_gate = d_activated * upward * sigmoid * (1.0 + gate * (1.0 - sigmoid))
    d_up = d_activated * gate * sigmoid
    d_gate_up = jnp.concatenate([d_gate, d_up], axis=1).astype(jnp.bfloat16)
    d_rows = contract_last(d_gate_up, gate_up_w).astype(jnp.bfloat16)
    grad_gate_up = contract_first(rows, d_gate_up)
    return out, d_rows, grad_gate_up, grad_down


def experts_split_hidden(w_gate_up, w_down, rows, d_rows_out):
    out, d_rows, grad_gate_up, grad_down = experts_call(
        rows, d_rows_out, chip_slices(w_gate_up), w_down[0]
    )
    return out, d_rows, grad_gate_up, grad_down[None]


def experts_gather_weights(w_gate_up, w_down, rows, d_rows_out):
    gate_up_w = lax.all_gather(w_gate_up, "dp", axis=1, tiled=True)[0]
    down_w = lax.all_gather(w_down, "dp", axis=1, tiled=True)[0]
    shape = rows.shape
    flat = (-1, shape[2])
    rows = exchange_experts(rows).reshape(flat)
    d_rows_out = exchange_experts(d_rows_out).reshape(flat)
    out, d_rows, grad_gate_up, grad_down = expert_step(gate_up_w, down_w, rows, d_rows_out)
    out = exchange_experts(out.reshape(shape))
    d_rows = exchange_experts(d_rows.reshape(shape))
    grad_gate_up = lax.psum_scatter(
        grad_gate_up.astype(jnp.bfloat16), "dp", scatter_dimension=0, tiled=True
    )
    grad_down = lax.psum_scatter(
        grad_down.astype(jnp.bfloat16), "dp", scatter_dimension=0, tiled=True
    )
    return (
        out,
        d_rows,
        grad_gate_up.astype(jnp.float32)[None],
        grad_down.astype(jnp.float32)[None],
    )


def attention_back_plain(
    lengths,
    d_attn,
    hat_all,
    whole,
    out_full,
    qkv_full,
    query,
    key_rows,
    value,
    attended,
    log_total,
    cosine,
    sine,
):
    seq_len, heads_local, head_size = query.shape
    local_width = heads_local * head_size
    position = jnp.arange(seq_len, dtype=jnp.int32)
    allowed = (position[None, :] <= position[:, None]) & (position < lengths[0])[None, :]
    whole_grad = lax.all_gather(d_attn, "expert", axis=0, tiled=True)
    d_attended = contract_last(whole_grad, out_full).astype(jnp.bfloat16)
    out_part = contract_first(attended, whole_grad)
    grad_out = lax.psum_scatter(
        out_part.astype(jnp.bfloat16), "dp", scatter_dimension=1, tiled=True
    ).astype(jnp.float32)
    d_heads = d_attended.reshape(seq_len, heads_local, head_size)
    probs = jnp.exp(masked_scores(query, key_rows, allowed) - log_total)
    probs_low = probs.astype(jnp.bfloat16)
    d_value = jnp.einsum(
        "hqk,qhd->khd", probs_low, d_heads, preferred_element_type=jnp.float32
    ).astype(jnp.bfloat16)
    d_probs = jnp.einsum("qhd,khd->hqk", d_heads, value, preferred_element_type=jnp.float32)
    row_delta = jnp.sum(probs * d_probs, axis=-1, keepdims=True)
    d_scores = (probs * (d_probs - row_delta)).astype(jnp.bfloat16)
    scale = head_size ** (-0.5)
    d_query = (
        jnp.einsum("hqk,khd->qhd", d_scores, key_rows, preferred_element_type=jnp.float32) * scale
    )
    d_key = jnp.einsum("hqk,qhd->khd", d_scores, query, preferred_element_type=jnp.float32) * scale
    d_query_pre = (
        rotate_back(d_query, cosine, sine).reshape(seq_len, local_width).astype(jnp.bfloat16)
    )
    d_key_pre = rotate_back(d_key, cosine, sine).reshape(seq_len, local_width).astype(jnp.bfloat16)
    d_projected = jnp.stack([d_query_pre, d_key_pre, d_value.reshape(seq_len, local_width)])
    d_normed_part = jnp.einsum(
        "cte,cde->td", d_projected, qkv_full, preferred_element_type=jnp.float32
    )
    grad_normalized = lax.psum_scatter(
        d_normed_part.astype(jnp.bfloat16), "expert", scatter_dimension=0, tiled=True
    ).astype(jnp.float32)
    qkv_part = jnp.einsum("td,cte->cde", whole, d_projected, preferred_element_type=jnp.float32)
    grad_qkv = lax.psum_scatter(
        qkv_part.astype(jnp.bfloat16), "dp", scatter_dimension=1, tiled=True
    ).astype(jnp.float32)
    first_gain_part = jnp.sum(d_normed_part * hat_all, axis=0)
    return grad_normalized, grad_qkv, grad_out, first_gain_part


def on_device(
    tokens,
    w_qkv,
    w_out,
    attention_norm_gain,
    gain_ffn,
    w_router,
    w_gate_up,
    w_down,
    lengths,
    routes,
    order,
    cotangent,
):
    group_size = lax.axis_size("expert")
    dp_size = lax.axis_size("dp")
    tok_dev = tokens.shape[0]
    seq_len = tok_dev * group_size
    width = tokens.shape[1]
    top_count = routes.shape[1]
    capacity = tok_dev * top_count // group_size
    slots = group_size * capacity
    head_size = HEAD_DIM
    local_width = w_qkv.shape[2]
    heads_local = local_width // head_size
    tokens_all = lax.all_gather(tokens, "expert", axis=0, tiled=True)
    small = jnp.concatenate(
        [attention_norm_gain[:, None], gain_ffn[:, None], w_router], axis=1
    )
    small_full = lax.all_gather(small, "dp", axis=0, tiled=True)
    qkv_full = lax.all_gather(w_qkv, "dp", axis=1, tiled=True)
    out_full = lax.all_gather(w_out, "dp", axis=1, tiled=True)
    first_norm_gain = small_full[:, 0].astype(jnp.float32)
    gain_two = small_full[:, 1].astype(jnp.float32)
    router_full = small_full[:, 2:]

    own_start = lax.axis_index("expert") * tok_dev
    own_position = own_start + jnp.arange(tok_dev, dtype=jnp.int32)
    live_own = own_position < lengths[0]
    live_rows = live_own.astype(jnp.float32)[:, None]
    split = dp_size == 8 and group_size == 4
    first_expert = lax.axis_index("expert") if split else 0
    target, kept_pair = slot_table(routes, order, live_own, capacity, first_expert, group_size)
    slot_ids = jnp.arange(slots, dtype=jnp.int32)
    pair_hits = (slot_ids[:, None, None] == target[None]) & kept_pair[None]
    select = jnp.sum(pair_hits.astype(jnp.float32), axis=2).astype(jnp.bfloat16)

    inputs_float = tokens.astype(jnp.float32)
    input_normalized_hat, first_inverse_rms = normalize(inputs_float)
    hat_all, inverse_all = normalize(tokens_all.astype(jnp.float32))
    whole = (hat_all * first_norm_gain).astype(jnp.bfloat16)
    cosine, sine = rotary_tables(seq_len, head_size)
    projected = jnp.einsum("td,cde->cte", whole, qkv_full, preferred_element_type=jnp.float32)
    query = rotate(projected[0].reshape(seq_len, heads_local, head_size), cosine, sine).astype(
        jnp.bfloat16
    )
    key_rows = rotate(projected[1].reshape(seq_len, heads_local, head_size), cosine, sine).astype(
        jnp.bfloat16
    )
    value = projected[2].astype(jnp.bfloat16).reshape(seq_len, heads_local, head_size)
    position = jnp.arange(seq_len, dtype=jnp.int32)
    live_all = position < lengths[0]
    allowed = (position[None, :] <= position[:, None]) & live_all[None, :]
    scores = masked_scores(query, key_rows, allowed)
    top_score = jnp.max(scores, axis=-1, keepdims=True)
    exponent = jnp.exp(scores - top_score)
    row_total = jnp.sum(exponent, axis=-1, keepdims=True)
    probs = exponent / row_total
    log_total = top_score + jnp.log(row_total)
    probs_low = probs.astype(jnp.bfloat16)
    attended = jnp.einsum("hqk,khd->qhd", probs_low, value, preferred_element_type=jnp.float32)
    attended = attended.reshape(seq_len, local_width).astype(jnp.bfloat16)
    attn_part = jnp.dot(attended, out_full, preferred_element_type=jnp.float32)
    attn_own = lax.psum_scatter(
        attn_part.astype(jnp.bfloat16), "expert", scatter_dimension=0, tiled=True
    ).astype(jnp.float32)
    resid = inputs_float + attn_own
    hhat, inverse_two = normalize(resid)
    hidden_in = (hhat * gain_two).astype(jnp.bfloat16)
    sent = jnp.dot(select, hidden_in, preferred_element_type=jnp.float32).astype(jnp.bfloat16)

    logits = jnp.dot(hidden_in, router_full, preferred_element_type=jnp.float32)
    chosen = jnp.take_along_axis(logits, routes, axis=1)
    gates = jax.nn.softmax(chosen, axis=1)
    d_out = live_rows * cotangent.astype(jnp.float32)
    d_back = jnp.zeros((slots, width), jnp.float32)
    for index in range(top_count):
        weighted = (gates[:, index : index + 1] * d_out).astype(jnp.bfloat16)
        d_back = d_back + jnp.dot(
            pair_hits[:, :, index].astype(jnp.bfloat16),
            weighted,
            preferred_element_type=jnp.float32,
        )
    d_back = d_back.astype(jnp.bfloat16)
    experts = experts_split_hidden if split else experts_gather_weights
    blocked = (group_size, capacity, width)
    returned, d_sent, grad_gate_up, grad_down = experts(
        w_gate_up, w_down, sent.reshape(blocked), d_back.reshape(blocked)
    )
    returned = returned.reshape(slots, width)
    d_sent = d_sent.reshape(slots, width)

    moe = jnp.zeros_like(resid)
    d_gates_list = []
    for index in range(top_count):
        one_hot = pair_hits[:, :, index].astype(jnp.bfloat16)
        picked = contract_first(one_hot, returned)
        d_gates_list.append(jnp.sum(d_out * picked, axis=-1))
        moe = moe + gates[:, index : index + 1] * picked
    output = (live_rows * (resid + moe)).astype(jnp.bfloat16)
    d_gates = jnp.stack(d_gates_list, axis=1)
    d_hidden = contract_first(select, d_sent)
    d_chosen = gates * (d_gates - jnp.sum(gates * d_gates, axis=1, keepdims=True))
    expert_ids = jnp.arange(group_size, dtype=jnp.int32)
    route_hits = (routes[:, :, None] == expert_ids[None, None, :]).astype(jnp.float32)
    d_logits = jnp.sum(route_hits * d_chosen[:, :, None], axis=1)
    router_f = router_full.astype(jnp.float32)
    d_hidden = d_hidden + jnp.dot(
        d_logits, router_f.T, precision=HIGH, preferred_element_type=jnp.float32
    )
    router_part = jnp.dot(
        hidden_in.astype(jnp.float32).T,
        d_logits,
        precision=HIGH,
        preferred_element_type=jnp.float32,
    )
    gain_two_part = jnp.sum(d_hidden * hhat, axis=0)
    scaled_two = d_hidden * gain_two
    d_resid = d_out + inverse_two * (
        scaled_two - hhat * jnp.mean(scaled_two * hhat, axis=-1, keepdims=True)
    )
    d_attn = d_resid.astype(jnp.bfloat16)
    if split:
        small_part = jnp.concatenate(
            [jnp.zeros((1, width)), gain_two_part[None], router_part.T, jnp.zeros((2, width))],
            axis=0,
        )
        grad_normalized, grad_weights, small_own, gate_got = attention_back_call(
            lengths,
            d_attn,
            tokens_all,
            inverse_all,
            whole,
            out_full,
            qkv_full,
            query.reshape(seq_len, local_width),
            key_rows.reshape(seq_len, local_width),
            value.reshape(seq_len, local_width),
            attended,
            log_total[:, :, 0].T,
            jnp.concatenate([cosine[:, 0], cosine[:, 0]], axis=1),
            jnp.concatenate([sine[:, 0], -sine[:, 0]], axis=1),
            small_part,
            grad_gate_up,
        )
        grad_gate_up = widen_slices(gate_got)
        grad_qkv = jnp.stack(
            [grad_weights[:, c * local_width : (c + 1) * local_width] for c in range(3)]
        )
        grad_out = grad_weights[:, 3 * local_width :].T
    else:
        grad_normalized, grad_qkv, grad_out, first_gain_part = attention_back_plain(
            lengths,
            d_attn,
            hat_all,
            whole,
            out_full,
            qkv_full,
            query,
            key_rows,
            value,
            attended,
            log_total,
            cosine,
            sine,
        )
        small_part = jnp.concatenate(
            [first_gain_part[None], gain_two_part[None], router_part.T], axis=0
        )
        small_sum = lax.psum(small_part, ("dp", "expert"))
        own_rows = width // dp_size
        small_own = lax.dynamic_slice_in_dim(
            small_sum, lax.axis_index("dp") * own_rows, own_rows, axis=1
        )
    first_scaled_input = grad_normalized * first_norm_gain
    grad_tokens = d_resid + first_inverse_rms * (
        first_scaled_input
        - input_normalized_hat
        * jnp.mean(first_scaled_input * input_normalized_hat, axis=-1, keepdims=True)
    )
    return (
        output,
        grad_tokens.astype(jnp.bfloat16),
        grad_qkv,
        grad_out,
        small_own[0],
        small_own[1],
        small_own[2 : 2 + group_size].T,
        grad_gate_up,
        grad_down,
    )


def solution(mesh):
    placed = (
        P(("dp", "expert"), None),
        P(None, "dp", "expert"),
        P("expert", "dp"),
        P("dp"),
        P("dp"),
        P("dp", None),
        P("expert", "dp", None),
        P("expert", "dp", None),
        P("dp"),
        P(("dp", "expert"), None),
        P(("dp", "expert")),
        P(("dp", "expert"), None),
    )
    return jax.shard_map(
        on_device,
        mesh=mesh,
        in_specs=placed,
        out_specs=(
            P(("dp", "expert"), None),
            P(("dp", "expert"), None),
            P(None, "dp", "expert"),
            P("expert", "dp"),
            P("dp"),
            P("dp"),
            P("dp", None),
            P("expert", "dp", None),
            P("expert", "dp", None),
        ),
        check_vma=False,
    )
```

```python
import functools

import jax
import jax.numpy as jnp
import numpy as np
from jax import lax
from jax.experimental import pallas as pl
from jax.experimental.pallas import tpu as pltpu
from jax.sharding import PartitionSpec as P

HEAD_DIM = 128
FF = 5632


NORM_EPSILON = 1e-05
NEGATIVE = -1e30
THETA = 10000.0
HIGH = lax.Precision.HIGHEST
MESH_ID = pl.DeviceIdType.MESH
LANES = 128


def remote(src, dst, send_sem, recv_sem, peer):
    return pltpu.make_async_remote_copy(
        src_ref=src,
        dst_ref=dst,
        send_sem=send_sem,
        recv_sem=recv_sem,
        device_id=peer,
        device_id_type=MESH_ID,
    )


def greet(peers):
    barrier = pltpu.get_barrier_semaphore()
    for peer in peers:
        pl.semaphore_signal(barrier, inc=1, device_id=peer, device_id_type=MESH_ID)
    pl.semaphore_wait(barrier, len(peers))


def dot_nn(left, right):
    return jnp.dot(left, right, preferred_element_type=jnp.float32)


def dot_nt(left, right):
    return lax.dot_general(
        left, right, (((1,), (1,)), ((), ())), preferred_element_type=jnp.float32
    )


def experts_kernel(
    group,
    sent,
    d_back,
    w_gate_up,
    w_got,
    w_down,
    ret,
    d_ret,
    grad_gate_up,
    grad_down,
    w_buf,
    down_buf,
    rows_buf,
    gate_buf,
    act_buf,
    part_buf,
    half_x,
    half_y,
    full_x,
    full_y,
    other_gate,
    other_down,
    stage,
    ag_sems,
    rs_sems,
    weight_sems,
    local_sems,
    grad_sems,
):
    cap, width = sent.shape[1], sent.shape[2]
    half = cap // 2
    piece, hidden2 = w_got.shape[1:]
    hidden = hidden2 // 2
    down_own = w_down.at[0]
    down_rows = down_own.shape[0]
    chunk = 4 * cap
    total = group * chunk

    index = lax.axis_index("dp")
    place = lax.axis_index("expert")
    core = index % 2
    at_x = (index // 2) % 2
    at_y = index // 4
    partner = {"dp": at_y * 4 + at_x * 2 + (1 - core)}
    along_x = {"dp": at_y * 4 + (1 - at_x) * 2 + core}
    along_y = {"dp": (1 - at_y) * 4 + at_x * 2 + core}
    chips = [
        at_y * 2 + at_x,
        at_y * 2 + (1 - at_x),
        (1 - at_y) * 2 + at_x,
        (1 - at_y) * 2 + (1 - at_x),
    ]

    def ahead(k):
        return {"expert": (place + k) % group}

    def behind(k):
        return {"expert": (place + group - k) % group}

    greet([partner, along_x, along_y] + [ahead(k) for k in range(1, group)])

    def block(t, k, r, start=0, size=None):
        size = cap if size is None else size
        return rows_buf.at[t, pl.ds((k * 4 + r) * cap + start, size), :]

    def part(t, k, r, start=0, size=None):
        size = cap if size is None else size
        return part_buf.at[t, pl.ds((k * 4 + r) * cap + start, size), :]

    def ag(kind, t, k):
        return ag_sems.at[0, kind, t, k], ag_sems.at[1, kind, t, k]

    def rs(kind, t, k):
        return rs_sems.at[0, kind, t, k], rs_sems.at[1, kind, t, k]

    sources = (sent, d_back)
    results = (ret, d_ret)

    def z_copy(t, k):
        return remote(sources[t].at[k], block(t, k, 0), *ag(0, t, k), ahead(k))

    def own_copy(t):
        return pltpu.make_async_copy(sources[t].at[0], block(t, 0, 0), local_sems.at[t])

    def x_copy(t, k):
        return remote(block(t, k, 0), block(t, k, 1), *ag(1, t, k), along_x)

    def y_copy(t, k):
        return remote(block(t, k, 0), block(t, k, 2), *ag(2, t, k), along_y)

    def a_copy(t, k):
        return remote(block(t, k, 2, 0, half), block(t, k, 3, 0, half), *ag(3, t, k), along_x)

    def b_copy(t, k):
        return remote(
            block(t, k, 1, half, half), block(t, k, 3, half, half), *ag(4, t, k), along_y
        )

    def spread(t, k):
        if k == 0:
            own_copy(t).wait()
        else:
            z_copy(t, k).wait_recv()
        x_copy(t, k).start()
        y_copy(t, k).start()

    def relay(t, k):
        y_copy(t, k).wait_recv()
        a_copy(t, k).start()
        x_copy(t, k).wait_recv()
        b_copy(t, k).start()

    def arrived(t, k):
        a_copy(t, k).wait_recv()
        b_copy(t, k).wait_recv()

    def half_x_copy(t, k):
        return remote(part(t, k, 3, 0, half), half_x.at[t, k], *rs(0, t, k), along_x)

    def half_y_copy(t, k):
        return remote(part(t, k, 3, half, half), half_y.at[t, k], *rs(1, t, k), along_y)

    def full_x_copy(t, k):
        return remote(part(t, k, 1), full_x.at[t, k], *rs(2, t, k), along_x)

    def full_y_copy(t, k):
        return remote(part(t, k, 2), full_y.at[t, k], *rs(3, t, k), along_y)

    def back_copy(t, k):
        return remote(part(t, k, 0), results[t].at[k], *rs(4, t, k), behind(k))

    def keep_copy(t):
        return pltpu.make_async_copy(part(t, 0, 0), results[t].at[0], local_sems.at[2 + t])

    def halves_out(t, k):
        half_x_copy(t, k).start()
        half_y_copy(t, k).start()

    def add_into(target, *others):
        value = target[...].astype(jnp.float32)
        for other in others:
            value = value + other[...].astype(jnp.float32)
        target[...] = value.astype(jnp.bfloat16)

    def fulls_out(t, k):
        half_x_copy(t, k).wait_recv()
        add_into(part(t, k, 2, 0, half), half_x.at[t, k])
        full_y_copy(t, k).start()
        half_y_copy(t, k).wait_recv()
        add_into(part(t, k, 1, half, half), half_y.at[t, k])
        full_x_copy(t, k).start()

    def home(t, k):
        full_x_copy(t, k).wait_recv()
        full_y_copy(t, k).wait_recv()
        add_into(part(t, k, 0), full_x.at[t, k], full_y.at[t, k])
        if k == 0:
            keep_copy(t).start()
        else:
            back_copy(t, k).start()

    def w_rows(r, which):
        return pl.ds(pl.multiple_of((chips[r] * 2 + which) * piece, piece), piece)

    def w_parts(r, which):
        rows = w_rows(r, which)
        if r > 0:
            return [(w_got.at[r - 1], w_buf.at[rows, :], r)]
        return [
            (
                w_gate_up.at[
                    0, :, pl.ds(pl.multiple_of((4 * part + chips[0]) * hidden, LANES), hidden)
                ],
                w_buf.at[rows, pl.ds(part * hidden, hidden)],
                4 * part,
            )
            for part in range(2)
        ]

    def w_share(r, which):
        return [
            remote(source, target, weight_sems.at[0, n], weight_sems.at[1, n], partner)
            for source, target, n in w_parts(r, which)
        ]

    def w_keep(r):
        return [
            pltpu.make_async_copy(source, target, local_sems.at[4 + n])
            for source, target, n in w_parts(r, core)
        ]

    def down_at(which):
        return down_buf.at[pl.ds(pl.multiple_of(which * down_rows, down_rows), down_rows), :]

    def down_share():
        return remote(
            down_own, down_at(core), weight_sems.at[0, 5], weight_sems.at[1, 5], partner
        )

    down_keep = pltpu.make_async_copy(down_own, down_at(core), local_sems.at[9])

    def forward(k):
        base = k * chunk

        def tile(first, count):
            gate_cols = pl.ds(pl.multiple_of(first * LANES, LANES), count * LANES)
            up_cols = pl.ds(pl.multiple_of(hidden + first * LANES, LANES), count * LANES)
            rows = rows_buf[0, base : base + chunk, :]
            if count == 1:
                weights = jnp.concatenate([w_buf[:, gate_cols], w_buf[:, up_cols]], axis=1)
                both = dot_nn(rows, weights)
                gate = both[:, :LANES]
                up = both[:, LANES:]
            else:
                gate = dot_nn(rows, w_buf[:, gate_cols])
                up = dot_nn(rows, w_buf[:, up_cols])
            sigmoid = 1.0 / (1.0 + jnp.exp(-gate))
            gate_buf[base : base + chunk, gate_cols] = gate.astype(jnp.bfloat16)
            gate_buf[base : base + chunk, up_cols] = up.astype(jnp.bfloat16)
            act_buf[base : base + chunk, gate_cols] = (gate * sigmoid * up).astype(jnp.bfloat16)

        def pair(j, carry):
            tile(2 * j, 2)
            return carry

        blocks = hidden // LANES
        lax.fori_loop(0, blocks // 2, pair, 0)
        if blocks % 2:
            tile(blocks - 1, 1)

        def out_tile(j, carry):
            cols = pl.ds(pl.multiple_of(j * 2 * LANES, 2 * LANES), 2 * LANES)
            out = dot_nn(act_buf[base : base + chunk, :], down_buf[:, cols])
            part_buf[0, base : base + chunk, cols] = out.astype(jnp.bfloat16)
            return carry

        lax.fori_loop(0, width // (2 * LANES), out_tile, 0)

    def backward(k):
        base = k * chunk

        def tile(first, count):
            rows = pl.ds(pl.multiple_of(first * LANES, LANES), count * LANES)
            d_act = dot_nt(rows_buf[1, base : base + chunk, :], down_buf[rows, :])
            up_rows = pl.ds(pl.multiple_of(hidden + first * LANES, LANES), count * LANES)
            gate = gate_buf[base : base + chunk, rows].astype(jnp.float32)
            up = gate_buf[base : base + chunk, up_rows].astype(jnp.float32)
            sigmoid = 1.0 / (1.0 + jnp.exp(-gate))
            scaled = d_act * sigmoid
            d_gate = scaled * up * (1.0 + gate * (1.0 - sigmoid))
            gate_buf[base : base + chunk, rows] = d_gate.astype(jnp.bfloat16)
            gate_buf[base : base + chunk, up_rows] = (scaled * gate).astype(jnp.bfloat16)

        def pair(j, carry):
            tile(2 * j, 2)
            return carry

        blocks = hidden // LANES
        lax.fori_loop(0, blocks // 2, pair, 0)
        if blocks % 2:
            tile(blocks - 1, 1)

        def out_tile(j, carry):
            cols = pl.ds(pl.multiple_of(j * 2 * LANES, 2 * LANES), 2 * LANES)
            out = dot_nt(gate_buf[base : base + chunk, :], w_buf[cols, :])
            part_buf[1, base : base + chunk, cols] = out.astype(jnp.bfloat16)
            return carry

        lax.fori_loop(0, width // (2 * LANES), out_tile, 0)

    own_copy(0).start()
    for k in range(1, group):
        z_copy(0, k).start()
    for r in range(4):
        for copy in w_share(r, core) + w_keep(r):
            copy.start()
    down_share().start()
    down_keep.start()
    own_copy(1).start()

    spread(0, 0)
    spread(0, 1)
    relay(0, 0)
    for k in range(1, group):
        z_copy(1, k).start()
    spread(0, 2)
    relay(0, 1)
    arrived(0, 0)
    for r in range(4):
        for copy in w_keep(r):
            copy.wait()
        for copy in w_share(r, 1 - core):
            copy.wait_recv()
    down_keep.wait()
    down_share().wait_recv()
    forward(0)
    spread(0, 3)
    relay(0, 2)
    arrived(0, 1)
    forward(1)
    spread(1, 0)
    relay(0, 3)
    arrived(0, 2)
    forward(2)
    spread(1, 1)
    relay(1, 0)
    arrived(0, 3)
    forward(3)
    spread(1, 2)
    relay(1, 1)
    arrived(1, 0)
    backward(0)
    spread(1, 3)
    relay(1, 2)
    arrived(1, 1)
    halves_out(0, 0)
    halves_out(0, 1)
    backward(1)
    relay(1, 3)
    arrived(1, 2)
    halves_out(0, 2)
    halves_out(0, 3)
    fulls_out(0, 0)
    fulls_out(0, 1)
    halves_out(1, 0)
    backward(2)
    arrived(1, 3)
    fulls_out(0, 2)
    fulls_out(0, 3)
    halves_out(1, 1)
    home(0, 0)
    home(0, 1)
    backward(3)
    halves_out(1, 2)
    halves_out(1, 3)
    fulls_out(1, 0)
    fulls_out(1, 1)

    act_t = down_buf.at[:, pl.ds(0, total)]
    rows_t = down_buf.at[pl.ds(0, piece), pl.ds(total, total)]
    send_down = w_buf.at[pl.ds(4 * piece, down_rows), pl.ds(0, width)]

    def send_gate(r):
        return w_buf.at[pl.ds(r * piece, piece), :]

    def turn(j, carry):
        cols = pl.ds(pl.multiple_of(j * LANES, LANES), LANES)
        act_t[cols, :] = act_buf[:, cols].T
        return carry

    lax.fori_loop(0, hidden // LANES, turn, 0)

    def down_grad(which, j):
        cols = pl.ds(pl.multiple_of(j * 2 * LANES, 2 * LANES), 2 * LANES)
        rows = pl.ds(pl.multiple_of(which * down_rows, down_rows), down_rows)
        return cols, dot_nn(act_t[rows, :], rows_buf[1, :, cols])

    def down_for_partner(j, carry):
        cols, value = down_grad(1 - core, j)
        send_down[:, cols] = value.astype(jnp.bfloat16)
        return carry

    tiles = width // (2 * LANES)
    lax.fori_loop(0, tiles, down_for_partner, 0)
    down_send = remote(
        send_down, other_down, grad_sems.at[0, 4], grad_sems.at[1, 4], partner
    )
    down_send.start()
    home(0, 2)
    home(0, 3)
    fulls_out(1, 2)
    fulls_out(1, 3)

    def gate_grad(r, which, store):
        start = pl.multiple_of((chips[r] * 2 + which) * piece, piece)
        rows_t[...] = rows_buf[0, :, pl.ds(start, piece)].T

        def tile(j, carry):
            cols = pl.ds(pl.multiple_of(j * 2 * LANES, 2 * LANES), 2 * LANES)
            store(cols, dot_nn(rows_t[...], gate_buf[:, cols]))
            return carry

        lax.fori_loop(0, hidden2 // (2 * LANES), tile, 0)

    def gate_send(r):
        return remote(
            send_gate(r), other_gate.at[r], grad_sems.at[0, r], grad_sems.at[1, r], partner
        )

    for r in range(4):
        target = send_gate(r)

        def store(cols, value, target=target):
            target[:, cols] = value.astype(jnp.bfloat16)

        gate_grad(r, 1 - core, store)
        gate_send(r).start()
        if r == 0:
            home(1, 0)
            home(1, 1)
        if r == 1:
            home(1, 2)
        if r == 2:
            home(1, 3)

    down_send.wait_recv()

    def stage_copy(j):
        cols = pl.ds(pl.multiple_of(j * 2 * LANES, 2 * LANES), 2 * LANES)
        return pltpu.make_async_copy(
            stage.at[j % 2], grad_down.at[:, cols], grad_sems.at[2, j % 2]
        )

    def down_for_self(j, carry):
        cols, value = down_grad(core, j)

        @pl.when(j >= 2)
        def _():
            stage_copy(j - 2).wait()

        stage[j % 2] = value + other_down[:, cols].astype(jnp.float32)
        stage_copy(j).start()
        return carry

    lax.fori_loop(0, tiles, down_for_self, 0)

    def gate_out(r):
        return pltpu.make_async_copy(other_gate.at[r], grad_gate_up.at[r], grad_sems.at[2, 2 + r])

    for r in range(4):
        gate_send(r).wait_recv()
        target = other_gate.at[r]

        def store(cols, value, target=target):
            target[:, cols] = (value + target[:, cols].astype(jnp.float32)).astype(jnp.bfloat16)

        gate_grad(r, core, store)
        gate_out(r).start()

    stage_copy(tiles - 2).wait()
    stage_copy(tiles - 1).wait()
    for r in range(4):
        gate_out(r).wait()
        gate_send(r).wait_send()
        for copy in w_share(r, core):
            copy.wait_send()
    down_share().wait_send()
    down_send.wait_send()
    for t in range(2):
        keep_copy(t).wait()
        for k in range(group):
            x_copy(t, k).wait_send()
            y_copy(t, k).wait_send()
            a_copy(t, k).wait_send()
            b_copy(t, k).wait_send()
            half_x_copy(t, k).wait_send()
            half_y_copy(t, k).wait_send()
            full_x_copy(t, k).wait_send()
            full_y_copy(t, k).wait_send()
            if k > 0:
                z_copy(t, k).wait_send()
                back_copy(t, k).wait_send()
                back_copy(t, k).wait_recv()


def experts_call(sent, d_back, w_gate_up, w_got, w_down):
    group, cap, width = sent.shape
    piece, hidden2 = w_got.shape[1:]
    hidden = hidden2 // 2
    down_rows = w_down.shape[1]
    chunk = 4 * cap
    total = group * chunk
    low = jnp.bfloat16
    anywhere = pl.BlockSpec(memory_space=pl.ANY)
    flops = 2 * total * width * hidden * 9
    moved = 2 * (4 * piece * hidden2 * 2 + down_rows * width * 3)
    return pl.pallas_call(
        functools.partial(experts_kernel, group),
        out_shape=(
            jax.ShapeDtypeStruct((group, cap, width), low),
            jax.ShapeDtypeStruct((group, cap, width), low),
            jax.ShapeDtypeStruct((4, piece, hidden2), low),
            jax.ShapeDtypeStruct((down_rows, width), jnp.float32),
        ),
        in_specs=[anywhere] * 5,
        out_specs=(anywhere,) * 4,
        scratch_shapes=[
            pltpu.VMEM((width, hidden2), low),
            pltpu.VMEM((hidden, width), low),
            pltpu.VMEM((2, total, width), low),
            pltpu.VMEM((total, hidden2), low),
            pltpu.VMEM((total, hidden), low),
            pltpu.VMEM((2, total, width), low),
            pltpu.VMEM((2, group, cap // 2, width), low),
            pltpu.VMEM((2, group, cap // 2, width), low),
            pltpu.VMEM((2, group, cap, width), low),
            pltpu.VMEM((2, group, cap, width), low),
            pltpu.VMEM((4, piece, hidden2), low),
            pltpu.VMEM((down_rows, width), low),
            pltpu.VMEM((2, down_rows, 2 * LANES), jnp.float32),
            pltpu.SemaphoreType.DMA((2, 5, 2, group)),
            pltpu.SemaphoreType.DMA((2, 5, 2, group)),
            pltpu.SemaphoreType.DMA((2, 6)),
            pltpu.SemaphoreType.DMA((10,)),
            pltpu.SemaphoreType.DMA((3, 6)),
        ],
        compiler_params=pltpu.CompilerParams(
            collective_id=1, has_side_effects=True, vmem_limit_bytes=67043328
        ),
        cost_estimate=pl.CostEstimate(flops=flops, bytes_accessed=moved, transcendentals=0),
        name="experts",
    )(sent, d_back, w_gate_up, w_got, w_down)


def rotary_tables(length_total, head_size):
    position = jnp.arange(length_total, dtype=jnp.float32)
    frequency = THETA ** (-(jnp.arange(head_size // 2, dtype=jnp.float32) * 2.0 / head_size))
    angles = position[:, None] * frequency[None, :]
    return (jnp.cos(angles)[:, None, :], jnp.sin(angles)[:, None, :])


def rotate(values, cosine, sine):
    half_size = values.shape[-1] // 2
    first = values[..., :half_size]
    second = values[..., half_size:]
    return jnp.concatenate(
        [first * cosine - second * sine, second * cosine + first * sine], axis=-1
    )


def rotate_back(grad_rows, cosine, sine):
    half_size = grad_rows.shape[-1] // 2
    first = grad_rows[..., :half_size]
    second = grad_rows[..., half_size:]
    return jnp.concatenate(
        [first * cosine + second * sine, second * cosine - first * sine], axis=-1
    )


def slot_table(routes, order, valid, capacity):
    row_count = routes.shape[0]
    top_count = routes.shape[1]
    pair_rank = order[:, None] + row_count * jnp.arange(top_count, dtype=jnp.int32)[None, :]
    flat_rank = pair_rank.reshape(-1)
    flat_expert = routes.reshape(-1)
    flat_valid = jnp.broadcast_to(valid[:, None], routes.shape).reshape(-1)
    earlier = (
        (flat_rank[None, :] < flat_rank[:, None])
        & (flat_expert[None, :] == flat_expert[:, None])
        & flat_valid[None, :]
    )
    slot_index = jnp.sum(earlier.astype(jnp.int32), axis=1).reshape(row_count, top_count)
    kept_pair = valid[:, None] & (slot_index < capacity)
    target = routes * capacity + jnp.minimum(slot_index, capacity - 1)
    return (target, kept_pair)


def masked_scores(query, key_rows, allowed):
    scale = query.shape[-1] ** (-0.5)
    raw = jnp.einsum("qhd,khd->hqk", query, key_rows, preferred_element_type=jnp.float32) * scale
    return jnp.where(allowed[None], raw, NEGATIVE)


def contract_first(left, right):
    return lax.dot_general(
        left, right, (((0,), (0,)), ((), ())), preferred_element_type=jnp.float32
    )


def contract_last(left, right):
    return lax.dot_general(
        left, right, (((1,), (1,)), ((), ())), preferred_element_type=jnp.float32
    )


def normalize(rows):
    inverse = lax.rsqrt(jnp.mean(rows * rows, axis=-1, keepdims=True) + NORM_EPSILON)
    return rows * inverse, inverse


def exchange_experts(blocks):
    return lax.all_to_all(blocks, "expert", split_axis=0, concat_axis=0, tiled=True)


def line_order(place, step):
    upper = place // 2
    low = place * (1 - upper) + (3 - place) * upper
    first = 1 - (step + 1) // 2
    block = step + first * (1 - low) + (1 - first)
    return block * (1 - upper) + (3 - block) * upper


def rotated(grad, cosine, sine):
    return grad * cosine + pltpu.roll(grad, grad.shape[1] // 2, 1) * sine


def attention_back_kernel(
    heads,
    length,
    d_attn,
    tokens_all,
    inverse_all,
    whole,
    w_out,
    w_qkv,
    query,
    key_rows,
    value,
    attended,
    log_total,
    cosine,
    sine,
    small_part,
    gate_grads,
    grad_normed,
    grad_weights,
    small_out,
    gate_got,
    da_buf,
    tokens_buf,
    inverse_buf,
    whole_buf,
    w_out_buf,
    w_qkv_buf,
    query_buf,
    key_buf,
    value_buf,
    attended_buf,
    log_buf,
    cosine_buf,
    sine_buf,
    d_key_acc,
    d_value_acc,
    d_proj,
    normed_part,
    from_left,
    from_right,
    send_pair,
    recv_pair,
    own_part,
    half_x,
    half_y,
    full_x,
    full_y,
    small_buf,
    small_recv,
    small_z,
    keep_buf,
    load_sems,
    line_sems,
    sum_sems,
    pair_sems,
    ring_sems,
    small_sems,
    gate_sems,
):
    tok, width = d_attn.shape
    seq_len = tokens_all.shape[0]
    group = seq_len // tok
    local_width = w_out.shape[0]
    head_size = local_width // heads
    piece = own_part.shape[1]
    half = piece // 2
    scale = head_size**-0.5

    index = lax.axis_index("dp")
    place = lax.axis_index("expert")
    core = index % 2
    at_x = (index // 2) % 2
    at_y = index // 4
    partner = {"dp": at_y * 4 + at_x * 2 + (1 - core)}
    along_x = {"dp": at_y * 4 + (1 - at_x) * 2 + core}
    along_y = {"dp": (1 - at_y) * 4 + at_x * 2 + core}
    over = {"dp": (1 - at_y) * 4 + (1 - at_x) * 2 + core}
    parts = width // piece

    def chip(r):
        step_y = r // 2
        step_x = r % 2
        return (at_y + step_y - 2 * at_y * step_y) * 2 + (at_x + step_x - 2 * at_x * step_x)

    def ring_peer(k):
        return {"dp": (index + k) % parts}

    def line_peer(k):
        return {"expert": (place + k) % group}

    right = {"expert": (place + 1) % group}
    left = {"expert": (place + group - 1) % group}

    loads = [
        pltpu.make_async_copy(source, target, load_sems.at[number])
        for number, (source, target) in enumerate(
            [
                (w_out, w_out_buf),
                (query, query_buf),
                (key_rows, key_buf),
                (value, value_buf),
                (log_total, log_buf),
                (cosine, cosine_buf),
                (sine, sine_buf),
                (w_qkv, w_qkv_buf),
                (tokens_all, tokens_buf),
                (inverse_all, inverse_buf),
                (whole, whole_buf),
                (attended, attended_buf),
                (small_part, small_buf),
                (gate_grads.at[0], keep_buf),
            ]
        )
    ]
    early = 7
    for load in loads[:early]:
        load.start()

    greet([ring_peer(k) for k in range(1, parts)] + [line_peer(k) for k in range(1, group)])

    def rows_of(block):
        return pl.ds(pl.multiple_of(block * tok, tok), tok)

    own_load = pltpu.make_async_copy(d_attn, da_buf.at[rows_of(place)], load_sems.at[14])
    own_load.start()

    def own_right():
        return remote(
            d_attn, da_buf.at[rows_of(place)], line_sems.at[0, place], line_sems.at[2, place], right
        )

    def own_left():
        return remote(
            d_attn, da_buf.at[rows_of(place)], line_sems.at[1, place], line_sems.at[2, place], left
        )

    def pass_right(block):
        spot = da_buf.at[rows_of(block)]
        return remote(spot, spot, line_sems.at[0, block], line_sems.at[2, block], right)

    def pass_left(block):
        spot = da_buf.at[rows_of(block)]
        return remote(spot, spot, line_sems.at[1, block], line_sems.at[2, block], left)

    @pl.when(place < group - 1)
    def _():
        own_right().start()

    @pl.when(place > 0)
    def _():
        own_left().start()

    def gate_copy(r, peer):
        return remote(
            gate_grads.at[r], gate_got.at[r], gate_sems.at[0, r], gate_sems.at[1, r], peer
        )

    peers = (None, along_x, along_y, over)
    for r in (3, 1, 2):
        gate_copy(r, peers[r]).start()
    for load in loads[early:]:
        load.start()
    d_key_acc[...] = jnp.zeros_like(d_key_acc)
    d_value_acc[...] = jnp.zeros_like(d_value_acc)

    def attend_back(block):
        rows = rows_of(block)
        d_heads = dot_nt(da_buf[rows, :], w_out_buf[...]).astype(jnp.bfloat16)
        shape = (tok, seq_len)
        at_query = block * tok + lax.broadcasted_iota(jnp.int32, shape, 0)
        at_key = lax.broadcasted_iota(jnp.int32, shape, 1)
        allowed = (at_key <= at_query) & (at_key < length[0])
        for head in range(heads):
            cols = slice(head * head_size, (head + 1) * head_size)
            one_query = query_buf[rows, cols]
            one_key = key_buf[:, cols]
            d_head = d_heads[:, cols]
            scores = jnp.where(allowed, dot_nt(one_query, one_key) * scale, NEGATIVE)
            probs = jnp.exp(scores - log_buf[rows, head : head + 1])
            d_probs = dot_nt(d_head, value_buf[:, cols])
            delta = jnp.sum(probs * d_probs, axis=-1, keepdims=True)
            d_scores = (probs * (d_probs - delta)).astype(jnp.bfloat16)
            d_query = dot_nn(d_scores, one_key) * scale
            d_key_acc[:, cols] += dot_nn(d_scores.T, one_query) * scale
            d_value_acc[:, cols] += dot_nn(probs.astype(jnp.bfloat16).T, d_head)
            d_proj[rows, cols] = rotated(d_query, cosine_buf[rows, :], -sine_buf[rows, :]).astype(
                jnp.bfloat16
            )

    for load in loads[:early]:
        load.wait()
    own_load.wait()
    attend_back(place)

    def arrive(step, carry):
        block = line_order(place, step)
        pass_right(block).wait_recv()

        @pl.when((block < place) & (place < group - 1))
        def _():
            pass_right(block).start()

        @pl.when((block > place) & (place > 0))
        def _():
            pass_left(block).start()

        attend_back(block)
        return carry

    lax.fori_loop(0, group - 1, arrive, 0)
    for load in loads[early:]:
        load.wait()
    keep = pltpu.make_async_copy(keep_buf, gate_got.at[0], load_sems.at[15])
    keep.start()

    for head in range(heads):
        cols = slice(head * head_size, (head + 1) * head_size)
        key_cols = slice(local_width + head * head_size, local_width + (head + 1) * head_size)
        d_proj[:, key_cols] = rotated(d_key_acc[:, cols], cosine_buf[...], -sine_buf[...]).astype(
            jnp.bfloat16
        )
    d_proj[:, 2 * local_width :] = d_value_acc[...].astype(jnp.bfloat16)

    def normed_tile(j, carry):
        cols = pl.ds(pl.multiple_of(j * piece, piece), piece)
        d_normed = jnp.zeros((seq_len, piece), jnp.float32)
        for c in range(3):
            d_normed += dot_nt(
                d_proj[:, c * local_width : (c + 1) * local_width], w_qkv_buf[c, cols, :]
            )
        hat = tokens_buf[:, cols].astype(jnp.float32) * inverse_buf[...]
        small_buf[0:1, cols] = jnp.sum(d_normed * hat, axis=0, keepdims=True)
        normed_part[:, cols] = d_normed.astype(jnp.bfloat16)
        return carry

    lax.fori_loop(0, parts, normed_tile, 0)

    def go_right(block):
        return remote(
            normed_part.at[pl.ds(block * tok, tok)],
            from_left.at[block],
            sum_sems.at[0, block],
            sum_sems.at[1, block],
            right,
        )

    def go_left(block):
        return remote(
            normed_part.at[pl.ds(block * tok, tok)],
            from_right.at[block],
            sum_sems.at[0, block],
            sum_sems.at[2, block],
            left,
        )

    def add_into(target, other):
        value = target[...].astype(jnp.float32) + other[...].astype(jnp.float32)
        target[...] = value.astype(jnp.bfloat16)

    def on_right(block):
        go_right(block).wait_recv()
        add_into(normed_part.at[pl.ds(block * tok, tok)], from_left.at[block])
        go_right(block).start()

    def on_left(block):
        go_left(block).wait_recv()
        add_into(normed_part.at[pl.ds(block * tok, tok)], from_right.at[block])
        go_left(block).start()

    @pl.when(place == 0)
    def _():
        for block in (3, 2, 1):
            go_right(block).start()

    @pl.when(place == 3)
    def _():
        for block in (0, 1, 2):
            go_left(block).start()

    def small_copy(k):
        to = (index + k) % parts
        cols = pl.ds(pl.multiple_of(to * piece, piece), piece)
        return remote(
            small_buf.at[:, cols],
            small_recv.at[k],
            small_sems.at[0, k],
            small_sems.at[1, k],
            ring_peer(k),
        )

    for k in range(1, parts):
        small_copy(k).start()

    def weight_grad(which, r):
        cols = pl.ds(pl.multiple_of((chip(r) * 2 + which) * piece, piece), piece)
        left_side = whole_buf[:, cols].T
        first = dot_nn(left_side, d_proj[...])
        second = dot_nn(da_buf[:, cols].T, attended_buf[...])
        return jnp.concatenate([first, second], axis=1)

    def pair_copy(r):
        return remote(
            send_pair.at[r], recv_pair.at[r], pair_sems.at[0, r], pair_sems.at[1, r], partner
        )

    def for_partner(i, carry):
        r = 3 - i
        send_pair[r] = weight_grad(1 - core, r).astype(jnp.bfloat16)
        pair_copy(r).start()
        return carry

    lax.fori_loop(0, 4, for_partner, 0)

    @pl.when(place == 1)
    def _():
        on_right(3)

    @pl.when(place == 2)
    def _():
        on_left(0)

    def half_x_copy():
        return remote(
            own_part.at[3, pl.ds(0, half)], half_x, ring_sems.at[0, 0], ring_sems.at[1, 0], along_x
        )

    def half_y_copy():
        return remote(
            own_part.at[3, pl.ds(half, half)],
            half_y,
            ring_sems.at[0, 1],
            ring_sems.at[1, 1],
            along_y,
        )

    def full_x_copy():
        return remote(own_part.at[1], full_x, ring_sems.at[0, 2], ring_sems.at[1, 2], along_x)

    def full_y_copy():
        return remote(own_part.at[2], full_y, ring_sems.at[0, 3], ring_sems.at[1, 3], along_y)

    def for_self(i, carry):
        r = 3 - i
        pair_copy(r).wait_recv()
        own_part[r] = (weight_grad(core, r) + recv_pair[r].astype(jnp.float32)).astype(
            jnp.bfloat16
        )

        @pl.when(i == 0)
        def _():
            half_x_copy().start()
            half_y_copy().start()

        return carry

    lax.fori_loop(0, 4, for_self, 0)

    total = small_buf[:, pl.ds(pl.multiple_of(index * piece, piece), piece)]
    for k in range(1, parts):
        small_copy(k).wait_recv()
        total = total + small_recv[k]
    small_z[0] = total

    @pl.when(place == 1)
    def _():
        on_right(2)

    @pl.when(place == 2)
    def _():
        on_left(1)

    def small_line_copy(k):
        return remote(
            small_z.at[0],
            small_z.at[k],
            small_sems.at[0, parts + k],
            small_sems.at[1, parts + k],
            line_peer(k),
        )

    for k in range(1, group):
        small_line_copy(k).start()

    half_x_copy().wait_recv()
    add_into(own_part.at[2, pl.ds(0, half)], half_x)
    full_y_copy().start()
    half_y_copy().wait_recv()
    add_into(own_part.at[1, pl.ds(half, half)], half_y)
    full_x_copy().start()

    @pl.when(place == 1)
    def _():
        on_left(0)

    @pl.when(place == 2)
    def _():
        on_right(3)

    total = small_z[0]
    for k in range(1, group):
        small_line_copy(k).wait_recv()
        total = total + small_z[k]
    small_out[...] = total

    grad_normed[...] = normed_part[rows_of(place), :].astype(jnp.float32)

    @pl.when(place > 0)
    def _():
        go_right(place).wait_recv()
        grad_normed[...] += from_left[place].astype(jnp.float32)

    @pl.when(place < group - 1)
    def _():
        go_left(place).wait_recv()
        grad_normed[...] += from_right[place].astype(jnp.float32)

    full_x_copy().wait_recv()
    full_y_copy().wait_recv()
    grad_weights[...] = (
        own_part[0].astype(jnp.float32)
        + full_x[...].astype(jnp.float32)
        + full_y[...].astype(jnp.float32)
    )

    for r in (1, 2, 3):
        gate_copy(r, peers[r]).wait()
    keep.wait()
    half_x_copy().wait_send()
    half_y_copy().wait_send()
    full_x_copy().wait_send()
    full_y_copy().wait_send()
    for r in range(4):
        pair_copy(r).wait_send()
    for k in range(1, parts):
        small_copy(k).wait_send()
    for k in range(1, group):
        small_line_copy(k).wait_send()
    for block in range(group):

        @pl.when(block > place)
        def _():
            go_right(block).wait_send()

        @pl.when(block < place)
        def _():
            go_left(block).wait_send()

        @pl.when((block <= place) & (place < group - 1))
        def _():
            pass_right(block).wait_send()

        @pl.when((block >= place) & (place > 0))
        def _():
            pass_left(block).wait_send()


def attention_back_call(
    lengths,
    d_attn,
    tokens_all,
    inverse_all,
    whole,
    w_out,
    w_qkv,
    query,
    key_rows,
    value,
    attended,
    log_total,
    cosine,
    sine,
    small_part,
    gate_grads,
):
    tok, width = d_attn.shape
    seq_len = tokens_all.shape[0]
    group = seq_len // tok
    local_width = w_out.shape[0]
    heads = log_total.shape[1]
    piece = gate_grads.shape[1]
    half = piece // 2
    parts = width // piece
    small_rows = small_part.shape[0]
    low, full = jnp.bfloat16, jnp.float32
    anywhere = pl.BlockSpec(memory_space=pl.ANY)
    inside = pl.BlockSpec(memory_space=pltpu.VMEM)

    def like(array):
        return pltpu.VMEM(array.shape, array.dtype)

    flops = 2 * seq_len * width * local_width * 8 + 10 * seq_len * seq_len * local_width
    return pl.pallas_call(
        functools.partial(attention_back_kernel, heads),
        out_shape=(
            jax.ShapeDtypeStruct((tok, width), full),
            jax.ShapeDtypeStruct((piece, 4 * local_width), full),
            jax.ShapeDtypeStruct((small_rows, piece), full),
            jax.ShapeDtypeStruct(gate_grads.shape, low),
        ),
        in_specs=[pl.BlockSpec(memory_space=pltpu.SMEM)] + [anywhere] * 15,
        out_specs=(inside, inside, inside, anywhere),
        scratch_shapes=[
            pltpu.VMEM((seq_len, width), low),
            like(tokens_all),
            like(inverse_all),
            like(whole),
            like(w_out),
            like(w_qkv),
            like(query),
            like(key_rows),
            like(value),
            like(attended),
            like(log_total),
            like(cosine),
            like(sine),
            pltpu.VMEM((seq_len, local_width), full),
            pltpu.VMEM((seq_len, local_width), full),
            pltpu.VMEM((seq_len, 3 * local_width), low),
            pltpu.VMEM((seq_len, width), low),
            pltpu.VMEM((group, tok, width), low),
            pltpu.VMEM((group, tok, width), low),
            pltpu.VMEM((4, piece, 4 * local_width), low),
            pltpu.VMEM((4, piece, 4 * local_width), low),
            pltpu.VMEM((4, piece, 4 * local_width), low),
            pltpu.VMEM((half, 4 * local_width), low),
            pltpu.VMEM((half, 4 * local_width), low),
            pltpu.VMEM((piece, 4 * local_width), low),
            pltpu.VMEM((piece, 4 * local_width), low),
            like(small_part),
            pltpu.VMEM((parts, small_rows, piece), full),
            pltpu.VMEM((group, small_rows, piece), full),
            pltpu.VMEM(gate_grads.shape[1:], low),
            pltpu.SemaphoreType.DMA((16,)),
            pltpu.SemaphoreType.DMA((3, group)),
            pltpu.SemaphoreType.DMA((3, group)),
            pltpu.SemaphoreType.DMA((2, 4)),
            pltpu.SemaphoreType.DMA((2, 4)),
            pltpu.SemaphoreType.DMA((2, parts + group)),
            pltpu.SemaphoreType.DMA((2, 4)),
        ],
        compiler_params=pltpu.CompilerParams(
            collective_id=2, has_side_effects=True, vmem_limit_bytes=67043328
        ),
        cost_estimate=pl.CostEstimate(flops=flops, bytes_accessed=40000000, transcendentals=0),
        name="attention_back",
    )(
        lengths,
        d_attn,
        tokens_all,
        inverse_all,
        whole,
        w_out,
        w_qkv,
        query,
        key_rows,
        value,
        attended,
        log_total,
        cosine,
        sine,
        small_part,
        gate_grads,
    )


def widen_slices(grads):
    chips, rows, hidden2 = grads.shape
    own = (lax.axis_index("dp") // 2).astype(jnp.int32).reshape(1)
    size = hidden2 // 2

    def body(own_ref, source, target):
        target[...] = source[0].astype(jnp.float32)

    wide = pl.pallas_call(
        body,
        out_shape=jax.ShapeDtypeStruct((rows, chips * hidden2), jnp.float32),
        grid_spec=pltpu.PrefetchScalarGridSpec(
            num_scalar_prefetch=1,
            grid=(2, chips),
            in_specs=[
                pl.BlockSpec((1, rows, size), lambda part, at, own_ref: (at ^ own_ref[0], 0, part))
            ],
            out_specs=pl.BlockSpec((rows, size), lambda part, at, own_ref: (0, part * chips + at)),
        ),
        name="widen",
    )(own, grads)
    return wide[None]


def rotary_constants(length_total, head_size):
    position = np.arange(length_total, dtype=np.float32)
    steps = np.arange(head_size // 2, dtype=np.float32) * np.float32(2.0) / np.float32(head_size)
    frequency = np.power(np.float32(THETA), -steps).astype(np.float32)
    angles = (position[:, None] * frequency[None, :]).astype(np.float32)
    cosine, sine = np.cos(angles), np.sin(angles)
    return (
        np.concatenate([cosine, cosine], axis=1).astype(np.float32),
        np.concatenate([-sine, sine], axis=1).astype(np.float32),
    )


def attention_kernel(
    heads,
    length,
    tokens,
    w_qkv,
    w_out,
    small,
    w_gate_up,
    pair_cols,
    pair_rows,
    cosine,
    sine,
    cotangent,
    tokens_all,
    whole,
    qkv_full,
    out_full,
    w_got,
    inverse_all,
    query,
    key_rows,
    value,
    attended,
    log_total,
    small_full,
    resid,
    inverse_two,
    gates,
    hits,
    sent,
    d_back,
    tokens_buf,
    whole_buf,
    w_qkv_buf,
    w_out_buf,
    part_buf,
    from_left,
    from_right,
    cols_buf,
    rows_buf,
    cosine_buf,
    sine_buf,
    cotangent_buf,
    load_sems,
    line_sems,
    sum_sems,
    gather_sems,
    small_sems,
    slice_sems,
):
    tok, width = tokens.shape
    seq_len = tokens_buf.shape[0]
    group = seq_len // tok
    local_width = w_out.shape[0]
    head_size = local_width // heads
    piece = w_qkv.shape[1]
    parts = width // piece
    ff = w_gate_up.shape[2] // 2
    hidden = ff // 4
    slots = hits.shape[1]
    cap = slots // group
    scale = head_size**-0.5

    index = lax.axis_index("dp")
    place = lax.axis_index("expert")
    core = index % 2
    at_x = (index // 2) % 2
    at_y = index // 4
    other = at_y * 4 + at_x * 2 + (1 - core)
    by_x = at_y * 4 + (1 - at_x) * 2 + core
    by_y = (1 - at_y) * 4 + at_x * 2 + core
    by_both = (1 - at_y) * 4 + (1 - at_x) * 2 + core
    partner = {"dp": other}
    along_x = {"dp": by_x}
    along_y = {"dp": by_y}
    over = {"dp": by_both}
    right = {"expert": (place + 1) % group}
    left = {"expert": (place + group - 1) % group}

    def ring_peer(k):
        return {"dp": (index + k) % parts}

    def rows_of(block):
        return pl.ds(pl.multiple_of(block * tok, tok), tok)

    def piece_of(number):
        return pl.ds(pl.multiple_of(number * piece, piece), piece)

    def qkv_spot(number):
        return w_qkv_buf.at[:, piece_of(number), :]

    def qkv_half(number, which):
        start = pl.multiple_of(number * piece + which * (piece // 2), piece // 2)
        return w_qkv_buf.at[:, pl.ds(start, piece // 2), :]

    def out_spot(number):
        return w_out_buf.at[:, piece_of(number)]

    def out_half(number, which):
        rows = pl.ds(which * (local_width // 2), local_width // 2)
        return w_out_buf.at[rows, piece_of(number)]

    class Gather:
        def __init__(self, number, source, spot, half_spot):
            self.number, self.source, self.spot, self.half_spot = number, source, spot, half_spot

        def copy(self, slot, source, target, peer):
            sems = gather_sems.at[self.number]
            return remote(source, target, sems.at[0, slot], sems.at[1, slot], peer)

        def own(self, slot, peer):
            return self.copy(slot, self.source, self.spot(index), peer)

        def keep(self):
            return pltpu.make_async_copy(
                self.source, self.spot(index), load_sems.at[8 + self.number]
            )

        def relay_x(self):
            spot = self.half_spot(by_y, 0)
            return self.copy(3, spot, spot, along_x)

        def relay_y(self):
            spot = self.half_spot(by_x, 1)
            return self.copy(4, spot, spot, along_y)

        def hand(self, slot):
            spot = (
                self.spot(by_x),
                self.spot(by_y),
                self.half_spot(by_both, 0),
                self.half_spot(by_both, 1),
            )[slot - 5]
            return self.copy(slot, spot, spot, partner)

        def begin(self):
            self.own(0, along_x).start()
            self.own(1, along_y).start()
            self.own(2, partner).start()
            self.keep().start()

        def relay(self):
            self.own(1, along_y).wait_recv()
            self.relay_x().start()
            self.own(0, along_x).wait_recv()
            self.relay_y().start()
            self.hand(5).start()
            self.hand(6).start()

        def finish(self):
            self.relay_x().wait_recv()
            self.hand(7).start()
            self.relay_y().wait_recv()
            self.hand(8).start()
            self.keep().wait()
            self.own(2, partner).wait_recv()
            for slot in (5, 6, 7, 8):
                self.hand(slot).wait_recv()

        def drain(self):
            for slot, peer in ((0, along_x), (1, along_y), (2, partner)):
                self.own(slot, peer).wait_send()
            self.relay_x().wait_send()
            self.relay_y().wait_send()
            for slot in (5, 6, 7, 8):
                self.hand(slot).wait_send()

    gather_qkv = Gather(0, w_qkv, qkv_spot, qkv_half)
    gather_out = Gather(1, w_out, out_spot, out_half)

    loads = [
        pltpu.make_async_copy(source, target, load_sems.at[number])
        for number, (source, target) in enumerate(
            [
                (tokens, tokens_buf.at[rows_of(place)]),
                (small, small_full.at[:, piece_of(index)]),
                (pair_cols, cols_buf),
                (pair_rows, rows_buf),
                (cosine, cosine_buf),
                (sine, sine_buf),
                (cotangent, cotangent_buf),
            ]
        )
    ]
    for load in loads:
        load.start()

    greet([ring_peer(k) for k in range(1, parts)] + [right, left])

    def own_pass(side, peer):
        return remote(
            tokens,
            tokens_buf.at[rows_of(place)],
            line_sems.at[side, place],
            line_sems.at[2, place],
            peer,
        )

    def pass_on(block, side, peer):
        spot = tokens_buf.at[rows_of(block)]
        return remote(spot, spot, line_sems.at[side, block], line_sems.at[2, block], peer)

    @pl.when(place < group - 1)
    def _():
        own_pass(0, right).start()

    @pl.when(place > 0)
    def _():
        own_pass(1, left).start()

    def small_copy(k):
        return remote(
            small,
            small_full.at[:, piece_of(index)],
            small_sems.at[0, k],
            small_sems.at[1, k],
            ring_peer(k),
        )

    for k in range(1, parts):
        small_copy(k).start()
    gather_qkv.begin()

    for load in loads:
        load.wait()

    cols = cols_buf[...]
    rows = rows_buf[...]
    first_col, second_col, order_col = cols[:, 0:1], cols[:, 1:2], cols[:, 2:3]
    first_row, second_row, order_row = rows[0:1], rows[1:2], rows[2:3]
    start = place * tok
    live_col = (start + lax.broadcasted_iota(jnp.int32, (tok, 1), 0)) < length[0]
    live_row = (start + lax.broadcasted_iota(jnp.int32, (1, tok), 1)) < length[0]
    before = order_col < order_row

    def count(mask):
        return jnp.sum(jnp.where(mask & live_col, 1.0, 0.0), axis=0, keepdims=True)

    slot_first = count((first_col == first_row) & before)
    slot_second = count(first_col == second_row) + count((second_col == second_row) & before)
    slot_ids = lax.broadcasted_iota(jnp.int32, (slots, tok), 0)
    for number, (named, slot) in enumerate(((first_row, slot_first), (second_row, slot_second))):
        slot = slot.astype(jnp.int32)
        step = named - place
        step = jnp.where(step < 0, step + group, step)
        target = jnp.where(live_row & (slot < cap), step * cap + slot, -1)
        hits[number] = jnp.where(slot_ids == target, 1.0, 0.0).astype(jnp.bfloat16)

    for k in range(1, parts):
        small_copy(k).wait_recv()

    def normalize_block(block):
        at = rows_of(block)
        value = tokens_buf[at, :].astype(jnp.float32)
        inverse = lax.rsqrt(jnp.mean(value * value, axis=-1, keepdims=True) + NORM_EPSILON)
        inverse_all[at, :] = inverse
        whole_buf[at, :] = (value * inverse * small_full[0:1, :]).astype(jnp.bfloat16)

    def arrive(step):
        block = line_order(place, step)
        pass_on(block, 0, right).wait_recv()

        @pl.when((block < place) & (place < group - 1))
        def _():
            pass_on(block, 0, right).start()

        @pl.when((block > place) & (place > 0))
        def _():
            pass_on(block, 1, left).start()

        normalize_block(block)

    normalize_block(place)
    arrive(0)
    gather_qkv.relay()
    gather_out.begin()
    arrive(1)
    gather_qkv.finish()

    def project(first, size):
        at = pl.ds(pl.multiple_of(first, tok), size)
        source = whole_buf[at, :]

        def two_heads(number, carry):
            lanes = pl.ds(pl.multiple_of(number * 2 * head_size, 2 * head_size), 2 * head_size)
            for c, target in ((0, query), (1, key_rows)):
                plain = dot_nn(source, w_qkv_buf[c, :, lanes])
                turned = [
                    rotated(
                        plain[:, side * head_size : (side + 1) * head_size],
                        cosine_buf[at, :],
                        sine_buf[at, :],
                    )
                    for side in range(2)
                ]
                target[at, lanes] = jnp.concatenate(turned, axis=1).astype(jnp.bfloat16)
            value[at, lanes] = dot_nn(source, w_qkv_buf[2, :, lanes]).astype(jnp.bfloat16)
            return carry

        lax.fori_loop(0, heads // 2, two_heads, 0)

    upper = place // 2
    project(upper * tok, seq_len - tok)
    gather_out.relay()

    def slice_copy(r, part):
        number = (by_x // 2, by_y // 2, by_both // 2)[r - 1]
        lanes = pl.ds(pl.multiple_of(part * ff + number * hidden, LANES), hidden)
        return remote(
            w_gate_up.at[0, :, lanes],
            w_got.at[r - 1, :, pl.ds(part * hidden, hidden)],
            slice_sems.at[0, r - 1, part],
            slice_sems.at[1, r - 1, part],
            (along_x, along_y, over)[r - 1],
        )

    for part in range(2):
        for r in (3, 1, 2):
            slice_copy(r, part).start()
    gather_out.finish()
    arrive(2)
    project((1 - upper) * (seq_len - tok), tok)

    stores = [
        pltpu.make_async_copy(source, target, load_sems.at[10 + number])
        for number, (source, target) in enumerate(
            [
                (w_qkv_buf, qkv_full),
                (w_out_buf, out_full),
                (tokens_buf, tokens_all),
                (whole_buf, whole),
            ]
        )
    ]
    for store in stores:
        store.start()

    for number in range(group):
        at = slice(number * tok, (number + 1) * tok)
        extent = (number + 1) * tok
        shape = (tok, extent)
        at_query = number * tok + lax.broadcasted_iota(jnp.int32, shape, 0)
        at_key = lax.broadcasted_iota(jnp.int32, shape, 1)
        allowed = (at_key <= at_query) & (at_key < length[0])
        for head in range(heads):
            lanes = slice(head * head_size, (head + 1) * head_size)
            scores = dot_nt(query[at, lanes], key_rows[0:extent, lanes]) * scale
            scores = jnp.where(allowed, scores, NEGATIVE)
            top = jnp.max(scores, axis=-1, keepdims=True)
            exponent = jnp.exp(scores - top)
            row_total = jnp.sum(exponent, axis=-1, keepdims=True)
            probs = (exponent / row_total).astype(jnp.bfloat16)
            attended[at, lanes] = dot_nn(probs, value[0:extent, lanes]).astype(jnp.bfloat16)
            log_total[at, head : head + 1] = top + jnp.log(row_total)

    def out_tile(j, carry):
        lanes = piece_of(j)
        part_buf[:, lanes] = dot_nn(attended[...], w_out_buf[:, lanes]).astype(jnp.bfloat16)
        return carry

    lax.fori_loop(0, parts, out_tile, 0)

    def go_right(block):
        return remote(
            part_buf.at[rows_of(block)],
            from_left.at[block],
            sum_sems.at[0, block],
            sum_sems.at[1, block],
            right,
        )

    def go_left(block):
        return remote(
            part_buf.at[rows_of(block)],
            from_right.at[block],
            sum_sems.at[0, block],
            sum_sems.at[2, block],
            left,
        )

    def add_into(target, added):
        total = target[...].astype(jnp.float32) + added[...].astype(jnp.float32)
        target[...] = total.astype(jnp.bfloat16)

    def on_right(block):
        go_right(block).wait_recv()
        add_into(part_buf.at[rows_of(block)], from_left.at[block])
        go_right(block).start()

    def on_left(block):
        go_left(block).wait_recv()
        add_into(part_buf.at[rows_of(block)], from_right.at[block])
        go_left(block).start()

    @pl.when(place == 0)
    def _():
        for block in (3, 2, 1):
            go_right(block).start()

    @pl.when(place == 3)
    def _():
        for block in (0, 1, 2):
            go_left(block).start()

    @pl.when(place == 1)
    def _():
        on_right(3)
        on_right(2)
        on_left(0)

    @pl.when(place == 2)
    def _():
        on_left(0)
        on_left(1)
        on_right(3)

    resid[...] = tokens_buf[rows_of(place), :].astype(jnp.float32) + part_buf[
        rows_of(place), :
    ].astype(jnp.float32)

    @pl.when(place > 0)
    def _():
        go_right(place).wait_recv()
        resid[...] += from_left[place].astype(jnp.float32)

    @pl.when(place < group - 1)
    def _():
        go_left(place).wait_recv()
        resid[...] += from_right[place].astype(jnp.float32)

    total = resid[...]
    inverse = lax.rsqrt(jnp.mean(total * total, axis=-1, keepdims=True) + NORM_EPSILON)
    inverse_two[...] = inverse
    hidden_in = (total * inverse * small_full[1:2, :]).astype(jnp.bfloat16)
    logits = dot_nt(hidden_in, small_full[...].astype(jnp.bfloat16))
    lane = lax.broadcasted_iota(jnp.int32, logits.shape, 1)
    chosen = [
        jnp.sum(jnp.where(lane == named + 2, logits, 0.0), axis=1, keepdims=True)
        for named in (first_col, second_col)
    ]
    top = jnp.maximum(chosen[0], chosen[1])
    raised = [jnp.exp(entry - top) for entry in chosen]
    both = raised[0] + raised[1]
    gate = [entry / both for entry in raised]
    for number in range(2):
        gates[:, number : number + 1] = gate[number]
    sent[...] = dot_nn(hits[0] + hits[1], hidden_in).astype(jnp.bfloat16)
    d_out = jnp.where(live_col, 1.0, 0.0) * cotangent_buf[...].astype(jnp.float32)
    d_back[...] = (
        dot_nn(hits[0], (gate[0] * d_out).astype(jnp.bfloat16))
        + dot_nn(hits[1], (gate[1] * d_out).astype(jnp.bfloat16))
    ).astype(jnp.bfloat16)

    for store in stores:
        store.wait()
    gather_qkv.drain()
    gather_out.drain()
    for k in range(1, parts):
        small_copy(k).wait_send()
    for block in range(group):

        @pl.when(block > place)
        def _():
            go_right(block).wait_send()

        @pl.when(block < place)
        def _():
            go_left(block).wait_send()

        @pl.when((block <= place) & (place < group - 1))
        def _():
            pass_on(block, 0, right).wait_send()

        @pl.when((block >= place) & (place > 0))
        def _():
            pass_on(block, 1, left).wait_send()

    for part in range(2):
        for r in (1, 2, 3):
            slice_copy(r, part).wait()


def attention_call(
    lengths, tokens, w_qkv, w_out, small, w_gate_up, routes, order, cosine, sine, cotangent, group
):
    tok, width = tokens.shape
    seq_len = tok * group
    local_width = w_qkv.shape[2]
    heads = local_width // HEAD_DIM
    slots = tok * routes.shape[1]
    piece = w_qkv.shape[1]
    low, full = jnp.bfloat16, jnp.float32
    pair_cols = jnp.concatenate([routes, order[:, None], jnp.zeros((tok, 5), jnp.int32)], axis=1)
    pair_rows = pair_cols.T
    anywhere = pl.BlockSpec(memory_space=pl.ANY)
    inside = pl.BlockSpec(memory_space=pltpu.VMEM)
    narrow = jax.ShapeDtypeStruct((seq_len, local_width), low)
    flops = 2 * seq_len * width * local_width * 4 + 4 * seq_len * seq_len * local_width
    return pl.pallas_call(
        functools.partial(attention_kernel, heads),
        out_shape=(
            jax.ShapeDtypeStruct((seq_len, width), low),
            jax.ShapeDtypeStruct((seq_len, width), low),
            jax.ShapeDtypeStruct((3, width, local_width), low),
            jax.ShapeDtypeStruct((local_width, width), low),
            jax.ShapeDtypeStruct((3, piece, w_gate_up.shape[2] // 4), low),
            jax.ShapeDtypeStruct((seq_len, 1), full),
            narrow,
            narrow,
            narrow,
            narrow,
            jax.ShapeDtypeStruct((seq_len, heads), full),
            jax.ShapeDtypeStruct((small.shape[0], width), full),
            jax.ShapeDtypeStruct((tok, width), full),
            jax.ShapeDtypeStruct((tok, 1), full),
            jax.ShapeDtypeStruct((tok, 2), full),
            jax.ShapeDtypeStruct((2, slots, tok), low),
            jax.ShapeDtypeStruct((slots, width), low),
            jax.ShapeDtypeStruct((slots, width), low),
        ),
        in_specs=[pl.BlockSpec(memory_space=pltpu.SMEM)] + [anywhere] * 10,
        out_specs=(anywhere,) * 5 + (inside,) * 13,
        scratch_shapes=[
            pltpu.VMEM((seq_len, width), low),
            pltpu.VMEM((seq_len, width), low),
            pltpu.VMEM((3, width, local_width), low),
            pltpu.VMEM((local_width, width), low),
            pltpu.VMEM((seq_len, width), low),
            pltpu.VMEM((group, tok, width), low),
            pltpu.VMEM((group, tok, width), low),
            pltpu.VMEM((tok, 8), jnp.int32),
            pltpu.VMEM((8, tok), jnp.int32),
            pltpu.VMEM(cosine.shape, full),
            pltpu.VMEM(sine.shape, full),
            pltpu.VMEM((tok, width), low),
            pltpu.SemaphoreType.DMA((14,)),
            pltpu.SemaphoreType.DMA((3, group)),
            pltpu.SemaphoreType.DMA((3, group)),
            pltpu.SemaphoreType.DMA((2, 2, 9)),
            pltpu.SemaphoreType.DMA((2, width // piece)),
            pltpu.SemaphoreType.DMA((2, 3, 2)),
        ],
        compiler_params=pltpu.CompilerParams(
            collective_id=3, has_side_effects=True, vmem_limit_bytes=67043328
        ),
        cost_estimate=pl.CostEstimate(flops=flops, bytes_accessed=40000000, transcendentals=0),
        name="attention",
    )(
        lengths,
        tokens,
        w_qkv,
        w_out,
        small,
        w_gate_up,
        pair_cols,
        pair_rows,
        cosine,
        sine,
        cotangent,
    )


def expert_step(gate_up_w, down_w, rows, d_rows_out):
    ff = down_w.shape[0]
    gate_up = jnp.dot(rows, gate_up_w, preferred_element_type=jnp.float32)
    gate = gate_up[:, :ff]
    upward = gate_up[:, ff:]
    sigmoid = jax.nn.sigmoid(gate)
    activated = (gate * sigmoid * upward).astype(jnp.bfloat16)
    out = jnp.dot(activated, down_w, preferred_element_type=jnp.float32).astype(jnp.bfloat16)
    d_activated = contract_last(d_rows_out, down_w)
    grad_down = contract_first(activated, d_rows_out)
    d_gate = d_activated * upward * sigmoid * (1.0 + gate * (1.0 - sigmoid))
    d_up = d_activated * gate * sigmoid
    d_gate_up = jnp.concatenate([d_gate, d_up], axis=1).astype(jnp.bfloat16)
    d_rows = contract_last(d_gate_up, gate_up_w).astype(jnp.bfloat16)
    grad_gate_up = contract_first(rows, d_gate_up)
    return out, d_rows, grad_gate_up, grad_down


def experts_gather_weights(w_gate_up, w_down, rows, d_rows_out):
    gate_up_w = lax.all_gather(w_gate_up, "dp", axis=1, tiled=True)[0]
    down_w = lax.all_gather(w_down, "dp", axis=1, tiled=True)[0]
    shape = rows.shape
    flat = (-1, shape[2])
    rows = exchange_experts(rows).reshape(flat)
    d_rows_out = exchange_experts(d_rows_out).reshape(flat)
    out, d_rows, grad_gate_up, grad_down = expert_step(gate_up_w, down_w, rows, d_rows_out)
    out = exchange_experts(out.reshape(shape))
    d_rows = exchange_experts(d_rows.reshape(shape))
    grad_gate_up = lax.psum_scatter(
        grad_gate_up.astype(jnp.bfloat16), "dp", scatter_dimension=0, tiled=True
    )
    grad_down = lax.psum_scatter(
        grad_down.astype(jnp.bfloat16), "dp", scatter_dimension=0, tiled=True
    )
    return (
        out,
        d_rows,
        grad_gate_up.astype(jnp.float32)[None],
        grad_down.astype(jnp.float32)[None],
    )


def attention_back_plain(
    lengths,
    d_attn,
    hat_all,
    whole,
    out_full,
    qkv_full,
    query,
    key_rows,
    value,
    attended,
    log_total,
    cosine,
    sine,
):
    seq_len, heads_local, head_size = query.shape
    local_width = heads_local * head_size
    position = jnp.arange(seq_len, dtype=jnp.int32)
    allowed = (position[None, :] <= position[:, None]) & (position < lengths[0])[None, :]
    whole_grad = lax.all_gather(d_attn, "expert", axis=0, tiled=True)
    d_attended = contract_last(whole_grad, out_full).astype(jnp.bfloat16)
    out_part = contract_first(attended, whole_grad)
    grad_out = lax.psum_scatter(
        out_part.astype(jnp.bfloat16), "dp", scatter_dimension=1, tiled=True
    ).astype(jnp.float32)
    d_heads = d_attended.reshape(seq_len, heads_local, head_size)
    probs = jnp.exp(masked_scores(query, key_rows, allowed) - log_total)
    probs_low = probs.astype(jnp.bfloat16)
    d_value = jnp.einsum(
        "hqk,qhd->khd", probs_low, d_heads, preferred_element_type=jnp.float32
    ).astype(jnp.bfloat16)
    d_probs = jnp.einsum("qhd,khd->hqk", d_heads, value, preferred_element_type=jnp.float32)
    row_delta = jnp.sum(probs * d_probs, axis=-1, keepdims=True)
    d_scores = (probs * (d_probs - row_delta)).astype(jnp.bfloat16)
    scale = head_size ** (-0.5)
    d_query = (
        jnp.einsum("hqk,khd->qhd", d_scores, key_rows, preferred_element_type=jnp.float32) * scale
    )
    d_key = jnp.einsum("hqk,qhd->khd", d_scores, query, preferred_element_type=jnp.float32) * scale
    d_query_pre = (
        rotate_back(d_query, cosine, sine).reshape(seq_len, local_width).astype(jnp.bfloat16)
    )
    d_key_pre = rotate_back(d_key, cosine, sine).reshape(seq_len, local_width).astype(jnp.bfloat16)
    d_projected = jnp.stack([d_query_pre, d_key_pre, d_value.reshape(seq_len, local_width)])
    d_normed_part = jnp.einsum(
        "cte,cde->td", d_projected, qkv_full, preferred_element_type=jnp.float32
    )
    grad_normalized = lax.psum_scatter(
        d_normed_part.astype(jnp.bfloat16), "expert", scatter_dimension=0, tiled=True
    ).astype(jnp.float32)
    qkv_part = jnp.einsum("td,cte->cde", whole, d_projected, preferred_element_type=jnp.float32)
    grad_qkv = lax.psum_scatter(
        qkv_part.astype(jnp.bfloat16), "dp", scatter_dimension=1, tiled=True
    ).astype(jnp.float32)
    first_gain_part = jnp.sum(d_normed_part * hat_all, axis=0)
    return grad_normalized, grad_qkv, grad_out, first_gain_part


def on_device(
    tokens,
    w_qkv,
    w_out,
    attention_norm_gain,
    gain_ffn,
    w_router,
    w_gate_up,
    w_down,
    lengths,
    routes,
    order,
    cotangent,
):
    group_size = lax.axis_size("expert")
    dp_size = lax.axis_size("dp")
    tok_dev = tokens.shape[0]
    seq_len = tok_dev * group_size
    width = tokens.shape[1]
    top_count = routes.shape[1]
    capacity = tok_dev * top_count // group_size
    slots = group_size * capacity
    head_size = HEAD_DIM
    local_width = w_qkv.shape[2]
    heads_local = local_width // head_size
    tokens_all = lax.all_gather(tokens, "expert", axis=0, tiled=True)
    small = jnp.concatenate(
        [attention_norm_gain[:, None], gain_ffn[:, None], w_router], axis=1
    )
    small_full = lax.all_gather(small, "dp", axis=0, tiled=True)
    qkv_full = lax.all_gather(w_qkv, "dp", axis=1, tiled=True)
    out_full = lax.all_gather(w_out, "dp", axis=1, tiled=True)
    first_norm_gain = small_full[:, 0].astype(jnp.float32)
    gain_two = small_full[:, 1].astype(jnp.float32)
    router_full = small_full[:, 2:]

    own_start = lax.axis_index("expert") * tok_dev
    own_position = own_start + jnp.arange(tok_dev, dtype=jnp.int32)
    live_own = own_position < lengths[0]
    live_rows = live_own.astype(jnp.float32)[:, None]
    target, kept_pair = slot_table(routes, order, live_own, capacity)
    slot_ids = jnp.arange(slots, dtype=jnp.int32)
    pair_hits = (slot_ids[:, None, None] == target[None]) & kept_pair[None]
    select = jnp.sum(pair_hits.astype(jnp.float32), axis=2).astype(jnp.bfloat16)

    inputs_float = tokens.astype(jnp.float32)
    input_normalized_hat, first_inverse_rms = normalize(inputs_float)
    hat_all, _ = normalize(tokens_all.astype(jnp.float32))
    whole = (hat_all * first_norm_gain).astype(jnp.bfloat16)
    cosine, sine = rotary_tables(seq_len, head_size)
    projected = jnp.einsum("td,cde->cte", whole, qkv_full, preferred_element_type=jnp.float32)
    query = rotate(projected[0].reshape(seq_len, heads_local, head_size), cosine, sine).astype(
        jnp.bfloat16
    )
    key_rows = rotate(projected[1].reshape(seq_len, heads_local, head_size), cosine, sine).astype(
        jnp.bfloat16
    )
    value = projected[2].astype(jnp.bfloat16).reshape(seq_len, heads_local, head_size)
    position = jnp.arange(seq_len, dtype=jnp.int32)
    live_all = position < lengths[0]
    allowed = (position[None, :] <= position[:, None]) & live_all[None, :]
    scores = masked_scores(query, key_rows, allowed)
    top_score = jnp.max(scores, axis=-1, keepdims=True)
    exponent = jnp.exp(scores - top_score)
    row_total = jnp.sum(exponent, axis=-1, keepdims=True)
    probs = exponent / row_total
    log_total = top_score + jnp.log(row_total)
    probs_low = probs.astype(jnp.bfloat16)
    attended = jnp.einsum("hqk,khd->qhd", probs_low, value, preferred_element_type=jnp.float32)
    attended = attended.reshape(seq_len, local_width).astype(jnp.bfloat16)
    attn_part = jnp.dot(attended, out_full, preferred_element_type=jnp.float32)
    attn_own = lax.psum_scatter(
        attn_part.astype(jnp.bfloat16), "expert", scatter_dimension=0, tiled=True
    ).astype(jnp.float32)
    resid = inputs_float + attn_own
    hhat, inverse_two = normalize(resid)
    hidden_in = (hhat * gain_two).astype(jnp.bfloat16)
    sent = jnp.dot(select, hidden_in, preferred_element_type=jnp.float32).astype(jnp.bfloat16)

    logits = jnp.dot(hidden_in, router_full, preferred_element_type=jnp.float32)
    chosen = jnp.take_along_axis(logits, routes, axis=1)
    gates = jax.nn.softmax(chosen, axis=1)
    d_out = live_rows * cotangent.astype(jnp.float32)
    d_back = jnp.zeros((slots, width), jnp.float32)
    for index in range(top_count):
        weighted = (gates[:, index : index + 1] * d_out).astype(jnp.bfloat16)
        d_back = d_back + jnp.dot(
            pair_hits[:, :, index].astype(jnp.bfloat16),
            weighted,
            preferred_element_type=jnp.float32,
        )
    d_back = d_back.astype(jnp.bfloat16)
    blocked = (group_size, capacity, width)
    returned, d_sent, grad_gate_up, grad_down = experts_gather_weights(
        w_gate_up, w_down, sent.reshape(blocked), d_back.reshape(blocked)
    )
    returned = returned.reshape(slots, width)
    d_sent = d_sent.reshape(slots, width)

    moe = jnp.zeros_like(resid)
    d_gates_list = []
    for index in range(top_count):
        one_hot = pair_hits[:, :, index].astype(jnp.bfloat16)
        picked = contract_first(one_hot, returned)
        d_gates_list.append(jnp.sum(d_out * picked, axis=-1))
        moe = moe + gates[:, index : index + 1] * picked
    output = (live_rows * (resid + moe)).astype(jnp.bfloat16)
    d_gates = jnp.stack(d_gates_list, axis=1)
    d_hidden = contract_first(select, d_sent)
    d_chosen = gates * (d_gates - jnp.sum(gates * d_gates, axis=1, keepdims=True))
    expert_ids = jnp.arange(group_size, dtype=jnp.int32)
    route_hits = (routes[:, :, None] == expert_ids[None, None, :]).astype(jnp.float32)
    d_logits = jnp.sum(route_hits * d_chosen[:, :, None], axis=1)
    router_f = router_full.astype(jnp.float32)
    d_hidden = d_hidden + jnp.dot(
        d_logits, router_f.T, precision=HIGH, preferred_element_type=jnp.float32
    )
    router_part = jnp.dot(
        hidden_in.astype(jnp.float32).T,
        d_logits,
        precision=HIGH,
        preferred_element_type=jnp.float32,
    )
    gain_two_part = jnp.sum(d_hidden * hhat, axis=0)
    scaled_two = d_hidden * gain_two
    d_resid = d_out + inverse_two * (
        scaled_two - hhat * jnp.mean(scaled_two * hhat, axis=-1, keepdims=True)
    )
    d_attn = d_resid.astype(jnp.bfloat16)
    grad_normalized, grad_qkv, grad_out, first_gain_part = attention_back_plain(
        lengths,
        d_attn,
        hat_all,
        whole,
        out_full,
        qkv_full,
        query,
        key_rows,
        value,
        attended,
        log_total,
        cosine,
        sine,
    )
    small_part = jnp.concatenate(
        [first_gain_part[None], gain_two_part[None], router_part.T], axis=0
    )
    small_sum = lax.psum(small_part, ("dp", "expert"))
    own_rows = width // dp_size
    small_own = lax.dynamic_slice_in_dim(
        small_sum, lax.axis_index("dp") * own_rows, own_rows, axis=1
    )
    first_scaled_input = grad_normalized * first_norm_gain
    grad_tokens = d_resid + first_inverse_rms * (
        first_scaled_input
        - input_normalized_hat
        * jnp.mean(first_scaled_input * input_normalized_hat, axis=-1, keepdims=True)
    )
    return (
        output,
        grad_tokens.astype(jnp.bfloat16),
        grad_qkv,
        grad_out,
        small_own[0],
        small_own[1],
        small_own[2 : 2 + group_size].T,
        grad_gate_up,
        grad_down,
    )


def on_device_split(
    tokens,
    w_qkv,
    w_out,
    attention_norm_gain,
    gain_ffn,
    w_router,
    w_gate_up,
    w_down,
    lengths,
    routes,
    order,
    cotangent,
):
    group = lax.axis_size("expert")
    tok, width = tokens.shape
    piece = w_router.shape[0]
    local_width = w_qkv.shape[2]
    slots = tok * routes.shape[1]
    cosine, sine = rotary_constants(tok * group, HEAD_DIM)
    small = jnp.concatenate(
        [
            attention_norm_gain[None],
            gain_ffn[None],
            w_router.T,
            jnp.zeros((2, piece), jnp.bfloat16),
        ],
        axis=0,
    ).astype(jnp.float32)
    (
        tokens_all,
        whole,
        qkv_full,
        out_full,
        w_got,
        inverse_all,
        query,
        key_rows,
        value,
        attended,
        log_total,
        small_full,
        resid,
        inverse_two,
        gates,
        hits,
        sent,
        d_back,
    ) = attention_call(
        lengths,
        tokens,
        w_qkv,
        w_out,
        small,
        w_gate_up,
        routes,
        order,
        cosine,
        sine,
        cotangent,
        group,
    )
    blocked = (group, slots // group, width)
    returned, d_sent, grad_gate_up, grad_down = experts_call(
        sent.reshape(blocked), d_back.reshape(blocked), w_gate_up, w_got, w_down
    )
    returned = returned.reshape(slots, width)
    d_sent = d_sent.reshape(slots, width)

    gain_one = small_full[0]
    gain_two = small_full[1]
    router_f = small_full[2 : 2 + group]
    position = lax.axis_index("expert") * tok + jnp.arange(tok, dtype=jnp.int32)
    live_rows = (position < lengths[0]).astype(jnp.float32)[:, None]
    d_out = live_rows * cotangent.astype(jnp.float32)
    hhat = resid * inverse_two
    hidden_in = (hhat * gain_two).astype(jnp.bfloat16)
    moe = jnp.zeros_like(resid)
    d_gates_list = []
    for index in range(2):
        picked = contract_first(hits[index], returned)
        d_gates_list.append(jnp.sum(d_out * picked, axis=-1))
        moe = moe + gates[:, index : index + 1] * picked
    output = (live_rows * (resid + moe)).astype(jnp.bfloat16)
    d_gates = jnp.stack(d_gates_list, axis=1)
    d_hidden = contract_first(hits[0] + hits[1], d_sent)
    d_chosen = gates * (d_gates - jnp.sum(gates * d_gates, axis=1, keepdims=True))
    expert_ids = jnp.arange(group, dtype=jnp.int32)
    route_hits = (routes[:, :, None] == expert_ids[None, None, :]).astype(jnp.float32)
    d_logits = jnp.sum(route_hits * d_chosen[:, :, None], axis=1)
    d_hidden = d_hidden + jnp.dot(
        d_logits, router_f, precision=HIGH, preferred_element_type=jnp.float32
    )
    router_part = jnp.dot(
        d_logits.T,
        hidden_in.astype(jnp.float32),
        precision=HIGH,
        preferred_element_type=jnp.float32,
    )
    gain_two_part = jnp.sum(d_hidden * hhat, axis=0)
    scaled_two = d_hidden * gain_two
    d_resid = d_out + inverse_two * (
        scaled_two - hhat * jnp.mean(scaled_two * hhat, axis=-1, keepdims=True)
    )
    d_attn = d_resid.astype(jnp.bfloat16)
    small_part = jnp.concatenate(
        [jnp.zeros((1, width)), gain_two_part[None], router_part, jnp.zeros((2, width))], axis=0
    )
    grad_normalized, grad_weights, small_own, gate_got = attention_back_call(
        lengths,
        d_attn,
        tokens_all,
        inverse_all,
        whole,
        out_full,
        qkv_full,
        query,
        key_rows,
        value,
        attended,
        log_total,
        cosine,
        sine,
        small_part,
        grad_gate_up,
    )
    grad_qkv = jnp.stack(
        [grad_weights[:, c * local_width : (c + 1) * local_width] for c in range(3)]
    )
    grad_out = grad_weights[:, 3 * local_width :].T
    hat, inverse_one = normalize(tokens.astype(jnp.float32))
    scaled_one = grad_normalized * gain_one
    grad_tokens = d_resid + inverse_one * (
        scaled_one - hat * jnp.mean(scaled_one * hat, axis=-1, keepdims=True)
    )
    return (
        output,
        grad_tokens.astype(jnp.bfloat16),
        grad_qkv,
        grad_out,
        small_own[0],
        small_own[1],
        small_own[2 : 2 + group].T,
        widen_slices(gate_got),
        grad_down[None],
    )


def solution(mesh):
    placed = (
        P(("dp", "expert"), None),
        P(None, "dp", "expert"),
        P("expert", "dp"),
        P("dp"),
        P("dp"),
        P("dp", None),
        P("expert", "dp", None),
        P("expert", "dp", None),
        P("dp"),
        P(("dp", "expert"), None),
        P(("dp", "expert")),
        P(("dp", "expert"), None),
    )
    split = mesh.shape["dp"] == 8 and mesh.shape["expert"] == 4
    return jax.shard_map(
        on_device_split if split else on_device,
        mesh=mesh,
        in_specs=placed,
        out_specs=(
            P(("dp", "expert"), None),
            P(("dp", "expert"), None),
            P(None, "dp", "expert"),
            P("expert", "dp"),
            P("dp"),
            P("dp"),
            P("dp", None),
            P("expert", "dp", None),
            P("expert", "dp", None),
        ),
        check_vma=False,
    )
```

```python
import functools

import jax
import jax.numpy as jnp
import numpy as np
from jax import lax
from jax.experimental import pallas as pl
from jax.experimental.pallas import tpu as pltpu
from jax.sharding import PartitionSpec as P

HEAD_DIM = 128
FF = 5632


NORM_EPSILON = 1e-05
NEGATIVE = -1e30
THETA = 10000.0
HIGH = lax.Precision.HIGHEST
MESH_ID = pl.DeviceIdType.MESH
LANES = 128


def remote(src, dst, send_sem, recv_sem, peer):
    return pltpu.make_async_remote_copy(
        src_ref=src,
        dst_ref=dst,
        send_sem=send_sem,
        recv_sem=recv_sem,
        device_id=peer,
        device_id_type=MESH_ID,
    )


def greet(peers):
    barrier = pltpu.get_barrier_semaphore()
    for peer in peers:
        pl.semaphore_signal(barrier, inc=1, device_id=peer, device_id_type=MESH_ID)
    pl.semaphore_wait(barrier, len(peers))


def dot_nn(left, right):
    return jnp.dot(left, right, preferred_element_type=jnp.float32)


def dot_nt(left, right):
    return lax.dot_general(
        left, right, (((1,), (1,)), ((), ())), preferred_element_type=jnp.float32
    )


def experts_kernel(
    group,
    sent,
    d_back,
    w_gate_up,
    w_got,
    w_down,
    ret,
    d_ret,
    grad_gate_up,
    grad_down,
    w_buf,
    down_buf,
    rows_buf,
    gate_buf,
    act_buf,
    part_buf,
    half_x,
    half_y,
    full_x,
    full_y,
    other_gate,
    other_down,
    ag_sems,
    rs_sems,
    weight_sems,
    local_sems,
    grad_sems,
):
    cap, width = sent.shape[1], sent.shape[2]
    half = cap // 2
    piece, hidden2 = w_got.shape[1:]
    hidden = hidden2 // 2
    down_own = w_down.at[0]
    down_rows = down_own.shape[0]
    chunk = 4 * cap
    total = group * chunk

    index = lax.axis_index("dp")
    place = lax.axis_index("expert")
    core = index % 2
    at_x = (index // 2) % 2
    at_y = index // 4
    partner = {"dp": at_y * 4 + at_x * 2 + (1 - core)}
    along_x = {"dp": at_y * 4 + (1 - at_x) * 2 + core}
    along_y = {"dp": (1 - at_y) * 4 + at_x * 2 + core}
    chips = [
        at_y * 2 + at_x,
        at_y * 2 + (1 - at_x),
        (1 - at_y) * 2 + at_x,
        (1 - at_y) * 2 + (1 - at_x),
    ]

    def ahead(k):
        return {"expert": (place + k) % group}

    def behind(k):
        return {"expert": (place + group - k) % group}

    greet([partner, along_x, along_y] + [ahead(k) for k in range(1, group)])

    def block(t, k, r, start=0, size=None):
        size = cap if size is None else size
        return rows_buf.at[t, pl.ds((k * 4 + r) * cap + start, size), :]

    def part(t, k, r, start=0, size=None):
        size = cap if size is None else size
        return part_buf.at[t, pl.ds((k * 4 + r) * cap + start, size), :]

    def ag(kind, t, k):
        return ag_sems.at[0, kind, t, k], ag_sems.at[1, kind, t, k]

    def rs(kind, t, k):
        return rs_sems.at[0, kind, t, k], rs_sems.at[1, kind, t, k]

    sources = (sent, d_back)
    results = (ret, d_ret)

    def z_copy(t, k):
        return remote(sources[t].at[k], block(t, k, 0), *ag(0, t, k), ahead(k))

    def own_copy(t):
        return pltpu.make_async_copy(sources[t].at[0], block(t, 0, 0), local_sems.at[t])

    def x_copy(t, k):
        return remote(block(t, k, 0), block(t, k, 1), *ag(1, t, k), along_x)

    def y_copy(t, k):
        return remote(block(t, k, 0), block(t, k, 2), *ag(2, t, k), along_y)

    def a_copy(t, k):
        return remote(block(t, k, 2, 0, half), block(t, k, 3, 0, half), *ag(3, t, k), along_x)

    def b_copy(t, k):
        return remote(
            block(t, k, 1, half, half), block(t, k, 3, half, half), *ag(4, t, k), along_y
        )

    def spread(t, k):
        if k == 0:
            own_copy(t).wait()
        else:
            z_copy(t, k).wait_recv()
        x_copy(t, k).start()
        y_copy(t, k).start()

    def relay_a(t, k):
        y_copy(t, k).wait_recv()
        a_copy(t, k).start()

    def relay_b(t, k):
        x_copy(t, k).wait_recv()
        b_copy(t, k).start()

    def arrived(t, k):
        a_copy(t, k).wait_recv()
        b_copy(t, k).wait_recv()
        if t == 0 and k == 0:
            for r in range(4):
                for copy in w_keep(r):
                    copy.wait()
                for copy in w_share(r, 1 - core):
                    copy.wait_recv()
            down_keep.wait()
            down_share().wait_recv()

    def half_x_copy(t, k):
        return remote(part(t, k, 3, 0, half), half_x.at[t, k], *rs(0, t, k), along_x)

    def half_y_copy(t, k):
        return remote(part(t, k, 3, half, half), half_y.at[t, k], *rs(1, t, k), along_y)

    def full_x_copy(t, k):
        return remote(part(t, k, 1), full_x.at[t, k], *rs(2, t, k), along_x)

    def full_y_copy(t, k):
        return remote(part(t, k, 2), full_y.at[t, k], *rs(3, t, k), along_y)

    def back_copy(t, k):
        return remote(part(t, k, 0), results[t].at[k], *rs(4, t, k), behind(k))

    def keep_copy(t):
        return pltpu.make_async_copy(part(t, 0, 0), results[t].at[0], local_sems.at[2 + t])

    def halves_out(t, k):
        half_x_copy(t, k).start()
        half_y_copy(t, k).start()

    def add_into(target, *others):
        value = target[...].astype(jnp.float32)
        for other in others:
            value = value + other[...].astype(jnp.float32)
        target[...] = value.astype(jnp.bfloat16)

    def full_y_out(t, k):
        half_x_copy(t, k).wait_recv()
        add_into(part(t, k, 2, 0, half), half_x.at[t, k])
        full_y_copy(t, k).start()

    def full_x_out(t, k):
        half_y_copy(t, k).wait_recv()
        add_into(part(t, k, 1, half, half), half_y.at[t, k])
        full_x_copy(t, k).start()

    def home(t, k):
        full_x_copy(t, k).wait_recv()
        full_y_copy(t, k).wait_recv()
        add_into(part(t, k, 0), full_x.at[t, k], full_y.at[t, k])
        if k == 0:
            keep_copy(t).start()
        else:
            back_copy(t, k).start()

    def w_rows(r, which):
        return pl.ds(pl.multiple_of((chips[r] * 2 + which) * piece, piece), piece)

    def w_parts(r, which):
        rows = w_rows(r, which)
        if r > 0:
            return [(w_got.at[r - 1], w_buf.at[rows, :], r)]
        return [
            (
                w_gate_up.at[
                    0, :, pl.ds(pl.multiple_of((4 * part + chips[0]) * hidden, LANES), hidden)
                ],
                w_buf.at[rows, pl.ds(part * hidden, hidden)],
                4 * part,
            )
            for part in range(2)
        ]

    def w_share(r, which):
        return [
            remote(source, target, weight_sems.at[0, n], weight_sems.at[1, n], partner)
            for source, target, n in w_parts(r, which)
        ]

    def w_keep(r):
        return [
            pltpu.make_async_copy(source, target, local_sems.at[4 + n])
            for source, target, n in w_parts(r, core)
        ]

    def down_at(which):
        return down_buf.at[pl.ds(pl.multiple_of(which * down_rows, down_rows), down_rows), :]

    def down_share():
        return remote(
            down_own, down_at(core), weight_sems.at[0, 5], weight_sems.at[1, 5], partner
        )

    down_keep = pltpu.make_async_copy(down_own, down_at(core), local_sems.at[9])

    def take(steps, k, number):
        for at in range(group):
            if (at, number) in steps:

                @pl.when(k == at)
                def _(events=steps[at, number]):
                    for event, t, which in events:
                        event(t, which)

    blocks = hidden // LANES
    spans = [(2 * j, min(2, blocks - 2 * j)) for j in range((blocks + 1) // 2)]
    tiles = width // (2 * LANES)

    def span(first, count):
        return pl.ds(first * LANES, count * LANES)

    def forward(k, carry):
        at = pl.ds(pl.multiple_of(k * chunk, chunk), chunk)

        def tile(first, count):
            gate_cols, up_cols = span(first, count), span(blocks + first, count)
            rows = rows_buf[0, at, :]
            if count == 1:
                weights = jnp.concatenate([w_buf[:, gate_cols], w_buf[:, up_cols]], axis=1)
                both = dot_nn(rows, weights)
                gate, up = both[:, :LANES], both[:, LANES:]
            else:
                gate = dot_nn(rows, w_buf[:, gate_cols])
                up = dot_nn(rows, w_buf[:, up_cols])
            sigmoid = 1.0 / (1.0 + jnp.exp(-gate))
            gate_buf[at, gate_cols] = gate.astype(jnp.bfloat16)
            gate_buf[at, up_cols] = up.astype(jnp.bfloat16)
            act_buf[at, gate_cols] = (gate * sigmoid * up).astype(jnp.bfloat16)

        take(forward_steps, k, 0)
        for first, count in spans[:3]:
            tile(first, count)
        take(forward_steps, k, 1)
        for first, count in spans[3:]:
            tile(first, count)
        take(forward_steps, k, 2)
        for j in range(tiles):
            cols = span(2 * j, 2)
            out = dot_nn(act_buf[at, :], down_buf[:, cols])
            part_buf[0, at, cols] = out.astype(jnp.bfloat16)
        return carry

    def backward(turn, carry):
        k = (turn + 1) % group
        at = pl.ds(pl.multiple_of(k * chunk, chunk), chunk)
        take(backward_steps, k, 0)
        for first, count in spans:
            gate_cols, up_cols = span(first, count), span(blocks + first, count)
            d_act = dot_nt(rows_buf[1, at, :], down_buf[gate_cols, :])
            gate = gate_buf[at, gate_cols].astype(jnp.float32)
            up = gate_buf[at, up_cols].astype(jnp.float32)
            sigmoid = 1.0 / (1.0 + jnp.exp(-gate))
            scaled = d_act * sigmoid
            d_gate = scaled * up * (1.0 + gate * (1.0 - sigmoid))
            gate_buf[at, gate_cols] = d_gate.astype(jnp.bfloat16)
            gate_buf[at, up_cols] = (scaled * gate).astype(jnp.bfloat16)
        for side in range(2):
            take(backward_steps, k, 1 + side)
            for j in range(side * (tiles // 2), (side + 1) * (tiles // 2)):
                cols = span(2 * j, 2)
                out = dot_nt(gate_buf[at, :], w_buf[cols, :])
                part_buf[1, at, cols] = out.astype(jnp.bfloat16)
        return carry

    forward_steps = {
        (0, 0): [(spread, 0, 0), (spread, 1, 0), (spread, 0, 1), (relay_a, 0, 0), (relay_b, 0, 0), (relay_a, 1, 0), (relay_b, 1, 0), (spread, 0, 2), (relay_a, 0, 1), (relay_b, 0, 1), (arrived, 0, 0)],
        (0, 2): [(spread, 0, 3)],
        (1, 0): [(halves_out, 0, 0), (relay_a, 0, 2), (relay_b, 0, 2), (arrived, 0, 1)],
        (1, 1): [(spread, 1, 1)],
        (2, 0): [(relay_a, 0, 3), (relay_b, 0, 3), (halves_out, 0, 1), (spread, 1, 2), (arrived, 0, 2)],
        (2, 2): [(spread, 1, 3)],
        (3, 0): [(arrived, 0, 3)],
        (3, 1): [(relay_a, 1, 1)],
        (3, 2): [(relay_b, 1, 1), (full_y_out, 0, 0)],
    }
    backward_steps = {
        (0, 0): [(arrived, 1, 0)],
        (0, 1): [(full_y_out, 0, 3), (full_y_out, 1, 1)],
        (0, 2): [(full_x_out, 1, 1)],
        (1, 0): [(relay_a, 1, 2), (relay_b, 1, 2), (relay_a, 1, 3), (relay_b, 1, 3), (full_x_out, 0, 0), (full_y_out, 0, 1), (arrived, 1, 1)],
        (1, 2): [(full_x_out, 0, 1), (halves_out, 0, 2)],
        (2, 0): [(arrived, 1, 2)],
        (2, 1): [(halves_out, 0, 3), (halves_out, 1, 1)],
        (3, 0): [(home, 0, 0), (arrived, 1, 3)],
        (3, 1): [(halves_out, 1, 2)],
        (3, 2): [(full_x_out, 0, 2), (home, 0, 1), (full_y_out, 0, 2), (full_x_out, 0, 3)],
    }
    grad_steps = {
        (0, 0): [(full_y_out, 1, 2)],
        (1, 0): [(home, 0, 2), (full_x_out, 1, 2)],
        (2, 0): [(halves_out, 1, 0), (halves_out, 1, 3)],
        (2, 1): [(home, 0, 3)],
        (2, 3): [(home, 1, 1)],
        (4, 0): [(full_x_out, 1, 0), (full_y_out, 1, 0), (full_x_out, 1, 3), (home, 1, 2)],
        (4, 1): [(full_y_out, 1, 3)],
        (5, 0): [(home, 1, 0), (home, 1, 3)],
    }

    own_copy(0).start()
    for k in range(1, group):
        z_copy(0, k).start()
    for r in range(4):
        for copy in w_share(r, core) + w_keep(r):
            copy.start()
    down_share().start()
    down_keep.start()
    own_copy(1).start()

    for k in range(1, group):
        z_copy(1, k).start()

    lax.fori_loop(0, group, forward, 0)
    lax.fori_loop(0, group, backward, 0)
    for event, t, which in grad_steps.get((0, 0), []):
        event(t, which)

    act_t = down_buf.at[:, pl.ds(0, total)]
    rows_t = down_buf.at[pl.ds(0, piece), pl.ds(total, total)]
    send_down = w_buf.at[pl.ds(4 * piece, down_rows), pl.ds(0, width)]

    def send_gate(r):
        return w_buf.at[pl.ds(pl.multiple_of(r * piece, piece), piece), :]

    for j in range(blocks):
        act_t[span(j, 1), :] = act_buf[:, span(j, 1)].T

    def down_grad(which, j):
        rows = pl.ds(pl.multiple_of(which * down_rows, down_rows), down_rows)
        return dot_nn(act_t[rows, :], rows_buf[1, :, span(2 * j, 2)])

    def after(steps, number, r):
        turns = {(turn, 0): events for (stage, turn), events in steps.items() if stage == number}
        take(turns, r, 0)

    after(grad_steps, 1, 0)
    for j in range(tiles):
        send_down[:, span(2 * j, 2)] = down_grad(1 - core, j).astype(jnp.bfloat16)
    down_send = remote(
        send_down, other_down, grad_sems.at[0, 4], grad_sems.at[1, 4], partner
    )
    down_send.start()

    def turned_rows(r, which):
        step_y = r // 2
        step_x = r % 2
        chip = (at_y + step_y - 2 * at_y * step_y) * 2 + (at_x + step_x - 2 * at_x * step_x)
        start = pl.multiple_of((chip * 2 + which) * piece, piece)
        rows_t[...] = rows_buf[0, :, pl.ds(start, piece)].T

    def gate_send(r):
        return remote(
            send_gate(r), other_gate.at[r], grad_sems.at[0, r], grad_sems.at[1, r], partner
        )

    def gate_for_partner(r, carry):
        after(grad_steps, 2, r)
        turned_rows(r, 1 - core)
        target = send_gate(r)
        for j in range(blocks):
            cols = span(2 * j, 2)
            target[:, cols] = dot_nn(rows_t[...], gate_buf[:, cols]).astype(jnp.bfloat16)
        gate_send(r).start()
        return carry

    lax.fori_loop(0, 4, gate_for_partner, 0)
    after(grad_steps, 3, 0)
    down_send.wait_recv()

    for j in range(tiles):
        cols = span(2 * j, 2)
        value = down_grad(core, j) + other_down[:, cols].astype(jnp.float32)
        other_down[:, cols] = value.astype(jnp.bfloat16)
    down_out = pltpu.make_async_copy(other_down, grad_down, grad_sems.at[2, 0])
    down_out.start()

    def gate_out(r):
        return pltpu.make_async_copy(other_gate.at[r], grad_gate_up.at[r], grad_sems.at[2, 2 + r])

    def gate_for_self(r, carry):
        after(grad_steps, 4, r)
        gate_send(r).wait_recv()
        turned_rows(r, core)
        target = other_gate.at[r]
        for j in range(blocks):
            cols = span(2 * j, 2)
            value = dot_nn(rows_t[...], gate_buf[:, cols])
            target[:, cols] = (value + target[:, cols].astype(jnp.float32)).astype(jnp.bfloat16)
        gate_out(r).start()
        return carry

    lax.fori_loop(0, 4, gate_for_self, 0)
    after(grad_steps, 5, 0)

    down_out.wait()
    for r in range(4):
        gate_out(r).wait()
        gate_send(r).wait_send()
        for copy in w_share(r, core):
            copy.wait_send()
    down_share().wait_send()
    down_send.wait_send()
    for t in range(2):
        keep_copy(t).wait()
        for k in range(group):
            x_copy(t, k).wait_send()
            y_copy(t, k).wait_send()
            a_copy(t, k).wait_send()
            b_copy(t, k).wait_send()
            half_x_copy(t, k).wait_send()
            half_y_copy(t, k).wait_send()
            full_x_copy(t, k).wait_send()
            full_y_copy(t, k).wait_send()
            if k > 0:
                z_copy(t, k).wait_send()
                back_copy(t, k).wait_send()
                back_copy(t, k).wait_recv()


def experts_call(sent, d_back, w_gate_up, w_got, w_down):
    group, cap, width = sent.shape
    piece, hidden2 = w_got.shape[1:]
    hidden = hidden2 // 2
    down_rows = w_down.shape[1]
    chunk = 4 * cap
    total = group * chunk
    low = jnp.bfloat16
    anywhere = pl.BlockSpec(memory_space=pl.ANY)
    flops = 2 * total * width * hidden * 9
    moved = 2 * (4 * piece * hidden2 * 2 + down_rows * width * 3)
    return pl.pallas_call(
        functools.partial(experts_kernel, group),
        out_shape=(
            jax.ShapeDtypeStruct((group, cap, width), low),
            jax.ShapeDtypeStruct((group, cap, width), low),
            jax.ShapeDtypeStruct((4, piece, hidden2), low),
            jax.ShapeDtypeStruct((down_rows, width), low),
        ),
        in_specs=[anywhere] * 5,
        out_specs=(anywhere,) * 4,
        scratch_shapes=[
            pltpu.VMEM((width, hidden2), low),
            pltpu.VMEM((hidden, width), low),
            pltpu.VMEM((2, total, width), low),
            pltpu.VMEM((total, hidden2), low),
            pltpu.VMEM((total, hidden), low),
            pltpu.VMEM((2, total, width), low),
            pltpu.VMEM((2, group, cap // 2, width), low),
            pltpu.VMEM((2, group, cap // 2, width), low),
            pltpu.VMEM((2, group, cap, width), low),
            pltpu.VMEM((2, group, cap, width), low),
            pltpu.VMEM((4, piece, hidden2), low),
            pltpu.VMEM((down_rows, width), low),
            pltpu.SemaphoreType.DMA((2, 5, 2, group)),
            pltpu.SemaphoreType.DMA((2, 5, 2, group)),
            pltpu.SemaphoreType.DMA((2, 6)),
            pltpu.SemaphoreType.DMA((10,)),
            pltpu.SemaphoreType.DMA((3, 6)),
        ],
        compiler_params=pltpu.CompilerParams(
            collective_id=1, has_side_effects=True, vmem_limit_bytes=67043328
        ),
        cost_estimate=pl.CostEstimate(flops=flops, bytes_accessed=moved, transcendentals=0),
        name="experts",
    )(sent, d_back, w_gate_up, w_got, w_down)


def rotary_tables(length_total, head_size):
    position = jnp.arange(length_total, dtype=jnp.float32)
    frequency = THETA ** (-(jnp.arange(head_size // 2, dtype=jnp.float32) * 2.0 / head_size))
    angles = position[:, None] * frequency[None, :]
    return (jnp.cos(angles)[:, None, :], jnp.sin(angles)[:, None, :])


def rotate(values, cosine, sine):
    half_size = values.shape[-1] // 2
    first = values[..., :half_size]
    second = values[..., half_size:]
    return jnp.concatenate(
        [first * cosine - second * sine, second * cosine + first * sine], axis=-1
    )


def rotate_back(grad_rows, cosine, sine):
    half_size = grad_rows.shape[-1] // 2
    first = grad_rows[..., :half_size]
    second = grad_rows[..., half_size:]
    return jnp.concatenate(
        [first * cosine + second * sine, second * cosine - first * sine], axis=-1
    )


def slot_table(routes, order, valid, capacity):
    row_count = routes.shape[0]
    top_count = routes.shape[1]
    pair_rank = order[:, None] + row_count * jnp.arange(top_count, dtype=jnp.int32)[None, :]
    flat_rank = pair_rank.reshape(-1)
    flat_expert = routes.reshape(-1)
    flat_valid = jnp.broadcast_to(valid[:, None], routes.shape).reshape(-1)
    earlier = (
        (flat_rank[None, :] < flat_rank[:, None])
        & (flat_expert[None, :] == flat_expert[:, None])
        & flat_valid[None, :]
    )
    slot_index = jnp.sum(earlier.astype(jnp.int32), axis=1).reshape(row_count, top_count)
    kept_pair = valid[:, None] & (slot_index < capacity)
    target = routes * capacity + jnp.minimum(slot_index, capacity - 1)
    return (target, kept_pair)


def masked_scores(query, key_rows, allowed):
    scale = query.shape[-1] ** (-0.5)
    raw = jnp.einsum("qhd,khd->hqk", query, key_rows, preferred_element_type=jnp.float32) * scale
    return jnp.where(allowed[None], raw, NEGATIVE)


def contract_first(left, right):
    return lax.dot_general(
        left, right, (((0,), (0,)), ((), ())), preferred_element_type=jnp.float32
    )


def contract_last(left, right):
    return lax.dot_general(
        left, right, (((1,), (1,)), ((), ())), preferred_element_type=jnp.float32
    )


def normalize(rows):
    inverse = lax.rsqrt(jnp.mean(rows * rows, axis=-1, keepdims=True) + NORM_EPSILON)
    return rows * inverse, inverse


def exchange_experts(blocks):
    return lax.all_to_all(blocks, "expert", split_axis=0, concat_axis=0, tiled=True)


def line_order(place, step):
    upper = place // 2
    low = place * (1 - upper) + (3 - place) * upper
    first = 1 - (step + 1) // 2
    block = step + first * (1 - low) + (1 - first)
    return block * (1 - upper) + (3 - block) * upper


def rotated(grad, cosine, sine):
    return grad * cosine + pltpu.roll(grad, grad.shape[1] // 2, 1) * sine


def attention_back_kernel(
    heads,
    length,
    returned,
    d_sent,
    resid,
    inverse_two,
    gates,
    hits,
    cotangent,
    pair_cols,
    small_full,
    tokens_all,
    inverse_all,
    whole,
    w_out,
    w_qkv,
    query,
    key_rows,
    value,
    attended,
    log_total,
    cosine,
    sine,
    gate_grads,
    output,
    grad_tokens,
    grad_weights,
    small_out,
    gate_got,
    returned_buf,
    d_sent_buf,
    resid_buf,
    inverse_two_buf,
    gates_buf,
    hits_buf,
    cotangent_buf,
    cols_buf,
    small_full_buf,
    da_buf,
    tokens_buf,
    inverse_buf,
    whole_buf,
    w_out_buf,
    w_qkv_buf,
    query_buf,
    key_buf,
    value_buf,
    attended_buf,
    log_buf,
    cosine_buf,
    sine_buf,
    d_key_acc,
    d_value_acc,
    d_proj,
    normed_part,
    from_left,
    from_right,
    send_pair,
    recv_pair,
    own_part,
    half_x,
    half_y,
    full_x,
    full_y,
    small_buf,
    small_recv,
    small_z,
    keep_buf,
    sum_buf,
    load_sems,
    line_sems,
    sum_sems,
    pair_sems,
    ring_sems,
    small_sems,
    gate_sems,
):
    tok, width = cotangent.shape
    seq_len = tokens_all.shape[0]
    group = seq_len // tok
    local_width = w_out.shape[0]
    head_size = local_width // heads
    piece = own_part.shape[1]
    half = piece // 2
    scale = head_size**-0.5

    index = lax.axis_index("dp")
    place = lax.axis_index("expert")
    core = index % 2
    at_x = (index // 2) % 2
    at_y = index // 4
    partner = {"dp": at_y * 4 + at_x * 2 + (1 - core)}
    along_x = {"dp": at_y * 4 + (1 - at_x) * 2 + core}
    along_y = {"dp": (1 - at_y) * 4 + at_x * 2 + core}
    over = {"dp": (1 - at_y) * 4 + (1 - at_x) * 2 + core}
    parts = width // piece

    def chip(r):
        step_y = r // 2
        step_x = r % 2
        return (at_y + step_y - 2 * at_y * step_y) * 2 + (at_x + step_x - 2 * at_x * step_x)

    def ring_peer(k):
        return {"dp": (index + k) % parts}

    def line_peer(k):
        return {"expert": (place + k) % group}

    right = {"expert": (place + 1) % group}
    left = {"expert": (place + group - 1) % group}

    loads = [
        pltpu.make_async_copy(source, target, load_sems.at[number])
        for number, (source, target) in enumerate(
            [
                (returned, returned_buf),
                (hits, hits_buf),
                (cotangent, cotangent_buf),
                (resid, resid_buf),
                (inverse_two, inverse_two_buf),
                (gates, gates_buf),
                (pair_cols, cols_buf),
                (small_full, small_full_buf),
                (d_sent, d_sent_buf),
                (w_out, w_out_buf),
                (query, query_buf),
                (key_rows, key_buf),
                (value, value_buf),
                (log_total, log_buf),
                (cosine, cosine_buf),
                (sine, sine_buf),
                (w_qkv, w_qkv_buf),
                (tokens_all, tokens_buf),
                (inverse_all, inverse_buf),
                (whole, whole_buf),
                (attended, attended_buf),
                (gate_grads.at[0], keep_buf),
            ]
        )
    ]
    first = 9
    early = first + 7
    for load in loads[:early]:
        load.start()

    greet([ring_peer(k) for k in range(1, parts)] + [line_peer(k) for k in range(1, group)])

    def rows_of(block):
        return pl.ds(pl.multiple_of(block * tok, tok), tok)

    def pass_right(block):
        spot = da_buf.at[rows_of(block)]
        return remote(spot, spot, line_sems.at[0, block], line_sems.at[2, block], right)

    def pass_left(block):
        spot = da_buf.at[rows_of(block)]
        return remote(spot, spot, line_sems.at[1, block], line_sems.at[2, block], left)

    def gate_copy(r, peer):
        return remote(
            gate_grads.at[r], gate_got.at[r], gate_sems.at[0, r], gate_sems.at[1, r], peer
        )

    peers = (None, along_x, along_y, over)
    for r in (3, 1, 2):
        gate_copy(r, peers[r]).start()
    for load in loads[early:]:
        load.start()
    for load in loads[:first]:
        load.wait()

    at = place * tok + lax.broadcasted_iota(jnp.int32, (tok, 1), 0)
    live = jnp.where(at < length[0], 1.0, 0.0)
    d_out = live * cotangent_buf[...].astype(jnp.float32)
    total = resid_buf[...]
    hhat = total * inverse_two_buf[...]
    gate = [gates_buf[:, number : number + 1] for number in range(2)]
    d_gate = []
    for number in range(2):
        picked = dot_nn(hits_buf[number].T, returned_buf[...])
        d_gate.append(jnp.sum(d_out * picked, axis=-1, keepdims=True))
        total = total + gate[number] * picked
    output[...] = (live * total).astype(jnp.bfloat16)
    mixed = gate[0] * d_gate[0] + gate[1] * d_gate[1]
    d_chosen = [gate[number] * (d_gate[number] - mixed) for number in range(2)]
    d_hidden = dot_nn((hits_buf[0] + hits_buf[1]).T, d_sent_buf[...])
    gain_two = small_full_buf[1:2, :]
    hidden_in = (hhat * gain_two).astype(jnp.bfloat16).astype(jnp.float32)
    small_buf[...] = jnp.zeros_like(small_buf)
    for expert in range(group):
        d_logit = sum(
            jnp.where(cols_buf[:, number : number + 1] == expert, d_chosen[number], 0.0)
            for number in range(2)
        )
        row = slice(2 + expert, 3 + expert)
        d_hidden = d_hidden + d_logit * small_full_buf[row, :]
        small_buf[row, :] = jnp.sum(d_logit * hidden_in, axis=0, keepdims=True)
    small_buf[1:2, :] = jnp.sum(d_hidden * hhat, axis=0, keepdims=True)
    scaled = d_hidden * gain_two
    shared = jnp.mean(scaled * hhat, axis=-1, keepdims=True)
    d_resid = d_out + inverse_two_buf[...] * (scaled - hhat * shared)
    resid_buf[...] = d_resid
    da_buf[rows_of(place), :] = d_resid.astype(jnp.bfloat16)

    @pl.when(place < group - 1)
    def _():
        pass_right(place).start()

    @pl.when(place > 0)
    def _():
        pass_left(place).start()

    d_key_acc[...] = jnp.zeros_like(d_key_acc)
    d_value_acc[...] = jnp.zeros_like(d_value_acc)

    def attend_back(block):
        rows = rows_of(block)
        d_heads = dot_nt(da_buf[rows, :], w_out_buf[...]).astype(jnp.bfloat16)
        shape = (tok, seq_len)
        at_query = block * tok + lax.broadcasted_iota(jnp.int32, shape, 0)
        at_key = lax.broadcasted_iota(jnp.int32, shape, 1)
        allowed = (at_key <= at_query) & (at_key < length[0])
        for head in range(heads):
            cols = slice(head * head_size, (head + 1) * head_size)
            one_query = query_buf[rows, cols]
            one_key = key_buf[:, cols]
            d_head = d_heads[:, cols]
            scores = jnp.where(allowed, dot_nt(one_query, one_key) * scale, NEGATIVE)
            probs = jnp.exp(scores - log_buf[rows, head : head + 1])
            d_probs = dot_nt(d_head, value_buf[:, cols])
            delta = jnp.sum(probs * d_probs, axis=-1, keepdims=True)
            d_scores = (probs * (d_probs - delta)).astype(jnp.bfloat16)
            d_query = dot_nn(d_scores, one_key) * scale
            d_key_acc[:, cols] += dot_nn(d_scores.T, one_query) * scale
            d_value_acc[:, cols] += dot_nn(probs.astype(jnp.bfloat16).T, d_head)
            d_proj[rows, cols] = rotated(d_query, cosine_buf[rows, :], -sine_buf[rows, :]).astype(
                jnp.bfloat16
            )

    for load in loads[first:early]:
        load.wait()
    attend_back(place)

    def arrive(step, carry):
        block = line_order(place, step)
        pass_right(block).wait_recv()

        @pl.when((block < place) & (place < group - 1))
        def _():
            pass_right(block).start()

        @pl.when((block > place) & (place > 0))
        def _():
            pass_left(block).start()

        attend_back(block)
        return carry

    lax.fori_loop(0, group - 1, arrive, 0)
    for load in loads[early:]:
        load.wait()
    keep = pltpu.make_async_copy(keep_buf, gate_got.at[0], load_sems.at[22])
    keep.start()

    for head in range(heads):
        cols = slice(head * head_size, (head + 1) * head_size)
        key_cols = slice(local_width + head * head_size, local_width + (head + 1) * head_size)
        d_proj[:, key_cols] = rotated(d_key_acc[:, cols], cosine_buf[...], -sine_buf[...]).astype(
            jnp.bfloat16
        )
    d_proj[:, 2 * local_width :] = d_value_acc[...].astype(jnp.bfloat16)

    def normed_tile(j, carry):
        cols = pl.ds(pl.multiple_of(j * piece, piece), piece)
        d_normed = jnp.zeros((seq_len, piece), jnp.float32)
        for c in range(3):
            d_normed += dot_nt(
                d_proj[:, c * local_width : (c + 1) * local_width], w_qkv_buf[c, cols, :]
            )
        hat = tokens_buf[:, cols].astype(jnp.float32) * inverse_buf[...]
        small_buf[0:1, cols] = jnp.sum(d_normed * hat, axis=0, keepdims=True)
        normed_part[:, cols] = d_normed.astype(jnp.bfloat16)
        return carry

    lax.fori_loop(0, parts, normed_tile, 0)

    def go_right(block):
        return remote(
            normed_part.at[pl.ds(block * tok, tok)],
            from_left.at[block],
            sum_sems.at[0, block],
            sum_sems.at[1, block],
            right,
        )

    def go_left(block):
        return remote(
            normed_part.at[pl.ds(block * tok, tok)],
            from_right.at[block],
            sum_sems.at[0, block],
            sum_sems.at[2, block],
            left,
        )

    def add_into(target, other):
        value = target[...].astype(jnp.float32) + other[...].astype(jnp.float32)
        target[...] = value.astype(jnp.bfloat16)

    def on_right(block):
        go_right(block).wait_recv()
        add_into(normed_part.at[pl.ds(block * tok, tok)], from_left.at[block])
        go_right(block).start()

    def on_left(block):
        go_left(block).wait_recv()
        add_into(normed_part.at[pl.ds(block * tok, tok)], from_right.at[block])
        go_left(block).start()

    @pl.when(place == 0)
    def _():
        for block in (3, 2, 1):
            go_right(block).start()

    @pl.when(place == 3)
    def _():
        for block in (0, 1, 2):
            go_left(block).start()

    def small_copy(k):
        to = (index + k) % parts
        cols = pl.ds(pl.multiple_of(to * piece, piece), piece)
        return remote(
            small_buf.at[:, cols],
            small_recv.at[k],
            small_sems.at[0, k],
            small_sems.at[1, k],
            ring_peer(k),
        )

    for k in range(1, parts):
        small_copy(k).start()

    def weight_grad(which, r):
        cols = pl.ds(pl.multiple_of((chip(r) * 2 + which) * piece, piece), piece)
        left_side = whole_buf[:, cols].T
        first = dot_nn(left_side, d_proj[...])
        second = dot_nn(da_buf[:, cols].T, attended_buf[...])
        return jnp.concatenate([first, second], axis=1)

    def pair_copy(r):
        return remote(
            send_pair.at[r], recv_pair.at[r], pair_sems.at[0, r], pair_sems.at[1, r], partner
        )

    def for_partner(i, carry):
        r = 3 - i
        send_pair[r] = weight_grad(1 - core, r).astype(jnp.bfloat16)
        pair_copy(r).start()
        return carry

    lax.fori_loop(0, 4, for_partner, 0)

    @pl.when(place == 1)
    def _():
        on_right(3)

    @pl.when(place == 2)
    def _():
        on_left(0)

    def half_x_copy():
        return remote(
            own_part.at[3, pl.ds(0, half)], half_x, ring_sems.at[0, 0], ring_sems.at[1, 0], along_x
        )

    def half_y_copy():
        return remote(
            own_part.at[3, pl.ds(half, half)],
            half_y,
            ring_sems.at[0, 1],
            ring_sems.at[1, 1],
            along_y,
        )

    def full_x_copy():
        return remote(own_part.at[1], full_x, ring_sems.at[0, 2], ring_sems.at[1, 2], along_x)

    def full_y_copy():
        return remote(own_part.at[2], full_y, ring_sems.at[0, 3], ring_sems.at[1, 3], along_y)

    def for_self(i, carry):
        r = 3 - i
        pair_copy(r).wait_recv()
        own_part[r] = (weight_grad(core, r) + recv_pair[r].astype(jnp.float32)).astype(
            jnp.bfloat16
        )

        @pl.when(i == 0)
        def _():
            half_x_copy().start()
            half_y_copy().start()

        return carry

    lax.fori_loop(0, 4, for_self, 0)

    total = small_buf[:, pl.ds(pl.multiple_of(index * piece, piece), piece)]
    for k in range(1, parts):
        small_copy(k).wait_recv()
        total = total + small_recv[k]
    small_z[0] = total

    @pl.when(place == 1)
    def _():
        on_right(2)

    @pl.when(place == 2)
    def _():
        on_left(1)

    def small_line_copy(k):
        return remote(
            small_z.at[0],
            small_z.at[k],
            small_sems.at[0, parts + k],
            small_sems.at[1, parts + k],
            line_peer(k),
        )

    for k in range(1, group):
        small_line_copy(k).start()

    half_x_copy().wait_recv()
    add_into(own_part.at[2, pl.ds(0, half)], half_x)
    full_y_copy().start()
    half_y_copy().wait_recv()
    add_into(own_part.at[1, pl.ds(half, half)], half_y)
    full_x_copy().start()

    @pl.when(place == 1)
    def _():
        on_left(0)

    @pl.when(place == 2)
    def _():
        on_right(3)

    total = small_z[0]
    for k in range(1, group):
        small_line_copy(k).wait_recv()
        total = total + small_z[k]
    small_out[...] = total

    sum_buf[...] = normed_part[rows_of(place), :].astype(jnp.float32)

    @pl.when(place > 0)
    def _():
        go_right(place).wait_recv()
        sum_buf[...] += from_left[place].astype(jnp.float32)

    @pl.when(place < group - 1)
    def _():
        go_left(place).wait_recv()
        sum_buf[...] += from_right[place].astype(jnp.float32)

    inverse_one = inverse_buf[rows_of(place), :]
    hat = tokens_buf[rows_of(place), :].astype(jnp.float32) * inverse_one
    scaled = sum_buf[...] * small_full_buf[0:1, :]
    shared = jnp.mean(scaled * hat, axis=-1, keepdims=True)
    grad_tokens[...] = (resid_buf[...] + inverse_one * (scaled - hat * shared)).astype(
        jnp.bfloat16
    )

    full_x_copy().wait_recv()
    full_y_copy().wait_recv()
    grad_weights[...] = (
        own_part[0].astype(jnp.float32)
        + full_x[...].astype(jnp.float32)
        + full_y[...].astype(jnp.float32)
    )

    for r in (1, 2, 3):
        gate_copy(r, peers[r]).wait()
    keep.wait()
    half_x_copy().wait_send()
    half_y_copy().wait_send()
    full_x_copy().wait_send()
    full_y_copy().wait_send()
    for r in range(4):
        pair_copy(r).wait_send()
    for k in range(1, parts):
        small_copy(k).wait_send()
    for k in range(1, group):
        small_line_copy(k).wait_send()
    for block in range(group):

        @pl.when(block > place)
        def _():
            go_right(block).wait_send()

        @pl.when(block < place)
        def _():
            go_left(block).wait_send()

        @pl.when((block <= place) & (place < group - 1))
        def _():
            pass_right(block).wait_send()

        @pl.when((block >= place) & (place > 0))
        def _():
            pass_left(block).wait_send()


def attention_back_call(
    lengths,
    returned,
    d_sent,
    resid,
    inverse_two,
    gates,
    hits,
    cotangent,
    pair_cols,
    small_full,
    tokens_all,
    inverse_all,
    whole,
    w_out,
    w_qkv,
    query,
    key_rows,
    value,
    attended,
    log_total,
    cosine,
    sine,
    gate_grads,
):
    tok, width = cotangent.shape
    seq_len = tokens_all.shape[0]
    group = seq_len // tok
    local_width = w_out.shape[0]
    heads = log_total.shape[1]
    piece = gate_grads.shape[1]
    half = piece // 2
    parts = width // piece
    small_rows = small_full.shape[0]
    low, full = jnp.bfloat16, jnp.float32
    anywhere = pl.BlockSpec(memory_space=pl.ANY)
    inside = pl.BlockSpec(memory_space=pltpu.VMEM)

    def like(array):
        return pltpu.VMEM(array.shape, array.dtype)

    flops = 2 * seq_len * width * local_width * 8 + 10 * seq_len * seq_len * local_width
    return pl.pallas_call(
        functools.partial(attention_back_kernel, heads),
        out_shape=(
            jax.ShapeDtypeStruct((tok, width), low),
            jax.ShapeDtypeStruct((tok, width), low),
            jax.ShapeDtypeStruct((piece, 4 * local_width), full),
            jax.ShapeDtypeStruct((small_rows, piece), full),
            jax.ShapeDtypeStruct(gate_grads.shape, low),
        ),
        in_specs=[pl.BlockSpec(memory_space=pltpu.SMEM)] + [anywhere] * 22,
        out_specs=(inside, inside, inside, inside, anywhere),
        scratch_shapes=[
            like(returned),
            like(d_sent),
            like(resid),
            like(inverse_two),
            like(gates),
            like(hits),
            like(cotangent),
            like(pair_cols),
            like(small_full),
            pltpu.VMEM((seq_len, width), low),
            like(tokens_all),
            like(inverse_all),
            like(whole),
            like(w_out),
            like(w_qkv),
            like(query),
            like(key_rows),
            like(value),
            like(attended),
            like(log_total),
            like(cosine),
            like(sine),
            pltpu.VMEM((seq_len, local_width), full),
            pltpu.VMEM((seq_len, local_width), full),
            pltpu.VMEM((seq_len, 3 * local_width), low),
            pltpu.VMEM((seq_len, width), low),
            pltpu.VMEM((group, tok, width), low),
            pltpu.VMEM((group, tok, width), low),
            pltpu.VMEM((4, piece, 4 * local_width), low),
            pltpu.VMEM((4, piece, 4 * local_width), low),
            pltpu.VMEM((4, piece, 4 * local_width), low),
            pltpu.VMEM((half, 4 * local_width), low),
            pltpu.VMEM((half, 4 * local_width), low),
            pltpu.VMEM((piece, 4 * local_width), low),
            pltpu.VMEM((piece, 4 * local_width), low),
            like(small_full),
            pltpu.VMEM((parts, small_rows, piece), full),
            pltpu.VMEM((group, small_rows, piece), full),
            pltpu.VMEM(gate_grads.shape[1:], low),
            like(resid),
            pltpu.SemaphoreType.DMA((23,)),
            pltpu.SemaphoreType.DMA((3, group)),
            pltpu.SemaphoreType.DMA((3, group)),
            pltpu.SemaphoreType.DMA((2, 4)),
            pltpu.SemaphoreType.DMA((2, 4)),
            pltpu.SemaphoreType.DMA((2, parts + group)),
            pltpu.SemaphoreType.DMA((2, 4)),
        ],
        compiler_params=pltpu.CompilerParams(
            collective_id=2, has_side_effects=True, vmem_limit_bytes=67043328
        ),
        cost_estimate=pl.CostEstimate(flops=flops, bytes_accessed=40000000, transcendentals=0),
        name="attention_back",
    )(
        lengths,
        returned,
        d_sent,
        resid,
        inverse_two,
        gates,
        hits,
        cotangent,
        pair_cols,
        small_full,
        tokens_all,
        inverse_all,
        whole,
        w_out,
        w_qkv,
        query,
        key_rows,
        value,
        attended,
        log_total,
        cosine,
        sine,
        gate_grads,
    )


def finish_kernel(
    gate_got,
    grad_down_low,
    grad_tokens_low,
    output_low,
    grad_weights,
    grad_gate_up,
    grad_down,
    grad_tokens,
    output,
    grad_qkv,
    grad_out,
    got_buf,
    wide_buf,
    low_buf,
    down_buf,
    tokens_buf,
    output_buf,
    weights_buf,
    out_buf,
    load_sems,
    store_sems,
):
    chips = gate_got.shape[0]
    size = gate_got.shape[2] // 2
    local_width = grad_qkv.shape[2]
    index = lax.axis_index("dp")
    at_x = (index // 2) % 2
    at_y = index // 4

    def load(number, source, target):
        return pltpu.make_async_copy(source, target, load_sems.at[number])

    loads = [load(r, gate_got.at[r], got_buf.at[r]) for r in range(chips)] + [
        load(4, grad_down_low, low_buf),
        load(5, grad_weights, weights_buf),
        load(6, grad_tokens_low, tokens_buf),
        load(7, output_low, output_buf),
    ]
    for copy in loads:
        copy.start()
    stores = []

    def store(source, target):
        copy = pltpu.make_async_copy(source, target, store_sems.at[len(stores)])
        copy.start()
        stores.append(copy)

    for r in range(chips):
        loads[r].wait()
        step_y = r // 2
        step_x = r % 2
        chip = (at_y + step_y - 2 * at_y * step_y) * 2 + (at_x + step_x - 2 * at_x * step_x)
        for part in range(2):
            wide_buf[2 * r + part] = got_buf[r, :, part * size : (part + 1) * size].astype(
                jnp.float32
            )
            lanes = pl.ds(pl.multiple_of((part * chips + chip) * size, LANES), size)
            store(wide_buf.at[2 * r + part], grad_gate_up.at[0, :, lanes])
    loads[4].wait()
    down_buf[...] = low_buf[...].astype(jnp.float32)
    store(down_buf, grad_down.at[0])
    loads[5].wait()
    out_buf[...] = weights_buf[:, 3 * local_width :].T
    for c in range(3):
        store(weights_buf.at[:, pl.ds(c * local_width, local_width)], grad_qkv.at[c])
    store(out_buf, grad_out)
    loads[6].wait()
    store(tokens_buf, grad_tokens)
    loads[7].wait()
    store(output_buf, output)
    for copy in stores:
        copy.wait()


def finish_call(gate_got, grad_down, grad_tokens, output, grad_weights):
    chips, rows, hidden2 = gate_got.shape
    local_width = grad_weights.shape[1] // 4
    full = jnp.float32
    anywhere = pl.BlockSpec(memory_space=pl.ANY)
    out_t = (local_width, rows)

    def like(array, kind=None):
        return pltpu.VMEM(array.shape, kind or array.dtype)

    return pl.pallas_call(
        finish_kernel,
        out_shape=(
            jax.ShapeDtypeStruct((1, rows, chips * hidden2), full),
            jax.ShapeDtypeStruct((1,) + grad_down.shape, full),
            jax.ShapeDtypeStruct(grad_tokens.shape, grad_tokens.dtype),
            jax.ShapeDtypeStruct(output.shape, output.dtype),
            jax.ShapeDtypeStruct((3, rows, local_width), full),
            jax.ShapeDtypeStruct(out_t, full),
        ),
        in_specs=[anywhere] * 5,
        out_specs=(anywhere,) * 6,
        scratch_shapes=[
            like(gate_got),
            pltpu.VMEM((2 * chips, rows, hidden2 // 2), full),
            like(grad_down),
            like(grad_down, full),
            like(grad_tokens),
            like(output),
            like(grad_weights),
            pltpu.VMEM(out_t, full),
            pltpu.SemaphoreType.DMA((8,)),
            pltpu.SemaphoreType.DMA((15,)),
        ],
        compiler_params=pltpu.CompilerParams(vmem_limit_bytes=67043328),
        name="finish",
    )(gate_got, grad_down, grad_tokens, output, grad_weights)


def rotary_constants(length_total, head_size):
    position = np.arange(length_total, dtype=np.float32)
    steps = np.arange(head_size // 2, dtype=np.float32) * np.float32(2.0) / np.float32(head_size)
    frequency = np.power(np.float32(THETA), -steps).astype(np.float32)
    angles = (position[:, None] * frequency[None, :]).astype(np.float32)
    cosine, sine = np.cos(angles), np.sin(angles)
    return (
        np.concatenate([cosine, cosine], axis=1).astype(np.float32),
        np.concatenate([-sine, sine], axis=1).astype(np.float32),
    )


def attention_kernel(
    heads,
    length,
    tokens,
    w_qkv,
    w_out,
    small,
    w_gate_up,
    pair_cols,
    pair_rows,
    cosine,
    sine,
    cotangent,
    tokens_all,
    whole,
    qkv_full,
    out_full,
    w_got,
    inverse_all,
    query,
    key_rows,
    value,
    attended,
    log_total,
    small_full,
    resid,
    inverse_two,
    gates,
    hits,
    sent,
    d_back,
    tokens_buf,
    whole_buf,
    w_qkv_buf,
    w_out_buf,
    part_buf,
    from_left,
    from_right,
    cols_buf,
    rows_buf,
    cosine_buf,
    sine_buf,
    cotangent_buf,
    load_sems,
    line_sems,
    sum_sems,
    gather_sems,
    small_sems,
    slice_sems,
):
    tok, width = tokens.shape
    seq_len = tokens_buf.shape[0]
    group = seq_len // tok
    local_width = w_out.shape[0]
    head_size = local_width // heads
    piece = w_qkv.shape[1]
    parts = width // piece
    ff = w_gate_up.shape[2] // 2
    hidden = ff // 4
    slots = hits.shape[1]
    cap = slots // group
    scale = head_size**-0.5

    index = lax.axis_index("dp")
    place = lax.axis_index("expert")
    core = index % 2
    at_x = (index // 2) % 2
    at_y = index // 4
    other = at_y * 4 + at_x * 2 + (1 - core)
    by_x = at_y * 4 + (1 - at_x) * 2 + core
    by_y = (1 - at_y) * 4 + at_x * 2 + core
    by_both = (1 - at_y) * 4 + (1 - at_x) * 2 + core
    partner = {"dp": other}
    along_x = {"dp": by_x}
    along_y = {"dp": by_y}
    over = {"dp": by_both}
    right = {"expert": (place + 1) % group}
    left = {"expert": (place + group - 1) % group}

    def ring_peer(k):
        return {"dp": (index + k) % parts}

    def rows_of(block):
        return pl.ds(pl.multiple_of(block * tok, tok), tok)

    def piece_of(number):
        return pl.ds(pl.multiple_of(number * piece, piece), piece)

    def qkv_spot(number):
        return w_qkv_buf.at[:, piece_of(number), :]

    def qkv_half(number, which):
        start = pl.multiple_of(number * piece + which * (piece // 2), piece // 2)
        return w_qkv_buf.at[:, pl.ds(start, piece // 2), :]

    def out_spot(number):
        return w_out_buf.at[:, piece_of(number)]

    def out_half(number, which):
        rows = pl.ds(which * (local_width // 2), local_width // 2)
        return w_out_buf.at[rows, piece_of(number)]

    class Gather:
        def __init__(self, number, source, spot, half_spot):
            self.number, self.source, self.spot, self.half_spot = number, source, spot, half_spot

        def copy(self, slot, source, target, peer):
            sems = gather_sems.at[self.number]
            return remote(source, target, sems.at[0, slot], sems.at[1, slot], peer)

        def own(self, slot, peer):
            return self.copy(slot, self.source, self.spot(index), peer)

        def keep(self):
            return pltpu.make_async_copy(
                self.source, self.spot(index), load_sems.at[8 + self.number]
            )

        def relay_x(self):
            spot = self.half_spot(by_y, 0)
            return self.copy(3, spot, spot, along_x)

        def relay_y(self):
            spot = self.half_spot(by_x, 1)
            return self.copy(4, spot, spot, along_y)

        def hand(self, slot):
            spot = (
                self.spot(by_x),
                self.spot(by_y),
                self.half_spot(by_both, 0),
                self.half_spot(by_both, 1),
            )[slot - 5]
            return self.copy(slot, spot, spot, partner)

        def begin(self):
            self.own(0, along_x).start()
            self.own(1, along_y).start()
            self.own(2, partner).start()
            self.keep().start()

        def relay(self):
            self.own(1, along_y).wait_recv()
            self.relay_x().start()
            self.own(0, along_x).wait_recv()
            self.relay_y().start()
            self.hand(5).start()
            self.hand(6).start()

        def finish(self):
            self.relay_x().wait_recv()
            self.hand(7).start()
            self.relay_y().wait_recv()
            self.hand(8).start()
            self.keep().wait()
            self.own(2, partner).wait_recv()
            for slot in (5, 6, 7, 8):
                self.hand(slot).wait_recv()

        def drain(self):
            for slot, peer in ((0, along_x), (1, along_y), (2, partner)):
                self.own(slot, peer).wait_send()
            self.relay_x().wait_send()
            self.relay_y().wait_send()
            for slot in (5, 6, 7, 8):
                self.hand(slot).wait_send()

    gather_qkv = Gather(0, w_qkv, qkv_spot, qkv_half)
    gather_out = Gather(1, w_out, out_spot, out_half)

    loads = [
        pltpu.make_async_copy(source, target, load_sems.at[number])
        for number, (source, target) in enumerate(
            [
                (tokens, tokens_buf.at[rows_of(place)]),
                (small, small_full.at[:, piece_of(index)]),
                (pair_cols, cols_buf),
                (pair_rows, rows_buf),
                (cosine, cosine_buf),
                (sine, sine_buf),
                (cotangent, cotangent_buf),
            ]
        )
    ]
    for load in loads:
        load.start()

    greet([ring_peer(k) for k in range(1, parts)] + [right, left])

    def own_pass(side, peer):
        return remote(
            tokens,
            tokens_buf.at[rows_of(place)],
            line_sems.at[side, place],
            line_sems.at[2, place],
            peer,
        )

    def pass_on(block, side, peer):
        spot = tokens_buf.at[rows_of(block)]
        return remote(spot, spot, line_sems.at[side, block], line_sems.at[2, block], peer)

    @pl.when(place < group - 1)
    def _():
        own_pass(0, right).start()

    @pl.when(place > 0)
    def _():
        own_pass(1, left).start()

    def small_copy(k):
        return remote(
            small,
            small_full.at[:, piece_of(index)],
            small_sems.at[0, k],
            small_sems.at[1, k],
            ring_peer(k),
        )

    for k in range(1, parts):
        small_copy(k).start()
    gather_qkv.begin()

    for load in loads:
        load.wait()

    cols = cols_buf[...]
    rows = rows_buf[...]
    first_col, second_col, order_col = cols[:, 0:1], cols[:, 1:2], cols[:, 2:3]
    first_row, second_row, order_row = rows[0:1], rows[1:2], rows[2:3]
    start = place * tok
    live_col = (start + lax.broadcasted_iota(jnp.int32, (tok, 1), 0)) < length[0]
    live_row = (start + lax.broadcasted_iota(jnp.int32, (1, tok), 1)) < length[0]
    before = order_col < order_row

    def count(mask):
        return jnp.sum(jnp.where(mask & live_col, 1.0, 0.0), axis=0, keepdims=True)

    slot_first = count((first_col == first_row) & before)
    slot_second = count(first_col == second_row) + count((second_col == second_row) & before)
    slot_ids = lax.broadcasted_iota(jnp.int32, (slots, tok), 0)
    for number, (named, slot) in enumerate(((first_row, slot_first), (second_row, slot_second))):
        slot = slot.astype(jnp.int32)
        step = named - place
        step = jnp.where(step < 0, step + group, step)
        target = jnp.where(live_row & (slot < cap), step * cap + slot, -1)
        hits[number] = jnp.where(slot_ids == target, 1.0, 0.0).astype(jnp.bfloat16)

    for k in range(1, parts):
        small_copy(k).wait_recv()

    def normalize_block(block):
        at = rows_of(block)
        value = tokens_buf[at, :].astype(jnp.float32)
        inverse = lax.rsqrt(jnp.mean(value * value, axis=-1, keepdims=True) + NORM_EPSILON)
        inverse_all[at, :] = inverse
        whole_buf[at, :] = (value * inverse * small_full[0:1, :]).astype(jnp.bfloat16)

    def arrive(step):
        block = line_order(place, step)
        pass_on(block, 0, right).wait_recv()

        @pl.when((block < place) & (place < group - 1))
        def _():
            pass_on(block, 0, right).start()

        @pl.when((block > place) & (place > 0))
        def _():
            pass_on(block, 1, left).start()

        normalize_block(block)

    normalize_block(place)
    arrive(0)
    gather_qkv.relay()
    gather_out.begin()
    arrive(1)
    gather_qkv.finish()

    def project(first, size):
        at = pl.ds(pl.multiple_of(first, tok), size)
        source = whole_buf[at, :]

        def two_heads(number, carry):
            lanes = pl.ds(pl.multiple_of(number * 2 * head_size, 2 * head_size), 2 * head_size)
            for c, target in ((0, query), (1, key_rows)):
                plain = dot_nn(source, w_qkv_buf[c, :, lanes])
                turned = [
                    rotated(
                        plain[:, side * head_size : (side + 1) * head_size],
                        cosine_buf[at, :],
                        sine_buf[at, :],
                    )
                    for side in range(2)
                ]
                target[at, lanes] = jnp.concatenate(turned, axis=1).astype(jnp.bfloat16)
            value[at, lanes] = dot_nn(source, w_qkv_buf[2, :, lanes]).astype(jnp.bfloat16)
            return carry

        lax.fori_loop(0, heads // 2, two_heads, 0)

    upper = place // 2
    project(upper * tok, seq_len - tok)
    gather_out.relay()

    def slice_copy(r, part):
        number = (by_x // 2, by_y // 2, by_both // 2)[r - 1]
        lanes = pl.ds(pl.multiple_of(part * ff + number * hidden, LANES), hidden)
        return remote(
            w_gate_up.at[0, :, lanes],
            w_got.at[r - 1, :, pl.ds(part * hidden, hidden)],
            slice_sems.at[0, r - 1, part],
            slice_sems.at[1, r - 1, part],
            (along_x, along_y, over)[r - 1],
        )

    for part in range(2):
        for r in (3, 1, 2):
            slice_copy(r, part).start()
    gather_out.finish()
    arrive(2)
    project((1 - upper) * (seq_len - tok), tok)

    stores = [
        pltpu.make_async_copy(source, target, load_sems.at[10 + number])
        for number, (source, target) in enumerate(
            [
                (w_qkv_buf, qkv_full),
                (w_out_buf, out_full),
                (tokens_buf, tokens_all),
                (whole_buf, whole),
            ]
        )
    ]
    for store in stores:
        store.start()

    for number in range(group):
        at = slice(number * tok, (number + 1) * tok)
        extent = (number + 1) * tok
        shape = (tok, extent)
        at_query = number * tok + lax.broadcasted_iota(jnp.int32, shape, 0)
        at_key = lax.broadcasted_iota(jnp.int32, shape, 1)
        allowed = (at_key <= at_query) & (at_key < length[0])
        for head in range(heads):
            lanes = slice(head * head_size, (head + 1) * head_size)
            scores = dot_nt(query[at, lanes], key_rows[0:extent, lanes]) * scale
            scores = jnp.where(allowed, scores, NEGATIVE)
            top = jnp.max(scores, axis=-1, keepdims=True)
            exponent = jnp.exp(scores - top)
            row_total = jnp.sum(exponent, axis=-1, keepdims=True)
            probs = (exponent / row_total).astype(jnp.bfloat16)
            attended[at, lanes] = dot_nn(probs, value[0:extent, lanes]).astype(jnp.bfloat16)
            log_total[at, head : head + 1] = top + jnp.log(row_total)

    def out_tile(j, carry):
        lanes = piece_of(j)
        part_buf[:, lanes] = dot_nn(attended[...], w_out_buf[:, lanes]).astype(jnp.bfloat16)
        return carry

    lax.fori_loop(0, parts, out_tile, 0)

    def go_right(block):
        return remote(
            part_buf.at[rows_of(block)],
            from_left.at[block],
            sum_sems.at[0, block],
            sum_sems.at[1, block],
            right,
        )

    def go_left(block):
        return remote(
            part_buf.at[rows_of(block)],
            from_right.at[block],
            sum_sems.at[0, block],
            sum_sems.at[2, block],
            left,
        )

    def add_into(target, added):
        total = target[...].astype(jnp.float32) + added[...].astype(jnp.float32)
        target[...] = total.astype(jnp.bfloat16)

    def on_right(block):
        go_right(block).wait_recv()
        add_into(part_buf.at[rows_of(block)], from_left.at[block])
        go_right(block).start()

    def on_left(block):
        go_left(block).wait_recv()
        add_into(part_buf.at[rows_of(block)], from_right.at[block])
        go_left(block).start()

    @pl.when(place == 0)
    def _():
        for block in (3, 2, 1):
            go_right(block).start()

    @pl.when(place == 3)
    def _():
        for block in (0, 1, 2):
            go_left(block).start()

    @pl.when(place == 1)
    def _():
        on_right(3)
        on_right(2)
        on_left(0)

    @pl.when(place == 2)
    def _():
        on_left(0)
        on_left(1)
        on_right(3)

    resid[...] = tokens_buf[rows_of(place), :].astype(jnp.float32) + part_buf[
        rows_of(place), :
    ].astype(jnp.float32)

    @pl.when(place > 0)
    def _():
        go_right(place).wait_recv()
        resid[...] += from_left[place].astype(jnp.float32)

    @pl.when(place < group - 1)
    def _():
        go_left(place).wait_recv()
        resid[...] += from_right[place].astype(jnp.float32)

    total = resid[...]
    inverse = lax.rsqrt(jnp.mean(total * total, axis=-1, keepdims=True) + NORM_EPSILON)
    inverse_two[...] = inverse
    hidden_in = (total * inverse * small_full[1:2, :]).astype(jnp.bfloat16)
    logits = dot_nt(hidden_in, small_full[...].astype(jnp.bfloat16))
    lane = lax.broadcasted_iota(jnp.int32, logits.shape, 1)
    chosen = [
        jnp.sum(jnp.where(lane == named + 2, logits, 0.0), axis=1, keepdims=True)
        for named in (first_col, second_col)
    ]
    top = jnp.maximum(chosen[0], chosen[1])
    raised = [jnp.exp(entry - top) for entry in chosen]
    both = raised[0] + raised[1]
    gate = [entry / both for entry in raised]
    for number in range(2):
        gates[:, number : number + 1] = gate[number]
    sent[...] = dot_nn(hits[0] + hits[1], hidden_in).astype(jnp.bfloat16)
    d_out = jnp.where(live_col, 1.0, 0.0) * cotangent_buf[...].astype(jnp.float32)
    d_back[...] = (
        dot_nn(hits[0], (gate[0] * d_out).astype(jnp.bfloat16))
        + dot_nn(hits[1], (gate[1] * d_out).astype(jnp.bfloat16))
    ).astype(jnp.bfloat16)

    for store in stores:
        store.wait()
    gather_qkv.drain()
    gather_out.drain()
    for k in range(1, parts):
        small_copy(k).wait_send()
    for block in range(group):

        @pl.when(block > place)
        def _():
            go_right(block).wait_send()

        @pl.when(block < place)
        def _():
            go_left(block).wait_send()

        @pl.when((block <= place) & (place < group - 1))
        def _():
            pass_on(block, 0, right).wait_send()

        @pl.when((block >= place) & (place > 0))
        def _():
            pass_on(block, 1, left).wait_send()

    for part in range(2):
        for r in (1, 2, 3):
            slice_copy(r, part).wait()


def attention_call(
    lengths, tokens, w_qkv, w_out, small, w_gate_up, pair_cols, cosine, sine, cotangent, group
):
    tok, width = tokens.shape
    seq_len = tok * group
    local_width = w_qkv.shape[2]
    heads = local_width // HEAD_DIM
    slots = tok * 2
    piece = w_qkv.shape[1]
    low, full = jnp.bfloat16, jnp.float32
    pair_rows = pair_cols.T
    anywhere = pl.BlockSpec(memory_space=pl.ANY)
    inside = pl.BlockSpec(memory_space=pltpu.VMEM)
    narrow = jax.ShapeDtypeStruct((seq_len, local_width), low)
    flops = 2 * seq_len * width * local_width * 4 + 4 * seq_len * seq_len * local_width
    return pl.pallas_call(
        functools.partial(attention_kernel, heads),
        out_shape=(
            jax.ShapeDtypeStruct((seq_len, width), low),
            jax.ShapeDtypeStruct((seq_len, width), low),
            jax.ShapeDtypeStruct((3, width, local_width), low),
            jax.ShapeDtypeStruct((local_width, width), low),
            jax.ShapeDtypeStruct((3, piece, w_gate_up.shape[2] // 4), low),
            jax.ShapeDtypeStruct((seq_len, 1), full),
            narrow,
            narrow,
            narrow,
            narrow,
            jax.ShapeDtypeStruct((seq_len, heads), full),
            jax.ShapeDtypeStruct((small.shape[0], width), full),
            jax.ShapeDtypeStruct((tok, width), full),
            jax.ShapeDtypeStruct((tok, 1), full),
            jax.ShapeDtypeStruct((tok, 2), full),
            jax.ShapeDtypeStruct((2, slots, tok), low),
            jax.ShapeDtypeStruct((slots, width), low),
            jax.ShapeDtypeStruct((slots, width), low),
        ),
        in_specs=[pl.BlockSpec(memory_space=pltpu.SMEM)] + [anywhere] * 10,
        out_specs=(anywhere,) * 5 + (inside,) * 13,
        scratch_shapes=[
            pltpu.VMEM((seq_len, width), low),
            pltpu.VMEM((seq_len, width), low),
            pltpu.VMEM((3, width, local_width), low),
            pltpu.VMEM((local_width, width), low),
            pltpu.VMEM((seq_len, width), low),
            pltpu.VMEM((group, tok, width), low),
            pltpu.VMEM((group, tok, width), low),
            pltpu.VMEM((tok, 8), jnp.int32),
            pltpu.VMEM((8, tok), jnp.int32),
            pltpu.VMEM(cosine.shape, full),
            pltpu.VMEM(sine.shape, full),
            pltpu.VMEM((tok, width), low),
            pltpu.SemaphoreType.DMA((14,)),
            pltpu.SemaphoreType.DMA((3, group)),
            pltpu.SemaphoreType.DMA((3, group)),
            pltpu.SemaphoreType.DMA((2, 2, 9)),
            pltpu.SemaphoreType.DMA((2, width // piece)),
            pltpu.SemaphoreType.DMA((2, 3, 2)),
        ],
        compiler_params=pltpu.CompilerParams(
            collective_id=3, has_side_effects=True, vmem_limit_bytes=67043328
        ),
        cost_estimate=pl.CostEstimate(flops=flops, bytes_accessed=40000000, transcendentals=0),
        name="attention",
    )(
        lengths,
        tokens,
        w_qkv,
        w_out,
        small,
        w_gate_up,
        pair_cols,
        pair_rows,
        cosine,
        sine,
        cotangent,
    )


def expert_step(gate_up_w, down_w, rows, d_rows_out):
    ff = down_w.shape[0]
    gate_up = jnp.dot(rows, gate_up_w, preferred_element_type=jnp.float32)
    gate = gate_up[:, :ff]
    upward = gate_up[:, ff:]
    sigmoid = jax.nn.sigmoid(gate)
    activated = (gate * sigmoid * upward).astype(jnp.bfloat16)
    out = jnp.dot(activated, down_w, preferred_element_type=jnp.float32).astype(jnp.bfloat16)
    d_activated = contract_last(d_rows_out, down_w)
    grad_down = contract_first(activated, d_rows_out)
    d_gate = d_activated * upward * sigmoid * (1.0 + gate * (1.0 - sigmoid))
    d_up = d_activated * gate * sigmoid
    d_gate_up = jnp.concatenate([d_gate, d_up], axis=1).astype(jnp.bfloat16)
    d_rows = contract_last(d_gate_up, gate_up_w).astype(jnp.bfloat16)
    grad_gate_up = contract_first(rows, d_gate_up)
    return out, d_rows, grad_gate_up, grad_down


def experts_gather_weights(w_gate_up, w_down, rows, d_rows_out):
    gate_up_w = lax.all_gather(w_gate_up, "dp", axis=1, tiled=True)[0]
    down_w = lax.all_gather(w_down, "dp", axis=1, tiled=True)[0]
    shape = rows.shape
    flat = (-1, shape[2])
    rows = exchange_experts(rows).reshape(flat)
    d_rows_out = exchange_experts(d_rows_out).reshape(flat)
    out, d_rows, grad_gate_up, grad_down = expert_step(gate_up_w, down_w, rows, d_rows_out)
    out = exchange_experts(out.reshape(shape))
    d_rows = exchange_experts(d_rows.reshape(shape))
    grad_gate_up = lax.psum_scatter(
        grad_gate_up.astype(jnp.bfloat16), "dp", scatter_dimension=0, tiled=True
    )
    grad_down = lax.psum_scatter(
        grad_down.astype(jnp.bfloat16), "dp", scatter_dimension=0, tiled=True
    )
    return (
        out,
        d_rows,
        grad_gate_up.astype(jnp.float32)[None],
        grad_down.astype(jnp.float32)[None],
    )


def attention_back_plain(
    lengths,
    d_attn,
    hat_all,
    whole,
    out_full,
    qkv_full,
    query,
    key_rows,
    value,
    attended,
    log_total,
    cosine,
    sine,
):
    seq_len, heads_local, head_size = query.shape
    local_width = heads_local * head_size
    position = jnp.arange(seq_len, dtype=jnp.int32)
    allowed = (position[None, :] <= position[:, None]) & (position < lengths[0])[None, :]
    whole_grad = lax.all_gather(d_attn, "expert", axis=0, tiled=True)
    d_attended = contract_last(whole_grad, out_full).astype(jnp.bfloat16)
    out_part = contract_first(attended, whole_grad)
    grad_out = lax.psum_scatter(
        out_part.astype(jnp.bfloat16), "dp", scatter_dimension=1, tiled=True
    ).astype(jnp.float32)
    d_heads = d_attended.reshape(seq_len, heads_local, head_size)
    probs = jnp.exp(masked_scores(query, key_rows, allowed) - log_total)
    probs_low = probs.astype(jnp.bfloat16)
    d_value = jnp.einsum(
        "hqk,qhd->khd", probs_low, d_heads, preferred_element_type=jnp.float32
    ).astype(jnp.bfloat16)
    d_probs = jnp.einsum("qhd,khd->hqk", d_heads, value, preferred_element_type=jnp.float32)
    row_delta = jnp.sum(probs * d_probs, axis=-1, keepdims=True)
    d_scores = (probs * (d_probs - row_delta)).astype(jnp.bfloat16)
    scale = head_size ** (-0.5)
    d_query = (
        jnp.einsum("hqk,khd->qhd", d_scores, key_rows, preferred_element_type=jnp.float32) * scale
    )
    d_key = jnp.einsum("hqk,qhd->khd", d_scores, query, preferred_element_type=jnp.float32) * scale
    d_query_pre = (
        rotate_back(d_query, cosine, sine).reshape(seq_len, local_width).astype(jnp.bfloat16)
    )
    d_key_pre = rotate_back(d_key, cosine, sine).reshape(seq_len, local_width).astype(jnp.bfloat16)
    d_projected = jnp.stack([d_query_pre, d_key_pre, d_value.reshape(seq_len, local_width)])
    d_normed_part = jnp.einsum(
        "cte,cde->td", d_projected, qkv_full, preferred_element_type=jnp.float32
    )
    grad_normalized = lax.psum_scatter(
        d_normed_part.astype(jnp.bfloat16), "expert", scatter_dimension=0, tiled=True
    ).astype(jnp.float32)
    qkv_part = jnp.einsum("td,cte->cde", whole, d_projected, preferred_element_type=jnp.float32)
    grad_qkv = lax.psum_scatter(
        qkv_part.astype(jnp.bfloat16), "dp", scatter_dimension=1, tiled=True
    ).astype(jnp.float32)
    first_gain_part = jnp.sum(d_normed_part * hat_all, axis=0)
    return grad_normalized, grad_qkv, grad_out, first_gain_part


def on_device(
    tokens,
    w_qkv,
    w_out,
    attention_norm_gain,
    gain_ffn,
    w_router,
    w_gate_up,
    w_down,
    lengths,
    routes,
    order,
    cotangent,
):
    group_size = lax.axis_size("expert")
    dp_size = lax.axis_size("dp")
    tok_dev = tokens.shape[0]
    seq_len = tok_dev * group_size
    width = tokens.shape[1]
    top_count = routes.shape[1]
    capacity = tok_dev * top_count // group_size
    slots = group_size * capacity
    head_size = HEAD_DIM
    local_width = w_qkv.shape[2]
    heads_local = local_width // head_size
    tokens_all = lax.all_gather(tokens, "expert", axis=0, tiled=True)
    small = jnp.concatenate(
        [attention_norm_gain[:, None], gain_ffn[:, None], w_router], axis=1
    )
    small_full = lax.all_gather(small, "dp", axis=0, tiled=True)
    qkv_full = lax.all_gather(w_qkv, "dp", axis=1, tiled=True)
    out_full = lax.all_gather(w_out, "dp", axis=1, tiled=True)
    first_norm_gain = small_full[:, 0].astype(jnp.float32)
    gain_two = small_full[:, 1].astype(jnp.float32)
    router_full = small_full[:, 2:]

    own_start = lax.axis_index("expert") * tok_dev
    own_position = own_start + jnp.arange(tok_dev, dtype=jnp.int32)
    live_own = own_position < lengths[0]
    live_rows = live_own.astype(jnp.float32)[:, None]
    target, kept_pair = slot_table(routes, order, live_own, capacity)
    slot_ids = jnp.arange(slots, dtype=jnp.int32)
    pair_hits = (slot_ids[:, None, None] == target[None]) & kept_pair[None]
    select = jnp.sum(pair_hits.astype(jnp.float32), axis=2).astype(jnp.bfloat16)

    inputs_float = tokens.astype(jnp.float32)
    input_normalized_hat, first_inverse_rms = normalize(inputs_float)
    hat_all, _ = normalize(tokens_all.astype(jnp.float32))
    whole = (hat_all * first_norm_gain).astype(jnp.bfloat16)
    cosine, sine = rotary_tables(seq_len, head_size)
    projected = jnp.einsum("td,cde->cte", whole, qkv_full, preferred_element_type=jnp.float32)
    query = rotate(projected[0].reshape(seq_len, heads_local, head_size), cosine, sine).astype(
        jnp.bfloat16
    )
    key_rows = rotate(projected[1].reshape(seq_len, heads_local, head_size), cosine, sine).astype(
        jnp.bfloat16
    )
    value = projected[2].astype(jnp.bfloat16).reshape(seq_len, heads_local, head_size)
    position = jnp.arange(seq_len, dtype=jnp.int32)
    live_all = position < lengths[0]
    allowed = (position[None, :] <= position[:, None]) & live_all[None, :]
    scores = masked_scores(query, key_rows, allowed)
    top_score = jnp.max(scores, axis=-1, keepdims=True)
    exponent = jnp.exp(scores - top_score)
    row_total = jnp.sum(exponent, axis=-1, keepdims=True)
    probs = exponent / row_total
    log_total = top_score + jnp.log(row_total)
    probs_low = probs.astype(jnp.bfloat16)
    attended = jnp.einsum("hqk,khd->qhd", probs_low, value, preferred_element_type=jnp.float32)
    attended = attended.reshape(seq_len, local_width).astype(jnp.bfloat16)
    attn_part = jnp.dot(attended, out_full, preferred_element_type=jnp.float32)
    attn_own = lax.psum_scatter(
        attn_part.astype(jnp.bfloat16), "expert", scatter_dimension=0, tiled=True
    ).astype(jnp.float32)
    resid = inputs_float + attn_own
    hhat, inverse_two = normalize(resid)
    hidden_in = (hhat * gain_two).astype(jnp.bfloat16)
    sent = jnp.dot(select, hidden_in, preferred_element_type=jnp.float32).astype(jnp.bfloat16)

    logits = jnp.dot(hidden_in, router_full, preferred_element_type=jnp.float32)
    chosen = jnp.take_along_axis(logits, routes, axis=1)
    gates = jax.nn.softmax(chosen, axis=1)
    d_out = live_rows * cotangent.astype(jnp.float32)
    d_back = jnp.zeros((slots, width), jnp.float32)
    for index in range(top_count):
        weighted = (gates[:, index : index + 1] * d_out).astype(jnp.bfloat16)
        d_back = d_back + jnp.dot(
            pair_hits[:, :, index].astype(jnp.bfloat16),
            weighted,
            preferred_element_type=jnp.float32,
        )
    d_back = d_back.astype(jnp.bfloat16)
    blocked = (group_size, capacity, width)
    returned, d_sent, grad_gate_up, grad_down = experts_gather_weights(
        w_gate_up, w_down, sent.reshape(blocked), d_back.reshape(blocked)
    )
    returned = returned.reshape(slots, width)
    d_sent = d_sent.reshape(slots, width)

    moe = jnp.zeros_like(resid)
    d_gates_list = []
    for index in range(top_count):
        one_hot = pair_hits[:, :, index].astype(jnp.bfloat16)
        picked = contract_first(one_hot, returned)
        d_gates_list.append(jnp.sum(d_out * picked, axis=-1))
        moe = moe + gates[:, index : index + 1] * picked
    output = (live_rows * (resid + moe)).astype(jnp.bfloat16)
    d_gates = jnp.stack(d_gates_list, axis=1)
    d_hidden = contract_first(select, d_sent)
    d_chosen = gates * (d_gates - jnp.sum(gates * d_gates, axis=1, keepdims=True))
    expert_ids = jnp.arange(group_size, dtype=jnp.int32)
    route_hits = (routes[:, :, None] == expert_ids[None, None, :]).astype(jnp.float32)
    d_logits = jnp.sum(route_hits * d_chosen[:, :, None], axis=1)
    router_f = router_full.astype(jnp.float32)
    d_hidden = d_hidden + jnp.dot(
        d_logits, router_f.T, precision=HIGH, preferred_element_type=jnp.float32
    )
    router_part = jnp.dot(
        hidden_in.astype(jnp.float32).T,
        d_logits,
        precision=HIGH,
        preferred_element_type=jnp.float32,
    )
    gain_two_part = jnp.sum(d_hidden * hhat, axis=0)
    scaled_two = d_hidden * gain_two
    d_resid = d_out + inverse_two * (
        scaled_two - hhat * jnp.mean(scaled_two * hhat, axis=-1, keepdims=True)
    )
    d_attn = d_resid.astype(jnp.bfloat16)
    grad_normalized, grad_qkv, grad_out, first_gain_part = attention_back_plain(
        lengths,
        d_attn,
        hat_all,
        whole,
        out_full,
        qkv_full,
        query,
        key_rows,
        value,
        attended,
        log_total,
        cosine,
        sine,
    )
    small_part = jnp.concatenate(
        [first_gain_part[None], gain_two_part[None], router_part.T], axis=0
    )
    small_sum = lax.psum(small_part, ("dp", "expert"))
    own_rows = width // dp_size
    small_own = lax.dynamic_slice_in_dim(
        small_sum, lax.axis_index("dp") * own_rows, own_rows, axis=1
    )
    first_scaled_input = grad_normalized * first_norm_gain
    grad_tokens = d_resid + first_inverse_rms * (
        first_scaled_input
        - input_normalized_hat
        * jnp.mean(first_scaled_input * input_normalized_hat, axis=-1, keepdims=True)
    )
    return (
        output,
        grad_tokens.astype(jnp.bfloat16),
        grad_qkv,
        grad_out,
        small_own[0],
        small_own[1],
        small_own[2 : 2 + group_size].T,
        grad_gate_up,
        grad_down,
    )


def on_device_split(
    tokens,
    w_qkv,
    w_out,
    attention_norm_gain,
    gain_ffn,
    w_router,
    w_gate_up,
    w_down,
    lengths,
    routes,
    order,
    cotangent,
):
    group = lax.axis_size("expert")
    tok, width = tokens.shape
    piece = w_router.shape[0]
    slots = tok * routes.shape[1]
    cosine, sine = rotary_constants(tok * group, HEAD_DIM)
    small = jnp.concatenate(
        [
            attention_norm_gain[None],
            gain_ffn[None],
            w_router.T,
            jnp.zeros((2, piece), jnp.bfloat16),
        ],
        axis=0,
    ).astype(jnp.float32)
    pair_cols = jnp.concatenate([routes, order[:, None], jnp.zeros((tok, 5), jnp.int32)], axis=1)
    (
        tokens_all,
        whole,
        qkv_full,
        out_full,
        w_got,
        inverse_all,
        query,
        key_rows,
        value,
        attended,
        log_total,
        small_full,
        resid,
        inverse_two,
        gates,
        hits,
        sent,
        d_back,
    ) = attention_call(
        lengths,
        tokens,
        w_qkv,
        w_out,
        small,
        w_gate_up,
        pair_cols,
        cosine,
        sine,
        cotangent,
        group,
    )
    blocked = (group, slots // group, width)
    returned, d_sent, grad_gate_up, grad_down = experts_call(
        sent.reshape(blocked), d_back.reshape(blocked), w_gate_up, w_got, w_down
    )
    output, grad_tokens, grad_weights, small_own, gate_got = attention_back_call(
        lengths,
        returned.reshape(slots, width),
        d_sent.reshape(slots, width),
        resid,
        inverse_two,
        gates,
        hits,
        cotangent,
        pair_cols,
        small_full,
        tokens_all,
        inverse_all,
        whole,
        out_full,
        qkv_full,
        query,
        key_rows,
        value,
        attended,
        log_total,
        cosine,
        sine,
        grad_gate_up,
    )
    grad_gate_up, grad_down, grad_tokens, output, grad_qkv, grad_out = finish_call(
        gate_got, grad_down, grad_tokens, output, grad_weights
    )
    return (
        output,
        grad_tokens,
        grad_qkv,
        grad_out,
        small_own[0],
        small_own[1],
        small_own[2 : 2 + group].T,
        grad_gate_up,
        grad_down,
    )


def solution(mesh):
    placed = (
        P(("dp", "expert"), None),
        P(None, "dp", "expert"),
        P("expert", "dp"),
        P("dp"),
        P("dp"),
        P("dp", None),
        P("expert", "dp", None),
        P("expert", "dp", None),
        P("dp"),
        P(("dp", "expert"), None),
        P(("dp", "expert")),
        P(("dp", "expert"), None),
    )
    split = mesh.shape["dp"] == 8 and mesh.shape["expert"] == 4
    return jax.shard_map(
        on_device_split if split else on_device,
        mesh=mesh,
        in_specs=placed,
        out_specs=(
            P(("dp", "expert"), None),
            P(("dp", "expert"), None),
            P(None, "dp", "expert"),
            P("expert", "dp"),
            P("dp"),
            P("dp"),
            P("dp", None),
            P("expert", "dp", None),
            P("expert", "dp", None),
        ),
        check_vma=False,
    )
```

```python
import functools

import jax
import jax.numpy as jnp
import numpy as np
from jax import lax
from jax.experimental import pallas as pl
from jax.experimental.pallas import tpu as pltpu
from jax.sharding import PartitionSpec as P

HEAD_DIM = 128
FF = 5632


NORM_EPSILON = 1e-05
NEGATIVE = -1e30
THETA = 10000.0
HIGH = lax.Precision.HIGHEST
MESH_ID = pl.DeviceIdType.MESH
LANES = 128


def remote(src, dst, send_sem, recv_sem, peer):
    return pltpu.make_async_remote_copy(
        src_ref=src,
        dst_ref=dst,
        send_sem=send_sem,
        recv_sem=recv_sem,
        device_id=peer,
        device_id_type=MESH_ID,
    )


def greet(peers):
    barrier = pltpu.get_barrier_semaphore()
    for peer in peers:
        pl.semaphore_signal(barrier, inc=1, device_id=peer, device_id_type=MESH_ID)
    pl.semaphore_wait(barrier, len(peers))


def dot_nn(left, right):
    return jnp.dot(left, right, preferred_element_type=jnp.float32)


def dot_nt(left, right):
    return lax.dot_general(
        left, right, (((1,), (1,)), ((), ())), preferred_element_type=jnp.float32
    )


def experts_kernel(
    group,
    sent,
    d_back,
    w_gate_up,
    w_got,
    w_down,
    ret,
    d_ret,
    grad_gate_up,
    grad_down,
    w_buf,
    down_buf,
    rows_buf,
    gate_buf,
    act_buf,
    part_buf,
    half_x,
    half_y,
    full_x,
    full_y,
    other_gate,
    other_down,
    ag_sems,
    rs_sems,
    weight_sems,
    local_sems,
    grad_sems,
):
    cap, width = sent.shape[1], sent.shape[2]
    half = cap // 2
    piece, hidden2 = w_got.shape[1:]
    hidden = hidden2 // 2
    down_own = w_down.at[0]
    down_rows = down_own.shape[0]
    chunk = 4 * cap
    total = group * chunk

    index = lax.axis_index("dp")
    place = lax.axis_index("expert")
    core = index % 2
    at_x = (index // 2) % 2
    at_y = index // 4
    partner = {"dp": at_y * 4 + at_x * 2 + (1 - core)}
    along_x = {"dp": at_y * 4 + (1 - at_x) * 2 + core}
    along_y = {"dp": (1 - at_y) * 4 + at_x * 2 + core}
    chips = [
        at_y * 2 + at_x,
        at_y * 2 + (1 - at_x),
        (1 - at_y) * 2 + at_x,
        (1 - at_y) * 2 + (1 - at_x),
    ]

    def ahead(k):
        return {"expert": (place + k) % group}

    def behind(k):
        return {"expert": (place + group - k) % group}

    greet([partner, along_x, along_y] + [ahead(k) for k in range(1, group)])

    def block(t, k, r, start=0, size=None):
        size = cap if size is None else size
        return rows_buf.at[t, pl.ds((k * 4 + r) * cap + start, size), :]

    def part(t, k, r, start=0, size=None):
        size = cap if size is None else size
        return part_buf.at[t, pl.ds((k * 4 + r) * cap + start, size), :]

    def ag(kind, t, k):
        return ag_sems.at[0, kind, t, k], ag_sems.at[1, kind, t, k]

    def rs(kind, t, k):
        return rs_sems.at[0, kind, t, k], rs_sems.at[1, kind, t, k]

    sources = (sent, d_back)
    results = (ret, d_ret)

    def z_copy(t, k):
        return remote(sources[t].at[k], block(t, k, 0), *ag(0, t, k), ahead(k))

    def own_copy(t):
        return pltpu.make_async_copy(sources[t].at[0], block(t, 0, 0), local_sems.at[t])

    def x_copy(t, k):
        return remote(block(t, k, 0), block(t, k, 1), *ag(1, t, k), along_x)

    def y_copy(t, k):
        return remote(block(t, k, 0), block(t, k, 2), *ag(2, t, k), along_y)

    def a_copy(t, k):
        return remote(block(t, k, 2, 0, half), block(t, k, 3, 0, half), *ag(3, t, k), along_x)

    def b_copy(t, k):
        return remote(
            block(t, k, 1, half, half), block(t, k, 3, half, half), *ag(4, t, k), along_y
        )

    def spread(t, k):
        if k == 0:
            own_copy(t).wait()
        else:
            z_copy(t, k).wait_recv()
        x_copy(t, k).start()
        y_copy(t, k).start()

    def relay_a(t, k):
        y_copy(t, k).wait_recv()
        a_copy(t, k).start()

    def relay_b(t, k):
        x_copy(t, k).wait_recv()
        b_copy(t, k).start()

    def arrived(t, k):
        a_copy(t, k).wait_recv()
        b_copy(t, k).wait_recv()
        if t == 0 and k == 0:
            for r in range(4):
                for copy in w_keep(r):
                    copy.wait()
                for copy in w_share(r, 1 - core):
                    copy.wait_recv()
            down_keep.wait()
            down_share().wait_recv()

    def half_x_copy(t, k):
        return remote(part(t, k, 3, 0, half), half_x.at[t, k], *rs(0, t, k), along_x)

    def half_y_copy(t, k):
        return remote(part(t, k, 3, half, half), half_y.at[t, k], *rs(1, t, k), along_y)

    def full_x_copy(t, k):
        return remote(part(t, k, 1), full_x.at[t, k], *rs(2, t, k), along_x)

    def full_y_copy(t, k):
        return remote(part(t, k, 2), full_y.at[t, k], *rs(3, t, k), along_y)

    def back_copy(t, k):
        return remote(part(t, k, 0), results[t].at[k], *rs(4, t, k), behind(k))

    def keep_copy(t):
        return pltpu.make_async_copy(part(t, 0, 0), results[t].at[0], local_sems.at[2 + t])

    def halves_out(t, k):
        half_x_copy(t, k).start()
        half_y_copy(t, k).start()

    def add_into(target, *others):
        value = target[...].astype(jnp.float32)
        for other in others:
            value = value + other[...].astype(jnp.float32)
        target[...] = value.astype(jnp.bfloat16)

    def full_y_out(t, k):
        half_x_copy(t, k).wait_recv()
        add_into(part(t, k, 2, 0, half), half_x.at[t, k])
        full_y_copy(t, k).start()

    def full_x_out(t, k):
        half_y_copy(t, k).wait_recv()
        add_into(part(t, k, 1, half, half), half_y.at[t, k])
        full_x_copy(t, k).start()

    def home(t, k):
        full_x_copy(t, k).wait_recv()
        full_y_copy(t, k).wait_recv()
        add_into(part(t, k, 0), full_x.at[t, k], full_y.at[t, k])
        if k == 0:
            keep_copy(t).start()
        else:
            back_copy(t, k).start()

    def w_rows(r, which):
        return pl.ds(pl.multiple_of((chips[r] * 2 + which) * piece, piece), piece)

    def w_parts(r, which):
        rows = w_rows(r, which)
        if r > 0:
            return [(w_got.at[r - 1], w_buf.at[rows, :], r)]
        return [
            (
                w_gate_up.at[
                    0, :, pl.ds(pl.multiple_of((4 * part + chips[0]) * hidden, LANES), hidden)
                ],
                w_buf.at[rows, pl.ds(part * hidden, hidden)],
                4 * part,
            )
            for part in range(2)
        ]

    def w_share(r, which):
        return [
            remote(source, target, weight_sems.at[0, n], weight_sems.at[1, n], partner)
            for source, target, n in w_parts(r, which)
        ]

    def w_keep(r):
        return [
            pltpu.make_async_copy(source, target, local_sems.at[4 + n])
            for source, target, n in w_parts(r, core)
        ]

    def down_at(which):
        return down_buf.at[pl.ds(pl.multiple_of(which * down_rows, down_rows), down_rows), :]

    def down_share():
        return remote(
            down_own, down_at(core), weight_sems.at[0, 5], weight_sems.at[1, 5], partner
        )

    down_keep = pltpu.make_async_copy(down_own, down_at(core), local_sems.at[9])

    def take(steps, k, number):
        for at in range(group):
            if (at, number) in steps:

                @pl.when(k == at)
                def _(events=steps[at, number]):
                    for event, t, which in events:
                        event(t, which)

    blocks = hidden // LANES
    spans = [(2 * j, min(2, blocks - 2 * j)) for j in range((blocks + 1) // 2)]
    tiles = width // (2 * LANES)

    def span(first, count):
        return pl.ds(first * LANES, count * LANES)

    def forward(k, carry):
        at = pl.ds(pl.multiple_of(k * chunk, chunk), chunk)

        def tile(first, count):
            gate_cols, up_cols = span(first, count), span(blocks + first, count)
            rows = rows_buf[0, at, :]
            if count == 1:
                weights = jnp.concatenate([w_buf[:, gate_cols], w_buf[:, up_cols]], axis=1)
                both = dot_nn(rows, weights)
                gate, up = both[:, :LANES], both[:, LANES:]
            else:
                gate = dot_nn(rows, w_buf[:, gate_cols])
                up = dot_nn(rows, w_buf[:, up_cols])
            sigmoid = 1.0 / (1.0 + jnp.exp(-gate))
            gate_buf[at, gate_cols] = gate.astype(jnp.bfloat16)
            gate_buf[at, up_cols] = up.astype(jnp.bfloat16)
            act_buf[at, gate_cols] = (gate * sigmoid * up).astype(jnp.bfloat16)

        take(forward_steps, k, 0)
        for first, count in spans[:3]:
            tile(first, count)
        take(forward_steps, k, 1)
        for first, count in spans[3:]:
            tile(first, count)
        take(forward_steps, k, 2)
        for j in range(tiles):
            cols = span(2 * j, 2)
            out = dot_nn(act_buf[at, :], down_buf[:, cols])
            part_buf[0, at, cols] = out.astype(jnp.bfloat16)
        return carry

    def backward(turn, carry):
        k = (turn + 1) % group
        at = pl.ds(pl.multiple_of(k * chunk, chunk), chunk)
        take(backward_steps, k, 0)
        for first, count in spans:
            gate_cols, up_cols = span(first, count), span(blocks + first, count)
            d_act = dot_nt(rows_buf[1, at, :], down_buf[gate_cols, :])
            gate = gate_buf[at, gate_cols].astype(jnp.float32)
            up = gate_buf[at, up_cols].astype(jnp.float32)
            sigmoid = 1.0 / (1.0 + jnp.exp(-gate))
            scaled = d_act * sigmoid
            d_gate = scaled * up * (1.0 + gate * (1.0 - sigmoid))
            gate_buf[at, gate_cols] = d_gate.astype(jnp.bfloat16)
            gate_buf[at, up_cols] = (scaled * gate).astype(jnp.bfloat16)
        for side in range(2):
            take(backward_steps, k, 1 + side)
            for j in range(side * (tiles // 2), (side + 1) * (tiles // 2)):
                cols = span(2 * j, 2)
                out = dot_nt(gate_buf[at, :], w_buf[cols, :])
                part_buf[1, at, cols] = out.astype(jnp.bfloat16)
        return carry

    forward_steps = {
        (0, 0): [(spread, 0, 0), (spread, 1, 0), (spread, 0, 1), (relay_a, 0, 0), (relay_b, 0, 0), (relay_a, 1, 0), (relay_b, 1, 0), (spread, 0, 2), (relay_a, 0, 1), (relay_b, 0, 1), (arrived, 0, 0)],
        (0, 2): [(spread, 0, 3)],
        (1, 0): [(halves_out, 0, 0), (relay_a, 0, 2), (relay_b, 0, 2), (arrived, 0, 1)],
        (1, 1): [(spread, 1, 1)],
        (2, 0): [(relay_a, 0, 3), (relay_b, 0, 3), (halves_out, 0, 1), (spread, 1, 2), (arrived, 0, 2)],
        (2, 2): [(spread, 1, 3)],
        (3, 0): [(arrived, 0, 3)],
        (3, 1): [(relay_a, 1, 1)],
        (3, 2): [(relay_b, 1, 1), (full_y_out, 0, 0)],
    }
    backward_steps = {
        (0, 0): [(arrived, 1, 0)],
        (0, 1): [(full_y_out, 0, 3), (full_y_out, 1, 1)],
        (0, 2): [(full_x_out, 1, 1)],
        (1, 0): [(relay_a, 1, 2), (relay_b, 1, 2), (relay_a, 1, 3), (relay_b, 1, 3), (full_x_out, 0, 0), (full_y_out, 0, 1), (arrived, 1, 1)],
        (1, 2): [(full_x_out, 0, 1), (halves_out, 0, 2)],
        (2, 0): [(arrived, 1, 2)],
        (2, 1): [(halves_out, 0, 3), (halves_out, 1, 1)],
        (3, 0): [(home, 0, 0), (arrived, 1, 3)],
        (3, 1): [(halves_out, 1, 2)],
        (3, 2): [(full_x_out, 0, 2), (home, 0, 1), (full_y_out, 0, 2), (full_x_out, 0, 3)],
    }
    grad_steps = {
        (0, 0): [(full_y_out, 1, 2)],
        (1, 0): [(home, 0, 2), (full_x_out, 1, 2)],
        (2, 0): [(halves_out, 1, 0), (halves_out, 1, 3)],
        (2, 1): [(home, 0, 3)],
        (2, 3): [(home, 1, 1)],
        (4, 0): [(full_x_out, 1, 0), (full_y_out, 1, 0), (full_x_out, 1, 3), (home, 1, 2)],
        (4, 1): [(full_y_out, 1, 3)],
        (5, 0): [(home, 1, 0), (home, 1, 3)],
    }

    own_copy(0).start()
    for k in range(1, group):
        z_copy(0, k).start()
    for r in range(4):
        for copy in w_share(r, core) + w_keep(r):
            copy.start()
    down_share().start()
    down_keep.start()
    own_copy(1).start()

    for k in range(1, group):
        z_copy(1, k).start()

    lax.fori_loop(0, group, forward, 0)
    lax.fori_loop(0, group, backward, 0)
    for event, t, which in grad_steps.get((0, 0), []):
        event(t, which)

    act_t = down_buf.at[:, pl.ds(0, total)]
    rows_t = down_buf.at[pl.ds(0, piece), pl.ds(total, total)]
    send_down = w_buf.at[pl.ds(4 * piece, down_rows), pl.ds(0, width)]

    def send_gate(r):
        return w_buf.at[pl.ds(pl.multiple_of(r * piece, piece), piece), :]

    for j in range(blocks):
        act_t[span(j, 1), :] = act_buf[:, span(j, 1)].T

    def down_grad(which, j):
        rows = pl.ds(pl.multiple_of(which * down_rows, down_rows), down_rows)
        return dot_nn(act_t[rows, :], rows_buf[1, :, span(2 * j, 2)])

    def after(steps, number, r):
        turns = {(turn, 0): events for (stage, turn), events in steps.items() if stage == number}
        take(turns, r, 0)

    after(grad_steps, 1, 0)
    for j in range(tiles):
        send_down[:, span(2 * j, 2)] = down_grad(1 - core, j).astype(jnp.bfloat16)
    down_send = remote(
        send_down, other_down, grad_sems.at[0, 4], grad_sems.at[1, 4], partner
    )
    down_send.start()

    def turned_rows(r, which):
        step_y = r // 2
        step_x = r % 2
        chip = (at_y + step_y - 2 * at_y * step_y) * 2 + (at_x + step_x - 2 * at_x * step_x)
        start = pl.multiple_of((chip * 2 + which) * piece, piece)
        rows_t[...] = rows_buf[0, :, pl.ds(start, piece)].T

    def gate_send(r):
        return remote(
            send_gate(r), other_gate.at[r], grad_sems.at[0, r], grad_sems.at[1, r], partner
        )

    def gate_for_partner(r, carry):
        after(grad_steps, 2, r)
        turned_rows(r, 1 - core)
        target = send_gate(r)
        for j in range(blocks):
            cols = span(2 * j, 2)
            target[:, cols] = dot_nn(rows_t[...], gate_buf[:, cols]).astype(jnp.bfloat16)
        gate_send(r).start()
        return carry

    lax.fori_loop(0, 4, gate_for_partner, 0)
    after(grad_steps, 3, 0)
    down_send.wait_recv()

    for j in range(tiles):
        cols = span(2 * j, 2)
        value = down_grad(core, j) + other_down[:, cols].astype(jnp.float32)
        other_down[:, cols] = value.astype(jnp.bfloat16)
    down_out = pltpu.make_async_copy(other_down, grad_down, grad_sems.at[2, 0])
    down_out.start()

    def gate_out(r):
        return pltpu.make_async_copy(other_gate.at[r], grad_gate_up.at[r], grad_sems.at[2, 2 + r])

    def gate_for_self(r, carry):
        after(grad_steps, 4, r)
        gate_send(r).wait_recv()
        turned_rows(r, core)
        target = other_gate.at[r]
        for j in range(blocks):
            cols = span(2 * j, 2)
            value = dot_nn(rows_t[...], gate_buf[:, cols])
            target[:, cols] = (value + target[:, cols].astype(jnp.float32)).astype(jnp.bfloat16)
        gate_out(r).start()
        return carry

    lax.fori_loop(0, 4, gate_for_self, 0)
    after(grad_steps, 5, 0)

    down_out.wait()
    for r in range(4):
        gate_out(r).wait()
        gate_send(r).wait_send()
        for copy in w_share(r, core):
            copy.wait_send()
    down_share().wait_send()
    down_send.wait_send()
    for t in range(2):
        keep_copy(t).wait()
        for k in range(group):
            x_copy(t, k).wait_send()
            y_copy(t, k).wait_send()
            a_copy(t, k).wait_send()
            b_copy(t, k).wait_send()
            half_x_copy(t, k).wait_send()
            half_y_copy(t, k).wait_send()
            full_x_copy(t, k).wait_send()
            full_y_copy(t, k).wait_send()
            if k > 0:
                z_copy(t, k).wait_send()
                back_copy(t, k).wait_send()
                back_copy(t, k).wait_recv()


def experts_call(sent, d_back, w_gate_up, w_got, w_down):
    group, cap, width = sent.shape
    piece, hidden2 = w_got.shape[1:]
    hidden = hidden2 // 2
    down_rows = w_down.shape[1]
    chunk = 4 * cap
    total = group * chunk
    low = jnp.bfloat16
    anywhere = pl.BlockSpec(memory_space=pl.ANY)
    flops = 2 * total * width * hidden * 9
    moved = 2 * (4 * piece * hidden2 * 2 + down_rows * width * 3)
    return pl.pallas_call(
        functools.partial(experts_kernel, group),
        out_shape=(
            jax.ShapeDtypeStruct((group, cap, width), low),
            jax.ShapeDtypeStruct((group, cap, width), low),
            jax.ShapeDtypeStruct((4, piece, hidden2), low),
            jax.ShapeDtypeStruct((down_rows, width), low),
        ),
        in_specs=[anywhere] * 5,
        out_specs=(anywhere,) * 4,
        scratch_shapes=[
            pltpu.VMEM((width, hidden2), low),
            pltpu.VMEM((hidden, width), low),
            pltpu.VMEM((2, total, width), low),
            pltpu.VMEM((total, hidden2), low),
            pltpu.VMEM((total, hidden), low),
            pltpu.VMEM((2, total, width), low),
            pltpu.VMEM((2, group, cap // 2, width), low),
            pltpu.VMEM((2, group, cap // 2, width), low),
            pltpu.VMEM((2, group, cap, width), low),
            pltpu.VMEM((2, group, cap, width), low),
            pltpu.VMEM((4, piece, hidden2), low),
            pltpu.VMEM((down_rows, width), low),
            pltpu.SemaphoreType.DMA((2, 5, 2, group)),
            pltpu.SemaphoreType.DMA((2, 5, 2, group)),
            pltpu.SemaphoreType.DMA((2, 6)),
            pltpu.SemaphoreType.DMA((10,)),
            pltpu.SemaphoreType.DMA((3, 6)),
        ],
        compiler_params=pltpu.CompilerParams(
            collective_id=1, has_side_effects=True, vmem_limit_bytes=67043328
        ),
        cost_estimate=pl.CostEstimate(flops=flops, bytes_accessed=moved, transcendentals=0),
        name="experts",
    )(sent, d_back, w_gate_up, w_got, w_down)


def rotary_tables(length_total, head_size):
    position = jnp.arange(length_total, dtype=jnp.float32)
    frequency = THETA ** (-(jnp.arange(head_size // 2, dtype=jnp.float32) * 2.0 / head_size))
    angles = position[:, None] * frequency[None, :]
    return (jnp.cos(angles)[:, None, :], jnp.sin(angles)[:, None, :])


def rotate(values, cosine, sine):
    half_size = values.shape[-1] // 2
    first = values[..., :half_size]
    second = values[..., half_size:]
    return jnp.concatenate(
        [first * cosine - second * sine, second * cosine + first * sine], axis=-1
    )


def rotate_back(grad_rows, cosine, sine):
    half_size = grad_rows.shape[-1] // 2
    first = grad_rows[..., :half_size]
    second = grad_rows[..., half_size:]
    return jnp.concatenate(
        [first * cosine + second * sine, second * cosine - first * sine], axis=-1
    )


def slot_table(routes, order, valid, capacity):
    row_count = routes.shape[0]
    top_count = routes.shape[1]
    pair_rank = order[:, None] + row_count * jnp.arange(top_count, dtype=jnp.int32)[None, :]
    flat_rank = pair_rank.reshape(-1)
    flat_expert = routes.reshape(-1)
    flat_valid = jnp.broadcast_to(valid[:, None], routes.shape).reshape(-1)
    earlier = (
        (flat_rank[None, :] < flat_rank[:, None])
        & (flat_expert[None, :] == flat_expert[:, None])
        & flat_valid[None, :]
    )
    slot_index = jnp.sum(earlier.astype(jnp.int32), axis=1).reshape(row_count, top_count)
    kept_pair = valid[:, None] & (slot_index < capacity)
    target = routes * capacity + jnp.minimum(slot_index, capacity - 1)
    return (target, kept_pair)


def masked_scores(query, key_rows, allowed):
    scale = query.shape[-1] ** (-0.5)
    raw = jnp.einsum("qhd,khd->hqk", query, key_rows, preferred_element_type=jnp.float32) * scale
    return jnp.where(allowed[None], raw, NEGATIVE)


def contract_first(left, right):
    return lax.dot_general(
        left, right, (((0,), (0,)), ((), ())), preferred_element_type=jnp.float32
    )


def contract_last(left, right):
    return lax.dot_general(
        left, right, (((1,), (1,)), ((), ())), preferred_element_type=jnp.float32
    )


def normalize(rows):
    inverse = lax.rsqrt(jnp.mean(rows * rows, axis=-1, keepdims=True) + NORM_EPSILON)
    return rows * inverse, inverse


def exchange_experts(blocks):
    return lax.all_to_all(blocks, "expert", split_axis=0, concat_axis=0, tiled=True)


def line_order(place, step):
    upper = place // 2
    low = place * (1 - upper) + (3 - place) * upper
    first = 1 - (step + 1) // 2
    block = step + first * (1 - low) + (1 - first)
    return block * (1 - upper) + (3 - block) * upper


def rotated(grad, cosine, sine):
    return grad * cosine + pltpu.roll(grad, grad.shape[1] // 2, 1) * sine


def attention_back_kernel(
    heads,
    length,
    returned,
    d_sent,
    resid,
    inverse_two,
    gates,
    hits,
    cotangent,
    pair_rows,
    small_full,
    tokens_all,
    inverse_all,
    whole,
    w_out,
    w_qkv,
    query,
    key_rows,
    value,
    attended,
    log_total,
    cosine,
    sine,
    gate_grads,
    output,
    grad_tokens,
    grad_weights,
    small_out,
    gate_got,
    returned_buf,
    d_sent_buf,
    resid_buf,
    inverse_two_buf,
    gates_buf,
    hits_buf,
    cotangent_buf,
    rows_buf,
    small_full_buf,
    da_buf,
    tokens_buf,
    inverse_buf,
    whole_buf,
    w_out_buf,
    w_qkv_buf,
    query_buf,
    key_buf,
    value_buf,
    attended_buf,
    log_buf,
    cosine_buf,
    sine_buf,
    d_key_acc,
    d_value_acc,
    d_proj,
    normed_part,
    from_left,
    from_right,
    send_pair,
    recv_pair,
    own_part,
    half_x,
    half_y,
    full_x,
    full_y,
    small_buf,
    small_recv,
    small_z,
    keep_buf,
    sum_buf,
    load_sems,
    line_sems,
    sum_sems,
    pair_sems,
    ring_sems,
    small_sems,
    gate_sems,
):
    tok, width = cotangent.shape
    seq_len = tokens_all.shape[0]
    group = seq_len // tok
    local_width = w_out.shape[0]
    head_size = local_width // heads
    piece = own_part.shape[1]
    half = piece // 2
    scale = head_size**-0.5

    index = lax.axis_index("dp")
    place = lax.axis_index("expert")
    core = index % 2
    at_x = (index // 2) % 2
    at_y = index // 4
    partner = {"dp": at_y * 4 + at_x * 2 + (1 - core)}
    along_x = {"dp": at_y * 4 + (1 - at_x) * 2 + core}
    along_y = {"dp": (1 - at_y) * 4 + at_x * 2 + core}
    over = {"dp": (1 - at_y) * 4 + (1 - at_x) * 2 + core}
    parts = width // piece

    def chip(r):
        step_y = r // 2
        step_x = r % 2
        return (at_y + step_y - 2 * at_y * step_y) * 2 + (at_x + step_x - 2 * at_x * step_x)

    def ring_peer(k):
        return {"dp": (index + k) % parts}

    def line_peer(k):
        return {"expert": (place + k) % group}

    right = {"expert": (place + 1) % group}
    left = {"expert": (place + group - 1) % group}

    loads = [
        pltpu.make_async_copy(source, target, load_sems.at[number])
        for number, (source, target) in enumerate(
            [
                (returned, returned_buf),
                (hits, hits_buf),
                (cotangent, cotangent_buf),
                (resid, resid_buf),
                (inverse_two, inverse_two_buf),
                (gates, gates_buf),
                (pair_rows, rows_buf),
                (small_full, small_full_buf),
                (d_sent, d_sent_buf),
                (w_out, w_out_buf),
                (query, query_buf),
                (key_rows, key_buf),
                (value, value_buf),
                (log_total, log_buf),
                (cosine, cosine_buf),
                (sine, sine_buf),
                (w_qkv, w_qkv_buf),
                (tokens_all, tokens_buf),
                (inverse_all, inverse_buf),
                (whole, whole_buf),
                (attended, attended_buf),
                (gate_grads.at[0], keep_buf),
            ]
        )
    ]
    first = 9
    early = first + 7
    for load in loads[:early]:
        load.start()

    greet([ring_peer(k) for k in range(1, parts)] + [line_peer(k) for k in range(1, group)])

    def rows_of(block):
        return pl.ds(pl.multiple_of(block * tok, tok), tok)

    def pass_right(block):
        spot = da_buf.at[rows_of(block)]
        return remote(spot, spot, line_sems.at[0, block], line_sems.at[2, block], right)

    def pass_left(block):
        spot = da_buf.at[rows_of(block)]
        return remote(spot, spot, line_sems.at[1, block], line_sems.at[2, block], left)

    def gate_copy(r, peer):
        return remote(
            gate_grads.at[r], gate_got.at[r], gate_sems.at[0, r], gate_sems.at[1, r], peer
        )

    peers = (None, along_x, along_y, over)
    for r in (3, 1, 2):
        gate_copy(r, peers[r]).start()
    for load in loads[early:]:
        load.start()
    for load in loads[:first]:
        load.wait()

    at = place * tok + lax.broadcasted_iota(jnp.int32, (tok, 1), 0)
    live = jnp.where(at < length[0], 1.0, 0.0)
    d_out = live * cotangent_buf[...].astype(jnp.float32)
    total = resid_buf[...]
    hhat = total * inverse_two_buf[...]
    gate = [gates_buf[:, number : number + 1] for number in range(2)]
    d_gate = []
    for number in range(2):
        picked = dot_nn(hits_buf[number].T, returned_buf[...])
        d_gate.append(jnp.sum(d_out * picked, axis=-1, keepdims=True))
        total = total + gate[number] * picked
    output[...] = (live * total).astype(jnp.bfloat16)
    mixed = gate[0] * d_gate[0] + gate[1] * d_gate[1]
    d_chosen = [gate[number] * (d_gate[number] - mixed) for number in range(2)]
    d_hidden = dot_nn((hits_buf[0] + hits_buf[1]).T, d_sent_buf[...])
    gain_two = small_full_buf[1:2, :]
    hidden_in = (hhat * gain_two).astype(jnp.bfloat16).astype(jnp.float32)
    small_buf[...] = jnp.zeros_like(small_buf)
    square = (tok, tok)
    same = lax.broadcasted_iota(jnp.int32, square, 0) == lax.broadcasted_iota(jnp.int32, square, 1)
    named = []
    for number in range(2):
        row = rows_buf[number : number + 1, :].astype(jnp.float32)
        kept = jnp.where(same, jnp.broadcast_to(row, square), 0.0)
        named.append(jnp.sum(kept, axis=1, keepdims=True).astype(jnp.int32))
    for expert in range(group):
        d_logit = sum(
            jnp.where(named[number] == expert, d_chosen[number], 0.0)
            for number in range(2)
        )
        row = slice(2 + expert, 3 + expert)
        d_hidden = d_hidden + d_logit * small_full_buf[row, :]
        small_buf[row, :] = jnp.sum(d_logit * hidden_in, axis=0, keepdims=True)
    small_buf[1:2, :] = jnp.sum(d_hidden * hhat, axis=0, keepdims=True)
    scaled = d_hidden * gain_two
    shared = jnp.mean(scaled * hhat, axis=-1, keepdims=True)
    d_resid = d_out + inverse_two_buf[...] * (scaled - hhat * shared)
    resid_buf[...] = d_resid
    da_buf[rows_of(place), :] = d_resid.astype(jnp.bfloat16)

    @pl.when(place < group - 1)
    def _():
        pass_right(place).start()

    @pl.when(place > 0)
    def _():
        pass_left(place).start()

    d_key_acc[...] = jnp.zeros_like(d_key_acc)
    d_value_acc[...] = jnp.zeros_like(d_value_acc)

    def attend_back(block):
        rows = rows_of(block)
        d_heads = dot_nt(da_buf[rows, :], w_out_buf[...]).astype(jnp.bfloat16)
        shape = (tok, seq_len)
        at_query = block * tok + lax.broadcasted_iota(jnp.int32, shape, 0)
        at_key = lax.broadcasted_iota(jnp.int32, shape, 1)
        allowed = (at_key <= at_query) & (at_key < length[0])
        for head in range(heads):
            cols = slice(head * head_size, (head + 1) * head_size)
            one_query = query_buf[rows, cols]
            one_key = key_buf[:, cols]
            d_head = d_heads[:, cols]
            scores = jnp.where(allowed, dot_nt(one_query, one_key) * scale, NEGATIVE)
            probs = jnp.exp(scores - log_buf[rows, head : head + 1])
            d_probs = dot_nt(d_head, value_buf[:, cols])
            delta = jnp.sum(probs * d_probs, axis=-1, keepdims=True)
            d_scores = (probs * (d_probs - delta)).astype(jnp.bfloat16)
            d_query = dot_nn(d_scores, one_key) * scale
            d_key_acc[:, cols] += dot_nn(d_scores.T, one_query) * scale
            d_value_acc[:, cols] += dot_nn(probs.astype(jnp.bfloat16).T, d_head)
            d_proj[rows, cols] = rotated(d_query, cosine_buf[rows, :], -sine_buf[rows, :]).astype(
                jnp.bfloat16
            )

    for load in loads[first:early]:
        load.wait()
    attend_back(place)

    def arrive(step, carry):
        block = line_order(place, step)
        pass_right(block).wait_recv()

        @pl.when((block < place) & (place < group - 1))
        def _():
            pass_right(block).start()

        @pl.when((block > place) & (place > 0))
        def _():
            pass_left(block).start()

        attend_back(block)
        return carry

    lax.fori_loop(0, group - 1, arrive, 0)
    for load in loads[early:]:
        load.wait()
    keep = pltpu.make_async_copy(keep_buf, gate_got.at[0], load_sems.at[22])
    keep.start()

    for head in range(heads):
        cols = slice(head * head_size, (head + 1) * head_size)
        key_cols = slice(local_width + head * head_size, local_width + (head + 1) * head_size)
        d_proj[:, key_cols] = rotated(d_key_acc[:, cols], cosine_buf[...], -sine_buf[...]).astype(
            jnp.bfloat16
        )
    d_proj[:, 2 * local_width :] = d_value_acc[...].astype(jnp.bfloat16)

    def normed_tile(j, carry):
        cols = pl.ds(pl.multiple_of(j * piece, piece), piece)
        d_normed = jnp.zeros((seq_len, piece), jnp.float32)
        for c in range(3):
            d_normed += dot_nt(
                d_proj[:, c * local_width : (c + 1) * local_width], w_qkv_buf[c, cols, :]
            )
        hat = tokens_buf[:, cols].astype(jnp.float32) * inverse_buf[...]
        small_buf[0:1, cols] = jnp.sum(d_normed * hat, axis=0, keepdims=True)
        normed_part[:, cols] = d_normed.astype(jnp.bfloat16)
        return carry

    lax.fori_loop(0, parts, normed_tile, 0)

    def go_right(block):
        return remote(
            normed_part.at[pl.ds(block * tok, tok)],
            from_left.at[block],
            sum_sems.at[0, block],
            sum_sems.at[1, block],
            right,
        )

    def go_left(block):
        return remote(
            normed_part.at[pl.ds(block * tok, tok)],
            from_right.at[block],
            sum_sems.at[0, block],
            sum_sems.at[2, block],
            left,
        )

    def add_into(target, other):
        value = target[...].astype(jnp.float32) + other[...].astype(jnp.float32)
        target[...] = value.astype(jnp.bfloat16)

    def on_right(block):
        go_right(block).wait_recv()
        add_into(normed_part.at[pl.ds(block * tok, tok)], from_left.at[block])
        go_right(block).start()

    def on_left(block):
        go_left(block).wait_recv()
        add_into(normed_part.at[pl.ds(block * tok, tok)], from_right.at[block])
        go_left(block).start()

    @pl.when(place == 0)
    def _():
        for block in (3, 2, 1):
            go_right(block).start()

    @pl.when(place == 3)
    def _():
        for block in (0, 1, 2):
            go_left(block).start()

    def small_copy(k):
        to = (index + k) % parts
        cols = pl.ds(pl.multiple_of(to * piece, piece), piece)
        return remote(
            small_buf.at[:, cols],
            small_recv.at[k],
            small_sems.at[0, k],
            small_sems.at[1, k],
            ring_peer(k),
        )

    for k in range(1, parts):
        small_copy(k).start()

    def weight_grad(which, r):
        cols = pl.ds(pl.multiple_of((chip(r) * 2 + which) * piece, piece), piece)
        left_side = whole_buf[:, cols].T
        first = dot_nn(left_side, d_proj[...])
        second = dot_nn(da_buf[:, cols].T, attended_buf[...])
        return jnp.concatenate([first, second], axis=1)

    def pair_copy(r):
        return remote(
            send_pair.at[r], recv_pair.at[r], pair_sems.at[0, r], pair_sems.at[1, r], partner
        )

    def for_partner(i, carry):
        r = 3 - i
        send_pair[r] = weight_grad(1 - core, r).astype(jnp.bfloat16)
        pair_copy(r).start()
        return carry

    lax.fori_loop(0, 4, for_partner, 0)

    @pl.when(place == 1)
    def _():
        on_right(3)

    @pl.when(place == 2)
    def _():
        on_left(0)

    def half_x_copy():
        return remote(
            own_part.at[3, pl.ds(0, half)], half_x, ring_sems.at[0, 0], ring_sems.at[1, 0], along_x
        )

    def half_y_copy():
        return remote(
            own_part.at[3, pl.ds(half, half)],
            half_y,
            ring_sems.at[0, 1],
            ring_sems.at[1, 1],
            along_y,
        )

    def full_x_copy():
        return remote(own_part.at[1], full_x, ring_sems.at[0, 2], ring_sems.at[1, 2], along_x)

    def full_y_copy():
        return remote(own_part.at[2], full_y, ring_sems.at[0, 3], ring_sems.at[1, 3], along_y)

    def for_self(i, carry):
        r = 3 - i
        pair_copy(r).wait_recv()
        own_part[r] = (weight_grad(core, r) + recv_pair[r].astype(jnp.float32)).astype(
            jnp.bfloat16
        )

        @pl.when(i == 0)
        def _():
            half_x_copy().start()
            half_y_copy().start()

        return carry

    lax.fori_loop(0, 4, for_self, 0)

    total = small_buf[:, pl.ds(pl.multiple_of(index * piece, piece), piece)]
    for k in range(1, parts):
        small_copy(k).wait_recv()
        total = total + small_recv[k]
    small_z[0] = total

    @pl.when(place == 1)
    def _():
        on_right(2)

    @pl.when(place == 2)
    def _():
        on_left(1)

    def small_line_copy(k):
        return remote(
            small_z.at[0],
            small_z.at[k],
            small_sems.at[0, parts + k],
            small_sems.at[1, parts + k],
            line_peer(k),
        )

    for k in range(1, group):
        small_line_copy(k).start()

    half_x_copy().wait_recv()
    add_into(own_part.at[2, pl.ds(0, half)], half_x)
    full_y_copy().start()
    half_y_copy().wait_recv()
    add_into(own_part.at[1, pl.ds(half, half)], half_y)
    full_x_copy().start()

    @pl.when(place == 1)
    def _():
        on_left(0)

    @pl.when(place == 2)
    def _():
        on_right(3)

    total = small_z[0]
    for k in range(1, group):
        small_line_copy(k).wait_recv()
        total = total + small_z[k]
    small_out[...] = total

    sum_buf[...] = normed_part[rows_of(place), :].astype(jnp.float32)

    @pl.when(place > 0)
    def _():
        go_right(place).wait_recv()
        sum_buf[...] += from_left[place].astype(jnp.float32)

    @pl.when(place < group - 1)
    def _():
        go_left(place).wait_recv()
        sum_buf[...] += from_right[place].astype(jnp.float32)

    inverse_one = inverse_buf[rows_of(place), :]
    hat = tokens_buf[rows_of(place), :].astype(jnp.float32) * inverse_one
    scaled = sum_buf[...] * small_full_buf[0:1, :]
    shared = jnp.mean(scaled * hat, axis=-1, keepdims=True)
    grad_tokens[...] = (resid_buf[...] + inverse_one * (scaled - hat * shared)).astype(
        jnp.bfloat16
    )

    full_x_copy().wait_recv()
    full_y_copy().wait_recv()
    grad_weights[...] = (
        own_part[0].astype(jnp.float32)
        + full_x[...].astype(jnp.float32)
        + full_y[...].astype(jnp.float32)
    )

    for r in (1, 2, 3):
        gate_copy(r, peers[r]).wait()
    keep.wait()
    half_x_copy().wait_send()
    half_y_copy().wait_send()
    full_x_copy().wait_send()
    full_y_copy().wait_send()
    for r in range(4):
        pair_copy(r).wait_send()
    for k in range(1, parts):
        small_copy(k).wait_send()
    for k in range(1, group):
        small_line_copy(k).wait_send()
    for block in range(group):

        @pl.when(block > place)
        def _():
            go_right(block).wait_send()

        @pl.when(block < place)
        def _():
            go_left(block).wait_send()

        @pl.when((block <= place) & (place < group - 1))
        def _():
            pass_right(block).wait_send()

        @pl.when((block >= place) & (place > 0))
        def _():
            pass_left(block).wait_send()


def attention_back_call(
    lengths,
    returned,
    d_sent,
    resid,
    inverse_two,
    gates,
    hits,
    cotangent,
    pair_rows,
    small_full,
    tokens_all,
    inverse_all,
    whole,
    w_out,
    w_qkv,
    query,
    key_rows,
    value,
    attended,
    log_total,
    cosine,
    sine,
    gate_grads,
):
    tok, width = cotangent.shape
    seq_len = tokens_all.shape[0]
    group = seq_len // tok
    local_width = w_out.shape[0]
    heads = log_total.shape[1]
    piece = gate_grads.shape[1]
    half = piece // 2
    parts = width // piece
    small_rows = small_full.shape[0]
    low, full = jnp.bfloat16, jnp.float32
    anywhere = pl.BlockSpec(memory_space=pl.ANY)
    inside = pl.BlockSpec(memory_space=pltpu.VMEM)

    def like(array):
        return pltpu.VMEM(array.shape, array.dtype)

    flops = 2 * seq_len * width * local_width * 8 + 10 * seq_len * seq_len * local_width
    return pl.pallas_call(
        functools.partial(attention_back_kernel, heads),
        out_shape=(
            jax.ShapeDtypeStruct((tok, width), low),
            jax.ShapeDtypeStruct((tok, width), low),
            jax.ShapeDtypeStruct((piece, 4 * local_width), full),
            jax.ShapeDtypeStruct((small_rows, piece), full),
            jax.ShapeDtypeStruct(gate_grads.shape, low),
        ),
        in_specs=[pl.BlockSpec(memory_space=pltpu.SMEM)] + [anywhere] * 22,
        out_specs=(inside, inside, inside, inside, anywhere),
        scratch_shapes=[
            like(returned),
            like(d_sent),
            like(resid),
            like(inverse_two),
            like(gates),
            like(hits),
            like(cotangent),
            like(pair_rows),
            like(small_full),
            pltpu.VMEM((seq_len, width), low),
            like(tokens_all),
            like(inverse_all),
            like(whole),
            like(w_out),
            like(w_qkv),
            like(query),
            like(key_rows),
            like(value),
            like(attended),
            like(log_total),
            like(cosine),
            like(sine),
            pltpu.VMEM((seq_len, local_width), full),
            pltpu.VMEM((seq_len, local_width), full),
            pltpu.VMEM((seq_len, 3 * local_width), low),
            pltpu.VMEM((seq_len, width), low),
            pltpu.VMEM((group, tok, width), low),
            pltpu.VMEM((group, tok, width), low),
            pltpu.VMEM((4, piece, 4 * local_width), low),
            pltpu.VMEM((4, piece, 4 * local_width), low),
            pltpu.VMEM((4, piece, 4 * local_width), low),
            pltpu.VMEM((half, 4 * local_width), low),
            pltpu.VMEM((half, 4 * local_width), low),
            pltpu.VMEM((piece, 4 * local_width), low),
            pltpu.VMEM((piece, 4 * local_width), low),
            like(small_full),
            pltpu.VMEM((parts, small_rows, piece), full),
            pltpu.VMEM((group, small_rows, piece), full),
            pltpu.VMEM(gate_grads.shape[1:], low),
            like(resid),
            pltpu.SemaphoreType.DMA((23,)),
            pltpu.SemaphoreType.DMA((3, group)),
            pltpu.SemaphoreType.DMA((3, group)),
            pltpu.SemaphoreType.DMA((2, 4)),
            pltpu.SemaphoreType.DMA((2, 4)),
            pltpu.SemaphoreType.DMA((2, parts + group)),
            pltpu.SemaphoreType.DMA((2, 4)),
        ],
        compiler_params=pltpu.CompilerParams(
            collective_id=2, has_side_effects=True, vmem_limit_bytes=67043328
        ),
        cost_estimate=pl.CostEstimate(flops=flops, bytes_accessed=40000000, transcendentals=0),
        name="attention_back",
    )(
        lengths,
        returned,
        d_sent,
        resid,
        inverse_two,
        gates,
        hits,
        cotangent,
        pair_rows,
        small_full,
        tokens_all,
        inverse_all,
        whole,
        w_out,
        w_qkv,
        query,
        key_rows,
        value,
        attended,
        log_total,
        cosine,
        sine,
        gate_grads,
    )


def finish_kernel(
    gate_got,
    grad_down_low,
    grad_tokens_low,
    output_low,
    grad_weights,
    grad_gate_up,
    grad_down,
    grad_tokens,
    output,
    grad_qkv,
    grad_out,
    got_buf,
    wide_buf,
    low_buf,
    down_buf,
    tokens_buf,
    output_buf,
    weights_buf,
    out_buf,
    load_sems,
    store_sems,
):
    chips = gate_got.shape[0]
    size = gate_got.shape[2] // 2
    local_width = grad_qkv.shape[2]
    index = lax.axis_index("dp")
    at_x = (index // 2) % 2
    at_y = index // 4

    def load(number, source, target):
        return pltpu.make_async_copy(source, target, load_sems.at[number])

    loads = [load(r, gate_got.at[r], got_buf.at[r]) for r in range(chips)] + [
        load(4, grad_down_low, low_buf),
        load(5, grad_weights, weights_buf),
        load(6, grad_tokens_low, tokens_buf),
        load(7, output_low, output_buf),
    ]
    for copy in loads:
        copy.start()
    stores = []

    def store(source, target):
        copy = pltpu.make_async_copy(source, target, store_sems.at[len(stores)])
        copy.start()
        stores.append(copy)

    for r in range(chips):
        loads[r].wait()
        step_y = r // 2
        step_x = r % 2
        chip = (at_y + step_y - 2 * at_y * step_y) * 2 + (at_x + step_x - 2 * at_x * step_x)
        for part in range(2):
            wide_buf[2 * r + part] = got_buf[r, :, part * size : (part + 1) * size].astype(
                jnp.float32
            )
            lanes = pl.ds(pl.multiple_of((part * chips + chip) * size, LANES), size)
            store(wide_buf.at[2 * r + part], grad_gate_up.at[0, :, lanes])
    loads[4].wait()
    down_buf[...] = low_buf[...].astype(jnp.float32)
    store(down_buf, grad_down.at[0])
    loads[5].wait()
    out_buf[...] = weights_buf[:, 3 * local_width :].T
    for c in range(3):
        store(weights_buf.at[:, pl.ds(c * local_width, local_width)], grad_qkv.at[c])
    store(out_buf, grad_out)
    loads[6].wait()
    store(tokens_buf, grad_tokens)
    loads[7].wait()
    store(output_buf, output)
    for copy in stores:
        copy.wait()


def finish_call(gate_got, grad_down, grad_tokens, output, grad_weights):
    chips, rows, hidden2 = gate_got.shape
    local_width = grad_weights.shape[1] // 4
    full = jnp.float32
    anywhere = pl.BlockSpec(memory_space=pl.ANY)
    out_t = (local_width, rows)

    def like(array, kind=None):
        return pltpu.VMEM(array.shape, kind or array.dtype)

    return pl.pallas_call(
        finish_kernel,
        out_shape=(
            jax.ShapeDtypeStruct((1, rows, chips * hidden2), full),
            jax.ShapeDtypeStruct((1,) + grad_down.shape, full),
            jax.ShapeDtypeStruct(grad_tokens.shape, grad_tokens.dtype),
            jax.ShapeDtypeStruct(output.shape, output.dtype),
            jax.ShapeDtypeStruct((3, rows, local_width), full),
            jax.ShapeDtypeStruct(out_t, full),
        ),
        in_specs=[anywhere] * 5,
        out_specs=(anywhere,) * 6,
        scratch_shapes=[
            like(gate_got),
            pltpu.VMEM((2 * chips, rows, hidden2 // 2), full),
            like(grad_down),
            like(grad_down, full),
            like(grad_tokens),
            like(output),
            like(grad_weights),
            pltpu.VMEM(out_t, full),
            pltpu.SemaphoreType.DMA((8,)),
            pltpu.SemaphoreType.DMA((15,)),
        ],
        compiler_params=pltpu.CompilerParams(vmem_limit_bytes=67043328),
        name="finish",
    )(gate_got, grad_down, grad_tokens, output, grad_weights)


def rotary_constants(length_total, head_size):
    low = 32
    steps = np.arange(head_size // 2, dtype=np.float32) * np.float32(2.0) / np.float32(head_size)
    frequency = np.power(np.float32(THETA), -steps).astype(np.float32).astype(np.float64)
    position = np.concatenate([np.arange(0, length_total, low), np.arange(low)])
    angles = position[:, None] * np.concatenate([frequency, frequency])[None, :]
    return np.stack([np.cos(angles), np.sin(angles)]).astype(np.float32)


def attention_kernel(
    heads,
    length,
    tokens,
    w_qkv,
    w_out,
    small,
    w_gate_up,
    pair_rows,
    angles,
    cotangent,
    tokens_all,
    whole,
    qkv_full,
    out_full,
    w_got,
    inverse_all,
    query,
    key_rows,
    value,
    attended,
    log_total,
    small_full,
    cosine_buf,
    sine_buf,
    resid,
    inverse_two,
    gates,
    hits,
    sent,
    d_back,
    tokens_buf,
    whole_buf,
    w_qkv_buf,
    w_out_buf,
    part_buf,
    from_left,
    from_right,
    rows_buf,
    angles_buf,
    cotangent_buf,
    load_sems,
    line_sems,
    sum_sems,
    gather_sems,
    small_sems,
    slice_sems,
):
    tok, width = tokens.shape
    seq_len = tokens_buf.shape[0]
    group = seq_len // tok
    local_width = w_out.shape[0]
    head_size = local_width // heads
    piece = w_qkv.shape[1]
    parts = width // piece
    ff = w_gate_up.shape[2] // 2
    hidden = ff // 4
    slots = hits.shape[1]
    cap = slots // group
    scale = head_size**-0.5

    index = lax.axis_index("dp")
    place = lax.axis_index("expert")
    core = index % 2
    at_x = (index // 2) % 2
    at_y = index // 4
    other = at_y * 4 + at_x * 2 + (1 - core)
    by_x = at_y * 4 + (1 - at_x) * 2 + core
    by_y = (1 - at_y) * 4 + at_x * 2 + core
    by_both = (1 - at_y) * 4 + (1 - at_x) * 2 + core
    partner = {"dp": other}
    along_x = {"dp": by_x}
    along_y = {"dp": by_y}
    over = {"dp": by_both}
    right = {"expert": (place + 1) % group}
    left = {"expert": (place + group - 1) % group}

    def ring_peer(k):
        return {"dp": (index + k) % parts}

    def rows_of(block):
        return pl.ds(pl.multiple_of(block * tok, tok), tok)

    def piece_of(number):
        return pl.ds(pl.multiple_of(number * piece, piece), piece)

    def qkv_spot(number):
        return w_qkv_buf.at[:, piece_of(number), :]

    def qkv_half(number, which):
        start = pl.multiple_of(number * piece + which * (piece // 2), piece // 2)
        return w_qkv_buf.at[:, pl.ds(start, piece // 2), :]

    def out_spot(number):
        return w_out_buf.at[:, piece_of(number)]

    def out_half(number, which):
        rows = pl.ds(which * (local_width // 2), local_width // 2)
        return w_out_buf.at[rows, piece_of(number)]

    class Gather:
        def __init__(self, number, source, spot, half_spot):
            self.number, self.source, self.spot, self.half_spot = number, source, spot, half_spot

        def copy(self, slot, source, target, peer):
            sems = gather_sems.at[self.number]
            return remote(source, target, sems.at[0, slot], sems.at[1, slot], peer)

        def own(self, slot, peer):
            return self.copy(slot, self.source, self.spot(index), peer)

        def keep(self):
            return pltpu.make_async_copy(
                self.source, self.spot(index), load_sems.at[8 + self.number]
            )

        def relay_x(self):
            spot = self.half_spot(by_y, 0)
            return self.copy(3, spot, spot, along_x)

        def relay_y(self):
            spot = self.half_spot(by_x, 1)
            return self.copy(4, spot, spot, along_y)

        def hand(self, slot):
            spot = (
                self.spot(by_x),
                self.spot(by_y),
                self.half_spot(by_both, 0),
                self.half_spot(by_both, 1),
            )[slot - 5]
            return self.copy(slot, spot, spot, partner)

        def begin(self):
            self.own(0, along_x).start()
            self.own(1, along_y).start()
            self.own(2, partner).start()
            self.keep().start()

        def relay(self):
            self.own(1, along_y).wait_recv()
            self.relay_x().start()
            self.own(0, along_x).wait_recv()
            self.relay_y().start()
            self.hand(5).start()
            self.hand(6).start()

        def finish(self):
            self.relay_x().wait_recv()
            self.hand(7).start()
            self.relay_y().wait_recv()
            self.hand(8).start()
            self.keep().wait()
            self.own(2, partner).wait_recv()
            for slot in (5, 6, 7, 8):
                self.hand(slot).wait_recv()

        def drain(self):
            for slot, peer in ((0, along_x), (1, along_y), (2, partner)):
                self.own(slot, peer).wait_send()
            self.relay_x().wait_send()
            self.relay_y().wait_send()
            for slot in (5, 6, 7, 8):
                self.hand(slot).wait_send()

    gather_qkv = Gather(0, w_qkv, qkv_spot, qkv_half)
    gather_out = Gather(1, w_out, out_spot, out_half)

    loads = [
        pltpu.make_async_copy(source, target, load_sems.at[number])
        for number, (source, target) in enumerate(
            [
                (tokens, tokens_buf.at[rows_of(place)]),
                (small, small_full.at[:, piece_of(index)]),
                (pair_rows, rows_buf),
                (angles, angles_buf),
                (cotangent, cotangent_buf),
            ]
        )
    ]
    for load in loads:
        load.start()

    greet([ring_peer(k) for k in range(1, parts)] + [right, left])

    def own_pass(side, peer):
        return remote(
            tokens,
            tokens_buf.at[rows_of(place)],
            line_sems.at[side, place],
            line_sems.at[2, place],
            peer,
        )

    def pass_on(block, side, peer):
        spot = tokens_buf.at[rows_of(block)]
        return remote(spot, spot, line_sems.at[side, block], line_sems.at[2, block], peer)

    @pl.when(place < group - 1)
    def _():
        own_pass(0, right).start()

    @pl.when(place > 0)
    def _():
        own_pass(1, left).start()

    def small_copy(k):
        return remote(
            small,
            small_full.at[:, piece_of(index)],
            small_sems.at[0, k],
            small_sems.at[1, k],
            ring_peer(k),
        )

    for k in range(1, parts):
        small_copy(k).start()
    gather_qkv.begin()

    for load in loads:
        load.wait()

    rows = rows_buf[...]
    first_row, second_row, order_row = rows[0:1], rows[1:2], rows[2:3]
    square = (tok, tok)
    same = lax.broadcasted_iota(jnp.int32, square, 0) == lax.broadcasted_iota(jnp.int32, square, 1)

    def as_column(row):
        kept = jnp.where(same, jnp.broadcast_to(row.astype(jnp.float32), square), 0.0)
        return jnp.sum(kept, axis=1, keepdims=True).astype(jnp.int32)

    first_col, second_col, order_col = [as_column(r) for r in (first_row, second_row, order_row)]
    start = place * tok
    live_col = (start + lax.broadcasted_iota(jnp.int32, (tok, 1), 0)) < length[0]
    live_row = (start + lax.broadcasted_iota(jnp.int32, (1, tok), 1)) < length[0]
    before = order_col < order_row

    def count(mask):
        return jnp.sum(jnp.where(mask & live_col, 1.0, 0.0), axis=0, keepdims=True)

    slot_first = count((first_col == first_row) & before)
    slot_second = count(first_col == second_row) + count((second_col == second_row) & before)
    slot_ids = lax.broadcasted_iota(jnp.int32, (slots, tok), 0)
    for number, (named, slot) in enumerate(((first_row, slot_first), (second_row, slot_second))):
        slot = slot.astype(jnp.int32)
        step = named - place
        step = jnp.where(step < 0, step + group, step)
        target = jnp.where(live_row & (slot < cap), step * cap + slot, -1)
        hits[number] = jnp.where(slot_ids == target, 1.0, 0.0).astype(jnp.bfloat16)

    low = 32
    highs = seq_len // low
    sign = jnp.where(
        lax.broadcasted_iota(jnp.int32, (low, head_size), 1) < head_size // 2, -1.0, 1.0
    )
    cosine_low, sine_low = angles_buf[0, highs:, :], angles_buf[1, highs:, :]
    for number in range(highs):
        at = slice(number * low, (number + 1) * low)
        cosine_high = angles_buf[0, number : number + 1, :]
        sine_high = angles_buf[1, number : number + 1, :]
        cosine_buf[at, :] = cosine_high * cosine_low - sine_high * sine_low
        sine_buf[at, :] = sign * (sine_high * cosine_low + cosine_high * sine_low)

    for k in range(1, parts):
        small_copy(k).wait_recv()

    def normalize_block(block):
        at = rows_of(block)
        value = tokens_buf[at, :].astype(jnp.float32)
        inverse = lax.rsqrt(jnp.mean(value * value, axis=-1, keepdims=True) + NORM_EPSILON)
        inverse_all[at, :] = inverse
        whole_buf[at, :] = (value * inverse * small_full[0:1, :]).astype(jnp.bfloat16)

    def arrive(step):
        block = line_order(place, step)
        pass_on(block, 0, right).wait_recv()

        @pl.when((block < place) & (place < group - 1))
        def _():
            pass_on(block, 0, right).start()

        @pl.when((block > place) & (place > 0))
        def _():
            pass_on(block, 1, left).start()

        normalize_block(block)

    def slice_copy(r, turn):
        number = (by_x // 2, by_y // 2, by_both // 2)[r - 1]
        part = turn
        lanes = pl.ds(pl.multiple_of(part * ff + number * hidden, LANES), hidden)
        return remote(
            w_gate_up.at[0, :, lanes],
            w_got.at[r - 1, :, pl.ds(part * hidden, hidden)],
            slice_sems.at[0, r - 1, turn],
            slice_sems.at[1, r - 1, turn],
            (along_x, along_y, over)[r - 1],
        )

    normalize_block(place)
    arrive(0)
    gather_qkv.relay()
    gather_out.begin()
    arrive(1)
    gather_qkv.finish()

    def project(first, size):
        at = pl.ds(pl.multiple_of(first, tok), size)
        source = whole_buf[at, :]

        def two_heads(number, carry):
            lanes = pl.ds(pl.multiple_of(number * 2 * head_size, 2 * head_size), 2 * head_size)
            for c, target in ((0, query), (1, key_rows)):
                plain = dot_nn(source, w_qkv_buf[c, :, lanes])
                turned = [
                    rotated(
                        plain[:, side * head_size : (side + 1) * head_size],
                        cosine_buf[at, :],
                        sine_buf[at, :],
                    )
                    for side in range(2)
                ]
                target[at, lanes] = jnp.concatenate(turned, axis=1).astype(jnp.bfloat16)
            value[at, lanes] = dot_nn(source, w_qkv_buf[2, :, lanes]).astype(jnp.bfloat16)
            return carry

        lax.fori_loop(0, heads // 2, two_heads, 0)

    upper = place // 2
    project(upper * tok, seq_len - tok)
    gather_out.relay()
    for turn in range(2):
        for r in (1, 2):
            slice_copy(r, turn).start()
    for turn in range(2):
        slice_copy(3, turn).start()
    gather_out.finish()
    arrive(2)
    project((1 - upper) * (seq_len - tok), tok)

    stores = [
        pltpu.make_async_copy(source, target, load_sems.at[10 + number])
        for number, (source, target) in enumerate(
            [
                (w_qkv_buf, qkv_full),
                (w_out_buf, out_full),
                (tokens_buf, tokens_all),
                (whole_buf, whole),
            ]
        )
    ]
    for store in stores:
        store.start()

    for number in range(group):
        at = slice(number * tok, (number + 1) * tok)
        extent = (number + 1) * tok
        shape = (tok, extent)
        at_query = number * tok + lax.broadcasted_iota(jnp.int32, shape, 0)
        at_key = lax.broadcasted_iota(jnp.int32, shape, 1)
        allowed = (at_key <= at_query) & (at_key < length[0])
        for head in range(heads):
            lanes = slice(head * head_size, (head + 1) * head_size)
            scores = dot_nt(query[at, lanes], key_rows[0:extent, lanes]) * scale
            scores = jnp.where(allowed, scores, NEGATIVE)
            top = jnp.max(scores, axis=-1, keepdims=True)
            exponent = jnp.exp(scores - top)
            row_total = jnp.sum(exponent, axis=-1, keepdims=True)
            probs = (exponent / row_total).astype(jnp.bfloat16)
            attended[at, lanes] = dot_nn(probs, value[0:extent, lanes]).astype(jnp.bfloat16)
            log_total[at, head : head + 1] = top + jnp.log(row_total)

    def out_tile(j, carry):
        lanes = piece_of(j)
        part_buf[:, lanes] = dot_nn(attended[...], w_out_buf[:, lanes]).astype(jnp.bfloat16)
        return carry

    lax.fori_loop(0, parts, out_tile, 0)

    def go_right(block):
        return remote(
            part_buf.at[rows_of(block)],
            from_left.at[block],
            sum_sems.at[0, block],
            sum_sems.at[1, block],
            right,
        )

    def go_left(block):
        return remote(
            part_buf.at[rows_of(block)],
            from_right.at[block],
            sum_sems.at[0, block],
            sum_sems.at[2, block],
            left,
        )

    def add_into(target, added):
        total = target[...].astype(jnp.float32) + added[...].astype(jnp.float32)
        target[...] = total.astype(jnp.bfloat16)

    def on_right(block):
        go_right(block).wait_recv()
        add_into(part_buf.at[rows_of(block)], from_left.at[block])
        go_right(block).start()

    def on_left(block):
        go_left(block).wait_recv()
        add_into(part_buf.at[rows_of(block)], from_right.at[block])
        go_left(block).start()

    @pl.when(place == 0)
    def _():
        for block in (3, 2, 1):
            go_right(block).start()

    @pl.when(place == 3)
    def _():
        for block in (0, 1, 2):
            go_left(block).start()

    @pl.when(place == 1)
    def _():
        on_right(3)
        on_right(2)
        on_left(0)

    @pl.when(place == 2)
    def _():
        on_left(0)
        on_left(1)
        on_right(3)

    resid[...] = tokens_buf[rows_of(place), :].astype(jnp.float32) + part_buf[
        rows_of(place), :
    ].astype(jnp.float32)

    @pl.when(place > 0)
    def _():
        go_right(place).wait_recv()
        resid[...] += from_left[place].astype(jnp.float32)

    @pl.when(place < group - 1)
    def _():
        go_left(place).wait_recv()
        resid[...] += from_right[place].astype(jnp.float32)

    total = resid[...]
    inverse = lax.rsqrt(jnp.mean(total * total, axis=-1, keepdims=True) + NORM_EPSILON)
    inverse_two[...] = inverse
    hidden_in = (total * inverse * small_full[1:2, :]).astype(jnp.bfloat16)
    logits = dot_nt(hidden_in, small_full[...].astype(jnp.bfloat16))
    lane = lax.broadcasted_iota(jnp.int32, logits.shape, 1)
    chosen = [
        jnp.sum(jnp.where(lane == named + 2, logits, 0.0), axis=1, keepdims=True)
        for named in (first_col, second_col)
    ]
    top = jnp.maximum(chosen[0], chosen[1])
    raised = [jnp.exp(entry - top) for entry in chosen]
    both = raised[0] + raised[1]
    gate = [entry / both for entry in raised]
    for number in range(2):
        gates[:, number : number + 1] = gate[number]
    sent[...] = dot_nn(hits[0] + hits[1], hidden_in).astype(jnp.bfloat16)
    d_out = jnp.where(live_col, 1.0, 0.0) * cotangent_buf[...].astype(jnp.float32)
    d_back[...] = (
        dot_nn(hits[0], (gate[0] * d_out).astype(jnp.bfloat16))
        + dot_nn(hits[1], (gate[1] * d_out).astype(jnp.bfloat16))
    ).astype(jnp.bfloat16)

    for store in stores:
        store.wait()
    gather_qkv.drain()
    gather_out.drain()
    for k in range(1, parts):
        small_copy(k).wait_send()
    for block in range(group):

        @pl.when(block > place)
        def _():
            go_right(block).wait_send()

        @pl.when(block < place)
        def _():
            go_left(block).wait_send()

        @pl.when((block <= place) & (place < group - 1))
        def _():
            pass_on(block, 0, right).wait_send()

        @pl.when((block >= place) & (place > 0))
        def _():
            pass_on(block, 1, left).wait_send()

    for turn in range(2):
        for r in (1, 2, 3):
            slice_copy(r, turn).wait()


def attention_call(
    lengths, tokens, w_qkv, w_out, small, w_gate_up, pair_rows, angles, cotangent, group
):
    tok, width = tokens.shape
    seq_len = tok * group
    local_width = w_qkv.shape[2]
    heads = local_width // HEAD_DIM
    slots = tok * 2
    piece = w_qkv.shape[1]
    low, full = jnp.bfloat16, jnp.float32
    anywhere = pl.BlockSpec(memory_space=pl.ANY)
    inside = pl.BlockSpec(memory_space=pltpu.VMEM)
    narrow = jax.ShapeDtypeStruct((seq_len, local_width), low)
    flops = 2 * seq_len * width * local_width * 4 + 4 * seq_len * seq_len * local_width
    return pl.pallas_call(
        functools.partial(attention_kernel, heads),
        out_shape=(
            jax.ShapeDtypeStruct((seq_len, width), low),
            jax.ShapeDtypeStruct((seq_len, width), low),
            jax.ShapeDtypeStruct((3, width, local_width), low),
            jax.ShapeDtypeStruct((local_width, width), low),
            jax.ShapeDtypeStruct((3, piece, w_gate_up.shape[2] // 4), low),
            jax.ShapeDtypeStruct((seq_len, 1), full),
            narrow,
            narrow,
            narrow,
            narrow,
            jax.ShapeDtypeStruct((seq_len, heads), full),
            jax.ShapeDtypeStruct((small.shape[0], width), full),
            jax.ShapeDtypeStruct((seq_len, HEAD_DIM), full),
            jax.ShapeDtypeStruct((seq_len, HEAD_DIM), full),
            jax.ShapeDtypeStruct((tok, width), full),
            jax.ShapeDtypeStruct((tok, 1), full),
            jax.ShapeDtypeStruct((tok, 2), full),
            jax.ShapeDtypeStruct((2, slots, tok), low),
            jax.ShapeDtypeStruct((slots, width), low),
            jax.ShapeDtypeStruct((slots, width), low),
        ),
        in_specs=[pl.BlockSpec(memory_space=pltpu.SMEM)] + [anywhere] * 8,
        out_specs=(anywhere,) * 5 + (inside,) * 15,
        scratch_shapes=[
            pltpu.VMEM((seq_len, width), low),
            pltpu.VMEM((seq_len, width), low),
            pltpu.VMEM((3, width, local_width), low),
            pltpu.VMEM((local_width, width), low),
            pltpu.VMEM((seq_len, width), low),
            pltpu.VMEM((group, tok, width), low),
            pltpu.VMEM((group, tok, width), low),
            pltpu.VMEM(pair_rows.shape, jnp.int32),
            pltpu.VMEM(angles.shape, full),
            pltpu.VMEM((tok, width), low),
            pltpu.SemaphoreType.DMA((14,)),
            pltpu.SemaphoreType.DMA((3, group)),
            pltpu.SemaphoreType.DMA((3, group)),
            pltpu.SemaphoreType.DMA((2, 2, 9)),
            pltpu.SemaphoreType.DMA((2, width // piece)),
            pltpu.SemaphoreType.DMA((2, 3, 2)),
        ],
        compiler_params=pltpu.CompilerParams(
            collective_id=3, has_side_effects=True, vmem_limit_bytes=67043328
        ),
        cost_estimate=pl.CostEstimate(flops=flops, bytes_accessed=40000000, transcendentals=0),
        name="attention",
    )(
        lengths,
        tokens,
        w_qkv,
        w_out,
        small,
        w_gate_up,
        pair_rows,
        angles,
        cotangent,
    )


def expert_step(gate_up_w, down_w, rows, d_rows_out):
    ff = down_w.shape[0]
    gate_up = jnp.dot(rows, gate_up_w, preferred_element_type=jnp.float32)
    gate = gate_up[:, :ff]
    upward = gate_up[:, ff:]
    sigmoid = jax.nn.sigmoid(gate)
    activated = (gate * sigmoid * upward).astype(jnp.bfloat16)
    out = jnp.dot(activated, down_w, preferred_element_type=jnp.float32).astype(jnp.bfloat16)
    d_activated = contract_last(d_rows_out, down_w)
    grad_down = contract_first(activated, d_rows_out)
    d_gate = d_activated * upward * sigmoid * (1.0 + gate * (1.0 - sigmoid))
    d_up = d_activated * gate * sigmoid
    d_gate_up = jnp.concatenate([d_gate, d_up], axis=1).astype(jnp.bfloat16)
    d_rows = contract_last(d_gate_up, gate_up_w).astype(jnp.bfloat16)
    grad_gate_up = contract_first(rows, d_gate_up)
    return out, d_rows, grad_gate_up, grad_down


def experts_gather_weights(w_gate_up, w_down, rows, d_rows_out):
    gate_up_w = lax.all_gather(w_gate_up, "dp", axis=1, tiled=True)[0]
    down_w = lax.all_gather(w_down, "dp", axis=1, tiled=True)[0]
    shape = rows.shape
    flat = (-1, shape[2])
    rows = exchange_experts(rows).reshape(flat)
    d_rows_out = exchange_experts(d_rows_out).reshape(flat)
    out, d_rows, grad_gate_up, grad_down = expert_step(gate_up_w, down_w, rows, d_rows_out)
    out = exchange_experts(out.reshape(shape))
    d_rows = exchange_experts(d_rows.reshape(shape))
    grad_gate_up = lax.psum_scatter(
        grad_gate_up.astype(jnp.bfloat16), "dp", scatter_dimension=0, tiled=True
    )
    grad_down = lax.psum_scatter(
        grad_down.astype(jnp.bfloat16), "dp", scatter_dimension=0, tiled=True
    )
    return (
        out,
        d_rows,
        grad_gate_up.astype(jnp.float32)[None],
        grad_down.astype(jnp.float32)[None],
    )


def attention_back_plain(
    lengths,
    d_attn,
    hat_all,
    whole,
    out_full,
    qkv_full,
    query,
    key_rows,
    value,
    attended,
    log_total,
    cosine,
    sine,
):
    seq_len, heads_local, head_size = query.shape
    local_width = heads_local * head_size
    position = jnp.arange(seq_len, dtype=jnp.int32)
    allowed = (position[None, :] <= position[:, None]) & (position < lengths[0])[None, :]
    whole_grad = lax.all_gather(d_attn, "expert", axis=0, tiled=True)
    d_attended = contract_last(whole_grad, out_full).astype(jnp.bfloat16)
    out_part = contract_first(attended, whole_grad)
    grad_out = lax.psum_scatter(
        out_part.astype(jnp.bfloat16), "dp", scatter_dimension=1, tiled=True
    ).astype(jnp.float32)
    d_heads = d_attended.reshape(seq_len, heads_local, head_size)
    probs = jnp.exp(masked_scores(query, key_rows, allowed) - log_total)
    probs_low = probs.astype(jnp.bfloat16)
    d_value = jnp.einsum(
        "hqk,qhd->khd", probs_low, d_heads, preferred_element_type=jnp.float32
    ).astype(jnp.bfloat16)
    d_probs = jnp.einsum("qhd,khd->hqk", d_heads, value, preferred_element_type=jnp.float32)
    row_delta = jnp.sum(probs * d_probs, axis=-1, keepdims=True)
    d_scores = (probs * (d_probs - row_delta)).astype(jnp.bfloat16)
    scale = head_size ** (-0.5)
    d_query = (
        jnp.einsum("hqk,khd->qhd", d_scores, key_rows, preferred_element_type=jnp.float32) * scale
    )
    d_key = jnp.einsum("hqk,qhd->khd", d_scores, query, preferred_element_type=jnp.float32) * scale
    d_query_pre = (
        rotate_back(d_query, cosine, sine).reshape(seq_len, local_width).astype(jnp.bfloat16)
    )
    d_key_pre = rotate_back(d_key, cosine, sine).reshape(seq_len, local_width).astype(jnp.bfloat16)
    d_projected = jnp.stack([d_query_pre, d_key_pre, d_value.reshape(seq_len, local_width)])
    d_normed_part = jnp.einsum(
        "cte,cde->td", d_projected, qkv_full, preferred_element_type=jnp.float32
    )
    grad_normalized = lax.psum_scatter(
        d_normed_part.astype(jnp.bfloat16), "expert", scatter_dimension=0, tiled=True
    ).astype(jnp.float32)
    qkv_part = jnp.einsum("td,cte->cde", whole, d_projected, preferred_element_type=jnp.float32)
    grad_qkv = lax.psum_scatter(
        qkv_part.astype(jnp.bfloat16), "dp", scatter_dimension=1, tiled=True
    ).astype(jnp.float32)
    first_gain_part = jnp.sum(d_normed_part * hat_all, axis=0)
    return grad_normalized, grad_qkv, grad_out, first_gain_part


def on_device(
    tokens,
    w_qkv,
    w_out,
    attention_norm_gain,
    gain_ffn,
    w_router,
    w_gate_up,
    w_down,
    lengths,
    routes,
    order,
    cotangent,
):
    group_size = lax.axis_size("expert")
    dp_size = lax.axis_size("dp")
    tok_dev = tokens.shape[0]
    seq_len = tok_dev * group_size
    width = tokens.shape[1]
    top_count = routes.shape[1]
    capacity = tok_dev * top_count // group_size
    slots = group_size * capacity
    head_size = HEAD_DIM
    local_width = w_qkv.shape[2]
    heads_local = local_width // head_size
    tokens_all = lax.all_gather(tokens, "expert", axis=0, tiled=True)
    small = jnp.concatenate(
        [attention_norm_gain[:, None], gain_ffn[:, None], w_router], axis=1
    )
    small_full = lax.all_gather(small, "dp", axis=0, tiled=True)
    qkv_full = lax.all_gather(w_qkv, "dp", axis=1, tiled=True)
    out_full = lax.all_gather(w_out, "dp", axis=1, tiled=True)
    first_norm_gain = small_full[:, 0].astype(jnp.float32)
    gain_two = small_full[:, 1].astype(jnp.float32)
    router_full = small_full[:, 2:]

    own_start = lax.axis_index("expert") * tok_dev
    own_position = own_start + jnp.arange(tok_dev, dtype=jnp.int32)
    live_own = own_position < lengths[0]
    live_rows = live_own.astype(jnp.float32)[:, None]
    target, kept_pair = slot_table(routes, order, live_own, capacity)
    slot_ids = jnp.arange(slots, dtype=jnp.int32)
    pair_hits = (slot_ids[:, None, None] == target[None]) & kept_pair[None]
    select = jnp.sum(pair_hits.astype(jnp.float32), axis=2).astype(jnp.bfloat16)

    inputs_float = tokens.astype(jnp.float32)
    input_normalized_hat, first_inverse_rms = normalize(inputs_float)
    hat_all, _ = normalize(tokens_all.astype(jnp.float32))
    whole = (hat_all * first_norm_gain).astype(jnp.bfloat16)
    cosine, sine = rotary_tables(seq_len, head_size)
    projected = jnp.einsum("td,cde->cte", whole, qkv_full, preferred_element_type=jnp.float32)
    query = rotate(projected[0].reshape(seq_len, heads_local, head_size), cosine, sine).astype(
        jnp.bfloat16
    )
    key_rows = rotate(projected[1].reshape(seq_len, heads_local, head_size), cosine, sine).astype(
        jnp.bfloat16
    )
    value = projected[2].astype(jnp.bfloat16).reshape(seq_len, heads_local, head_size)
    position = jnp.arange(seq_len, dtype=jnp.int32)
    live_all = position < lengths[0]
    allowed = (position[None, :] <= position[:, None]) & live_all[None, :]
    scores = masked_scores(query, key_rows, allowed)
    top_score = jnp.max(scores, axis=-1, keepdims=True)
    exponent = jnp.exp(scores - top_score)
    row_total = jnp.sum(exponent, axis=-1, keepdims=True)
    probs = exponent / row_total
    log_total = top_score + jnp.log(row_total)
    probs_low = probs.astype(jnp.bfloat16)
    attended = jnp.einsum("hqk,khd->qhd", probs_low, value, preferred_element_type=jnp.float32)
    attended = attended.reshape(seq_len, local_width).astype(jnp.bfloat16)
    attn_part = jnp.dot(attended, out_full, preferred_element_type=jnp.float32)
    attn_own = lax.psum_scatter(
        attn_part.astype(jnp.bfloat16), "expert", scatter_dimension=0, tiled=True
    ).astype(jnp.float32)
    resid = inputs_float + attn_own
    hhat, inverse_two = normalize(resid)
    hidden_in = (hhat * gain_two).astype(jnp.bfloat16)
    sent = jnp.dot(select, hidden_in, preferred_element_type=jnp.float32).astype(jnp.bfloat16)

    logits = jnp.dot(hidden_in, router_full, preferred_element_type=jnp.float32)
    chosen = jnp.take_along_axis(logits, routes, axis=1)
    gates = jax.nn.softmax(chosen, axis=1)
    d_out = live_rows * cotangent.astype(jnp.float32)
    d_back = jnp.zeros((slots, width), jnp.float32)
    for index in range(top_count):
        weighted = (gates[:, index : index + 1] * d_out).astype(jnp.bfloat16)
        d_back = d_back + jnp.dot(
            pair_hits[:, :, index].astype(jnp.bfloat16),
            weighted,
            preferred_element_type=jnp.float32,
        )
    d_back = d_back.astype(jnp.bfloat16)
    blocked = (group_size, capacity, width)
    returned, d_sent, grad_gate_up, grad_down = experts_gather_weights(
        w_gate_up, w_down, sent.reshape(blocked), d_back.reshape(blocked)
    )
    returned = returned.reshape(slots, width)
    d_sent = d_sent.reshape(slots, width)

    moe = jnp.zeros_like(resid)
    d_gates_list = []
    for index in range(top_count):
        one_hot = pair_hits[:, :, index].astype(jnp.bfloat16)
        picked = contract_first(one_hot, returned)
        d_gates_list.append(jnp.sum(d_out * picked, axis=-1))
        moe = moe + gates[:, index : index + 1] * picked
    output = (live_rows * (resid + moe)).astype(jnp.bfloat16)
    d_gates = jnp.stack(d_gates_list, axis=1)
    d_hidden = contract_first(select, d_sent)
    d_chosen = gates * (d_gates - jnp.sum(gates * d_gates, axis=1, keepdims=True))
    expert_ids = jnp.arange(group_size, dtype=jnp.int32)
    route_hits = (routes[:, :, None] == expert_ids[None, None, :]).astype(jnp.float32)
    d_logits = jnp.sum(route_hits * d_chosen[:, :, None], axis=1)
    router_f = router_full.astype(jnp.float32)
    d_hidden = d_hidden + jnp.dot(
        d_logits, router_f.T, precision=HIGH, preferred_element_type=jnp.float32
    )
    router_part = jnp.dot(
        hidden_in.astype(jnp.float32).T,
        d_logits,
        precision=HIGH,
        preferred_element_type=jnp.float32,
    )
    gain_two_part = jnp.sum(d_hidden * hhat, axis=0)
    scaled_two = d_hidden * gain_two
    d_resid = d_out + inverse_two * (
        scaled_two - hhat * jnp.mean(scaled_two * hhat, axis=-1, keepdims=True)
    )
    d_attn = d_resid.astype(jnp.bfloat16)
    grad_normalized, grad_qkv, grad_out, first_gain_part = attention_back_plain(
        lengths,
        d_attn,
        hat_all,
        whole,
        out_full,
        qkv_full,
        query,
        key_rows,
        value,
        attended,
        log_total,
        cosine,
        sine,
    )
    small_part = jnp.concatenate(
        [first_gain_part[None], gain_two_part[None], router_part.T], axis=0
    )
    small_sum = lax.psum(small_part, ("dp", "expert"))
    own_rows = width // dp_size
    small_own = lax.dynamic_slice_in_dim(
        small_sum, lax.axis_index("dp") * own_rows, own_rows, axis=1
    )
    first_scaled_input = grad_normalized * first_norm_gain
    grad_tokens = d_resid + first_inverse_rms * (
        first_scaled_input
        - input_normalized_hat
        * jnp.mean(first_scaled_input * input_normalized_hat, axis=-1, keepdims=True)
    )
    return (
        output,
        grad_tokens.astype(jnp.bfloat16),
        grad_qkv,
        grad_out,
        small_own[0],
        small_own[1],
        small_own[2 : 2 + group_size].T,
        grad_gate_up,
        grad_down,
    )


def on_device_split(
    tokens,
    w_qkv,
    w_out,
    attention_norm_gain,
    gain_ffn,
    w_router,
    w_gate_up,
    w_down,
    lengths,
    routes,
    order,
    cotangent,
):
    group = lax.axis_size("expert")
    tok, width = tokens.shape
    piece = w_router.shape[0]
    slots = tok * routes.shape[1]
    angles = rotary_constants(tok * group, HEAD_DIM)
    small = jnp.concatenate(
        [
            attention_norm_gain[None],
            gain_ffn[None],
            w_router.T,
            jnp.zeros((2, piece), jnp.bfloat16),
        ],
        axis=0,
    ).astype(jnp.float32)
    pair_rows = jnp.concatenate([routes.T, order[None]], axis=0)
    (
        tokens_all,
        whole,
        qkv_full,
        out_full,
        w_got,
        inverse_all,
        query,
        key_rows,
        value,
        attended,
        log_total,
        small_full,
        cosine,
        sine,
        resid,
        inverse_two,
        gates,
        hits,
        sent,
        d_back,
    ) = attention_call(
        lengths,
        tokens,
        w_qkv,
        w_out,
        small,
        w_gate_up,
        pair_rows,
        angles,
        cotangent,
        group,
    )
    blocked = (group, slots // group, width)
    returned, d_sent, grad_gate_up, grad_down = experts_call(
        sent.reshape(blocked), d_back.reshape(blocked), w_gate_up, w_got, w_down
    )
    output, grad_tokens, grad_weights, small_own, gate_got = attention_back_call(
        lengths,
        returned.reshape(slots, width),
        d_sent.reshape(slots, width),
        resid,
        inverse_two,
        gates,
        hits,
        cotangent,
        pair_rows,
        small_full,
        tokens_all,
        inverse_all,
        whole,
        out_full,
        qkv_full,
        query,
        key_rows,
        value,
        attended,
        log_total,
        cosine,
        sine,
        grad_gate_up,
    )
    grad_gate_up, grad_down, grad_tokens, output, grad_qkv, grad_out = finish_call(
        gate_got, grad_down, grad_tokens, output, grad_weights
    )
    return (
        output,
        grad_tokens,
        grad_qkv,
        grad_out,
        small_own[0],
        small_own[1],
        small_own[2 : 2 + group].T,
        grad_gate_up,
        grad_down,
    )


def solution(mesh):
    placed = (
        P(("dp", "expert"), None),
        P(None, "dp", "expert"),
        P("expert", "dp"),
        P("dp"),
        P("dp"),
        P("dp", None),
        P("expert", "dp", None),
        P("expert", "dp", None),
        P("dp"),
        P(("dp", "expert"), None),
        P(("dp", "expert")),
        P(("dp", "expert"), None),
    )
    split = mesh.shape["dp"] == 8 and mesh.shape["expert"] == 4
    return jax.shard_map(
        on_device_split if split else on_device,
        mesh=mesh,
        in_specs=placed,
        out_specs=(
            P(("dp", "expert"), None),
            P(("dp", "expert"), None),
            P(None, "dp", "expert"),
            P("expert", "dp"),
            P("dp"),
            P("dp"),
            P("dp", None),
            P("expert", "dp", None),
            P("expert", "dp", None),
        ),
        check_vma=False,
    )
```

```python
import functools

import jax
import jax.numpy as jnp
import numpy as np
from jax import lax
from jax.experimental import pallas as pl
from jax.experimental.pallas import tpu as pltpu
from jax.sharding import PartitionSpec as P

HEAD_DIM = 128
FF = 5632


NORM_EPSILON = 1e-05
NEGATIVE = -1e30
THETA = 10000.0
HIGH = lax.Precision.HIGHEST
MESH_ID = pl.DeviceIdType.MESH
LANES = 128


def remote(src, dst, send_sem, recv_sem, peer):
    return pltpu.make_async_remote_copy(
        src_ref=src,
        dst_ref=dst,
        send_sem=send_sem,
        recv_sem=recv_sem,
        device_id=peer,
        device_id_type=MESH_ID,
    )


def greet(peers):
    barrier = pltpu.get_barrier_semaphore()
    for peer in peers:
        pl.semaphore_signal(barrier, inc=1, device_id=peer, device_id_type=MESH_ID)
    pl.semaphore_wait(barrier, len(peers))


def dot_nn(left, right):
    return jnp.dot(left, right, preferred_element_type=jnp.float32)


def dot_nt(left, right):
    return lax.dot_general(
        left, right, (((1,), (1,)), ((), ())), preferred_element_type=jnp.float32
    )


def experts_kernel(
    group,
    sent,
    d_back,
    w_gate_up,
    w_got,
    w_down,
    ret,
    d_ret,
    grad_gate_up,
    grad_down,
    w_buf,
    down_buf,
    rows_buf,
    gate_buf,
    act_buf,
    part_buf,
    half_x,
    half_y,
    full_x,
    full_y,
    other_gate,
    other_down,
    ag_sems,
    rs_sems,
    weight_sems,
    local_sems,
    grad_sems,
):
    cap, width = sent.shape[1], sent.shape[2]
    half = cap // 2
    piece, hidden2 = w_got.shape[1:]
    hidden = hidden2 // 2
    down_own = w_down.at[0]
    down_rows = down_own.shape[0]
    chunk = 4 * cap
    total = group * chunk

    index = lax.axis_index("dp")
    place = lax.axis_index("expert")
    core = index % 2
    at_x = (index // 2) % 2
    at_y = index // 4
    partner = {"dp": at_y * 4 + at_x * 2 + (1 - core)}
    along_x = {"dp": at_y * 4 + (1 - at_x) * 2 + core}
    along_y = {"dp": (1 - at_y) * 4 + at_x * 2 + core}
    chips = [
        at_y * 2 + at_x,
        at_y * 2 + (1 - at_x),
        (1 - at_y) * 2 + at_x,
        (1 - at_y) * 2 + (1 - at_x),
    ]

    def ahead(k):
        return {"expert": (place + k) % group}

    def behind(k):
        return {"expert": (place + group - k) % group}

    greet([partner, along_x, along_y] + [ahead(k) for k in range(1, group)])

    def block(t, k, r, start=0, size=None):
        size = cap if size is None else size
        return rows_buf.at[t, pl.ds((k * 4 + r) * cap + start, size), :]

    def part(t, k, r, start=0, size=None):
        size = cap if size is None else size
        return part_buf.at[t, pl.ds((k * 4 + r) * cap + start, size), :]

    def ag(kind, t, k):
        return ag_sems.at[0, kind, t, k], ag_sems.at[1, kind, t, k]

    def rs(kind, t, k):
        return rs_sems.at[0, kind, t, k], rs_sems.at[1, kind, t, k]

    sources = (sent, d_back)
    results = (ret, d_ret)

    def z_copy(t, k):
        return remote(sources[t].at[k], block(t, k, 0), *ag(0, t, k), ahead(k))

    def own_copy(t):
        return pltpu.make_async_copy(sources[t].at[0], block(t, 0, 0), local_sems.at[t])

    def x_copy(t, k):
        return remote(block(t, k, 0), block(t, k, 1), *ag(1, t, k), along_x)

    def y_copy(t, k):
        return remote(block(t, k, 0), block(t, k, 2), *ag(2, t, k), along_y)

    def a_copy(t, k):
        return remote(block(t, k, 2, 0, half), block(t, k, 3, 0, half), *ag(3, t, k), along_x)

    def b_copy(t, k):
        return remote(
            block(t, k, 1, half, half), block(t, k, 3, half, half), *ag(4, t, k), along_y
        )

    def spread(t, k):
        if k == 0:
            own_copy(t).wait()
        else:
            z_copy(t, k).wait_recv()
        x_copy(t, k).start()
        y_copy(t, k).start()

    def relay_a(t, k):
        y_copy(t, k).wait_recv()
        a_copy(t, k).start()

    def relay_b(t, k):
        x_copy(t, k).wait_recv()
        b_copy(t, k).start()

    def arrived(t, k):
        a_copy(t, k).wait_recv()
        b_copy(t, k).wait_recv()
        if t == 0 and k == 0:
            for r in range(4):
                for copy in w_keep(r):
                    copy.wait()
                for copy in w_share(r, 1 - core):
                    copy.wait_recv()
            down_keep.wait()
            down_share().wait_recv()

    def half_x_copy(t, k):
        return remote(part(t, k, 3, 0, half), half_x.at[t, k], *rs(0, t, k), along_x)

    def half_y_copy(t, k):
        return remote(part(t, k, 3, half, half), half_y.at[t, k], *rs(1, t, k), along_y)

    def full_x_copy(t, k):
        return remote(part(t, k, 1), full_x.at[t, k], *rs(2, t, k), along_x)

    def full_y_copy(t, k):
        return remote(part(t, k, 2), full_y.at[t, k], *rs(3, t, k), along_y)

    def back_copy(t, k):
        return remote(part(t, k, 0), results[t].at[k], *rs(4, t, k), behind(k))

    def keep_copy(t):
        return pltpu.make_async_copy(part(t, 0, 0), results[t].at[0], local_sems.at[2 + t])

    def halves_out(t, k):
        half_x_copy(t, k).start()
        half_y_copy(t, k).start()

    def add_into(target, *others):
        value = target[...].astype(jnp.float32)
        for other in others:
            value = value + other[...].astype(jnp.float32)
        target[...] = value.astype(jnp.bfloat16)

    def full_y_out(t, k):
        half_x_copy(t, k).wait_recv()
        add_into(part(t, k, 2, 0, half), half_x.at[t, k])
        full_y_copy(t, k).start()

    def full_x_out(t, k):
        half_y_copy(t, k).wait_recv()
        add_into(part(t, k, 1, half, half), half_y.at[t, k])
        full_x_copy(t, k).start()

    def home(t, k):
        full_x_copy(t, k).wait_recv()
        full_y_copy(t, k).wait_recv()
        add_into(part(t, k, 0), full_x.at[t, k], full_y.at[t, k])
        if k == 0:
            keep_copy(t).start()
        else:
            back_copy(t, k).start()

    def w_rows(r, which):
        return pl.ds(pl.multiple_of((chips[r] * 2 + which) * piece, piece), piece)

    def w_parts(r, which):
        rows = w_rows(r, which)
        if r > 0:
            return [(w_got.at[r - 1], w_buf.at[rows, :], r)]
        return [
            (
                w_gate_up.at[
                    0, :, pl.ds(pl.multiple_of((4 * part + chips[0]) * hidden, LANES), hidden)
                ],
                w_buf.at[rows, pl.ds(part * hidden, hidden)],
                4 * part,
            )
            for part in range(2)
        ]

    def w_share(r, which):
        return [
            remote(source, target, weight_sems.at[0, n], weight_sems.at[1, n], partner)
            for source, target, n in w_parts(r, which)
        ]

    def w_keep(r):
        return [
            pltpu.make_async_copy(source, target, local_sems.at[4 + n])
            for source, target, n in w_parts(r, core)
        ]

    def down_at(which):
        return down_buf.at[pl.ds(pl.multiple_of(which * down_rows, down_rows), down_rows), :]

    def down_share():
        return remote(
            down_own, down_at(core), weight_sems.at[0, 5], weight_sems.at[1, 5], partner
        )

    down_keep = pltpu.make_async_copy(down_own, down_at(core), local_sems.at[9])

    def take(steps, k, number):
        for at in range(group):
            if (at, number) in steps:

                @pl.when(k == at)
                def _(events=steps[at, number]):
                    for event, t, which in events:
                        event(t, which)

    blocks = hidden // LANES
    spans = [(2 * j, min(2, blocks - 2 * j)) for j in range((blocks + 1) // 2)]
    tiles = width // (2 * LANES)

    def span(first, count):
        return pl.ds(first * LANES, count * LANES)

    def forward(k, carry):
        at = pl.ds(pl.multiple_of(k * chunk, chunk), chunk)

        def tile(first, count):
            gate_cols, up_cols = span(first, count), span(blocks + first, count)
            rows = rows_buf[0, at, :]
            if count == 1:
                weights = jnp.concatenate([w_buf[:, gate_cols], w_buf[:, up_cols]], axis=1)
                both = dot_nn(rows, weights)
                gate, up = both[:, :LANES], both[:, LANES:]
            else:
                gate = dot_nn(rows, w_buf[:, gate_cols])
                up = dot_nn(rows, w_buf[:, up_cols])
            sigmoid = 1.0 / (1.0 + jnp.exp(-gate))
            gate_buf[at, gate_cols] = gate.astype(jnp.bfloat16)
            gate_buf[at, up_cols] = up.astype(jnp.bfloat16)
            act_buf[at, gate_cols] = (gate * sigmoid * up).astype(jnp.bfloat16)

        take(forward_steps, k, 0)
        for first, count in spans[:3]:
            tile(first, count)
        take(forward_steps, k, 1)
        for first, count in spans[3:]:
            tile(first, count)
        take(forward_steps, k, 2)
        for j in range(tiles):
            cols = span(2 * j, 2)
            out = dot_nn(act_buf[at, :], down_buf[:, cols])
            part_buf[0, at, cols] = out.astype(jnp.bfloat16)
        return carry

    def backward(turn, carry):
        k = (turn + 1) % group
        at = pl.ds(pl.multiple_of(k * chunk, chunk), chunk)
        take(backward_steps, k, 0)
        for first, count in spans:
            gate_cols, up_cols = span(first, count), span(blocks + first, count)
            d_act = dot_nt(rows_buf[1, at, :], down_buf[gate_cols, :])
            gate = gate_buf[at, gate_cols].astype(jnp.float32)
            up = gate_buf[at, up_cols].astype(jnp.float32)
            sigmoid = 1.0 / (1.0 + jnp.exp(-gate))
            scaled = d_act * sigmoid
            d_gate = scaled * up * (1.0 + gate * (1.0 - sigmoid))
            gate_buf[at, gate_cols] = d_gate.astype(jnp.bfloat16)
            gate_buf[at, up_cols] = (scaled * gate).astype(jnp.bfloat16)
        for side in range(2):
            take(backward_steps, k, 1 + side)
            for j in range(side * (tiles // 2), (side + 1) * (tiles // 2)):
                cols = span(2 * j, 2)
                out = dot_nt(gate_buf[at, :], w_buf[cols, :])
                part_buf[1, at, cols] = out.astype(jnp.bfloat16)
        return carry

    forward_steps = {
        (0, 0): [(spread, 0, 0), (spread, 1, 0), (spread, 0, 1), (relay_a, 0, 0), (relay_b, 0, 0), (relay_a, 1, 0), (relay_b, 1, 0), (spread, 0, 2), (relay_a, 0, 1), (relay_b, 0, 1), (arrived, 0, 0)],
        (0, 2): [(spread, 0, 3)],
        (1, 0): [(halves_out, 0, 0), (relay_a, 0, 2), (relay_b, 0, 2), (arrived, 0, 1)],
        (1, 1): [(spread, 1, 1)],
        (2, 0): [(relay_a, 0, 3), (relay_b, 0, 3), (halves_out, 0, 1), (spread, 1, 2), (arrived, 0, 2)],
        (2, 2): [(spread, 1, 3)],
        (3, 0): [(arrived, 0, 3)],
        (3, 1): [(relay_a, 1, 1)],
        (3, 2): [(relay_b, 1, 1), (full_y_out, 0, 0)],
    }
    backward_steps = {
        (0, 0): [(arrived, 1, 0)],
        (0, 1): [(full_y_out, 0, 3), (full_y_out, 1, 1)],
        (0, 2): [(full_x_out, 1, 1)],
        (1, 0): [(relay_a, 1, 2), (relay_b, 1, 2), (relay_a, 1, 3), (relay_b, 1, 3), (full_x_out, 0, 0), (full_y_out, 0, 1), (arrived, 1, 1)],
        (1, 2): [(full_x_out, 0, 1), (halves_out, 0, 2)],
        (2, 0): [(arrived, 1, 2)],
        (2, 1): [(halves_out, 0, 3), (halves_out, 1, 1)],
        (3, 0): [(home, 0, 0), (arrived, 1, 3)],
        (3, 1): [(halves_out, 1, 2)],
        (3, 2): [(full_x_out, 0, 2), (home, 0, 1), (full_y_out, 0, 2), (full_x_out, 0, 3)],
    }
    grad_steps = {
        (0, 0): [(full_y_out, 1, 2)],
        (1, 0): [(home, 0, 2), (full_x_out, 1, 2)],
        (2, 0): [(halves_out, 1, 0), (halves_out, 1, 3)],
        (2, 1): [(home, 0, 3)],
        (2, 3): [(home, 1, 1)],
        (4, 0): [(full_x_out, 1, 0), (full_y_out, 1, 0), (full_x_out, 1, 3), (home, 1, 2)],
        (4, 1): [(full_y_out, 1, 3)],
        (5, 0): [(home, 1, 0), (home, 1, 3)],
    }

    own_copy(0).start()
    for k in range(1, group):
        z_copy(0, k).start()
    for r in range(4):
        for copy in w_share(r, core) + w_keep(r):
            copy.start()
    down_share().start()
    down_keep.start()
    own_copy(1).start()

    for k in range(1, group):
        z_copy(1, k).start()

    lax.fori_loop(0, group, forward, 0)
    lax.fori_loop(0, group, backward, 0)
    for event, t, which in grad_steps.get((0, 0), []):
        event(t, which)

    act_t = down_buf.at[:, pl.ds(0, total)]
    rows_t = down_buf.at[pl.ds(0, piece), pl.ds(total, total)]
    send_down = w_buf.at[pl.ds(4 * piece, down_rows), pl.ds(0, width)]

    def send_gate(r):
        return w_buf.at[pl.ds(pl.multiple_of(r * piece, piece), piece), :]

    def turn(j, carry):
        lanes = pl.ds(pl.multiple_of(j * LANES, LANES), LANES)
        act_t[lanes, :] = act_buf[:, lanes].T
        return carry

    lax.fori_loop(0, blocks, turn, 0)

    def pair_span(j):
        return pl.ds(pl.multiple_of(j * 2 * LANES, 2 * LANES), 2 * LANES)

    def down_grad(which, j):
        rows = pl.ds(pl.multiple_of(which * down_rows, down_rows), down_rows)
        return dot_nn(act_t[rows, :], rows_buf[1, :, pair_span(j)])

    def after(steps, number, r):
        turns = {(turn, 0): events for (stage, turn), events in steps.items() if stage == number}
        take(turns, r, 0)

    after(grad_steps, 1, 0)
    def down_for_partner(j, carry):
        send_down[:, pair_span(j)] = down_grad(1 - core, j).astype(jnp.bfloat16)
        return carry

    lax.fori_loop(0, tiles, down_for_partner, 0)
    down_send = remote(
        send_down, other_down, grad_sems.at[0, 4], grad_sems.at[1, 4], partner
    )
    down_send.start()

    def turned_rows(r, which):
        step_y = r // 2
        step_x = r % 2
        chip = (at_y + step_y - 2 * at_y * step_y) * 2 + (at_x + step_x - 2 * at_x * step_x)
        start = pl.multiple_of((chip * 2 + which) * piece, piece)
        rows_t[...] = rows_buf[0, :, pl.ds(start, piece)].T

    def gate_send(r):
        return remote(
            send_gate(r), other_gate.at[r], grad_sems.at[0, r], grad_sems.at[1, r], partner
        )

    def gate_for_partner(r, carry):
        after(grad_steps, 2, r)
        turned_rows(r, 1 - core)
        target = send_gate(r)
        for j in range(blocks):
            cols = span(2 * j, 2)
            target[:, cols] = dot_nn(rows_t[...], gate_buf[:, cols]).astype(jnp.bfloat16)
        gate_send(r).start()
        return carry

    lax.fori_loop(0, 4, gate_for_partner, 0)
    after(grad_steps, 3, 0)
    down_send.wait_recv()

    def down_for_self(j, carry):
        cols = pair_span(j)
        value = down_grad(core, j) + other_down[:, cols].astype(jnp.float32)
        other_down[:, cols] = value.astype(jnp.bfloat16)
        return carry

    lax.fori_loop(0, tiles, down_for_self, 0)
    down_out = pltpu.make_async_copy(other_down, grad_down, grad_sems.at[2, 0])
    down_out.start()

    def gate_out(r):
        return pltpu.make_async_copy(other_gate.at[r], grad_gate_up.at[r], grad_sems.at[2, 2 + r])

    def gate_for_self(r, carry):
        after(grad_steps, 4, r)
        gate_send(r).wait_recv()
        turned_rows(r, core)
        target = other_gate.at[r]
        for j in range(blocks):
            cols = span(2 * j, 2)
            value = dot_nn(rows_t[...], gate_buf[:, cols])
            target[:, cols] = (value + target[:, cols].astype(jnp.float32)).astype(jnp.bfloat16)
        gate_out(r).start()
        return carry

    lax.fori_loop(0, 4, gate_for_self, 0)
    after(grad_steps, 5, 0)

    down_out.wait()
    for r in range(4):
        gate_out(r).wait()
        gate_send(r).wait_send()
        for copy in w_share(r, core):
            copy.wait_send()
    down_share().wait_send()
    down_send.wait_send()
    for t in range(2):
        keep_copy(t).wait()
        for k in range(group):
            x_copy(t, k).wait_send()
            y_copy(t, k).wait_send()
            a_copy(t, k).wait_send()
            b_copy(t, k).wait_send()
            half_x_copy(t, k).wait_send()
            half_y_copy(t, k).wait_send()
            full_x_copy(t, k).wait_send()
            full_y_copy(t, k).wait_send()
            if k > 0:
                z_copy(t, k).wait_send()
                back_copy(t, k).wait_send()
                back_copy(t, k).wait_recv()


def experts_call(sent, d_back, w_gate_up, w_got, w_down):
    group, cap, width = sent.shape
    piece, hidden2 = w_got.shape[1:]
    hidden = hidden2 // 2
    down_rows = w_down.shape[1]
    chunk = 4 * cap
    total = group * chunk
    low = jnp.bfloat16
    anywhere = pl.BlockSpec(memory_space=pl.ANY)
    flops = 2 * total * width * hidden * 9
    moved = 2 * (4 * piece * hidden2 * 2 + down_rows * width * 3)
    return pl.pallas_call(
        functools.partial(experts_kernel, group),
        out_shape=(
            jax.ShapeDtypeStruct((group, cap, width), low),
            jax.ShapeDtypeStruct((group, cap, width), low),
            jax.ShapeDtypeStruct((4, piece, hidden2), low),
            jax.ShapeDtypeStruct((down_rows, width), low),
        ),
        in_specs=[anywhere] * 5,
        out_specs=(anywhere,) * 4,
        scratch_shapes=[
            pltpu.VMEM((width, hidden2), low),
            pltpu.VMEM((hidden, width), low),
            pltpu.VMEM((2, total, width), low),
            pltpu.VMEM((total, hidden2), low),
            pltpu.VMEM((total, hidden), low),
            pltpu.VMEM((2, total, width), low),
            pltpu.VMEM((2, group, cap // 2, width), low),
            pltpu.VMEM((2, group, cap // 2, width), low),
            pltpu.VMEM((2, group, cap, width), low),
            pltpu.VMEM((2, group, cap, width), low),
            pltpu.VMEM((4, piece, hidden2), low),
            pltpu.VMEM((down_rows, width), low),
            pltpu.SemaphoreType.DMA((2, 5, 2, group)),
            pltpu.SemaphoreType.DMA((2, 5, 2, group)),
            pltpu.SemaphoreType.DMA((2, 6)),
            pltpu.SemaphoreType.DMA((10,)),
            pltpu.SemaphoreType.DMA((3, 6)),
        ],
        compiler_params=pltpu.CompilerParams(
            collective_id=1, has_side_effects=True, vmem_limit_bytes=67043328
        ),
        cost_estimate=pl.CostEstimate(flops=flops, bytes_accessed=moved, transcendentals=0),
        name="experts",
    )(sent, d_back, w_gate_up, w_got, w_down)


def rotary_tables(length_total, head_size):
    position = jnp.arange(length_total, dtype=jnp.float32)
    frequency = THETA ** (-(jnp.arange(head_size // 2, dtype=jnp.float32) * 2.0 / head_size))
    angles = position[:, None] * frequency[None, :]
    return (jnp.cos(angles)[:, None, :], jnp.sin(angles)[:, None, :])


def rotate(values, cosine, sine):
    half_size = values.shape[-1] // 2
    first = values[..., :half_size]
    second = values[..., half_size:]
    return jnp.concatenate(
        [first * cosine - second * sine, second * cosine + first * sine], axis=-1
    )


def rotate_back(grad_rows, cosine, sine):
    half_size = grad_rows.shape[-1] // 2
    first = grad_rows[..., :half_size]
    second = grad_rows[..., half_size:]
    return jnp.concatenate(
        [first * cosine + second * sine, second * cosine - first * sine], axis=-1
    )


def slot_table(routes, order, valid, capacity):
    row_count = routes.shape[0]
    top_count = routes.shape[1]
    pair_rank = order[:, None] + row_count * jnp.arange(top_count, dtype=jnp.int32)[None, :]
    flat_rank = pair_rank.reshape(-1)
    flat_expert = routes.reshape(-1)
    flat_valid = jnp.broadcast_to(valid[:, None], routes.shape).reshape(-1)
    earlier = (
        (flat_rank[None, :] < flat_rank[:, None])
        & (flat_expert[None, :] == flat_expert[:, None])
        & flat_valid[None, :]
    )
    slot_index = jnp.sum(earlier.astype(jnp.int32), axis=1).reshape(row_count, top_count)
    kept_pair = valid[:, None] & (slot_index < capacity)
    target = routes * capacity + jnp.minimum(slot_index, capacity - 1)
    return (target, kept_pair)


def masked_scores(query, key_rows, allowed):
    scale = query.shape[-1] ** (-0.5)
    raw = jnp.einsum("qhd,khd->hqk", query, key_rows, preferred_element_type=jnp.float32) * scale
    return jnp.where(allowed[None], raw, NEGATIVE)


def contract_first(left, right):
    return lax.dot_general(
        left, right, (((0,), (0,)), ((), ())), preferred_element_type=jnp.float32
    )


def contract_last(left, right):
    return lax.dot_general(
        left, right, (((1,), (1,)), ((), ())), preferred_element_type=jnp.float32
    )


def normalize(rows):
    inverse = lax.rsqrt(jnp.mean(rows * rows, axis=-1, keepdims=True) + NORM_EPSILON)
    return rows * inverse, inverse


def exchange_experts(blocks):
    return lax.all_to_all(blocks, "expert", split_axis=0, concat_axis=0, tiled=True)


def line_order(place, step):
    upper = place // 2
    low = place * (1 - upper) + (3 - place) * upper
    first = 1 - (step + 1) // 2
    block = step + first * (1 - low) + (1 - first)
    return block * (1 - upper) + (3 - block) * upper


def rotated(grad, cosine, sine):
    return grad * cosine + pltpu.roll(grad, grad.shape[1] // 2, 1) * sine


def attention_back_kernel(
    heads,
    length,
    returned,
    d_sent,
    resid,
    inverse_two,
    gates,
    hits,
    cotangent,
    routes_t,
    small_full,
    tokens_all,
    inverse_all,
    whole,
    w_out,
    w_qkv,
    query,
    key_rows,
    value,
    attended,
    log_total,
    cosine,
    sine,
    gate_grads,
    output,
    grad_tokens,
    grad_weights,
    small_out,
    gate_got,
    returned_buf,
    d_sent_buf,
    resid_buf,
    inverse_two_buf,
    gates_buf,
    hits_buf,
    cotangent_buf,
    rows_buf,
    small_full_buf,
    da_buf,
    tokens_buf,
    inverse_buf,
    whole_buf,
    w_out_buf,
    w_qkv_buf,
    query_buf,
    key_buf,
    value_buf,
    attended_buf,
    log_buf,
    cosine_buf,
    sine_buf,
    d_key_acc,
    d_value_acc,
    d_proj,
    normed_part,
    from_left,
    from_right,
    send_pair,
    recv_pair,
    own_part,
    half_x,
    half_y,
    full_x,
    full_y,
    small_buf,
    small_recv,
    small_z,
    keep_buf,
    sum_buf,
    load_sems,
    line_sems,
    sum_sems,
    pair_sems,
    ring_sems,
    small_sems,
    gate_sems,
):
    tok, width = cotangent.shape
    seq_len = tokens_all.shape[0]
    group = seq_len // tok
    local_width = w_out.shape[0]
    head_size = local_width // heads
    piece = own_part.shape[1]
    half = piece // 2
    scale = head_size**-0.5

    index = lax.axis_index("dp")
    place = lax.axis_index("expert")
    core = index % 2
    at_x = (index // 2) % 2
    at_y = index // 4
    partner = {"dp": at_y * 4 + at_x * 2 + (1 - core)}
    along_x = {"dp": at_y * 4 + (1 - at_x) * 2 + core}
    along_y = {"dp": (1 - at_y) * 4 + at_x * 2 + core}
    over = {"dp": (1 - at_y) * 4 + (1 - at_x) * 2 + core}
    parts = width // piece

    def chip(r):
        step_y = r // 2
        step_x = r % 2
        return (at_y + step_y - 2 * at_y * step_y) * 2 + (at_x + step_x - 2 * at_x * step_x)

    def ring_peer(k):
        return {"dp": (index + k) % parts}

    def line_peer(k):
        return {"expert": (place + k) % group}

    right = {"expert": (place + 1) % group}
    left = {"expert": (place + group - 1) % group}

    loads = [
        pltpu.make_async_copy(source, target, load_sems.at[number])
        for number, (source, target) in enumerate(
            [
                (returned, returned_buf),
                (hits, hits_buf),
                (cotangent, cotangent_buf),
                (resid, resid_buf),
                (inverse_two, inverse_two_buf),
                (gates, gates_buf),
                (routes_t, rows_buf),
                (small_full, small_full_buf),
                (d_sent, d_sent_buf),
                (w_out, w_out_buf),
                (query, query_buf),
                (key_rows, key_buf),
                (value, value_buf),
                (log_total, log_buf),
                (cosine, cosine_buf),
                (sine, sine_buf),
                (w_qkv, w_qkv_buf),
                (tokens_all, tokens_buf),
                (inverse_all, inverse_buf),
                (whole, whole_buf),
                (attended, attended_buf),
                (gate_grads.at[0], keep_buf),
            ]
        )
    ]
    first = 9
    early = first + 7
    for load in loads[:early]:
        load.start()

    greet([ring_peer(k) for k in range(1, parts)] + [line_peer(k) for k in range(1, group)])

    def rows_of(block):
        return pl.ds(pl.multiple_of(block * tok, tok), tok)

    def pass_right(block):
        spot = da_buf.at[rows_of(block)]
        return remote(spot, spot, line_sems.at[0, block], line_sems.at[2, block], right)

    def pass_left(block):
        spot = da_buf.at[rows_of(block)]
        return remote(spot, spot, line_sems.at[1, block], line_sems.at[2, block], left)

    def gate_copy(r, peer):
        return remote(
            gate_grads.at[r], gate_got.at[r], gate_sems.at[0, r], gate_sems.at[1, r], peer
        )

    peers = (None, along_x, along_y, over)
    for r in (3, 1, 2):
        gate_copy(r, peers[r]).start()
    for load in loads[early:]:
        load.start()
    for load in loads[:first]:
        load.wait()

    at = place * tok + lax.broadcasted_iota(jnp.int32, (tok, 1), 0)
    live = jnp.where(at < length[0], 1.0, 0.0)
    d_out = live * cotangent_buf[...].astype(jnp.float32)
    total = resid_buf[...]
    hhat = total * inverse_two_buf[...]
    gate = [gates_buf[:, number : number + 1] for number in range(2)]
    d_gate = []
    for number in range(2):
        picked = dot_nn(hits_buf[number].T, returned_buf[...])
        d_gate.append(jnp.sum(d_out * picked, axis=-1, keepdims=True))
        total = total + gate[number] * picked
    output[...] = (live * total).astype(jnp.bfloat16)
    mixed = gate[0] * d_gate[0] + gate[1] * d_gate[1]
    d_chosen = [gate[number] * (d_gate[number] - mixed) for number in range(2)]
    d_hidden = dot_nn((hits_buf[0] + hits_buf[1]).T, d_sent_buf[...])
    gain_two = small_full_buf[1:2, :]
    hidden_in = (hhat * gain_two).astype(jnp.bfloat16).astype(jnp.float32)
    small_buf[...] = jnp.zeros_like(small_buf)
    square = (tok, tok)
    same = lax.broadcasted_iota(jnp.int32, square, 0) == lax.broadcasted_iota(jnp.int32, square, 1)
    named = []
    for number in range(2):
        row = rows_buf[number : number + 1, :].astype(jnp.float32)
        kept = jnp.where(same, jnp.broadcast_to(row, square), 0.0)
        named.append(jnp.sum(kept, axis=1, keepdims=True).astype(jnp.int32))
    for expert in range(group):
        d_logit = sum(
            jnp.where(named[number] == expert, d_chosen[number], 0.0)
            for number in range(2)
        )
        row = slice(2 + expert, 3 + expert)
        d_hidden = d_hidden + d_logit * small_full_buf[row, :]
        small_buf[row, :] = jnp.sum(d_logit * hidden_in, axis=0, keepdims=True)
    small_buf[1:2, :] = jnp.sum(d_hidden * hhat, axis=0, keepdims=True)
    scaled = d_hidden * gain_two
    shared = jnp.mean(scaled * hhat, axis=-1, keepdims=True)
    d_resid = d_out + inverse_two_buf[...] * (scaled - hhat * shared)
    resid_buf[...] = d_resid
    da_buf[rows_of(place), :] = d_resid.astype(jnp.bfloat16)

    @pl.when(place < group - 1)
    def _():
        pass_right(place).start()

    @pl.when(place > 0)
    def _():
        pass_left(place).start()

    d_key_acc[...] = jnp.zeros_like(d_key_acc)
    d_value_acc[...] = jnp.zeros_like(d_value_acc)

    def attend_back(block):
        rows = rows_of(block)
        d_heads = dot_nt(da_buf[rows, :], w_out_buf[...]).astype(jnp.bfloat16)
        shape = (tok, seq_len)
        at_query = block * tok + lax.broadcasted_iota(jnp.int32, shape, 0)
        at_key = lax.broadcasted_iota(jnp.int32, shape, 1)
        allowed = (at_key <= at_query) & (at_key < length[0])
        for head in range(heads):
            cols = slice(head * head_size, (head + 1) * head_size)
            one_query = query_buf[rows, cols]
            one_key = key_buf[:, cols]
            d_head = d_heads[:, cols]
            scores = jnp.where(allowed, dot_nt(one_query, one_key) * scale, NEGATIVE)
            probs = jnp.exp(scores - log_buf[rows, head : head + 1])
            d_probs = dot_nt(d_head, value_buf[:, cols])
            delta = jnp.sum(probs * d_probs, axis=-1, keepdims=True)
            d_scores = (probs * (d_probs - delta)).astype(jnp.bfloat16)
            d_query = dot_nn(d_scores, one_key) * scale
            d_key_acc[:, cols] += dot_nn(d_scores.T, one_query) * scale
            d_value_acc[:, cols] += dot_nn(probs.astype(jnp.bfloat16).T, d_head)
            d_proj[rows, cols] = rotated(d_query, cosine_buf[rows, :], -sine_buf[rows, :]).astype(
                jnp.bfloat16
            )

    for load in loads[first:early]:
        load.wait()

    def arrive(step, carry):
        later = (step + group - 2) // (group - 1)
        block = place * (1 - later) + line_order(place, step - later) * later

        @pl.when(step > 0)
        def _():
            pass_right(block).wait_recv()

        @pl.when((block < place) & (place < group - 1))
        def _():
            pass_right(block).start()

        @pl.when((block > place) & (place > 0))
        def _():
            pass_left(block).start()

        attend_back(block)
        return carry

    lax.fori_loop(0, group, arrive, 0)
    for load in loads[early:]:
        load.wait()
    keep = pltpu.make_async_copy(keep_buf, gate_got.at[0], load_sems.at[22])
    keep.start()

    for head in range(heads):
        cols = slice(head * head_size, (head + 1) * head_size)
        key_cols = slice(local_width + head * head_size, local_width + (head + 1) * head_size)
        d_proj[:, key_cols] = rotated(d_key_acc[:, cols], cosine_buf[...], -sine_buf[...]).astype(
            jnp.bfloat16
        )
    d_proj[:, 2 * local_width :] = d_value_acc[...].astype(jnp.bfloat16)

    def normed_tile(j, carry):
        cols = pl.ds(pl.multiple_of(j * piece, piece), piece)
        d_normed = jnp.zeros((seq_len, piece), jnp.float32)
        for c in range(3):
            d_normed += dot_nt(
                d_proj[:, c * local_width : (c + 1) * local_width], w_qkv_buf[c, cols, :]
            )
        hat = tokens_buf[:, cols].astype(jnp.float32) * inverse_buf[...]
        small_buf[0:1, cols] = jnp.sum(d_normed * hat, axis=0, keepdims=True)
        normed_part[:, cols] = d_normed.astype(jnp.bfloat16)
        return carry

    lax.fori_loop(0, parts, normed_tile, 0)

    def go_right(block):
        return remote(
            normed_part.at[pl.ds(block * tok, tok)],
            from_left.at[block],
            sum_sems.at[0, block],
            sum_sems.at[1, block],
            right,
        )

    def go_left(block):
        return remote(
            normed_part.at[pl.ds(block * tok, tok)],
            from_right.at[block],
            sum_sems.at[0, block],
            sum_sems.at[2, block],
            left,
        )

    def add_into(target, other):
        value = target[...].astype(jnp.float32) + other[...].astype(jnp.float32)
        target[...] = value.astype(jnp.bfloat16)

    def on_right(block):
        go_right(block).wait_recv()
        add_into(normed_part.at[pl.ds(block * tok, tok)], from_left.at[block])
        go_right(block).start()

    def on_left(block):
        go_left(block).wait_recv()
        add_into(normed_part.at[pl.ds(block * tok, tok)], from_right.at[block])
        go_left(block).start()

    @pl.when(place == 0)
    def _():
        for block in (3, 2, 1):
            go_right(block).start()

    @pl.when(place == 3)
    def _():
        for block in (0, 1, 2):
            go_left(block).start()

    def small_copy(k):
        to = (index + k) % parts
        cols = pl.ds(pl.multiple_of(to * piece, piece), piece)
        return remote(
            small_buf.at[:, cols],
            small_recv.at[k],
            small_sems.at[0, k],
            small_sems.at[1, k],
            ring_peer(k),
        )

    for k in range(1, parts):
        small_copy(k).start()

    def weight_grad(which, r):
        cols = pl.ds(pl.multiple_of((chip(r) * 2 + which) * piece, piece), piece)
        left_side = whole_buf[:, cols].T
        first = dot_nn(left_side, d_proj[...])
        second = dot_nn(da_buf[:, cols].T, attended_buf[...])
        return jnp.concatenate([first, second], axis=1)

    def pair_copy(r):
        return remote(
            send_pair.at[r], recv_pair.at[r], pair_sems.at[0, r], pair_sems.at[1, r], partner
        )

    def for_partner(i, carry):
        r = 3 - i
        send_pair[r] = weight_grad(1 - core, r).astype(jnp.bfloat16)
        pair_copy(r).start()
        return carry

    lax.fori_loop(0, 4, for_partner, 0)

    @pl.when(place == 1)
    def _():
        on_right(3)

    @pl.when(place == 2)
    def _():
        on_left(0)

    def half_x_copy():
        return remote(
            own_part.at[3, pl.ds(0, half)], half_x, ring_sems.at[0, 0], ring_sems.at[1, 0], along_x
        )

    def half_y_copy():
        return remote(
            own_part.at[3, pl.ds(half, half)],
            half_y,
            ring_sems.at[0, 1],
            ring_sems.at[1, 1],
            along_y,
        )

    def full_x_copy():
        return remote(own_part.at[1], full_x, ring_sems.at[0, 2], ring_sems.at[1, 2], along_x)

    def full_y_copy():
        return remote(own_part.at[2], full_y, ring_sems.at[0, 3], ring_sems.at[1, 3], along_y)

    def for_self(i, carry):
        r = 3 - i
        pair_copy(r).wait_recv()
        own_part[r] = (weight_grad(core, r) + recv_pair[r].astype(jnp.float32)).astype(
            jnp.bfloat16
        )

        @pl.when(i == 0)
        def _():
            half_x_copy().start()
            half_y_copy().start()

        return carry

    lax.fori_loop(0, 4, for_self, 0)

    total = small_buf[:, pl.ds(pl.multiple_of(index * piece, piece), piece)]
    for k in range(1, parts):
        small_copy(k).wait_recv()
        total = total + small_recv[k]
    small_z[0] = total

    @pl.when(place == 1)
    def _():
        on_right(2)

    @pl.when(place == 2)
    def _():
        on_left(1)

    def small_line_copy(k):
        return remote(
            small_z.at[0],
            small_z.at[k],
            small_sems.at[0, parts + k],
            small_sems.at[1, parts + k],
            line_peer(k),
        )

    for k in range(1, group):
        small_line_copy(k).start()

    half_x_copy().wait_recv()
    add_into(own_part.at[2, pl.ds(0, half)], half_x)
    full_y_copy().start()
    half_y_copy().wait_recv()
    add_into(own_part.at[1, pl.ds(half, half)], half_y)
    full_x_copy().start()

    @pl.when(place == 1)
    def _():
        on_left(0)

    @pl.when(place == 2)
    def _():
        on_right(3)

    total = small_z[0]
    for k in range(1, group):
        small_line_copy(k).wait_recv()
        total = total + small_z[k]
    small_out[...] = total

    sum_buf[...] = normed_part[rows_of(place), :].astype(jnp.float32)

    @pl.when(place > 0)
    def _():
        go_right(place).wait_recv()
        sum_buf[...] += from_left[place].astype(jnp.float32)

    @pl.when(place < group - 1)
    def _():
        go_left(place).wait_recv()
        sum_buf[...] += from_right[place].astype(jnp.float32)

    inverse_one = inverse_buf[rows_of(place), :]
    hat = tokens_buf[rows_of(place), :].astype(jnp.float32) * inverse_one
    scaled = sum_buf[...] * small_full_buf[0:1, :]
    shared = jnp.mean(scaled * hat, axis=-1, keepdims=True)
    grad_tokens[...] = (resid_buf[...] + inverse_one * (scaled - hat * shared)).astype(
        jnp.bfloat16
    )

    full_x_copy().wait_recv()
    full_y_copy().wait_recv()
    grad_weights[...] = (
        own_part[0].astype(jnp.float32)
        + full_x[...].astype(jnp.float32)
        + full_y[...].astype(jnp.float32)
    )

    for r in (1, 2, 3):
        gate_copy(r, peers[r]).wait()
    keep.wait()
    half_x_copy().wait_send()
    half_y_copy().wait_send()
    full_x_copy().wait_send()
    full_y_copy().wait_send()
    for r in range(4):
        pair_copy(r).wait_send()
    for k in range(1, parts):
        small_copy(k).wait_send()
    for k in range(1, group):
        small_line_copy(k).wait_send()
    for block in range(group):

        @pl.when(block > place)
        def _():
            go_right(block).wait_send()

        @pl.when(block < place)
        def _():
            go_left(block).wait_send()

        @pl.when((block <= place) & (place < group - 1))
        def _():
            pass_right(block).wait_send()

        @pl.when((block >= place) & (place > 0))
        def _():
            pass_left(block).wait_send()


def attention_back_call(
    lengths,
    returned,
    d_sent,
    resid,
    inverse_two,
    gates,
    hits,
    cotangent,
    routes_t,
    small_full,
    tokens_all,
    inverse_all,
    whole,
    w_out,
    w_qkv,
    query,
    key_rows,
    value,
    attended,
    log_total,
    cosine,
    sine,
    gate_grads,
):
    tok, width = cotangent.shape
    seq_len = tokens_all.shape[0]
    group = seq_len // tok
    local_width = w_out.shape[0]
    heads = log_total.shape[1]
    piece = gate_grads.shape[1]
    half = piece // 2
    parts = width // piece
    small_rows = small_full.shape[0]
    low, full = jnp.bfloat16, jnp.float32
    anywhere = pl.BlockSpec(memory_space=pl.ANY)
    inside = pl.BlockSpec(memory_space=pltpu.VMEM)

    def like(array):
        return pltpu.VMEM(array.shape, array.dtype)

    flops = 2 * seq_len * width * local_width * 8 + 10 * seq_len * seq_len * local_width
    return pl.pallas_call(
        functools.partial(attention_back_kernel, heads),
        out_shape=(
            jax.ShapeDtypeStruct((tok, width), low),
            jax.ShapeDtypeStruct((tok, width), low),
            jax.ShapeDtypeStruct((piece, 4 * local_width), full),
            jax.ShapeDtypeStruct((small_rows, piece), full),
            jax.ShapeDtypeStruct(gate_grads.shape, low),
        ),
        in_specs=[pl.BlockSpec(memory_space=pltpu.SMEM)] + [anywhere] * 22,
        out_specs=(inside, inside, inside, inside, anywhere),
        scratch_shapes=[
            like(returned),
            like(d_sent),
            like(resid),
            like(inverse_two),
            like(gates),
            like(hits),
            like(cotangent),
            like(routes_t),
            like(small_full),
            pltpu.VMEM((seq_len, width), low),
            like(tokens_all),
            like(inverse_all),
            like(whole),
            like(w_out),
            like(w_qkv),
            like(query),
            like(key_rows),
            like(value),
            like(attended),
            like(log_total),
            like(cosine),
            like(sine),
            pltpu.VMEM((seq_len, local_width), full),
            pltpu.VMEM((seq_len, local_width), full),
            pltpu.VMEM((seq_len, 3 * local_width), low),
            pltpu.VMEM((seq_len, width), low),
            pltpu.VMEM((group, tok, width), low),
            pltpu.VMEM((group, tok, width), low),
            pltpu.VMEM((4, piece, 4 * local_width), low),
            pltpu.VMEM((4, piece, 4 * local_width), low),
            pltpu.VMEM((4, piece, 4 * local_width), low),
            pltpu.VMEM((half, 4 * local_width), low),
            pltpu.VMEM((half, 4 * local_width), low),
            pltpu.VMEM((piece, 4 * local_width), low),
            pltpu.VMEM((piece, 4 * local_width), low),
            like(small_full),
            pltpu.VMEM((parts, small_rows, piece), full),
            pltpu.VMEM((group, small_rows, piece), full),
            pltpu.VMEM(gate_grads.shape[1:], low),
            like(resid),
            pltpu.SemaphoreType.DMA((23,)),
            pltpu.SemaphoreType.DMA((3, group)),
            pltpu.SemaphoreType.DMA((3, group)),
            pltpu.SemaphoreType.DMA((2, 4)),
            pltpu.SemaphoreType.DMA((2, 4)),
            pltpu.SemaphoreType.DMA((2, parts + group)),
            pltpu.SemaphoreType.DMA((2, 4)),
        ],
        compiler_params=pltpu.CompilerParams(
            collective_id=2, has_side_effects=True, vmem_limit_bytes=67043328
        ),
        cost_estimate=pl.CostEstimate(flops=flops, bytes_accessed=40000000, transcendentals=0),
        name="attention_back",
    )(
        lengths,
        returned,
        d_sent,
        resid,
        inverse_two,
        gates,
        hits,
        cotangent,
        routes_t,
        small_full,
        tokens_all,
        inverse_all,
        whole,
        w_out,
        w_qkv,
        query,
        key_rows,
        value,
        attended,
        log_total,
        cosine,
        sine,
        gate_grads,
    )


def finish_kernel(
    gate_got,
    grad_down_low,
    grad_tokens_low,
    output_low,
    grad_weights,
    small,
    grad_gate_up,
    grad_down,
    grad_tokens,
    output,
    grad_qkv,
    grad_out,
    gain_one,
    gain_two,
    router,
    got_buf,
    wide_buf,
    low_buf,
    down_buf,
    tokens_buf,
    output_buf,
    weights_buf,
    out_buf,
    small_buf,
    load_sems,
    store_sems,
):
    chips = gate_got.shape[0]
    size = gate_got.shape[2] // 2
    local_width = grad_qkv.shape[2]
    index = lax.axis_index("dp")
    at_x = (index // 2) % 2
    at_y = index // 4

    def load(number, source, target):
        return pltpu.make_async_copy(source, target, load_sems.at[number])

    loads = [load(r, gate_got.at[r], got_buf.at[r]) for r in range(chips)] + [
        load(4, grad_down_low, low_buf),
        load(5, grad_weights, weights_buf),
        load(6, grad_tokens_low, tokens_buf),
        load(7, output_low, output_buf),
        load(8, small, small_buf),
    ]
    for copy in loads:
        copy.start()
    stores = []

    def store(source, target):
        copy = pltpu.make_async_copy(source, target, store_sems.at[len(stores)])
        copy.start()
        stores.append(copy)

    for r in range(chips):
        loads[r].wait()
        step_y = r // 2
        step_x = r % 2
        chip = (at_y + step_y - 2 * at_y * step_y) * 2 + (at_x + step_x - 2 * at_x * step_x)
        for part in range(2):
            wide_buf[2 * r + part] = got_buf[r, :, part * size : (part + 1) * size].astype(
                jnp.float32
            )
            lanes = pl.ds(pl.multiple_of((part * chips + chip) * size, LANES), size)
            store(wide_buf.at[2 * r + part], grad_gate_up.at[0, :, lanes])
    loads[4].wait()
    down_buf[...] = low_buf[...].astype(jnp.float32)
    store(down_buf, grad_down.at[0])
    loads[5].wait()
    out_buf[...] = weights_buf[:, 3 * local_width :].T
    for c in range(3):
        store(weights_buf.at[:, pl.ds(c * local_width, local_width)], grad_qkv.at[c])
    store(out_buf, grad_out)
    loads[6].wait()
    store(tokens_buf, grad_tokens)
    loads[7].wait()
    store(output_buf, output)
    loads[8].wait()
    gain_one[...] = small_buf[0:1, :]
    gain_two[...] = small_buf[1:2, :]
    router[...] = small_buf[2 : 2 + router.shape[0], :]
    for copy in stores:
        copy.wait()


def finish_call(gate_got, grad_down, grad_tokens, output, grad_weights, small, experts):
    chips, rows, hidden2 = gate_got.shape
    local_width = grad_weights.shape[1] // 4
    full = jnp.float32
    anywhere = pl.BlockSpec(memory_space=pl.ANY)
    out_t = (local_width, rows)

    def like(array, kind=None):
        return pltpu.VMEM(array.shape, kind or array.dtype)

    return pl.pallas_call(
        finish_kernel,
        out_shape=(
            jax.ShapeDtypeStruct((1, rows, chips * hidden2), full),
            jax.ShapeDtypeStruct((1,) + grad_down.shape, full),
            jax.ShapeDtypeStruct(grad_tokens.shape, grad_tokens.dtype),
            jax.ShapeDtypeStruct(output.shape, output.dtype),
            jax.ShapeDtypeStruct((3, rows, local_width), full),
            jax.ShapeDtypeStruct(out_t, full),
            jax.ShapeDtypeStruct((1, rows), full),
            jax.ShapeDtypeStruct((1, rows), full),
            jax.ShapeDtypeStruct((experts, rows), full),
        ),
        in_specs=[anywhere] * 6,
        out_specs=(anywhere,) * 6 + (pl.BlockSpec(memory_space=pltpu.VMEM),) * 3,
        scratch_shapes=[
            like(gate_got),
            pltpu.VMEM((2 * chips, rows, hidden2 // 2), full),
            like(grad_down),
            like(grad_down, full),
            like(grad_tokens),
            like(output),
            like(grad_weights),
            pltpu.VMEM(out_t, full),
            like(small),
            pltpu.SemaphoreType.DMA((9,)),
            pltpu.SemaphoreType.DMA((15,)),
        ],
        compiler_params=pltpu.CompilerParams(vmem_limit_bytes=67043328),
        name="finish",
    )(gate_got, grad_down, grad_tokens, output, grad_weights, small)


def rotary_constants(length_total, head_size):
    low = 32
    steps = np.arange(head_size // 2, dtype=np.float32) * np.float32(2.0) / np.float32(head_size)
    frequency = np.power(np.float32(THETA), -steps).astype(np.float32).astype(np.float64)
    position = np.concatenate([np.arange(0, length_total, low), np.arange(low)])
    angles = position[:, None] * np.concatenate([frequency, frequency])[None, :]
    return np.stack([np.cos(angles), np.sin(angles)]).astype(np.float32)


def attention_kernel(
    heads,
    length,
    tokens,
    w_qkv,
    w_out,
    gain_one,
    gain_two,
    router_t,
    w_gate_up,
    routes_t,
    order_row,
    angles,
    cotangent,
    tokens_all,
    whole,
    qkv_full,
    out_full,
    w_got,
    inverse_all,
    query,
    key_rows,
    value,
    attended,
    log_total,
    small_full,
    cosine_buf,
    sine_buf,
    resid,
    inverse_two,
    gates,
    hits,
    sent,
    d_back,
    tokens_buf,
    whole_buf,
    w_qkv_buf,
    w_out_buf,
    part_buf,
    from_left,
    from_right,
    rows_buf,
    order_buf,
    angles_buf,
    cotangent_buf,
    gain_one_buf,
    gain_two_buf,
    router_buf,
    small,
    load_sems,
    line_sems,
    sum_sems,
    gather_sems,
    small_sems,
    slice_sems,
):
    tok, width = tokens.shape
    seq_len = tokens_buf.shape[0]
    group = seq_len // tok
    local_width = w_out.shape[0]
    head_size = local_width // heads
    piece = w_qkv.shape[1]
    parts = width // piece
    ff = w_gate_up.shape[2] // 2
    hidden = ff // 4
    slots = hits.shape[1]
    cap = slots // group
    scale = head_size**-0.5

    index = lax.axis_index("dp")
    place = lax.axis_index("expert")
    core = index % 2
    at_x = (index // 2) % 2
    at_y = index // 4
    other = at_y * 4 + at_x * 2 + (1 - core)
    by_x = at_y * 4 + (1 - at_x) * 2 + core
    by_y = (1 - at_y) * 4 + at_x * 2 + core
    by_both = (1 - at_y) * 4 + (1 - at_x) * 2 + core
    partner = {"dp": other}
    along_x = {"dp": by_x}
    along_y = {"dp": by_y}
    over = {"dp": by_both}
    right = {"expert": (place + 1) % group}
    left = {"expert": (place + group - 1) % group}

    def ring_peer(k):
        return {"dp": (index + k) % parts}

    def rows_of(block):
        return pl.ds(pl.multiple_of(block * tok, tok), tok)

    def piece_of(number):
        return pl.ds(pl.multiple_of(number * piece, piece), piece)

    def qkv_spot(number):
        return w_qkv_buf.at[:, piece_of(number), :]

    def qkv_half(number, which):
        start = pl.multiple_of(number * piece + which * (piece // 2), piece // 2)
        return w_qkv_buf.at[:, pl.ds(start, piece // 2), :]

    def out_spot(number):
        return w_out_buf.at[:, piece_of(number)]

    def out_half(number, which):
        rows = pl.ds(which * (local_width // 2), local_width // 2)
        return w_out_buf.at[rows, piece_of(number)]

    class Gather:
        def __init__(self, number, source, spot, half_spot):
            self.number, self.source, self.spot, self.half_spot = number, source, spot, half_spot

        def copy(self, slot, source, target, peer):
            sems = gather_sems.at[self.number]
            return remote(source, target, sems.at[0, slot], sems.at[1, slot], peer)

        def own(self, slot, peer):
            return self.copy(slot, self.source, self.spot(index), peer)

        def keep(self):
            return pltpu.make_async_copy(
                self.source, self.spot(index), load_sems.at[16 + self.number]
            )

        def relay_x(self):
            spot = self.half_spot(by_y, 0)
            return self.copy(3, spot, spot, along_x)

        def relay_y(self):
            spot = self.half_spot(by_x, 1)
            return self.copy(4, spot, spot, along_y)

        def hand(self, slot):
            spot = (
                self.spot(by_x),
                self.spot(by_y),
                self.half_spot(by_both, 0),
                self.half_spot(by_both, 1),
            )[slot - 5]
            return self.copy(slot, spot, spot, partner)

        def begin(self):
            self.own(0, along_x).start()
            self.own(1, along_y).start()
            self.own(2, partner).start()
            self.keep().start()

        def relay(self):
            self.own(1, along_y).wait_recv()
            self.relay_x().start()
            self.own(0, along_x).wait_recv()
            self.relay_y().start()
            self.hand(5).start()
            self.hand(6).start()

        def finish(self):
            self.relay_x().wait_recv()
            self.hand(7).start()
            self.relay_y().wait_recv()
            self.hand(8).start()
            self.keep().wait()
            self.own(2, partner).wait_recv()
            for slot in (5, 6, 7, 8):
                self.hand(slot).wait_recv()

        def drain(self):
            for slot, peer in ((0, along_x), (1, along_y), (2, partner)):
                self.own(slot, peer).wait_send()
            self.relay_x().wait_send()
            self.relay_y().wait_send()
            for slot in (5, 6, 7, 8):
                self.hand(slot).wait_send()

    gather_qkv = Gather(0, w_qkv, qkv_spot, qkv_half)
    gather_out = Gather(1, w_out, out_spot, out_half)

    loads = [
        pltpu.make_async_copy(source, target, load_sems.at[number])
        for number, (source, target) in enumerate(
            [
                (tokens, tokens_buf.at[rows_of(place)]),
                (gain_one, gain_one_buf),
                (gain_two, gain_two_buf),
                (router_t, router_buf),
                (routes_t, rows_buf),
                (order_row, order_buf),
                (angles, angles_buf),
                (cotangent, cotangent_buf),
            ]
        )
    ]
    for load in loads:
        load.start()

    greet([ring_peer(k) for k in range(1, parts)] + [right, left])

    def own_pass(side, peer):
        return remote(
            tokens,
            tokens_buf.at[rows_of(place)],
            line_sems.at[side, place],
            line_sems.at[2, place],
            peer,
        )

    def pass_on(block, side, peer):
        spot = tokens_buf.at[rows_of(block)]
        return remote(spot, spot, line_sems.at[side, block], line_sems.at[2, block], peer)

    @pl.when(place < group - 1)
    def _():
        own_pass(0, right).start()

    @pl.when(place > 0)
    def _():
        own_pass(1, left).start()

    def small_copy(k):
        return remote(
            small,
            small_full.at[:, piece_of(index)],
            small_sems.at[0, k],
            small_sems.at[1, k],
            ring_peer(k),
        )

    gather_qkv.begin()

    for load in loads:
        load.wait()
    experts = router_t.shape[0]
    small[...] = jnp.zeros_like(small)
    small[0:1, :] = gain_one_buf[...].astype(jnp.float32)
    small[1:2, :] = gain_two_buf[...].astype(jnp.float32)
    small[2 : 2 + experts, :] = router_buf[...].astype(jnp.float32)
    small_full[:, piece_of(index)] = small[...]
    for k in range(1, parts):
        small_copy(k).start()

    rows = rows_buf[...]
    first_row, second_row, order_at = rows[0:1], rows[1:2], order_buf[...]
    square = (tok, tok)
    same = lax.broadcasted_iota(jnp.int32, square, 0) == lax.broadcasted_iota(jnp.int32, square, 1)

    def as_column(row):
        kept = jnp.where(same, jnp.broadcast_to(row.astype(jnp.float32), square), 0.0)
        return jnp.sum(kept, axis=1, keepdims=True).astype(jnp.int32)

    first_col, second_col, order_col = [as_column(r) for r in (first_row, second_row, order_at)]
    start = place * tok
    live_col = (start + lax.broadcasted_iota(jnp.int32, (tok, 1), 0)) < length[0]
    live_row = (start + lax.broadcasted_iota(jnp.int32, (1, tok), 1)) < length[0]
    before = order_col < order_at

    def count(mask):
        return jnp.sum(jnp.where(mask & live_col, 1.0, 0.0), axis=0, keepdims=True)

    slot_first = count((first_col == first_row) & before)
    slot_second = count(first_col == second_row) + count((second_col == second_row) & before)
    slot_ids = lax.broadcasted_iota(jnp.int32, (slots, tok), 0)
    for number, (named, slot) in enumerate(((first_row, slot_first), (second_row, slot_second))):
        slot = slot.astype(jnp.int32)
        step = named - place
        step = jnp.where(step < 0, step + group, step)
        target = jnp.where(live_row & (slot < cap), step * cap + slot, -1)
        hits[number] = jnp.where(slot_ids == target, 1.0, 0.0).astype(jnp.bfloat16)

    low = 32
    highs = seq_len // low
    sign = jnp.where(
        lax.broadcasted_iota(jnp.int32, (low, head_size), 1) < head_size // 2, -1.0, 1.0
    )
    cosine_low, sine_low = angles_buf[0, highs:, :], angles_buf[1, highs:, :]
    for number in range(highs):
        at = slice(number * low, (number + 1) * low)
        cosine_high = angles_buf[0, number : number + 1, :]
        sine_high = angles_buf[1, number : number + 1, :]
        cosine_buf[at, :] = cosine_high * cosine_low - sine_high * sine_low
        sine_buf[at, :] = sign * (sine_high * cosine_low + cosine_high * sine_low)

    for k in range(1, parts):
        small_copy(k).wait_recv()

    def normalize_block(block):
        at = rows_of(block)
        value = tokens_buf[at, :].astype(jnp.float32)
        inverse = lax.rsqrt(jnp.mean(value * value, axis=-1, keepdims=True) + NORM_EPSILON)
        inverse_all[at, :] = inverse
        whole_buf[at, :] = (value * inverse * small_full[0:1, :]).astype(jnp.bfloat16)

    def arrive(step):
        block = line_order(place, step)
        pass_on(block, 0, right).wait_recv()

        @pl.when((block < place) & (place < group - 1))
        def _():
            pass_on(block, 0, right).start()

        @pl.when((block > place) & (place > 0))
        def _():
            pass_on(block, 1, left).start()

        normalize_block(block)

    def slice_copy(r, turn):
        number = (by_x // 2, by_y // 2, by_both // 2)[r - 1]
        part = turn
        lanes = pl.ds(pl.multiple_of(part * ff + number * hidden, LANES), hidden)
        return remote(
            w_gate_up.at[0, :, lanes],
            w_got.at[r - 1, :, pl.ds(part * hidden, hidden)],
            slice_sems.at[0, r - 1, turn],
            slice_sems.at[1, r - 1, turn],
            (along_x, along_y, over)[r - 1],
        )

    normalize_block(place)
    arrive(0)
    gather_qkv.relay()
    gather_out.begin()
    arrive(1)
    gather_qkv.finish()

    def project(first, size):
        at = pl.ds(pl.multiple_of(first, tok), size)
        source = whole_buf[at, :]

        def two_heads(number, carry):
            lanes = pl.ds(pl.multiple_of(number * 2 * head_size, 2 * head_size), 2 * head_size)
            for c, target in ((0, query), (1, key_rows)):
                plain = dot_nn(source, w_qkv_buf[c, :, lanes])
                turned = [
                    rotated(
                        plain[:, side * head_size : (side + 1) * head_size],
                        cosine_buf[at, :],
                        sine_buf[at, :],
                    )
                    for side in range(2)
                ]
                target[at, lanes] = jnp.concatenate(turned, axis=1).astype(jnp.bfloat16)
            value[at, lanes] = dot_nn(source, w_qkv_buf[2, :, lanes]).astype(jnp.bfloat16)
            return carry

        lax.fori_loop(0, heads // 2, two_heads, 0)

    upper = place // 2
    project(upper * tok, seq_len - tok)
    gather_out.relay()
    for turn in range(2):
        for r in (1, 2):
            slice_copy(r, turn).start()
    for turn in range(2):
        slice_copy(3, turn).start()
    gather_out.finish()
    arrive(2)
    project((1 - upper) * (seq_len - tok), tok)

    stores = [
        pltpu.make_async_copy(source, target, load_sems.at[10 + number])
        for number, (source, target) in enumerate(
            [
                (w_qkv_buf, qkv_full),
                (w_out_buf, out_full),
                (tokens_buf, tokens_all),
                (whole_buf, whole),
            ]
        )
    ]
    for store in stores:
        store.start()

    for number in range(group):
        at = slice(number * tok, (number + 1) * tok)
        extent = (number + 1) * tok
        shape = (tok, extent)
        at_query = number * tok + lax.broadcasted_iota(jnp.int32, shape, 0)
        at_key = lax.broadcasted_iota(jnp.int32, shape, 1)
        allowed = (at_key <= at_query) & (at_key < length[0])
        for head in range(heads):
            lanes = slice(head * head_size, (head + 1) * head_size)
            scores = dot_nt(query[at, lanes], key_rows[0:extent, lanes]) * scale
            scores = jnp.where(allowed, scores, NEGATIVE)
            top = jnp.max(scores, axis=-1, keepdims=True)
            exponent = jnp.exp(scores - top)
            row_total = jnp.sum(exponent, axis=-1, keepdims=True)
            probs = (exponent / row_total).astype(jnp.bfloat16)
            attended[at, lanes] = dot_nn(probs, value[0:extent, lanes]).astype(jnp.bfloat16)
            log_total[at, head : head + 1] = top + jnp.log(row_total)

    def out_tile(j, carry):
        lanes = piece_of(j)
        part_buf[:, lanes] = dot_nn(attended[...], w_out_buf[:, lanes]).astype(jnp.bfloat16)
        return carry

    lax.fori_loop(0, parts, out_tile, 0)

    def go_right(block):
        return remote(
            part_buf.at[rows_of(block)],
            from_left.at[block],
            sum_sems.at[0, block],
            sum_sems.at[1, block],
            right,
        )

    def go_left(block):
        return remote(
            part_buf.at[rows_of(block)],
            from_right.at[block],
            sum_sems.at[0, block],
            sum_sems.at[2, block],
            left,
        )

    def add_into(target, added):
        total = target[...].astype(jnp.float32) + added[...].astype(jnp.float32)
        target[...] = total.astype(jnp.bfloat16)

    def on_right(block):
        go_right(block).wait_recv()
        add_into(part_buf.at[rows_of(block)], from_left.at[block])
        go_right(block).start()

    def on_left(block):
        go_left(block).wait_recv()
        add_into(part_buf.at[rows_of(block)], from_right.at[block])
        go_left(block).start()

    @pl.when(place == 0)
    def _():
        for block in (3, 2, 1):
            go_right(block).start()

    @pl.when(place == 3)
    def _():
        for block in (0, 1, 2):
            go_left(block).start()

    @pl.when(place == 1)
    def _():
        on_right(3)
        on_right(2)
        on_left(0)

    @pl.when(place == 2)
    def _():
        on_left(0)
        on_left(1)
        on_right(3)

    resid[...] = tokens_buf[rows_of(place), :].astype(jnp.float32) + part_buf[
        rows_of(place), :
    ].astype(jnp.float32)

    @pl.when(place > 0)
    def _():
        go_right(place).wait_recv()
        resid[...] += from_left[place].astype(jnp.float32)

    @pl.when(place < group - 1)
    def _():
        go_left(place).wait_recv()
        resid[...] += from_right[place].astype(jnp.float32)

    total = resid[...]
    inverse = lax.rsqrt(jnp.mean(total * total, axis=-1, keepdims=True) + NORM_EPSILON)
    inverse_two[...] = inverse
    hidden_in = (total * inverse * small_full[1:2, :]).astype(jnp.bfloat16)
    logits = dot_nt(hidden_in, small_full[...].astype(jnp.bfloat16))
    lane = lax.broadcasted_iota(jnp.int32, logits.shape, 1)
    chosen = [
        jnp.sum(jnp.where(lane == named + 2, logits, 0.0), axis=1, keepdims=True)
        for named in (first_col, second_col)
    ]
    top = jnp.maximum(chosen[0], chosen[1])
    raised = [jnp.exp(entry - top) for entry in chosen]
    both = raised[0] + raised[1]
    gate = [entry / both for entry in raised]
    for number in range(2):
        gates[:, number : number + 1] = gate[number]
    sent[...] = dot_nn(hits[0] + hits[1], hidden_in).astype(jnp.bfloat16)
    d_out = jnp.where(live_col, 1.0, 0.0) * cotangent_buf[...].astype(jnp.float32)
    d_back[...] = (
        dot_nn(hits[0], (gate[0] * d_out).astype(jnp.bfloat16))
        + dot_nn(hits[1], (gate[1] * d_out).astype(jnp.bfloat16))
    ).astype(jnp.bfloat16)

    for store in stores:
        store.wait()
    gather_qkv.drain()
    gather_out.drain()
    for k in range(1, parts):
        small_copy(k).wait_send()
    for block in range(group):

        @pl.when(block > place)
        def _():
            go_right(block).wait_send()

        @pl.when(block < place)
        def _():
            go_left(block).wait_send()

        @pl.when((block <= place) & (place < group - 1))
        def _():
            pass_on(block, 0, right).wait_send()

        @pl.when((block >= place) & (place > 0))
        def _():
            pass_on(block, 1, left).wait_send()

    for turn in range(2):
        for r in (1, 2, 3):
            slice_copy(r, turn).wait()


def attention_call(
    lengths,
    tokens,
    w_qkv,
    w_out,
    gain_one,
    gain_two,
    router_t,
    w_gate_up,
    routes_t,
    order_row,
    angles,
    cotangent,
    group,
):
    tok, width = tokens.shape
    seq_len = tok * group
    local_width = w_qkv.shape[2]
    heads = local_width // HEAD_DIM
    slots = tok * 2
    piece = w_qkv.shape[1]
    low, full = jnp.bfloat16, jnp.float32
    anywhere = pl.BlockSpec(memory_space=pl.ANY)
    inside = pl.BlockSpec(memory_space=pltpu.VMEM)
    narrow = jax.ShapeDtypeStruct((seq_len, local_width), low)
    flops = 2 * seq_len * width * local_width * 4 + 4 * seq_len * seq_len * local_width
    return pl.pallas_call(
        functools.partial(attention_kernel, heads),
        out_shape=(
            jax.ShapeDtypeStruct((seq_len, width), low),
            jax.ShapeDtypeStruct((seq_len, width), low),
            jax.ShapeDtypeStruct((3, width, local_width), low),
            jax.ShapeDtypeStruct((local_width, width), low),
            jax.ShapeDtypeStruct((3, piece, w_gate_up.shape[2] // 4), low),
            jax.ShapeDtypeStruct((seq_len, 1), full),
            narrow,
            narrow,
            narrow,
            narrow,
            jax.ShapeDtypeStruct((seq_len, heads), full),
            jax.ShapeDtypeStruct((8, width), full),
            jax.ShapeDtypeStruct((seq_len, HEAD_DIM), full),
            jax.ShapeDtypeStruct((seq_len, HEAD_DIM), full),
            jax.ShapeDtypeStruct((tok, width), full),
            jax.ShapeDtypeStruct((tok, 1), full),
            jax.ShapeDtypeStruct((tok, 2), full),
            jax.ShapeDtypeStruct((2, slots, tok), low),
            jax.ShapeDtypeStruct((slots, width), low),
            jax.ShapeDtypeStruct((slots, width), low),
        ),
        in_specs=[pl.BlockSpec(memory_space=pltpu.SMEM)] + [anywhere] * 11,
        out_specs=(anywhere,) * 5 + (inside,) * 15,
        scratch_shapes=[
            pltpu.VMEM((seq_len, width), low),
            pltpu.VMEM((seq_len, width), low),
            pltpu.VMEM((3, width, local_width), low),
            pltpu.VMEM((local_width, width), low),
            pltpu.VMEM((seq_len, width), low),
            pltpu.VMEM((group, tok, width), low),
            pltpu.VMEM((group, tok, width), low),
            pltpu.VMEM(routes_t.shape, jnp.int32),
            pltpu.VMEM(order_row.shape, jnp.int32),
            pltpu.VMEM(angles.shape, full),
            pltpu.VMEM((tok, width), low),
            pltpu.VMEM(gain_one.shape, low),
            pltpu.VMEM(gain_two.shape, low),
            pltpu.VMEM(router_t.shape, low),
            pltpu.VMEM((8, piece), full),
            pltpu.SemaphoreType.DMA((18,)),
            pltpu.SemaphoreType.DMA((3, group)),
            pltpu.SemaphoreType.DMA((3, group)),
            pltpu.SemaphoreType.DMA((2, 2, 9)),
            pltpu.SemaphoreType.DMA((2, width // piece)),
            pltpu.SemaphoreType.DMA((2, 3, 2)),
        ],
        compiler_params=pltpu.CompilerParams(
            collective_id=3, has_side_effects=True, vmem_limit_bytes=67043328
        ),
        cost_estimate=pl.CostEstimate(flops=flops, bytes_accessed=40000000, transcendentals=0),
        name="attention",
    )(
        lengths,
        tokens,
        w_qkv,
        w_out,
        gain_one,
        gain_two,
        router_t,
        w_gate_up,
        routes_t,
        order_row,
        angles,
        cotangent,
    )


def expert_step(gate_up_w, down_w, rows, d_rows_out):
    ff = down_w.shape[0]
    gate_up = jnp.dot(rows, gate_up_w, preferred_element_type=jnp.float32)
    gate = gate_up[:, :ff]
    upward = gate_up[:, ff:]
    sigmoid = jax.nn.sigmoid(gate)
    activated = (gate * sigmoid * upward).astype(jnp.bfloat16)
    out = jnp.dot(activated, down_w, preferred_element_type=jnp.float32).astype(jnp.bfloat16)
    d_activated = contract_last(d_rows_out, down_w)
    grad_down = contract_first(activated, d_rows_out)
    d_gate = d_activated * upward * sigmoid * (1.0 + gate * (1.0 - sigmoid))
    d_up = d_activated * gate * sigmoid
    d_gate_up = jnp.concatenate([d_gate, d_up], axis=1).astype(jnp.bfloat16)
    d_rows = contract_last(d_gate_up, gate_up_w).astype(jnp.bfloat16)
    grad_gate_up = contract_first(rows, d_gate_up)
    return out, d_rows, grad_gate_up, grad_down


def experts_gather_weights(w_gate_up, w_down, rows, d_rows_out):
    gate_up_w = lax.all_gather(w_gate_up, "dp", axis=1, tiled=True)[0]
    down_w = lax.all_gather(w_down, "dp", axis=1, tiled=True)[0]
    shape = rows.shape
    flat = (-1, shape[2])
    rows = exchange_experts(rows).reshape(flat)
    d_rows_out = exchange_experts(d_rows_out).reshape(flat)
    out, d_rows, grad_gate_up, grad_down = expert_step(gate_up_w, down_w, rows, d_rows_out)
    out = exchange_experts(out.reshape(shape))
    d_rows = exchange_experts(d_rows.reshape(shape))
    grad_gate_up = lax.psum_scatter(
        grad_gate_up.astype(jnp.bfloat16), "dp", scatter_dimension=0, tiled=True
    )
    grad_down = lax.psum_scatter(
        grad_down.astype(jnp.bfloat16), "dp", scatter_dimension=0, tiled=True
    )
    return (
        out,
        d_rows,
        grad_gate_up.astype(jnp.float32)[None],
        grad_down.astype(jnp.float32)[None],
    )


def attention_back_plain(
    lengths,
    d_attn,
    hat_all,
    whole,
    out_full,
    qkv_full,
    query,
    key_rows,
    value,
    attended,
    log_total,
    cosine,
    sine,
):
    seq_len, heads_local, head_size = query.shape
    local_width = heads_local * head_size
    position = jnp.arange(seq_len, dtype=jnp.int32)
    allowed = (position[None, :] <= position[:, None]) & (position < lengths[0])[None, :]
    whole_grad = lax.all_gather(d_attn, "expert", axis=0, tiled=True)
    d_attended = contract_last(whole_grad, out_full).astype(jnp.bfloat16)
    out_part = contract_first(attended, whole_grad)
    grad_out = lax.psum_scatter(
        out_part.astype(jnp.bfloat16), "dp", scatter_dimension=1, tiled=True
    ).astype(jnp.float32)
    d_heads = d_attended.reshape(seq_len, heads_local, head_size)
    probs = jnp.exp(masked_scores(query, key_rows, allowed) - log_total)
    probs_low = probs.astype(jnp.bfloat16)
    d_value = jnp.einsum(
        "hqk,qhd->khd", probs_low, d_heads, preferred_element_type=jnp.float32
    ).astype(jnp.bfloat16)
    d_probs = jnp.einsum("qhd,khd->hqk", d_heads, value, preferred_element_type=jnp.float32)
    row_delta = jnp.sum(probs * d_probs, axis=-1, keepdims=True)
    d_scores = (probs * (d_probs - row_delta)).astype(jnp.bfloat16)
    scale = head_size ** (-0.5)
    d_query = (
        jnp.einsum("hqk,khd->qhd", d_scores, key_rows, preferred_element_type=jnp.float32) * scale
    )
    d_key = jnp.einsum("hqk,qhd->khd", d_scores, query, preferred_element_type=jnp.float32) * scale
    d_query_pre = (
        rotate_back(d_query, cosine, sine).reshape(seq_len, local_width).astype(jnp.bfloat16)
    )
    d_key_pre = rotate_back(d_key, cosine, sine).reshape(seq_len, local_width).astype(jnp.bfloat16)
    d_projected = jnp.stack([d_query_pre, d_key_pre, d_value.reshape(seq_len, local_width)])
    d_normed_part = jnp.einsum(
        "cte,cde->td", d_projected, qkv_full, preferred_element_type=jnp.float32
    )
    grad_normalized = lax.psum_scatter(
        d_normed_part.astype(jnp.bfloat16), "expert", scatter_dimension=0, tiled=True
    ).astype(jnp.float32)
    qkv_part = jnp.einsum("td,cte->cde", whole, d_projected, preferred_element_type=jnp.float32)
    grad_qkv = lax.psum_scatter(
        qkv_part.astype(jnp.bfloat16), "dp", scatter_dimension=1, tiled=True
    ).astype(jnp.float32)
    first_gain_part = jnp.sum(d_normed_part * hat_all, axis=0)
    return grad_normalized, grad_qkv, grad_out, first_gain_part


def on_device(
    tokens,
    w_qkv,
    w_out,
    attention_norm_gain,
    gain_ffn,
    w_router,
    w_gate_up,
    w_down,
    lengths,
    routes,
    order,
    cotangent,
):
    group_size = lax.axis_size("expert")
    dp_size = lax.axis_size("dp")
    tok_dev = tokens.shape[0]
    seq_len = tok_dev * group_size
    width = tokens.shape[1]
    top_count = routes.shape[1]
    capacity = tok_dev * top_count // group_size
    slots = group_size * capacity
    head_size = HEAD_DIM
    local_width = w_qkv.shape[2]
    heads_local = local_width // head_size
    tokens_all = lax.all_gather(tokens, "expert", axis=0, tiled=True)
    small = jnp.concatenate(
        [attention_norm_gain[:, None], gain_ffn[:, None], w_router], axis=1
    )
    small_full = lax.all_gather(small, "dp", axis=0, tiled=True)
    qkv_full = lax.all_gather(w_qkv, "dp", axis=1, tiled=True)
    out_full = lax.all_gather(w_out, "dp", axis=1, tiled=True)
    first_norm_gain = small_full[:, 0].astype(jnp.float32)
    gain_two = small_full[:, 1].astype(jnp.float32)
    router_full = small_full[:, 2:]

    own_start = lax.axis_index("expert") * tok_dev
    own_position = own_start + jnp.arange(tok_dev, dtype=jnp.int32)
    live_own = own_position < lengths[0]
    live_rows = live_own.astype(jnp.float32)[:, None]
    target, kept_pair = slot_table(routes, order, live_own, capacity)
    slot_ids = jnp.arange(slots, dtype=jnp.int32)
    pair_hits = (slot_ids[:, None, None] == target[None]) & kept_pair[None]
    select = jnp.sum(pair_hits.astype(jnp.float32), axis=2).astype(jnp.bfloat16)

    inputs_float = tokens.astype(jnp.float32)
    input_normalized_hat, first_inverse_rms = normalize(inputs_float)
    hat_all, _ = normalize(tokens_all.astype(jnp.float32))
    whole = (hat_all * first_norm_gain).astype(jnp.bfloat16)
    cosine, sine = rotary_tables(seq_len, head_size)
    projected = jnp.einsum("td,cde->cte", whole, qkv_full, preferred_element_type=jnp.float32)
    query = rotate(projected[0].reshape(seq_len, heads_local, head_size), cosine, sine).astype(
        jnp.bfloat16
    )
    key_rows = rotate(projected[1].reshape(seq_len, heads_local, head_size), cosine, sine).astype(
        jnp.bfloat16
    )
    value = projected[2].astype(jnp.bfloat16).reshape(seq_len, heads_local, head_size)
    position = jnp.arange(seq_len, dtype=jnp.int32)
    live_all = position < lengths[0]
    allowed = (position[None, :] <= position[:, None]) & live_all[None, :]
    scores = masked_scores(query, key_rows, allowed)
    top_score = jnp.max(scores, axis=-1, keepdims=True)
    exponent = jnp.exp(scores - top_score)
    row_total = jnp.sum(exponent, axis=-1, keepdims=True)
    probs = exponent / row_total
    log_total = top_score + jnp.log(row_total)
    probs_low = probs.astype(jnp.bfloat16)
    attended = jnp.einsum("hqk,khd->qhd", probs_low, value, preferred_element_type=jnp.float32)
    attended = attended.reshape(seq_len, local_width).astype(jnp.bfloat16)
    attn_part = jnp.dot(attended, out_full, preferred_element_type=jnp.float32)
    attn_own = lax.psum_scatter(
        attn_part.astype(jnp.bfloat16), "expert", scatter_dimension=0, tiled=True
    ).astype(jnp.float32)
    resid = inputs_float + attn_own
    hhat, inverse_two = normalize(resid)
    hidden_in = (hhat * gain_two).astype(jnp.bfloat16)
    sent = jnp.dot(select, hidden_in, preferred_element_type=jnp.float32).astype(jnp.bfloat16)

    logits = jnp.dot(hidden_in, router_full, preferred_element_type=jnp.float32)
    chosen = jnp.take_along_axis(logits, routes, axis=1)
    gates = jax.nn.softmax(chosen, axis=1)
    d_out = live_rows * cotangent.astype(jnp.float32)
    d_back = jnp.zeros((slots, width), jnp.float32)
    for index in range(top_count):
        weighted = (gates[:, index : index + 1] * d_out).astype(jnp.bfloat16)
        d_back = d_back + jnp.dot(
            pair_hits[:, :, index].astype(jnp.bfloat16),
            weighted,
            preferred_element_type=jnp.float32,
        )
    d_back = d_back.astype(jnp.bfloat16)
    blocked = (group_size, capacity, width)
    returned, d_sent, grad_gate_up, grad_down = experts_gather_weights(
        w_gate_up, w_down, sent.reshape(blocked), d_back.reshape(blocked)
    )
    returned = returned.reshape(slots, width)
    d_sent = d_sent.reshape(slots, width)

    moe = jnp.zeros_like(resid)
    d_gates_list = []
    for index in range(top_count):
        one_hot = pair_hits[:, :, index].astype(jnp.bfloat16)
        picked = contract_first(one_hot, returned)
        d_gates_list.append(jnp.sum(d_out * picked, axis=-1))
        moe = moe + gates[:, index : index + 1] * picked
    output = (live_rows * (resid + moe)).astype(jnp.bfloat16)
    d_gates = jnp.stack(d_gates_list, axis=1)
    d_hidden = contract_first(select, d_sent)
    d_chosen = gates * (d_gates - jnp.sum(gates * d_gates, axis=1, keepdims=True))
    expert_ids = jnp.arange(group_size, dtype=jnp.int32)
    route_hits = (routes[:, :, None] == expert_ids[None, None, :]).astype(jnp.float32)
    d_logits = jnp.sum(route_hits * d_chosen[:, :, None], axis=1)
    router_f = router_full.astype(jnp.float32)
    d_hidden = d_hidden + jnp.dot(
        d_logits, router_f.T, precision=HIGH, preferred_element_type=jnp.float32
    )
    router_part = jnp.dot(
        hidden_in.astype(jnp.float32).T,
        d_logits,
        precision=HIGH,
        preferred_element_type=jnp.float32,
    )
    gain_two_part = jnp.sum(d_hidden * hhat, axis=0)
    scaled_two = d_hidden * gain_two
    d_resid = d_out + inverse_two * (
        scaled_two - hhat * jnp.mean(scaled_two * hhat, axis=-1, keepdims=True)
    )
    d_attn = d_resid.astype(jnp.bfloat16)
    grad_normalized, grad_qkv, grad_out, first_gain_part = attention_back_plain(
        lengths,
        d_attn,
        hat_all,
        whole,
        out_full,
        qkv_full,
        query,
        key_rows,
        value,
        attended,
        log_total,
        cosine,
        sine,
    )
    small_part = jnp.concatenate(
        [first_gain_part[None], gain_two_part[None], router_part.T], axis=0
    )
    small_sum = lax.psum(small_part, ("dp", "expert"))
    own_rows = width // dp_size
    small_own = lax.dynamic_slice_in_dim(
        small_sum, lax.axis_index("dp") * own_rows, own_rows, axis=1
    )
    first_scaled_input = grad_normalized * first_norm_gain
    grad_tokens = d_resid + first_inverse_rms * (
        first_scaled_input
        - input_normalized_hat
        * jnp.mean(first_scaled_input * input_normalized_hat, axis=-1, keepdims=True)
    )
    return (
        output,
        grad_tokens.astype(jnp.bfloat16),
        grad_qkv,
        grad_out,
        small_own[0],
        small_own[1],
        small_own[2 : 2 + group_size].T,
        grad_gate_up,
        grad_down,
    )


def on_device_split(
    tokens,
    w_qkv,
    w_out,
    attention_norm_gain,
    gain_ffn,
    w_router,
    w_gate_up,
    w_down,
    lengths,
    routes,
    order,
    cotangent,
):
    group = lax.axis_size("expert")
    tok, width = tokens.shape
    piece = w_router.shape[0]
    slots = tok * routes.shape[1]
    angles = rotary_constants(tok * group, HEAD_DIM)
    routes_t = routes.T
    (
        tokens_all,
        whole,
        qkv_full,
        out_full,
        w_got,
        inverse_all,
        query,
        key_rows,
        value,
        attended,
        log_total,
        small_full,
        cosine,
        sine,
        resid,
        inverse_two,
        gates,
        hits,
        sent,
        d_back,
    ) = attention_call(
        lengths,
        tokens,
        w_qkv,
        w_out,
        attention_norm_gain[None],
        gain_ffn[None],
        w_router.T,
        w_gate_up,
        routes_t,
        order.reshape(1, tok),
        angles,
        cotangent,
        group,
    )
    blocked = (group, slots // group, width)
    returned, d_sent, grad_gate_up, grad_down = experts_call(
        sent.reshape(blocked), d_back.reshape(blocked), w_gate_up, w_got, w_down
    )
    output, grad_tokens, grad_weights, small_own, gate_got = attention_back_call(
        lengths,
        returned.reshape(slots, width),
        d_sent.reshape(slots, width),
        resid,
        inverse_two,
        gates,
        hits,
        cotangent,
        routes_t,
        small_full,
        tokens_all,
        inverse_all,
        whole,
        out_full,
        qkv_full,
        query,
        key_rows,
        value,
        attended,
        log_total,
        cosine,
        sine,
        grad_gate_up,
    )
    (
        grad_gate_up,
        grad_down,
        grad_tokens,
        output,
        grad_qkv,
        grad_out,
        gain_one,
        gain_two,
        router,
    ) = finish_call(gate_got, grad_down, grad_tokens, output, grad_weights, small_own, group)
    return (
        output,
        grad_tokens,
        grad_qkv,
        grad_out,
        gain_one.reshape(piece),
        gain_two.reshape(piece),
        router.T,
        grad_gate_up,
        grad_down,
    )


def solution(mesh):
    placed = (
        P(("dp", "expert"), None),
        P(None, "dp", "expert"),
        P("expert", "dp"),
        P("dp"),
        P("dp"),
        P("dp", None),
        P("expert", "dp", None),
        P("expert", "dp", None),
        P("dp"),
        P(("dp", "expert"), None),
        P(("dp", "expert")),
        P(("dp", "expert"), None),
    )
    split = mesh.shape["dp"] == 8 and mesh.shape["expert"] == 4
    return jax.shard_map(
        on_device_split if split else on_device,
        mesh=mesh,
        in_specs=placed,
        out_specs=(
            P(("dp", "expert"), None),
            P(("dp", "expert"), None),
            P(None, "dp", "expert"),
            P("expert", "dp"),
            P("dp"),
            P("dp"),
            P("dp", None),
            P("expert", "dp", None),
            P("expert", "dp", None),
        ),
        check_vma=False,
    )
```

```python
import functools

import jax
import jax.numpy as jnp
import numpy as np
from jax import lax
from jax.experimental import pallas as pl
from jax.experimental.pallas import tpu as pltpu
from jax.sharding import PartitionSpec as P

HEAD_DIM = 128
FF = 5632


NORM_EPSILON = 1e-05
NEGATIVE = -1e30
THETA = 10000.0
HIGH = lax.Precision.HIGHEST
MESH_ID = pl.DeviceIdType.MESH
LANES = 128


def remote(src, dst, send_sem, recv_sem, peer):
    return pltpu.make_async_remote_copy(
        src_ref=src,
        dst_ref=dst,
        send_sem=send_sem,
        recv_sem=recv_sem,
        device_id=peer,
        device_id_type=MESH_ID,
    )


def greet(peers):
    barrier = pltpu.get_barrier_semaphore()
    for peer in peers:
        pl.semaphore_signal(barrier, inc=1, device_id=peer, device_id_type=MESH_ID)
    pl.semaphore_wait(barrier, len(peers))


def dot_nn(left, right):
    return jnp.dot(left, right, preferred_element_type=jnp.float32)


def dot_nt(left, right):
    return lax.dot_general(
        left, right, (((1,), (1,)), ((), ())), preferred_element_type=jnp.float32
    )


def experts_kernel(
    group,
    sent,
    d_back,
    w_gate_up,
    w_got,
    w_down,
    ret,
    d_ret,
    grad_gate_up,
    grad_down,
    w_buf,
    down_buf,
    rows_buf,
    gate_buf,
    act_buf,
    part_buf,
    half_x,
    half_y,
    full_x,
    full_y,
    other_gate,
    other_down,
    ag_sems,
    rs_sems,
    weight_sems,
    local_sems,
    grad_sems,
):
    cap, width = sent.shape[1], sent.shape[2]
    half = cap // 2
    piece, hidden2 = w_got.shape[1:]
    hidden = hidden2 // 2
    down_own = w_down.at[0]
    down_rows = down_own.shape[0]
    chunk = 4 * cap
    total = group * chunk

    index = lax.axis_index("dp")
    place = lax.axis_index("expert")
    core = index % 2
    at_x = (index // 2) % 2
    at_y = index // 4
    partner = {"dp": at_y * 4 + at_x * 2 + (1 - core)}
    along_x = {"dp": at_y * 4 + (1 - at_x) * 2 + core}
    along_y = {"dp": (1 - at_y) * 4 + at_x * 2 + core}
    chips = [
        at_y * 2 + at_x,
        at_y * 2 + (1 - at_x),
        (1 - at_y) * 2 + at_x,
        (1 - at_y) * 2 + (1 - at_x),
    ]

    def ahead(k):
        return {"expert": (place + k) % group}

    def behind(k):
        return {"expert": (place + group - k) % group}

    greet([partner, along_x, along_y] + [ahead(k) for k in range(1, group)])

    def block(t, k, r, start=0, size=None):
        size = cap if size is None else size
        return rows_buf.at[t, pl.ds((k * 4 + r) * cap + start, size), :]

    def part(t, k, r, start=0, size=None):
        size = cap if size is None else size
        return part_buf.at[t, pl.ds((k * 4 + r) * cap + start, size), :]

    def ag(kind, t, k):
        return ag_sems.at[0, kind, t, k], ag_sems.at[1, kind, t, k]

    def rs(kind, t, k):
        return rs_sems.at[0, kind, t, k], rs_sems.at[1, kind, t, k]

    sources = (sent, d_back)
    results = (ret, d_ret)

    def z_copy(t, k):
        return remote(sources[t].at[k], block(t, k, 0), *ag(0, t, k), ahead(k))

    def own_copy(t):
        return pltpu.make_async_copy(sources[t].at[0], block(t, 0, 0), local_sems.at[t])

    def x_copy(t, k):
        return remote(block(t, k, 0), block(t, k, 1), *ag(1, t, k), along_x)

    def y_copy(t, k):
        return remote(block(t, k, 0), block(t, k, 2), *ag(2, t, k), along_y)

    def a_copy(t, k):
        return remote(block(t, k, 2, 0, half), block(t, k, 3, 0, half), *ag(3, t, k), along_x)

    def b_copy(t, k):
        return remote(
            block(t, k, 1, half, half), block(t, k, 3, half, half), *ag(4, t, k), along_y
        )

    def spread(t, k):
        if k == 0:
            own_copy(t).wait()
        else:
            z_copy(t, k).wait_recv()
        x_copy(t, k).start()
        y_copy(t, k).start()

    def relay_a(t, k):
        y_copy(t, k).wait_recv()
        a_copy(t, k).start()

    def relay_b(t, k):
        x_copy(t, k).wait_recv()
        b_copy(t, k).start()

    def arrived(t, k):
        a_copy(t, k).wait_recv()
        b_copy(t, k).wait_recv()
        if t == 0 and k == 0:
            for r in range(4):
                for copy in w_keep(r):
                    copy.wait()
                for copy in w_share(r, 1 - core):
                    copy.wait_recv()
            down_keep.wait()
            down_share().wait_recv()

    def half_x_copy(t, k):
        return remote(part(t, k, 3, 0, half), half_x.at[t, k], *rs(0, t, k), along_x)

    def half_y_copy(t, k):
        return remote(part(t, k, 3, half, half), half_y.at[t, k], *rs(1, t, k), along_y)

    def full_x_copy(t, k):
        return remote(part(t, k, 1), full_x.at[t, k], *rs(2, t, k), along_x)

    def full_y_copy(t, k):
        return remote(part(t, k, 2), full_y.at[t, k], *rs(3, t, k), along_y)

    def back_copy(t, k):
        return remote(part(t, k, 0), results[t].at[k], *rs(4, t, k), behind(k))

    def keep_copy(t):
        return pltpu.make_async_copy(part(t, 0, 0), results[t].at[0], local_sems.at[2 + t])

    def halves_out(t, k):
        half_x_copy(t, k).start()
        half_y_copy(t, k).start()

    def add_into(target, *others):
        value = target[...].astype(jnp.float32)
        for other in others:
            value = value + other[...].astype(jnp.float32)
        target[...] = value.astype(jnp.bfloat16)

    def full_y_out(t, k):
        half_x_copy(t, k).wait_recv()
        add_into(part(t, k, 2, 0, half), half_x.at[t, k])
        full_y_copy(t, k).start()

    def full_x_out(t, k):
        half_y_copy(t, k).wait_recv()
        add_into(part(t, k, 1, half, half), half_y.at[t, k])
        full_x_copy(t, k).start()

    def home(t, k):
        full_x_copy(t, k).wait_recv()
        full_y_copy(t, k).wait_recv()
        add_into(part(t, k, 0), full_x.at[t, k], full_y.at[t, k])
        if k == 0:
            keep_copy(t).start()
        else:
            back_copy(t, k).start()

    def w_rows(r, which):
        return pl.ds(pl.multiple_of((chips[r] * 2 + which) * piece, piece), piece)

    def w_parts(r, which):
        rows = w_rows(r, which)
        if r > 0:
            return [(w_got.at[r - 1], w_buf.at[rows, :], r)]
        return [
            (
                w_gate_up.at[
                    0, :, pl.ds(pl.multiple_of((4 * part + chips[0]) * hidden, LANES), hidden)
                ],
                w_buf.at[rows, pl.ds(part * hidden, hidden)],
                4 * part,
            )
            for part in range(2)
        ]

    def w_share(r, which):
        return [
            remote(source, target, weight_sems.at[0, n], weight_sems.at[1, n], partner)
            for source, target, n in w_parts(r, which)
        ]

    def w_keep(r):
        return [
            pltpu.make_async_copy(source, target, local_sems.at[4 + n])
            for source, target, n in w_parts(r, core)
        ]

    def down_at(which):
        return down_buf.at[pl.ds(pl.multiple_of(which * down_rows, down_rows), down_rows), :]

    def down_share():
        return remote(
            down_own, down_at(core), weight_sems.at[0, 5], weight_sems.at[1, 5], partner
        )

    down_keep = pltpu.make_async_copy(down_own, down_at(core), local_sems.at[9])

    def take(steps, k, number):
        for at in range(group):
            if (at, number) in steps:

                @pl.when(k == at)
                def _(events=steps[at, number]):
                    for event, t, which in events:
                        event(t, which)

    blocks = hidden // LANES
    spans = [(2 * j, min(2, blocks - 2 * j)) for j in range((blocks + 1) // 2)]
    tiles = width // (2 * LANES)

    def span(first, count):
        return pl.ds(first * LANES, count * LANES)

    def forward(k, carry):
        at = pl.ds(pl.multiple_of(k * chunk, chunk), chunk)

        def tile(first, count):
            gate_cols, up_cols = span(first, count), span(blocks + first, count)
            rows = rows_buf[0, at, :]
            if count == 1:
                weights = jnp.concatenate([w_buf[:, gate_cols], w_buf[:, up_cols]], axis=1)
                both = dot_nn(rows, weights)
                gate, up = both[:, :LANES], both[:, LANES:]
            else:
                gate = dot_nn(rows, w_buf[:, gate_cols])
                up = dot_nn(rows, w_buf[:, up_cols])
            sigmoid = 1.0 / (1.0 + jnp.exp(-gate))
            gate_buf[at, gate_cols] = gate.astype(jnp.bfloat16)
            gate_buf[at, up_cols] = up.astype(jnp.bfloat16)
            act_buf[at, gate_cols] = (gate * sigmoid * up).astype(jnp.bfloat16)

        take(forward_steps, k, 0)
        for first, count in spans[:3]:
            tile(first, count)
        take(forward_steps, k, 1)
        for first, count in spans[3:]:
            tile(first, count)
        take(forward_steps, k, 2)
        for j in range(tiles):
            cols = span(2 * j, 2)
            out = dot_nn(act_buf[at, :], down_buf[:, cols])
            part_buf[0, at, cols] = out.astype(jnp.bfloat16)
        return carry

    def backward(turn, carry):
        k = (turn + 1) % group
        at = pl.ds(pl.multiple_of(k * chunk, chunk), chunk)
        take(backward_steps, k, 0)
        for first, count in spans:
            gate_cols, up_cols = span(first, count), span(blocks + first, count)
            d_act = dot_nt(rows_buf[1, at, :], down_buf[gate_cols, :])
            gate = gate_buf[at, gate_cols].astype(jnp.float32)
            up = gate_buf[at, up_cols].astype(jnp.float32)
            sigmoid = 1.0 / (1.0 + jnp.exp(-gate))
            scaled = d_act * sigmoid
            d_gate = scaled * up * (1.0 + gate * (1.0 - sigmoid))
            gate_buf[at, gate_cols] = d_gate.astype(jnp.bfloat16)
            gate_buf[at, up_cols] = (scaled * gate).astype(jnp.bfloat16)
        for side in range(2):
            take(backward_steps, k, 1 + side)
            for j in range(side * (tiles // 2), (side + 1) * (tiles // 2)):
                cols = span(2 * j, 2)
                out = dot_nt(gate_buf[at, :], w_buf[cols, :])
                part_buf[1, at, cols] = out.astype(jnp.bfloat16)
        return carry

    forward_steps = {
        (0, 0): [(spread, 0, 0), (spread, 1, 0), (relay_a, 0, 0), (relay_b, 0, 0), (spread, 0, 1), (relay_a, 1, 0), (relay_b, 1, 0), (arrived, 0, 0)],
        (0, 2): [(spread, 0, 2)],
        (1, 0): [(relay_a, 0, 1), (relay_b, 0, 1), (spread, 0, 3), (halves_out, 0, 0), (relay_a, 0, 2), (relay_b, 0, 2), (spread, 1, 1), (arrived, 0, 1)],
        (2, 0): [(relay_a, 0, 3), (relay_b, 0, 3), (halves_out, 0, 1), (spread, 1, 2), (arrived, 0, 2)],
        (2, 1): [(spread, 1, 3)],
        (3, 0): [(relay_a, 1, 1), (arrived, 0, 3)],
        (3, 1): [(relay_b, 1, 1), (full_y_out, 0, 0)],
    }
    backward_steps = {
        (0, 0): [(home, 0, 2), (halves_out, 1, 3), (arrived, 1, 0)],
        (0, 2): [(home, 0, 3), (full_y_out, 1, 2), (full_x_out, 1, 2)],
        (1, 0): [(full_x_out, 0, 0), (full_y_out, 0, 1), (relay_a, 1, 2), (relay_b, 1, 2), (relay_a, 1, 3), (relay_b, 1, 3), (arrived, 1, 1)],
        (1, 1): [(full_x_out, 0, 1), (halves_out, 0, 2)],
        (1, 2): [(halves_out, 0, 3), (home, 0, 0)],
        (2, 0): [(halves_out, 1, 1), (arrived, 1, 2)],
        (2, 2): [(home, 0, 1), (full_y_out, 0, 2), (full_x_out, 0, 2)],
        (3, 0): [(full_y_out, 0, 3), (full_x_out, 0, 3), (halves_out, 1, 2), (arrived, 1, 3)],
        (3, 1): [(full_y_out, 1, 1)],
        (3, 2): [(full_x_out, 1, 1)],
    }
    grad_steps = {
        (1, 0): [(halves_out, 1, 0)],
        (2, 0): [(full_y_out, 1, 3), (full_x_out, 1, 3), (home, 1, 1)],
        (2, 2): [(home, 1, 2)],
        (2, 3): [(full_y_out, 1, 0), (full_x_out, 1, 0)],
        (4, 0): [(home, 1, 3)],
        (4, 2): [(home, 1, 0)],
    }

    own_copy(0).start()
    for k in range(1, group):
        z_copy(0, k).start()
    for r in range(4):
        for copy in w_share(r, core) + w_keep(r):
            copy.start()
    down_share().start()
    down_keep.start()
    own_copy(1).start()

    for k in range(1, group):
        z_copy(1, k).start()

    lax.fori_loop(0, group, forward, 0)
    lax.fori_loop(0, group, backward, 0)
    for event, t, which in grad_steps.get((0, 0), []):
        event(t, which)

    act_t = down_buf.at[:, pl.ds(0, total)]
    rows_t = down_buf.at[pl.ds(0, piece), pl.ds(total, total)]
    send_down = w_buf.at[pl.ds(4 * piece, down_rows), pl.ds(0, width)]

    def send_gate(r):
        return w_buf.at[pl.ds(pl.multiple_of(r * piece, piece), piece), :]

    def turn(j, carry):
        lanes = pl.ds(pl.multiple_of(j * LANES, LANES), LANES)
        act_t[lanes, :] = act_buf[:, lanes].T
        return carry

    lax.fori_loop(0, blocks, turn, 0)

    def pair_span(j):
        return pl.ds(pl.multiple_of(j * 2 * LANES, 2 * LANES), 2 * LANES)

    def down_grad(which, j):
        rows = pl.ds(pl.multiple_of(which * down_rows, down_rows), down_rows)
        return dot_nn(act_t[rows, :], rows_buf[1, :, pair_span(j)])

    def after(steps, number, r):
        turns = {(turn, 0): events for (stage, turn), events in steps.items() if stage == number}
        take(turns, r, 0)

    after(grad_steps, 1, 0)
    def down_for_partner(j, carry):
        send_down[:, pair_span(j)] = down_grad(1 - core, j).astype(jnp.bfloat16)
        return carry

    lax.fori_loop(0, tiles, down_for_partner, 0)
    down_send = remote(
        send_down, other_down, grad_sems.at[0, 4], grad_sems.at[1, 4], partner
    )
    down_send.start()

    def turned_rows(r, which):
        step_y = r // 2
        step_x = r % 2
        chip = (at_y + step_y - 2 * at_y * step_y) * 2 + (at_x + step_x - 2 * at_x * step_x)
        start = pl.multiple_of((chip * 2 + which) * piece, piece)
        rows_t[...] = rows_buf[0, :, pl.ds(start, piece)].T

    def gate_send(r):
        return remote(
            send_gate(r), other_gate.at[r], grad_sems.at[0, r], grad_sems.at[1, r], partner
        )

    def gate_for_partner(r, carry):
        after(grad_steps, 2, r)
        turned_rows(r, 1 - core)
        target = send_gate(r)
        for j in range(blocks):
            cols = span(2 * j, 2)
            target[:, cols] = dot_nn(rows_t[...], gate_buf[:, cols]).astype(jnp.bfloat16)
        gate_send(r).start()
        return carry

    lax.fori_loop(0, 4, gate_for_partner, 0)
    after(grad_steps, 3, 0)
    down_send.wait_recv()

    def down_for_self(j, carry):
        cols = pair_span(j)
        value = down_grad(core, j) + other_down[:, cols].astype(jnp.float32)
        other_down[:, cols] = value.astype(jnp.bfloat16)
        return carry

    lax.fori_loop(0, tiles, down_for_self, 0)
    down_out = pltpu.make_async_copy(other_down, grad_down, grad_sems.at[2, 0])
    down_out.start()

    def gate_out(r):
        return pltpu.make_async_copy(other_gate.at[r], grad_gate_up.at[r], grad_sems.at[2, 2 + r])

    def gate_for_self(r, carry):
        after(grad_steps, 4, r)
        gate_send(r).wait_recv()
        turned_rows(r, core)
        target = other_gate.at[r]
        for j in range(blocks):
            cols = span(2 * j, 2)
            value = dot_nn(rows_t[...], gate_buf[:, cols])
            target[:, cols] = (value + target[:, cols].astype(jnp.float32)).astype(jnp.bfloat16)
        gate_out(r).start()
        return carry

    lax.fori_loop(0, 4, gate_for_self, 0)
    after(grad_steps, 5, 0)

    down_out.wait()
    for r in range(4):
        gate_out(r).wait()
        gate_send(r).wait_send()
        for copy in w_share(r, core):
            copy.wait_send()
    down_share().wait_send()
    down_send.wait_send()
    for t in range(2):
        keep_copy(t).wait()
        for k in range(group):
            x_copy(t, k).wait_send()
            y_copy(t, k).wait_send()
            a_copy(t, k).wait_send()
            b_copy(t, k).wait_send()
            half_x_copy(t, k).wait_send()
            half_y_copy(t, k).wait_send()
            full_x_copy(t, k).wait_send()
            full_y_copy(t, k).wait_send()
            if k > 0:
                z_copy(t, k).wait_send()
                back_copy(t, k).wait_send()
                back_copy(t, k).wait_recv()


def experts_call(sent, d_back, w_gate_up, w_got, w_down):
    group, cap, width = sent.shape
    piece, hidden2 = w_got.shape[1:]
    hidden = hidden2 // 2
    down_rows = w_down.shape[1]
    chunk = 4 * cap
    total = group * chunk
    low = jnp.bfloat16
    anywhere = pl.BlockSpec(memory_space=pl.ANY)
    flops = 2 * total * width * hidden * 9
    moved = 2 * (4 * piece * hidden2 * 2 + down_rows * width * 3)
    return pl.pallas_call(
        functools.partial(experts_kernel, group),
        out_shape=(
            jax.ShapeDtypeStruct((group, cap, width), low),
            jax.ShapeDtypeStruct((group, cap, width), low),
            jax.ShapeDtypeStruct((4, piece, hidden2), low),
            jax.ShapeDtypeStruct((down_rows, width), low),
        ),
        in_specs=[anywhere] * 5,
        out_specs=(anywhere,) * 4,
        scratch_shapes=[
            pltpu.VMEM((width, hidden2), low),
            pltpu.VMEM((hidden, width), low),
            pltpu.VMEM((2, total, width), low),
            pltpu.VMEM((total, hidden2), low),
            pltpu.VMEM((total, hidden), low),
            pltpu.VMEM((2, total, width), low),
            pltpu.VMEM((2, group, cap // 2, width), low),
            pltpu.VMEM((2, group, cap // 2, width), low),
            pltpu.VMEM((2, group, cap, width), low),
            pltpu.VMEM((2, group, cap, width), low),
            pltpu.VMEM((4, piece, hidden2), low),
            pltpu.VMEM((down_rows, width), low),
            pltpu.SemaphoreType.DMA((2, 5, 2, group)),
            pltpu.SemaphoreType.DMA((2, 5, 2, group)),
            pltpu.SemaphoreType.DMA((2, 6)),
            pltpu.SemaphoreType.DMA((10,)),
            pltpu.SemaphoreType.DMA((3, 6)),
        ],
        compiler_params=pltpu.CompilerParams(
            collective_id=1, has_side_effects=True, vmem_limit_bytes=67043328
        ),
        cost_estimate=pl.CostEstimate(flops=flops, bytes_accessed=moved, transcendentals=0),
        name="experts",
    )(sent, d_back, w_gate_up, w_got, w_down)


def rotary_tables(length_total, head_size):
    position = jnp.arange(length_total, dtype=jnp.float32)
    frequency = THETA ** (-(jnp.arange(head_size // 2, dtype=jnp.float32) * 2.0 / head_size))
    angles = position[:, None] * frequency[None, :]
    return (jnp.cos(angles)[:, None, :], jnp.sin(angles)[:, None, :])


def rotate(values, cosine, sine):
    half_size = values.shape[-1] // 2
    first = values[..., :half_size]
    second = values[..., half_size:]
    return jnp.concatenate(
        [first * cosine - second * sine, second * cosine + first * sine], axis=-1
    )


def rotate_back(grad_rows, cosine, sine):
    half_size = grad_rows.shape[-1] // 2
    first = grad_rows[..., :half_size]
    second = grad_rows[..., half_size:]
    return jnp.concatenate(
        [first * cosine + second * sine, second * cosine - first * sine], axis=-1
    )


def slot_table(routes, order, valid, capacity):
    row_count = routes.shape[0]
    top_count = routes.shape[1]
    pair_rank = order[:, None] + row_count * jnp.arange(top_count, dtype=jnp.int32)[None, :]
    flat_rank = pair_rank.reshape(-1)
    flat_expert = routes.reshape(-1)
    flat_valid = jnp.broadcast_to(valid[:, None], routes.shape).reshape(-1)
    earlier = (
        (flat_rank[None, :] < flat_rank[:, None])
        & (flat_expert[None, :] == flat_expert[:, None])
        & flat_valid[None, :]
    )
    slot_index = jnp.sum(earlier.astype(jnp.int32), axis=1).reshape(row_count, top_count)
    kept_pair = valid[:, None] & (slot_index < capacity)
    target = routes * capacity + jnp.minimum(slot_index, capacity - 1)
    return (target, kept_pair)


def masked_scores(query, key_rows, allowed):
    scale = query.shape[-1] ** (-0.5)
    raw = jnp.einsum("qhd,khd->hqk", query, key_rows, preferred_element_type=jnp.float32) * scale
    return jnp.where(allowed[None], raw, NEGATIVE)


def contract_first(left, right):
    return lax.dot_general(
        left, right, (((0,), (0,)), ((), ())), preferred_element_type=jnp.float32
    )


def contract_last(left, right):
    return lax.dot_general(
        left, right, (((1,), (1,)), ((), ())), preferred_element_type=jnp.float32
    )


def normalize(rows):
    inverse = lax.rsqrt(jnp.mean(rows * rows, axis=-1, keepdims=True) + NORM_EPSILON)
    return rows * inverse, inverse


def exchange_experts(blocks):
    return lax.all_to_all(blocks, "expert", split_axis=0, concat_axis=0, tiled=True)


def line_order(place, step):
    upper = place // 2
    low = place * (1 - upper) + (3 - place) * upper
    first = 1 - (step + 1) // 2
    block = step + first * (1 - low) + (1 - first)
    return block * (1 - upper) + (3 - block) * upper


def rotated(grad, cosine, sine):
    return grad * cosine + pltpu.roll(grad, grad.shape[1] // 2, 1) * sine


def attention_back_kernel(
    heads,
    length,
    returned,
    d_sent,
    resid,
    inverse_two,
    gates,
    hits,
    cotangent,
    routes_t,
    small_full,
    tokens_all,
    inverse_all,
    whole,
    w_out,
    w_qkv,
    query,
    key_rows,
    value,
    attended,
    log_total,
    cosine,
    sine,
    gate_grads,
    output,
    grad_tokens,
    grad_weights,
    small_out,
    gate_got,
    returned_buf,
    d_sent_buf,
    resid_buf,
    inverse_two_buf,
    gates_buf,
    hits_buf,
    cotangent_buf,
    rows_buf,
    small_full_buf,
    da_buf,
    tokens_buf,
    inverse_buf,
    whole_buf,
    w_out_buf,
    w_qkv_buf,
    query_buf,
    key_buf,
    value_buf,
    attended_buf,
    log_buf,
    cosine_buf,
    sine_buf,
    d_key_acc,
    d_value_acc,
    d_proj,
    normed_part,
    from_left,
    from_right,
    send_pair,
    recv_pair,
    own_part,
    half_x,
    half_y,
    full_x,
    full_y,
    small_buf,
    small_recv,
    small_z,
    keep_buf,
    sum_buf,
    load_sems,
    line_sems,
    sum_sems,
    pair_sems,
    ring_sems,
    small_sems,
    gate_sems,
):
    tok, width = cotangent.shape
    seq_len = tokens_all.shape[0]
    group = seq_len // tok
    local_width = w_out.shape[0]
    head_size = local_width // heads
    piece = own_part.shape[1]
    half = piece // 2
    scale = head_size**-0.5

    index = lax.axis_index("dp")
    place = lax.axis_index("expert")
    core = index % 2
    at_x = (index // 2) % 2
    at_y = index // 4
    partner = {"dp": at_y * 4 + at_x * 2 + (1 - core)}
    along_x = {"dp": at_y * 4 + (1 - at_x) * 2 + core}
    along_y = {"dp": (1 - at_y) * 4 + at_x * 2 + core}
    over = {"dp": (1 - at_y) * 4 + (1 - at_x) * 2 + core}
    parts = width // piece

    def chip(r):
        step_y = r // 2
        step_x = r % 2
        return (at_y + step_y - 2 * at_y * step_y) * 2 + (at_x + step_x - 2 * at_x * step_x)

    def ring_peer(k):
        return {"dp": (index + k) % parts}

    def line_peer(k):
        return {"expert": (place + k) % group}

    right = {"expert": (place + 1) % group}
    left = {"expert": (place + group - 1) % group}

    loads = [
        pltpu.make_async_copy(source, target, load_sems.at[number])
        for number, (source, target) in enumerate(
            [
                (returned, returned_buf),
                (hits, hits_buf),
                (cotangent, cotangent_buf),
                (resid, resid_buf),
                (inverse_two, inverse_two_buf),
                (gates, gates_buf),
                (routes_t, rows_buf),
                (small_full, small_full_buf),
                (d_sent, d_sent_buf),
                (w_out, w_out_buf),
                (query, query_buf),
                (key_rows, key_buf),
                (value, value_buf),
                (log_total, log_buf),
                (cosine, cosine_buf),
                (sine, sine_buf),
                (w_qkv, w_qkv_buf),
                (tokens_all, tokens_buf),
                (inverse_all, inverse_buf),
                (whole, whole_buf),
                (attended, attended_buf),
                (gate_grads.at[0], keep_buf),
            ]
        )
    ]
    first = 9
    early = first + 7
    for load in loads[:early]:
        load.start()

    greet([ring_peer(k) for k in range(1, parts)] + [line_peer(k) for k in range(1, group)])

    def rows_of(block):
        return pl.ds(pl.multiple_of(block * tok, tok), tok)

    def pass_right(block):
        spot = da_buf.at[rows_of(block)]
        return remote(spot, spot, line_sems.at[0, block], line_sems.at[2, block], right)

    def pass_left(block):
        spot = da_buf.at[rows_of(block)]
        return remote(spot, spot, line_sems.at[1, block], line_sems.at[2, block], left)

    def gate_copy(r, peer):
        return remote(
            gate_grads.at[r], gate_got.at[r], gate_sems.at[0, r], gate_sems.at[1, r], peer
        )

    peers = (None, along_x, along_y, over)
    for r in (3, 1, 2):
        gate_copy(r, peers[r]).start()
    for load in loads[early:]:
        load.start()
    for load in loads[:first]:
        load.wait()

    at = place * tok + lax.broadcasted_iota(jnp.int32, (tok, 1), 0)
    live = jnp.where(at < length[0], 1.0, 0.0)
    d_out = live * cotangent_buf[...].astype(jnp.float32)
    total = resid_buf[...]
    hhat = total * inverse_two_buf[...]
    gate = [gates_buf[:, number : number + 1] for number in range(2)]
    d_gate = []
    for number in range(2):
        picked = dot_nn(hits_buf[number].T, returned_buf[...])
        d_gate.append(jnp.sum(d_out * picked, axis=-1, keepdims=True))
        total = total + gate[number] * picked
    output[...] = (live * total).astype(jnp.bfloat16)
    mixed = gate[0] * d_gate[0] + gate[1] * d_gate[1]
    d_chosen = [gate[number] * (d_gate[number] - mixed) for number in range(2)]
    d_hidden = dot_nn((hits_buf[0] + hits_buf[1]).T, d_sent_buf[...])
    gain_two = small_full_buf[1:2, :]
    hidden_in = (hhat * gain_two).astype(jnp.bfloat16).astype(jnp.float32)
    small_buf[...] = jnp.zeros_like(small_buf)
    square = (tok, tok)
    same = lax.broadcasted_iota(jnp.int32, square, 0) == lax.broadcasted_iota(jnp.int32, square, 1)
    named = []
    for number in range(2):
        row = rows_buf[number : number + 1, :].astype(jnp.float32)
        kept = jnp.where(same, jnp.broadcast_to(row, square), 0.0)
        named.append(jnp.sum(kept, axis=1, keepdims=True).astype(jnp.int32))
    for expert in range(group):
        d_logit = sum(
            jnp.where(named[number] == expert, d_chosen[number], 0.0)
            for number in range(2)
        )
        row = slice(2 + expert, 3 + expert)
        d_hidden = d_hidden + d_logit * small_full_buf[row, :]
        small_buf[row, :] = jnp.sum(d_logit * hidden_in, axis=0, keepdims=True)
    small_buf[1:2, :] = jnp.sum(d_hidden * hhat, axis=0, keepdims=True)
    scaled = d_hidden * gain_two
    shared = jnp.mean(scaled * hhat, axis=-1, keepdims=True)
    d_resid = d_out + inverse_two_buf[...] * (scaled - hhat * shared)
    resid_buf[...] = d_resid
    da_buf[rows_of(place), :] = d_resid.astype(jnp.bfloat16)

    @pl.when(place < group - 1)
    def _():
        pass_right(place).start()

    @pl.when(place > 0)
    def _():
        pass_left(place).start()

    d_key_acc[...] = jnp.zeros_like(d_key_acc)
    d_value_acc[...] = jnp.zeros_like(d_value_acc)

    def attend_back(block):
        rows = rows_of(block)
        d_heads = dot_nt(da_buf[rows, :], w_out_buf[...]).astype(jnp.bfloat16)
        shape = (tok, seq_len)
        at_query = block * tok + lax.broadcasted_iota(jnp.int32, shape, 0)
        at_key = lax.broadcasted_iota(jnp.int32, shape, 1)
        allowed = (at_key <= at_query) & (at_key < length[0])
        for head in range(heads):
            cols = slice(head * head_size, (head + 1) * head_size)
            one_query = query_buf[rows, cols]
            one_key = key_buf[:, cols]
            d_head = d_heads[:, cols]
            scores = jnp.where(allowed, dot_nt(one_query, one_key) * scale, NEGATIVE)
            probs = jnp.exp(scores - log_buf[rows, head : head + 1])
            d_probs = dot_nt(d_head, value_buf[:, cols])
            delta = jnp.sum(probs * d_probs, axis=-1, keepdims=True)
            d_scores = (probs * (d_probs - delta)).astype(jnp.bfloat16)
            d_query = dot_nn(d_scores, one_key) * scale
            d_key_acc[:, cols] += dot_nn(d_scores.T, one_query) * scale
            d_value_acc[:, cols] += dot_nn(probs.astype(jnp.bfloat16).T, d_head)
            d_proj[rows, cols] = rotated(d_query, cosine_buf[rows, :], -sine_buf[rows, :]).astype(
                jnp.bfloat16
            )

    for load in loads[first:early]:
        load.wait()

    def arrive(step, carry):
        later = (step + group - 2) // (group - 1)
        block = place * (1 - later) + line_order(place, step - later) * later

        @pl.when(step > 0)
        def _():
            pass_right(block).wait_recv()

        @pl.when((block < place) & (place < group - 1))
        def _():
            pass_right(block).start()

        @pl.when((block > place) & (place > 0))
        def _():
            pass_left(block).start()

        attend_back(block)
        return carry

    lax.fori_loop(0, group, arrive, 0)
    for load in loads[early:]:
        load.wait()
    keep = pltpu.make_async_copy(keep_buf, gate_got.at[0], load_sems.at[22])
    keep.start()

    for head in range(heads):
        cols = slice(head * head_size, (head + 1) * head_size)
        key_cols = slice(local_width + head * head_size, local_width + (head + 1) * head_size)
        d_proj[:, key_cols] = rotated(d_key_acc[:, cols], cosine_buf[...], -sine_buf[...]).astype(
            jnp.bfloat16
        )
    d_proj[:, 2 * local_width :] = d_value_acc[...].astype(jnp.bfloat16)

    def normed_tile(j, carry):
        cols = pl.ds(pl.multiple_of(j * piece, piece), piece)
        d_normed = jnp.zeros((seq_len, piece), jnp.float32)
        for c in range(3):
            d_normed += dot_nt(
                d_proj[:, c * local_width : (c + 1) * local_width], w_qkv_buf[c, cols, :]
            )
        hat = tokens_buf[:, cols].astype(jnp.float32) * inverse_buf[...]
        small_buf[0:1, cols] = jnp.sum(d_normed * hat, axis=0, keepdims=True)
        normed_part[:, cols] = d_normed.astype(jnp.bfloat16)
        return carry

    lax.fori_loop(0, parts, normed_tile, 0)

    def go_right(block):
        return remote(
            normed_part.at[pl.ds(block * tok, tok)],
            from_left.at[block],
            sum_sems.at[0, block],
            sum_sems.at[1, block],
            right,
        )

    def go_left(block):
        return remote(
            normed_part.at[pl.ds(block * tok, tok)],
            from_right.at[block],
            sum_sems.at[0, block],
            sum_sems.at[2, block],
            left,
        )

    def add_into(target, other):
        value = target[...].astype(jnp.float32) + other[...].astype(jnp.float32)
        target[...] = value.astype(jnp.bfloat16)

    def on_right(block):
        go_right(block).wait_recv()
        add_into(normed_part.at[pl.ds(block * tok, tok)], from_left.at[block])
        go_right(block).start()

    def on_left(block):
        go_left(block).wait_recv()
        add_into(normed_part.at[pl.ds(block * tok, tok)], from_right.at[block])
        go_left(block).start()

    @pl.when(place == 0)
    def _():
        for block in (3, 2, 1):
            go_right(block).start()

    @pl.when(place == 3)
    def _():
        for block in (0, 1, 2):
            go_left(block).start()

    def small_copy(k):
        to = (index + k) % parts
        cols = pl.ds(pl.multiple_of(to * piece, piece), piece)
        return remote(
            small_buf.at[:, cols],
            small_recv.at[k],
            small_sems.at[0, k],
            small_sems.at[1, k],
            ring_peer(k),
        )

    for k in range(1, parts):
        small_copy(k).start()

    def weight_grad(which, r):
        cols = pl.ds(pl.multiple_of((chip(r) * 2 + which) * piece, piece), piece)
        left_side = whole_buf[:, cols].T
        first = dot_nn(left_side, d_proj[...])
        second = dot_nn(da_buf[:, cols].T, attended_buf[...])
        return jnp.concatenate([first, second], axis=1)

    def pair_copy(r):
        return remote(
            send_pair.at[r], recv_pair.at[r], pair_sems.at[0, r], pair_sems.at[1, r], partner
        )

    def for_partner(i, carry):
        r = 3 - i
        send_pair[r] = weight_grad(1 - core, r).astype(jnp.bfloat16)
        pair_copy(r).start()
        return carry

    lax.fori_loop(0, 4, for_partner, 0)

    @pl.when(place == 1)
    def _():
        on_right(3)

    @pl.when(place == 2)
    def _():
        on_left(0)

    def half_x_copy():
        return remote(
            own_part.at[3, pl.ds(0, half)], half_x, ring_sems.at[0, 0], ring_sems.at[1, 0], along_x
        )

    def half_y_copy():
        return remote(
            own_part.at[3, pl.ds(half, half)],
            half_y,
            ring_sems.at[0, 1],
            ring_sems.at[1, 1],
            along_y,
        )

    def full_x_copy():
        return remote(own_part.at[1], full_x, ring_sems.at[0, 2], ring_sems.at[1, 2], along_x)

    def full_y_copy():
        return remote(own_part.at[2], full_y, ring_sems.at[0, 3], ring_sems.at[1, 3], along_y)

    def for_self(i, carry):
        r = 3 - i
        pair_copy(r).wait_recv()
        own_part[r] = (weight_grad(core, r) + recv_pair[r].astype(jnp.float32)).astype(
            jnp.bfloat16
        )

        @pl.when(i == 0)
        def _():
            half_x_copy().start()
            half_y_copy().start()

        return carry

    lax.fori_loop(0, 4, for_self, 0)

    total = small_buf[:, pl.ds(pl.multiple_of(index * piece, piece), piece)]
    for k in range(1, parts):
        small_copy(k).wait_recv()
        total = total + small_recv[k]
    small_z[0] = total

    @pl.when(place == 1)
    def _():
        on_right(2)

    @pl.when(place == 2)
    def _():
        on_left(1)

    def small_line_copy(k):
        return remote(
            small_z.at[0],
            small_z.at[k],
            small_sems.at[0, parts + k],
            small_sems.at[1, parts + k],
            line_peer(k),
        )

    for k in range(1, group):
        small_line_copy(k).start()

    half_x_copy().wait_recv()
    add_into(own_part.at[2, pl.ds(0, half)], half_x)
    full_y_copy().start()
    half_y_copy().wait_recv()
    add_into(own_part.at[1, pl.ds(half, half)], half_y)
    full_x_copy().start()

    @pl.when(place == 1)
    def _():
        on_left(0)

    @pl.when(place == 2)
    def _():
        on_right(3)

    total = small_z[0]
    for k in range(1, group):
        small_line_copy(k).wait_recv()
        total = total + small_z[k]
    small_out[...] = total

    sum_buf[...] = normed_part[rows_of(place), :].astype(jnp.float32)

    @pl.when(place > 0)
    def _():
        go_right(place).wait_recv()
        sum_buf[...] += from_left[place].astype(jnp.float32)

    @pl.when(place < group - 1)
    def _():
        go_left(place).wait_recv()
        sum_buf[...] += from_right[place].astype(jnp.float32)

    inverse_one = inverse_buf[rows_of(place), :]
    hat = tokens_buf[rows_of(place), :].astype(jnp.float32) * inverse_one
    scaled = sum_buf[...] * small_full_buf[0:1, :]
    shared = jnp.mean(scaled * hat, axis=-1, keepdims=True)
    grad_tokens[...] = (resid_buf[...] + inverse_one * (scaled - hat * shared)).astype(
        jnp.bfloat16
    )

    full_x_copy().wait_recv()
    full_y_copy().wait_recv()
    grad_weights[...] = (
        own_part[0].astype(jnp.float32)
        + full_x[...].astype(jnp.float32)
        + full_y[...].astype(jnp.float32)
    )

    for r in (1, 2, 3):
        gate_copy(r, peers[r]).wait()
    keep.wait()
    half_x_copy().wait_send()
    half_y_copy().wait_send()
    full_x_copy().wait_send()
    full_y_copy().wait_send()
    for r in range(4):
        pair_copy(r).wait_send()
    for k in range(1, parts):
        small_copy(k).wait_send()
    for k in range(1, group):
        small_line_copy(k).wait_send()
    for block in range(group):

        @pl.when(block > place)
        def _():
            go_right(block).wait_send()

        @pl.when(block < place)
        def _():
            go_left(block).wait_send()

        @pl.when((block <= place) & (place < group - 1))
        def _():
            pass_right(block).wait_send()

        @pl.when((block >= place) & (place > 0))
        def _():
            pass_left(block).wait_send()


def attention_back_call(
    lengths,
    returned,
    d_sent,
    resid,
    inverse_two,
    gates,
    hits,
    cotangent,
    routes_t,
    small_full,
    tokens_all,
    inverse_all,
    whole,
    w_out,
    w_qkv,
    query,
    key_rows,
    value,
    attended,
    log_total,
    cosine,
    sine,
    gate_grads,
):
    tok, width = cotangent.shape
    seq_len = tokens_all.shape[0]
    group = seq_len // tok
    local_width = w_out.shape[0]
    heads = log_total.shape[1]
    piece = gate_grads.shape[1]
    half = piece // 2
    parts = width // piece
    small_rows = small_full.shape[0]
    low, full = jnp.bfloat16, jnp.float32
    anywhere = pl.BlockSpec(memory_space=pl.ANY)
    inside = pl.BlockSpec(memory_space=pltpu.VMEM)

    def like(array):
        return pltpu.VMEM(array.shape, array.dtype)

    flops = 2 * seq_len * width * local_width * 8 + 10 * seq_len * seq_len * local_width
    return pl.pallas_call(
        functools.partial(attention_back_kernel, heads),
        out_shape=(
            jax.ShapeDtypeStruct((tok, width), low),
            jax.ShapeDtypeStruct((tok, width), low),
            jax.ShapeDtypeStruct((piece, 4 * local_width), full),
            jax.ShapeDtypeStruct((small_rows, piece), full),
            jax.ShapeDtypeStruct(gate_grads.shape, low),
        ),
        in_specs=[pl.BlockSpec(memory_space=pltpu.SMEM)] + [anywhere] * 22,
        out_specs=(inside, inside, inside, inside, anywhere),
        scratch_shapes=[
            like(returned),
            like(d_sent),
            like(resid),
            like(inverse_two),
            like(gates),
            like(hits),
            like(cotangent),
            like(routes_t),
            like(small_full),
            pltpu.VMEM((seq_len, width), low),
            like(tokens_all),
            like(inverse_all),
            like(whole),
            like(w_out),
            like(w_qkv),
            like(query),
            like(key_rows),
            like(value),
            like(attended),
            like(log_total),
            like(cosine),
            like(sine),
            pltpu.VMEM((seq_len, local_width), full),
            pltpu.VMEM((seq_len, local_width), full),
            pltpu.VMEM((seq_len, 3 * local_width), low),
            pltpu.VMEM((seq_len, width), low),
            pltpu.VMEM((group, tok, width), low),
            pltpu.VMEM((group, tok, width), low),
            pltpu.VMEM((4, piece, 4 * local_width), low),
            pltpu.VMEM((4, piece, 4 * local_width), low),
            pltpu.VMEM((4, piece, 4 * local_width), low),
            pltpu.VMEM((half, 4 * local_width), low),
            pltpu.VMEM((half, 4 * local_width), low),
            pltpu.VMEM((piece, 4 * local_width), low),
            pltpu.VMEM((piece, 4 * local_width), low),
            like(small_full),
            pltpu.VMEM((parts, small_rows, piece), full),
            pltpu.VMEM((group, small_rows, piece), full),
            pltpu.VMEM(gate_grads.shape[1:], low),
            like(resid),
            pltpu.SemaphoreType.DMA((23,)),
            pltpu.SemaphoreType.DMA((3, group)),
            pltpu.SemaphoreType.DMA((3, group)),
            pltpu.SemaphoreType.DMA((2, 4)),
            pltpu.SemaphoreType.DMA((2, 4)),
            pltpu.SemaphoreType.DMA((2, parts + group)),
            pltpu.SemaphoreType.DMA((2, 4)),
        ],
        compiler_params=pltpu.CompilerParams(
            collective_id=2, has_side_effects=True, vmem_limit_bytes=67043328
        ),
        cost_estimate=pl.CostEstimate(flops=flops, bytes_accessed=40000000, transcendentals=0),
        name="attention_back",
    )(
        lengths,
        returned,
        d_sent,
        resid,
        inverse_two,
        gates,
        hits,
        cotangent,
        routes_t,
        small_full,
        tokens_all,
        inverse_all,
        whole,
        w_out,
        w_qkv,
        query,
        key_rows,
        value,
        attended,
        log_total,
        cosine,
        sine,
        gate_grads,
    )


def finish_kernel(
    gate_got,
    grad_down_low,
    grad_tokens_low,
    output_low,
    grad_weights,
    small,
    grad_gate_up,
    grad_down,
    grad_tokens,
    output,
    grad_qkv,
    grad_out,
    gain_one,
    gain_two,
    router,
    got_buf,
    wide_buf,
    low_buf,
    down_buf,
    tokens_buf,
    output_buf,
    weights_buf,
    out_buf,
    small_buf,
    load_sems,
    store_sems,
):
    chips = gate_got.shape[0]
    size = gate_got.shape[2] // 2
    local_width = grad_qkv.shape[2]
    index = lax.axis_index("dp")
    at_x = (index // 2) % 2
    at_y = index // 4

    def load(number, source, target):
        return pltpu.make_async_copy(source, target, load_sems.at[number])

    loads = [load(r, gate_got.at[r], got_buf.at[r]) for r in range(chips)] + [
        load(4, grad_down_low, low_buf),
        load(5, grad_weights, weights_buf),
        load(6, grad_tokens_low, tokens_buf),
        load(7, output_low, output_buf),
        load(8, small, small_buf),
    ]
    for copy in loads:
        copy.start()
    stores = []

    def store(source, target):
        copy = pltpu.make_async_copy(source, target, store_sems.at[len(stores)])
        copy.start()
        stores.append(copy)

    for r in range(chips):
        loads[r].wait()
        step_y = r // 2
        step_x = r % 2
        chip = (at_y + step_y - 2 * at_y * step_y) * 2 + (at_x + step_x - 2 * at_x * step_x)
        for part in range(2):
            wide_buf[2 * r + part] = got_buf[r, :, part * size : (part + 1) * size].astype(
                jnp.float32
            )
            lanes = pl.ds(pl.multiple_of((part * chips + chip) * size, LANES), size)
            store(wide_buf.at[2 * r + part], grad_gate_up.at[0, :, lanes])
    loads[4].wait()
    down_buf[...] = low_buf[...].astype(jnp.float32)
    store(down_buf, grad_down.at[0])
    loads[5].wait()
    out_buf[...] = weights_buf[:, 3 * local_width :].T
    for c in range(3):
        store(weights_buf.at[:, pl.ds(c * local_width, local_width)], grad_qkv.at[c])
    store(out_buf, grad_out)
    loads[6].wait()
    store(tokens_buf, grad_tokens)
    loads[7].wait()
    store(output_buf, output)
    loads[8].wait()
    gain_one[...] = small_buf[0:1, :]
    gain_two[...] = small_buf[1:2, :]
    router[...] = small_buf[2 : 2 + router.shape[0], :]
    for copy in stores:
        copy.wait()


def finish_call(gate_got, grad_down, grad_tokens, output, grad_weights, small, experts):
    chips, rows, hidden2 = gate_got.shape
    local_width = grad_weights.shape[1] // 4
    full = jnp.float32
    anywhere = pl.BlockSpec(memory_space=pl.ANY)
    out_t = (local_width, rows)

    def like(array, kind=None):
        return pltpu.VMEM(array.shape, kind or array.dtype)

    return pl.pallas_call(
        finish_kernel,
        out_shape=(
            jax.ShapeDtypeStruct((1, rows, chips * hidden2), full),
            jax.ShapeDtypeStruct((1,) + grad_down.shape, full),
            jax.ShapeDtypeStruct(grad_tokens.shape, grad_tokens.dtype),
            jax.ShapeDtypeStruct(output.shape, output.dtype),
            jax.ShapeDtypeStruct((3, rows, local_width), full),
            jax.ShapeDtypeStruct(out_t, full),
            jax.ShapeDtypeStruct((1, rows), full),
            jax.ShapeDtypeStruct((1, rows), full),
            jax.ShapeDtypeStruct((experts, rows), full),
        ),
        in_specs=[anywhere] * 6,
        out_specs=(anywhere,) * 6 + (pl.BlockSpec(memory_space=pltpu.VMEM),) * 3,
        scratch_shapes=[
            like(gate_got),
            pltpu.VMEM((2 * chips, rows, hidden2 // 2), full),
            like(grad_down),
            like(grad_down, full),
            like(grad_tokens),
            like(output),
            like(grad_weights),
            pltpu.VMEM(out_t, full),
            like(small),
            pltpu.SemaphoreType.DMA((9,)),
            pltpu.SemaphoreType.DMA((15,)),
        ],
        compiler_params=pltpu.CompilerParams(vmem_limit_bytes=67043328),
        name="finish",
    )(gate_got, grad_down, grad_tokens, output, grad_weights, small)


def rotary_constants(length_total, head_size):
    low = 32
    steps = np.arange(head_size // 2, dtype=np.float32) * np.float32(2.0) / np.float32(head_size)
    frequency = np.power(np.float32(THETA), -steps).astype(np.float32).astype(np.float64)
    position = np.concatenate([np.arange(0, length_total, low), np.arange(low)])
    angles = position[:, None] * np.concatenate([frequency, frequency])[None, :]
    return np.stack([np.cos(angles), np.sin(angles)]).astype(np.float32)


def attention_kernel(
    heads,
    length,
    tokens,
    w_qkv,
    w_out,
    gain_one,
    gain_two,
    router_t,
    w_gate_up,
    routes_t,
    order_row,
    angles,
    cotangent,
    tokens_all,
    whole,
    qkv_full,
    out_full,
    w_got,
    inverse_all,
    query,
    key_rows,
    value,
    attended,
    log_total,
    small_full,
    cosine_buf,
    sine_buf,
    resid,
    inverse_two,
    gates,
    hits,
    sent,
    d_back,
    tokens_buf,
    whole_buf,
    w_qkv_buf,
    w_out_buf,
    part_buf,
    from_left,
    from_right,
    rows_buf,
    order_buf,
    angles_buf,
    cotangent_buf,
    gain_one_buf,
    gain_two_buf,
    router_buf,
    small,
    load_sems,
    line_sems,
    sum_sems,
    gather_sems,
    small_sems,
    slice_sems,
):
    tok, width = tokens.shape
    seq_len = tokens_buf.shape[0]
    group = seq_len // tok
    local_width = w_out.shape[0]
    head_size = local_width // heads
    piece = w_qkv.shape[1]
    parts = width // piece
    ff = w_gate_up.shape[2] // 2
    hidden = ff // 4
    slots = hits.shape[1]
    cap = slots // group
    scale = head_size**-0.5

    index = lax.axis_index("dp")
    place = lax.axis_index("expert")
    core = index % 2
    at_x = (index // 2) % 2
    at_y = index // 4
    other = at_y * 4 + at_x * 2 + (1 - core)
    by_x = at_y * 4 + (1 - at_x) * 2 + core
    by_y = (1 - at_y) * 4 + at_x * 2 + core
    by_both = (1 - at_y) * 4 + (1 - at_x) * 2 + core
    partner = {"dp": other}
    along_x = {"dp": by_x}
    along_y = {"dp": by_y}
    over = {"dp": by_both}
    right = {"expert": (place + 1) % group}
    left = {"expert": (place + group - 1) % group}

    def ring_peer(k):
        return {"dp": (index + k) % parts}

    def rows_of(block):
        return pl.ds(pl.multiple_of(block * tok, tok), tok)

    def piece_of(number):
        return pl.ds(pl.multiple_of(number * piece, piece), piece)

    def qkv_spot(number):
        return w_qkv_buf.at[:, piece_of(number), :]

    def qkv_half(number, which):
        start = pl.multiple_of(number * piece + which * (piece // 2), piece // 2)
        return w_qkv_buf.at[:, pl.ds(start, piece // 2), :]

    def out_spot(number):
        return w_out_buf.at[:, piece_of(number)]

    def out_half(number, which):
        rows = pl.ds(which * (local_width // 2), local_width // 2)
        return w_out_buf.at[rows, piece_of(number)]

    class Gather:
        def __init__(self, number, source, spot, half_spot):
            self.number, self.source, self.spot, self.half_spot = number, source, spot, half_spot

        def copy(self, slot, source, target, peer):
            sems = gather_sems.at[self.number]
            return remote(source, target, sems.at[0, slot], sems.at[1, slot], peer)

        def own(self, slot, peer):
            return self.copy(slot, self.source, self.spot(index), peer)

        def keep(self):
            return pltpu.make_async_copy(
                self.source, self.spot(index), load_sems.at[16 + self.number]
            )

        def relay_x(self):
            spot = self.half_spot(by_y, 0)
            return self.copy(3, spot, spot, along_x)

        def relay_y(self):
            spot = self.half_spot(by_x, 1)
            return self.copy(4, spot, spot, along_y)

        def hand(self, slot):
            spot = (
                self.spot(by_x),
                self.spot(by_y),
                self.half_spot(by_both, 0),
                self.half_spot(by_both, 1),
            )[slot - 5]
            return self.copy(slot, spot, spot, partner)

        def begin(self):
            self.own(0, along_x).start()
            self.own(1, along_y).start()
            self.own(2, partner).start()
            self.keep().start()

        def relay(self):
            self.own(1, along_y).wait_recv()
            self.relay_x().start()
            self.own(0, along_x).wait_recv()
            self.relay_y().start()
            self.hand(5).start()
            self.hand(6).start()

        def finish(self):
            self.relay_x().wait_recv()
            self.hand(7).start()
            self.relay_y().wait_recv()
            self.hand(8).start()
            self.keep().wait()
            self.own(2, partner).wait_recv()
            for slot in (5, 6, 7, 8):
                self.hand(slot).wait_recv()

        def drain(self):
            for slot, peer in ((0, along_x), (1, along_y), (2, partner)):
                self.own(slot, peer).wait_send()
            self.relay_x().wait_send()
            self.relay_y().wait_send()
            for slot in (5, 6, 7, 8):
                self.hand(slot).wait_send()

    gather_qkv = Gather(0, w_qkv, qkv_spot, qkv_half)
    gather_out = Gather(1, w_out, out_spot, out_half)

    loads = [
        pltpu.make_async_copy(source, target, load_sems.at[number])
        for number, (source, target) in enumerate(
            [
                (tokens, tokens_buf.at[rows_of(place)]),
                (gain_one, gain_one_buf),
                (gain_two, gain_two_buf),
                (router_t, router_buf),
                (routes_t, rows_buf),
                (order_row, order_buf),
                (angles, angles_buf),
                (cotangent, cotangent_buf),
            ]
        )
    ]
    for load in loads:
        load.start()

    greet([ring_peer(k) for k in range(1, parts)] + [right, left])

    def own_pass(side, peer):
        return remote(
            tokens,
            tokens_buf.at[rows_of(place)],
            line_sems.at[side, place],
            line_sems.at[2, place],
            peer,
        )

    def pass_on(block, side, peer):
        spot = tokens_buf.at[rows_of(block)]
        return remote(spot, spot, line_sems.at[side, block], line_sems.at[2, block], peer)

    @pl.when(place < group - 1)
    def _():
        own_pass(0, right).start()

    @pl.when(place > 0)
    def _():
        own_pass(1, left).start()

    def small_copy(k):
        return remote(
            small,
            small_full.at[:, piece_of(index)],
            small_sems.at[0, k],
            small_sems.at[1, k],
            ring_peer(k),
        )

    gather_qkv.begin()

    for load in loads:
        load.wait()
    experts = router_t.shape[0]
    small[...] = jnp.zeros_like(small)
    small[0:1, :] = gain_one_buf[...].astype(jnp.float32)
    small[1:2, :] = gain_two_buf[...].astype(jnp.float32)
    small[2 : 2 + experts, :] = router_buf[...].astype(jnp.float32)
    small_full[:, piece_of(index)] = small[...]
    for k in range(1, parts):
        small_copy(k).start()

    rows = rows_buf[...]
    first_row, second_row, order_at = rows[0:1], rows[1:2], order_buf[...]
    square = (tok, tok)
    same = lax.broadcasted_iota(jnp.int32, square, 0) == lax.broadcasted_iota(jnp.int32, square, 1)

    def as_column(row):
        kept = jnp.where(same, jnp.broadcast_to(row.astype(jnp.float32), square), 0.0)
        return jnp.sum(kept, axis=1, keepdims=True).astype(jnp.int32)

    first_col, second_col, order_col = [as_column(r) for r in (first_row, second_row, order_at)]
    start = place * tok
    live_col = (start + lax.broadcasted_iota(jnp.int32, (tok, 1), 0)) < length[0]
    live_row = (start + lax.broadcasted_iota(jnp.int32, (1, tok), 1)) < length[0]
    before = order_col < order_at

    def count(mask):
        return jnp.sum(jnp.where(mask & live_col, 1.0, 0.0), axis=0, keepdims=True)

    slot_first = count((first_col == first_row) & before)
    slot_second = count(first_col == second_row) + count((second_col == second_row) & before)
    slot_ids = lax.broadcasted_iota(jnp.int32, (slots, tok), 0)
    for number, (named, slot) in enumerate(((first_row, slot_first), (second_row, slot_second))):
        slot = slot.astype(jnp.int32)
        step = named - place
        step = jnp.where(step < 0, step + group, step)
        target = jnp.where(live_row & (slot < cap), step * cap + slot, -1)
        hits[number] = jnp.where(slot_ids == target, 1.0, 0.0).astype(jnp.bfloat16)

    low = 32
    highs = seq_len // low
    sign = jnp.where(
        lax.broadcasted_iota(jnp.int32, (low, head_size), 1) < head_size // 2, -1.0, 1.0
    )
    cosine_low, sine_low = angles_buf[0, highs:, :], angles_buf[1, highs:, :]
    for number in range(highs):
        at = slice(number * low, (number + 1) * low)
        cosine_high = angles_buf[0, number : number + 1, :]
        sine_high = angles_buf[1, number : number + 1, :]
        cosine_buf[at, :] = cosine_high * cosine_low - sine_high * sine_low
        sine_buf[at, :] = sign * (sine_high * cosine_low + cosine_high * sine_low)

    for k in range(1, parts):
        small_copy(k).wait_recv()

    def normalize_block(block):
        at = rows_of(block)
        value = tokens_buf[at, :].astype(jnp.float32)
        inverse = lax.rsqrt(jnp.mean(value * value, axis=-1, keepdims=True) + NORM_EPSILON)
        inverse_all[at, :] = inverse
        whole_buf[at, :] = (value * inverse * small_full[0:1, :]).astype(jnp.bfloat16)

    def arrive(step):
        block = line_order(place, step)
        pass_on(block, 0, right).wait_recv()

        @pl.when((block < place) & (place < group - 1))
        def _():
            pass_on(block, 0, right).start()

        @pl.when((block > place) & (place > 0))
        def _():
            pass_on(block, 1, left).start()

        normalize_block(block)

    early = piece // 4

    def slice_copy(r, turn):
        number = (by_x // 2, by_y // 2, by_both // 2)[r - 1]
        part = turn // 2
        lanes = pl.ds(pl.multiple_of(part * ff + number * hidden, LANES), hidden)
        at = (pl.ds(0, early), pl.ds(early, piece - early), pl.ds(0, piece))[turn]
        return remote(
            w_gate_up.at[0, at, lanes],
            w_got.at[r - 1, at, pl.ds(part * hidden, hidden)],
            slice_sems.at[0, r - 1, turn],
            slice_sems.at[1, r - 1, turn],
            (along_x, along_y, over)[r - 1],
        )

    normalize_block(place)
    arrive(0)
    gather_qkv.relay()
    gather_out.begin()
    for r in (1, 2):
        slice_copy(r, 0).start()
    arrive(1)
    gather_qkv.finish()

    def project(first, size):
        at = pl.ds(pl.multiple_of(first, tok), size)
        source = whole_buf[at, :]

        def two_heads(number, carry):
            lanes = pl.ds(pl.multiple_of(number * 2 * head_size, 2 * head_size), 2 * head_size)
            for c, target in ((0, query), (1, key_rows)):
                plain = dot_nn(source, w_qkv_buf[c, :, lanes])
                turned = [
                    rotated(
                        plain[:, side * head_size : (side + 1) * head_size],
                        cosine_buf[at, :],
                        sine_buf[at, :],
                    )
                    for side in range(2)
                ]
                target[at, lanes] = jnp.concatenate(turned, axis=1).astype(jnp.bfloat16)
            value[at, lanes] = dot_nn(source, w_qkv_buf[2, :, lanes]).astype(jnp.bfloat16)
            return carry

        lax.fori_loop(0, heads // 2, two_heads, 0)

    upper = place // 2
    project(upper * tok, seq_len - tok)
    gather_out.relay()
    for turn in (1, 2):
        for r in (1, 2):
            slice_copy(r, turn).start()
    for turn in range(3):
        slice_copy(3, turn).start()
    arrive(2)
    project((1 - upper) * (seq_len - tok), tok)

    stores = [
        pltpu.make_async_copy(source, target, load_sems.at[10 + number])
        for number, (source, target) in enumerate(
            [
                (w_qkv_buf, qkv_full),
                (tokens_buf, tokens_all),
                (whole_buf, whole),
                (w_out_buf, out_full),
            ]
        )
    ]
    for store in stores[:3]:
        store.start()

    for number in range(group):
        at = slice(number * tok, (number + 1) * tok)
        extent = (number + 1) * tok
        shape = (tok, extent)
        at_query = number * tok + lax.broadcasted_iota(jnp.int32, shape, 0)
        at_key = lax.broadcasted_iota(jnp.int32, shape, 1)
        allowed = (at_key <= at_query) & (at_key < length[0])
        for head in range(heads):
            lanes = slice(head * head_size, (head + 1) * head_size)
            scores = dot_nt(query[at, lanes], key_rows[0:extent, lanes]) * scale
            scores = jnp.where(allowed, scores, NEGATIVE)
            top = jnp.max(scores, axis=-1, keepdims=True)
            exponent = jnp.exp(scores - top)
            row_total = jnp.sum(exponent, axis=-1, keepdims=True)
            probs = (exponent / row_total).astype(jnp.bfloat16)
            attended[at, lanes] = dot_nn(probs, value[0:extent, lanes]).astype(jnp.bfloat16)
            log_total[at, head : head + 1] = top + jnp.log(row_total)

    gather_out.finish()
    stores[3].start()

    def out_tile(j, carry):
        lanes = piece_of(j)
        part_buf[:, lanes] = dot_nn(attended[...], w_out_buf[:, lanes]).astype(jnp.bfloat16)
        return carry

    lax.fori_loop(0, parts, out_tile, 0)

    def go_right(block):
        return remote(
            part_buf.at[rows_of(block)],
            from_left.at[block],
            sum_sems.at[0, block],
            sum_sems.at[1, block],
            right,
        )

    def go_left(block):
        return remote(
            part_buf.at[rows_of(block)],
            from_right.at[block],
            sum_sems.at[0, block],
            sum_sems.at[2, block],
            left,
        )

    def add_into(target, added):
        total = target[...].astype(jnp.float32) + added[...].astype(jnp.float32)
        target[...] = total.astype(jnp.bfloat16)

    def on_right(block):
        go_right(block).wait_recv()
        add_into(part_buf.at[rows_of(block)], from_left.at[block])
        go_right(block).start()

    def on_left(block):
        go_left(block).wait_recv()
        add_into(part_buf.at[rows_of(block)], from_right.at[block])
        go_left(block).start()

    @pl.when(place == 0)
    def _():
        for block in (3, 2, 1):
            go_right(block).start()

    @pl.when(place == 3)
    def _():
        for block in (0, 1, 2):
            go_left(block).start()

    @pl.when(place == 1)
    def _():
        on_right(3)
        on_right(2)
        on_left(0)

    @pl.when(place == 2)
    def _():
        on_left(0)
        on_left(1)
        on_right(3)

    resid[...] = tokens_buf[rows_of(place), :].astype(jnp.float32) + part_buf[
        rows_of(place), :
    ].astype(jnp.float32)

    @pl.when(place > 0)
    def _():
        go_right(place).wait_recv()
        resid[...] += from_left[place].astype(jnp.float32)

    @pl.when(place < group - 1)
    def _():
        go_left(place).wait_recv()
        resid[...] += from_right[place].astype(jnp.float32)

    total = resid[...]
    inverse = lax.rsqrt(jnp.mean(total * total, axis=-1, keepdims=True) + NORM_EPSILON)
    inverse_two[...] = inverse
    hidden_in = (total * inverse * small_full[1:2, :]).astype(jnp.bfloat16)
    logits = dot_nt(hidden_in, small_full[...].astype(jnp.bfloat16))
    lane = lax.broadcasted_iota(jnp.int32, logits.shape, 1)
    chosen = [
        jnp.sum(jnp.where(lane == named + 2, logits, 0.0), axis=1, keepdims=True)
        for named in (first_col, second_col)
    ]
    top = jnp.maximum(chosen[0], chosen[1])
    raised = [jnp.exp(entry - top) for entry in chosen]
    both = raised[0] + raised[1]
    gate = [entry / both for entry in raised]
    for number in range(2):
        gates[:, number : number + 1] = gate[number]
    sent[...] = dot_nn(hits[0] + hits[1], hidden_in).astype(jnp.bfloat16)
    d_out = jnp.where(live_col, 1.0, 0.0) * cotangent_buf[...].astype(jnp.float32)
    d_back[...] = (
        dot_nn(hits[0], (gate[0] * d_out).astype(jnp.bfloat16))
        + dot_nn(hits[1], (gate[1] * d_out).astype(jnp.bfloat16))
    ).astype(jnp.bfloat16)

    for store in stores:
        store.wait()
    gather_qkv.drain()
    gather_out.drain()
    for k in range(1, parts):
        small_copy(k).wait_send()
    for block in range(group):

        @pl.when(block > place)
        def _():
            go_right(block).wait_send()

        @pl.when(block < place)
        def _():
            go_left(block).wait_send()

        @pl.when((block <= place) & (place < group - 1))
        def _():
            pass_on(block, 0, right).wait_send()

        @pl.when((block >= place) & (place > 0))
        def _():
            pass_on(block, 1, left).wait_send()

    for turn in range(3):
        for r in (1, 2, 3):
            slice_copy(r, turn).wait()


def attention_call(
    lengths,
    tokens,
    w_qkv,
    w_out,
    gain_one,
    gain_two,
    router_t,
    w_gate_up,
    routes_t,
    order_row,
    angles,
    cotangent,
    group,
):
    tok, width = tokens.shape
    seq_len = tok * group
    local_width = w_qkv.shape[2]
    heads = local_width // HEAD_DIM
    slots = tok * 2
    piece = w_qkv.shape[1]
    low, full = jnp.bfloat16, jnp.float32
    anywhere = pl.BlockSpec(memory_space=pl.ANY)
    inside = pl.BlockSpec(memory_space=pltpu.VMEM)
    narrow = jax.ShapeDtypeStruct((seq_len, local_width), low)
    flops = 2 * seq_len * width * local_width * 4 + 4 * seq_len * seq_len * local_width
    return pl.pallas_call(
        functools.partial(attention_kernel, heads),
        out_shape=(
            jax.ShapeDtypeStruct((seq_len, width), low),
            jax.ShapeDtypeStruct((seq_len, width), low),
            jax.ShapeDtypeStruct((3, width, local_width), low),
            jax.ShapeDtypeStruct((local_width, width), low),
            jax.ShapeDtypeStruct((3, piece, w_gate_up.shape[2] // 4), low),
            jax.ShapeDtypeStruct((seq_len, 1), full),
            narrow,
            narrow,
            narrow,
            narrow,
            jax.ShapeDtypeStruct((seq_len, heads), full),
            jax.ShapeDtypeStruct((8, width), full),
            jax.ShapeDtypeStruct((seq_len, HEAD_DIM), full),
            jax.ShapeDtypeStruct((seq_len, HEAD_DIM), full),
            jax.ShapeDtypeStruct((tok, width), full),
            jax.ShapeDtypeStruct((tok, 1), full),
            jax.ShapeDtypeStruct((tok, 2), full),
            jax.ShapeDtypeStruct((2, slots, tok), low),
            jax.ShapeDtypeStruct((slots, width), low),
            jax.ShapeDtypeStruct((slots, width), low),
        ),
        in_specs=[pl.BlockSpec(memory_space=pltpu.SMEM)] + [anywhere] * 11,
        out_specs=(anywhere,) * 5 + (inside,) * 15,
        scratch_shapes=[
            pltpu.VMEM((seq_len, width), low),
            pltpu.VMEM((seq_len, width), low),
            pltpu.VMEM((3, width, local_width), low),
            pltpu.VMEM((local_width, width), low),
            pltpu.VMEM((seq_len, width), low),
            pltpu.VMEM((group, tok, width), low),
            pltpu.VMEM((group, tok, width), low),
            pltpu.VMEM(routes_t.shape, jnp.int32),
            pltpu.VMEM(order_row.shape, jnp.int32),
            pltpu.VMEM(angles.shape, full),
            pltpu.VMEM((tok, width), low),
            pltpu.VMEM(gain_one.shape, low),
            pltpu.VMEM(gain_two.shape, low),
            pltpu.VMEM(router_t.shape, low),
            pltpu.VMEM((8, piece), full),
            pltpu.SemaphoreType.DMA((18,)),
            pltpu.SemaphoreType.DMA((3, group)),
            pltpu.SemaphoreType.DMA((3, group)),
            pltpu.SemaphoreType.DMA((2, 2, 9)),
            pltpu.SemaphoreType.DMA((2, width // piece)),
            pltpu.SemaphoreType.DMA((2, 3, 3)),
        ],
        compiler_params=pltpu.CompilerParams(
            collective_id=3, has_side_effects=True, vmem_limit_bytes=67043328
        ),
        cost_estimate=pl.CostEstimate(flops=flops, bytes_accessed=40000000, transcendentals=0),
        name="attention",
    )(
        lengths,
        tokens,
        w_qkv,
        w_out,
        gain_one,
        gain_two,
        router_t,
        w_gate_up,
        routes_t,
        order_row,
        angles,
        cotangent,
    )


def expert_step(gate_up_w, down_w, rows, d_rows_out):
    ff = down_w.shape[0]
    gate_up = jnp.dot(rows, gate_up_w, preferred_element_type=jnp.float32)
    gate = gate_up[:, :ff]
    upward = gate_up[:, ff:]
    sigmoid = jax.nn.sigmoid(gate)
    activated = (gate * sigmoid * upward).astype(jnp.bfloat16)
    out = jnp.dot(activated, down_w, preferred_element_type=jnp.float32).astype(jnp.bfloat16)
    d_activated = contract_last(d_rows_out, down_w)
    grad_down = contract_first(activated, d_rows_out)
    d_gate = d_activated * upward * sigmoid * (1.0 + gate * (1.0 - sigmoid))
    d_up = d_activated * gate * sigmoid
    d_gate_up = jnp.concatenate([d_gate, d_up], axis=1).astype(jnp.bfloat16)
    d_rows = contract_last(d_gate_up, gate_up_w).astype(jnp.bfloat16)
    grad_gate_up = contract_first(rows, d_gate_up)
    return out, d_rows, grad_gate_up, grad_down


def experts_gather_weights(w_gate_up, w_down, rows, d_rows_out):
    gate_up_w = lax.all_gather(w_gate_up, "dp", axis=1, tiled=True)[0]
    down_w = lax.all_gather(w_down, "dp", axis=1, tiled=True)[0]
    shape = rows.shape
    flat = (-1, shape[2])
    rows = exchange_experts(rows).reshape(flat)
    d_rows_out = exchange_experts(d_rows_out).reshape(flat)
    out, d_rows, grad_gate_up, grad_down = expert_step(gate_up_w, down_w, rows, d_rows_out)
    out = exchange_experts(out.reshape(shape))
    d_rows = exchange_experts(d_rows.reshape(shape))
    grad_gate_up = lax.psum_scatter(
        grad_gate_up.astype(jnp.bfloat16), "dp", scatter_dimension=0, tiled=True
    )
    grad_down = lax.psum_scatter(
        grad_down.astype(jnp.bfloat16), "dp", scatter_dimension=0, tiled=True
    )
    return (
        out,
        d_rows,
        grad_gate_up.astype(jnp.float32)[None],
        grad_down.astype(jnp.float32)[None],
    )


def attention_back_plain(
    lengths,
    d_attn,
    hat_all,
    whole,
    out_full,
    qkv_full,
    query,
    key_rows,
    value,
    attended,
    log_total,
    cosine,
    sine,
):
    seq_len, heads_local, head_size = query.shape
    local_width = heads_local * head_size
    position = jnp.arange(seq_len, dtype=jnp.int32)
    allowed = (position[None, :] <= position[:, None]) & (position < lengths[0])[None, :]
    whole_grad = lax.all_gather(d_attn, "expert", axis=0, tiled=True)
    d_attended = contract_last(whole_grad, out_full).astype(jnp.bfloat16)
    out_part = contract_first(attended, whole_grad)
    grad_out = lax.psum_scatter(
        out_part.astype(jnp.bfloat16), "dp", scatter_dimension=1, tiled=True
    ).astype(jnp.float32)
    d_heads = d_attended.reshape(seq_len, heads_local, head_size)
    probs = jnp.exp(masked_scores(query, key_rows, allowed) - log_total)
    probs_low = probs.astype(jnp.bfloat16)
    d_value = jnp.einsum(
        "hqk,qhd->khd", probs_low, d_heads, preferred_element_type=jnp.float32
    ).astype(jnp.bfloat16)
    d_probs = jnp.einsum("qhd,khd->hqk", d_heads, value, preferred_element_type=jnp.float32)
    row_delta = jnp.sum(probs * d_probs, axis=-1, keepdims=True)
    d_scores = (probs * (d_probs - row_delta)).astype(jnp.bfloat16)
    scale = head_size ** (-0.5)
    d_query = (
        jnp.einsum("hqk,khd->qhd", d_scores, key_rows, preferred_element_type=jnp.float32) * scale
    )
    d_key = jnp.einsum("hqk,qhd->khd", d_scores, query, preferred_element_type=jnp.float32) * scale
    d_query_pre = (
        rotate_back(d_query, cosine, sine).reshape(seq_len, local_width).astype(jnp.bfloat16)
    )
    d_key_pre = rotate_back(d_key, cosine, sine).reshape(seq_len, local_width).astype(jnp.bfloat16)
    d_projected = jnp.stack([d_query_pre, d_key_pre, d_value.reshape(seq_len, local_width)])
    d_normed_part = jnp.einsum(
        "cte,cde->td", d_projected, qkv_full, preferred_element_type=jnp.float32
    )
    grad_normalized = lax.psum_scatter(
        d_normed_part.astype(jnp.bfloat16), "expert", scatter_dimension=0, tiled=True
    ).astype(jnp.float32)
    qkv_part = jnp.einsum("td,cte->cde", whole, d_projected, preferred_element_type=jnp.float32)
    grad_qkv = lax.psum_scatter(
        qkv_part.astype(jnp.bfloat16), "dp", scatter_dimension=1, tiled=True
    ).astype(jnp.float32)
    first_gain_part = jnp.sum(d_normed_part * hat_all, axis=0)
    return grad_normalized, grad_qkv, grad_out, first_gain_part


def on_device(
    tokens,
    w_qkv,
    w_out,
    attention_norm_gain,
    gain_ffn,
    w_router,
    w_gate_up,
    w_down,
    lengths,
    routes,
    order,
    cotangent,
):
    group_size = lax.axis_size("expert")
    dp_size = lax.axis_size("dp")
    tok_dev = tokens.shape[0]
    seq_len = tok_dev * group_size
    width = tokens.shape[1]
    top_count = routes.shape[1]
    capacity = tok_dev * top_count // group_size
    slots = group_size * capacity
    head_size = HEAD_DIM
    local_width = w_qkv.shape[2]
    heads_local = local_width // head_size
    tokens_all = lax.all_gather(tokens, "expert", axis=0, tiled=True)
    small = jnp.concatenate(
        [attention_norm_gain[:, None], gain_ffn[:, None], w_router], axis=1
    )
    small_full = lax.all_gather(small, "dp", axis=0, tiled=True)
    qkv_full = lax.all_gather(w_qkv, "dp", axis=1, tiled=True)
    out_full = lax.all_gather(w_out, "dp", axis=1, tiled=True)
    first_norm_gain = small_full[:, 0].astype(jnp.float32)
    gain_two = small_full[:, 1].astype(jnp.float32)
    router_full = small_full[:, 2:]

    own_start = lax.axis_index("expert") * tok_dev
    own_position = own_start + jnp.arange(tok_dev, dtype=jnp.int32)
    live_own = own_position < lengths[0]
    live_rows = live_own.astype(jnp.float32)[:, None]
    target, kept_pair = slot_table(routes, order, live_own, capacity)
    slot_ids = jnp.arange(slots, dtype=jnp.int32)
    pair_hits = (slot_ids[:, None, None] == target[None]) & kept_pair[None]
    select = jnp.sum(pair_hits.astype(jnp.float32), axis=2).astype(jnp.bfloat16)

    inputs_float = tokens.astype(jnp.float32)
    input_normalized_hat, first_inverse_rms = normalize(inputs_float)
    hat_all, _ = normalize(tokens_all.astype(jnp.float32))
    whole = (hat_all * first_norm_gain).astype(jnp.bfloat16)
    cosine, sine = rotary_tables(seq_len, head_size)
    projected = jnp.einsum("td,cde->cte", whole, qkv_full, preferred_element_type=jnp.float32)
    query = rotate(projected[0].reshape(seq_len, heads_local, head_size), cosine, sine).astype(
        jnp.bfloat16
    )
    key_rows = rotate(projected[1].reshape(seq_len, heads_local, head_size), cosine, sine).astype(
        jnp.bfloat16
    )
    value = projected[2].astype(jnp.bfloat16).reshape(seq_len, heads_local, head_size)
    position = jnp.arange(seq_len, dtype=jnp.int32)
    live_all = position < lengths[0]
    allowed = (position[None, :] <= position[:, None]) & live_all[None, :]
    scores = masked_scores(query, key_rows, allowed)
    top_score = jnp.max(scores, axis=-1, keepdims=True)
    exponent = jnp.exp(scores - top_score)
    row_total = jnp.sum(exponent, axis=-1, keepdims=True)
    probs = exponent / row_total
    log_total = top_score + jnp.log(row_total)
    probs_low = probs.astype(jnp.bfloat16)
    attended = jnp.einsum("hqk,khd->qhd", probs_low, value, preferred_element_type=jnp.float32)
    attended = attended.reshape(seq_len, local_width).astype(jnp.bfloat16)
    attn_part = jnp.dot(attended, out_full, preferred_element_type=jnp.float32)
    attn_own = lax.psum_scatter(
        attn_part.astype(jnp.bfloat16), "expert", scatter_dimension=0, tiled=True
    ).astype(jnp.float32)
    resid = inputs_float + attn_own
    hhat, inverse_two = normalize(resid)
    hidden_in = (hhat * gain_two).astype(jnp.bfloat16)
    sent = jnp.dot(select, hidden_in, preferred_element_type=jnp.float32).astype(jnp.bfloat16)

    logits = jnp.dot(hidden_in, router_full, preferred_element_type=jnp.float32)
    chosen = jnp.take_along_axis(logits, routes, axis=1)
    gates = jax.nn.softmax(chosen, axis=1)
    d_out = live_rows * cotangent.astype(jnp.float32)
    d_back = jnp.zeros((slots, width), jnp.float32)
    for index in range(top_count):
        weighted = (gates[:, index : index + 1] * d_out).astype(jnp.bfloat16)
        d_back = d_back + jnp.dot(
            pair_hits[:, :, index].astype(jnp.bfloat16),
            weighted,
            preferred_element_type=jnp.float32,
        )
    d_back = d_back.astype(jnp.bfloat16)
    blocked = (group_size, capacity, width)
    returned, d_sent, grad_gate_up, grad_down = experts_gather_weights(
        w_gate_up, w_down, sent.reshape(blocked), d_back.reshape(blocked)
    )
    returned = returned.reshape(slots, width)
    d_sent = d_sent.reshape(slots, width)

    moe = jnp.zeros_like(resid)
    d_gates_list = []
    for index in range(top_count):
        one_hot = pair_hits[:, :, index].astype(jnp.bfloat16)
        picked = contract_first(one_hot, returned)
        d_gates_list.append(jnp.sum(d_out * picked, axis=-1))
        moe = moe + gates[:, index : index + 1] * picked
    output = (live_rows * (resid + moe)).astype(jnp.bfloat16)
    d_gates = jnp.stack(d_gates_list, axis=1)
    d_hidden = contract_first(select, d_sent)
    d_chosen = gates * (d_gates - jnp.sum(gates * d_gates, axis=1, keepdims=True))
    expert_ids = jnp.arange(group_size, dtype=jnp.int32)
    route_hits = (routes[:, :, None] == expert_ids[None, None, :]).astype(jnp.float32)
    d_logits = jnp.sum(route_hits * d_chosen[:, :, None], axis=1)
    router_f = router_full.astype(jnp.float32)
    d_hidden = d_hidden + jnp.dot(
        d_logits, router_f.T, precision=HIGH, preferred_element_type=jnp.float32
    )
    router_part = jnp.dot(
        hidden_in.astype(jnp.float32).T,
        d_logits,
        precision=HIGH,
        preferred_element_type=jnp.float32,
    )
    gain_two_part = jnp.sum(d_hidden * hhat, axis=0)
    scaled_two = d_hidden * gain_two
    d_resid = d_out + inverse_two * (
        scaled_two - hhat * jnp.mean(scaled_two * hhat, axis=-1, keepdims=True)
    )
    d_attn = d_resid.astype(jnp.bfloat16)
    grad_normalized, grad_qkv, grad_out, first_gain_part = attention_back_plain(
        lengths,
        d_attn,
        hat_all,
        whole,
        out_full,
        qkv_full,
        query,
        key_rows,
        value,
        attended,
        log_total,
        cosine,
        sine,
    )
    small_part = jnp.concatenate(
        [first_gain_part[None], gain_two_part[None], router_part.T], axis=0
    )
    small_sum = lax.psum(small_part, ("dp", "expert"))
    own_rows = width // dp_size
    small_own = lax.dynamic_slice_in_dim(
        small_sum, lax.axis_index("dp") * own_rows, own_rows, axis=1
    )
    first_scaled_input = grad_normalized * first_norm_gain
    grad_tokens = d_resid + first_inverse_rms * (
        first_scaled_input
        - input_normalized_hat
        * jnp.mean(first_scaled_input * input_normalized_hat, axis=-1, keepdims=True)
    )
    return (
        output,
        grad_tokens.astype(jnp.bfloat16),
        grad_qkv,
        grad_out,
        small_own[0],
        small_own[1],
        small_own[2 : 2 + group_size].T,
        grad_gate_up,
        grad_down,
    )


def on_device_split(
    tokens,
    w_qkv,
    w_out,
    attention_norm_gain,
    gain_ffn,
    w_router,
    w_gate_up,
    w_down,
    lengths,
    routes,
    order,
    cotangent,
):
    group = lax.axis_size("expert")
    tok, width = tokens.shape
    piece = w_router.shape[0]
    slots = tok * routes.shape[1]
    angles = rotary_constants(tok * group, HEAD_DIM)
    routes_t = routes.T
    (
        tokens_all,
        whole,
        qkv_full,
        out_full,
        w_got,
        inverse_all,
        query,
        key_rows,
        value,
        attended,
        log_total,
        small_full,
        cosine,
        sine,
        resid,
        inverse_two,
        gates,
        hits,
        sent,
        d_back,
    ) = attention_call(
        lengths,
        tokens,
        w_qkv,
        w_out,
        attention_norm_gain[None],
        gain_ffn[None],
        w_router.T,
        w_gate_up,
        routes_t,
        order.reshape(1, tok),
        angles,
        cotangent,
        group,
    )
    blocked = (group, slots // group, width)
    returned, d_sent, grad_gate_up, grad_down = experts_call(
        sent.reshape(blocked), d_back.reshape(blocked), w_gate_up, w_got, w_down
    )
    output, grad_tokens, grad_weights, small_own, gate_got = attention_back_call(
        lengths,
        returned.reshape(slots, width),
        d_sent.reshape(slots, width),
        resid,
        inverse_two,
        gates,
        hits,
        cotangent,
        routes_t,
        small_full,
        tokens_all,
        inverse_all,
        whole,
        out_full,
        qkv_full,
        query,
        key_rows,
        value,
        attended,
        log_total,
        cosine,
        sine,
        grad_gate_up,
    )
    (
        grad_gate_up,
        grad_down,
        grad_tokens,
        output,
        grad_qkv,
        grad_out,
        gain_one,
        gain_two,
        router,
    ) = finish_call(gate_got, grad_down, grad_tokens, output, grad_weights, small_own, group)
    return (
        output,
        grad_tokens,
        grad_qkv,
        grad_out,
        gain_one.reshape(piece),
        gain_two.reshape(piece),
        router.T,
        grad_gate_up,
        grad_down,
    )


def solution(mesh):
    placed = (
        P(("dp", "expert"), None),
        P(None, "dp", "expert"),
        P("expert", "dp"),
        P("dp"),
        P("dp"),
        P("dp", None),
        P("expert", "dp", None),
        P("expert", "dp", None),
        P("dp"),
        P(("dp", "expert"), None),
        P(("dp", "expert")),
        P(("dp", "expert"), None),
    )
    split = mesh.shape["dp"] == 8 and mesh.shape["expert"] == 4
    return jax.shard_map(
        on_device_split if split else on_device,
        mesh=mesh,
        in_specs=placed,
        out_specs=(
            P(("dp", "expert"), None),
            P(("dp", "expert"), None),
            P(None, "dp", "expert"),
            P("expert", "dp"),
            P("dp"),
            P("dp"),
            P("dp", None),
            P("expert", "dp", None),
            P("expert", "dp", None),
        ),
        check_vma=False,
    )
```

```python
import functools

import jax
import jax.numpy as jnp
import numpy as np
from jax import lax
from jax.experimental import pallas as pl
from jax.experimental.pallas import tpu as pltpu
from jax.sharding import PartitionSpec as P

HEAD_DIM = 128
FF = 5632


NORM_EPSILON = 1e-05
NEGATIVE = -1e30
THETA = 10000.0
HIGH = lax.Precision.HIGHEST
MESH_ID = pl.DeviceIdType.MESH
LANES = 128


def remote(src, dst, send_sem, recv_sem, peer):
    return pltpu.make_async_remote_copy(
        src_ref=src,
        dst_ref=dst,
        send_sem=send_sem,
        recv_sem=recv_sem,
        device_id=peer,
        device_id_type=MESH_ID,
    )


def greet(peers):
    barrier = pltpu.get_barrier_semaphore()
    for peer in peers:
        pl.semaphore_signal(barrier, inc=1, device_id=peer, device_id_type=MESH_ID)
    pl.semaphore_wait(barrier, len(peers))


def dot_nn(left, right):
    return jnp.dot(left, right, preferred_element_type=jnp.float32)


def dot_nt(left, right):
    return lax.dot_general(
        left, right, (((1,), (1,)), ((), ())), preferred_element_type=jnp.float32
    )


def experts_kernel(
    group,
    sent,
    d_back,
    w_gate_up,
    w_got,
    w_down,
    ret,
    d_ret,
    grad_gate_up,
    grad_down,
    w_buf,
    down_buf,
    rows_buf,
    gate_buf,
    act_buf,
    part_buf,
    half_x,
    half_y,
    full_x,
    full_y,
    other_gate,
    other_down,
    ag_sems,
    rs_sems,
    weight_sems,
    local_sems,
    grad_sems,
):
    cap, width = sent.shape[1], sent.shape[2]
    half = cap // 2
    piece, hidden2 = w_got.shape[1:]
    hidden = hidden2 // 2
    down_own = w_down.at[0]
    down_rows = down_own.shape[0]
    chunk = 4 * cap
    total = group * chunk

    index = lax.axis_index("dp")
    place = lax.axis_index("expert")
    core = index % 2
    at_x = (index // 2) % 2
    at_y = index // 4
    partner = {"dp": at_y * 4 + at_x * 2 + (1 - core)}
    along_x = {"dp": at_y * 4 + (1 - at_x) * 2 + core}
    along_y = {"dp": (1 - at_y) * 4 + at_x * 2 + core}
    chips = [
        at_y * 2 + at_x,
        at_y * 2 + (1 - at_x),
        (1 - at_y) * 2 + at_x,
        (1 - at_y) * 2 + (1 - at_x),
    ]

    def ahead(k):
        return {"expert": (place + k) % group}

    def behind(k):
        return {"expert": (place + group - k) % group}

    greet([partner, along_x, along_y] + [ahead(k) for k in range(1, group)])

    def block(t, k, r, start=0, size=None):
        size = cap if size is None else size
        return rows_buf.at[t, pl.ds((k * 4 + r) * cap + start, size), :]

    def part(t, k, r, start=0, size=None):
        size = cap if size is None else size
        return part_buf.at[t, pl.ds((k * 4 + r) * cap + start, size), :]

    def ag(kind, t, k):
        return ag_sems.at[0, kind, t, k], ag_sems.at[1, kind, t, k]

    def rs(kind, t, k):
        return rs_sems.at[0, kind, t, k], rs_sems.at[1, kind, t, k]

    sources = (sent, d_back)
    results = (ret, d_ret)

    def z_copy(t, k):
        return remote(sources[t].at[k], block(t, k, 0), *ag(0, t, k), ahead(k))

    def own_copy(t):
        return pltpu.make_async_copy(sources[t].at[0], block(t, 0, 0), local_sems.at[t])

    def x_copy(t, k):
        return remote(block(t, k, 0), block(t, k, 1), *ag(1, t, k), along_x)

    def y_copy(t, k):
        return remote(block(t, k, 0), block(t, k, 2), *ag(2, t, k), along_y)

    def a_copy(t, k):
        return remote(block(t, k, 2, 0, half), block(t, k, 3, 0, half), *ag(3, t, k), along_x)

    def b_copy(t, k):
        return remote(
            block(t, k, 1, half, half), block(t, k, 3, half, half), *ag(4, t, k), along_y
        )

    def spread(t, k):
        if k == 0:
            own_copy(t).wait()
        else:
            z_copy(t, k).wait_recv()
        x_copy(t, k).start()
        y_copy(t, k).start()

    def relay_a(t, k):
        y_copy(t, k).wait_recv()
        a_copy(t, k).start()

    def relay_b(t, k):
        x_copy(t, k).wait_recv()
        b_copy(t, k).start()

    def arrived(t, k):
        a_copy(t, k).wait_recv()
        b_copy(t, k).wait_recv()
        if t == 0 and k == 0:
            for r in range(4):
                for copy in w_keep(r):
                    copy.wait()
                for copy in w_share(r, 1 - core):
                    copy.wait_recv()
            down_keep.wait()
            down_share().wait_recv()

    def half_x_copy(t, k):
        return remote(part(t, k, 3, 0, half), half_x.at[t, k], *rs(0, t, k), along_x)

    def half_y_copy(t, k):
        return remote(part(t, k, 3, half, half), half_y.at[t, k], *rs(1, t, k), along_y)

    def full_x_copy(t, k):
        return remote(part(t, k, 1), full_x.at[t, k], *rs(2, t, k), along_x)

    def full_y_copy(t, k):
        return remote(part(t, k, 2), full_y.at[t, k], *rs(3, t, k), along_y)

    def back_copy(t, k):
        return remote(part(t, k, 0), results[t].at[k], *rs(4, t, k), behind(k))

    def keep_copy(t):
        return pltpu.make_async_copy(part(t, 0, 0), results[t].at[0], local_sems.at[2 + t])

    def halves_out(t, k):
        half_x_copy(t, k).start()
        half_y_copy(t, k).start()

    def add_into(target, *others):
        value = target[...].astype(jnp.float32)
        for other in others:
            value = value + other[...].astype(jnp.float32)
        target[...] = value.astype(jnp.bfloat16)

    def full_y_out(t, k):
        half_x_copy(t, k).wait_recv()
        add_into(part(t, k, 2, 0, half), half_x.at[t, k])
        full_y_copy(t, k).start()

    def full_x_out(t, k):
        half_y_copy(t, k).wait_recv()
        add_into(part(t, k, 1, half, half), half_y.at[t, k])
        full_x_copy(t, k).start()

    def home(t, k):
        full_x_copy(t, k).wait_recv()
        full_y_copy(t, k).wait_recv()
        add_into(part(t, k, 0), full_x.at[t, k], full_y.at[t, k])
        if k == 0:
            keep_copy(t).start()
        else:
            back_copy(t, k).start()

    def w_rows(r, which):
        return pl.ds(pl.multiple_of((chips[r] * 2 + which) * piece, piece), piece)

    def w_parts(r, which):
        rows = w_rows(r, which)
        if r > 0:
            return [(w_got.at[r - 1], w_buf.at[rows, :], r)]
        return [
            (
                w_gate_up.at[
                    0, :, pl.ds(pl.multiple_of((4 * part + chips[0]) * hidden, LANES), hidden)
                ],
                w_buf.at[rows, pl.ds(part * hidden, hidden)],
                4 * part,
            )
            for part in range(2)
        ]

    def w_share(r, which):
        return [
            remote(source, target, weight_sems.at[0, n], weight_sems.at[1, n], partner)
            for source, target, n in w_parts(r, which)
        ]

    def w_keep(r):
        return [
            pltpu.make_async_copy(source, target, local_sems.at[4 + n])
            for source, target, n in w_parts(r, core)
        ]

    def down_at(which):
        return down_buf.at[pl.ds(pl.multiple_of(which * down_rows, down_rows), down_rows), :]

    def down_share():
        return remote(
            down_own, down_at(core), weight_sems.at[0, 5], weight_sems.at[1, 5], partner
        )

    down_keep = pltpu.make_async_copy(down_own, down_at(core), local_sems.at[9])

    def take(steps, k, number):
        for at in range(group):
            if (at, number) in steps:

                @pl.when(k == at)
                def _(events=steps[at, number]):
                    for event, t, which in events:
                        event(t, which)

    blocks = hidden // LANES
    spans = [(2 * j, min(2, blocks - 2 * j)) for j in range((blocks + 1) // 2)]
    tiles = width // (2 * LANES)

    def span(first, count):
        return pl.ds(first * LANES, count * LANES)

    def forward(k, carry):
        at = pl.ds(pl.multiple_of(k * chunk, chunk), chunk)

        def tile(first, count):
            gate_cols, up_cols = span(first, count), span(blocks + first, count)
            rows = rows_buf[0, at, :]
            if count == 1:
                weights = jnp.concatenate([w_buf[:, gate_cols], w_buf[:, up_cols]], axis=1)
                both = dot_nn(rows, weights)
                gate, up = both[:, :LANES], both[:, LANES:]
            else:
                gate = dot_nn(rows, w_buf[:, gate_cols])
                up = dot_nn(rows, w_buf[:, up_cols])
            sigmoid = 1.0 / (1.0 + jnp.exp(-gate))
            gate_buf[at, gate_cols] = gate.astype(jnp.bfloat16)
            gate_buf[at, up_cols] = up.astype(jnp.bfloat16)
            act_buf[at, gate_cols] = (gate * sigmoid * up).astype(jnp.bfloat16)

        take(forward_steps, k, 0)
        for first, count in spans[:3]:
            tile(first, count)
        take(forward_steps, k, 1)
        for first, count in spans[3:]:
            tile(first, count)
        take(forward_steps, k, 2)
        for j in range(tiles):
            cols = span(2 * j, 2)
            out = dot_nn(act_buf[at, :], down_buf[:, cols])
            part_buf[0, at, cols] = out.astype(jnp.bfloat16)
        return carry

    def backward(turn, carry):
        k = (turn + 1) % group
        at = pl.ds(pl.multiple_of(k * chunk, chunk), chunk)
        take(backward_steps, k, 0)
        for first, count in spans:
            gate_cols, up_cols = span(first, count), span(blocks + first, count)
            d_act = dot_nt(rows_buf[1, at, :], down_buf[gate_cols, :])
            gate = gate_buf[at, gate_cols].astype(jnp.float32)
            up = gate_buf[at, up_cols].astype(jnp.float32)
            sigmoid = 1.0 / (1.0 + jnp.exp(-gate))
            scaled = d_act * sigmoid
            d_gate = scaled * up * (1.0 + gate * (1.0 - sigmoid))
            gate_buf[at, gate_cols] = d_gate.astype(jnp.bfloat16)
            gate_buf[at, up_cols] = (scaled * gate).astype(jnp.bfloat16)
        for side in range(2):
            take(backward_steps, k, 1 + side)
            for j in range(side * (tiles // 2), (side + 1) * (tiles // 2)):
                cols = span(2 * j, 2)
                out = dot_nt(gate_buf[at, :], w_buf[cols, :])
                part_buf[1, at, cols] = out.astype(jnp.bfloat16)
        return carry

    forward_steps = {
        (0, 0): [(spread, 0, 0), (spread, 1, 0), (relay_a, 0, 0), (relay_b, 0, 0), (spread, 0, 1), (relay_a, 1, 0), (relay_b, 1, 0), (arrived, 0, 0)],
        (0, 2): [(spread, 0, 2)],
        (1, 0): [(relay_a, 0, 1), (relay_b, 0, 1), (spread, 0, 3), (halves_out, 0, 0), (relay_a, 0, 2), (relay_b, 0, 2), (spread, 1, 1), (arrived, 0, 1)],
        (2, 0): [(relay_a, 0, 3), (relay_b, 0, 3), (halves_out, 0, 1), (spread, 1, 2), (arrived, 0, 2)],
        (2, 1): [(spread, 1, 3)],
        (3, 0): [(relay_a, 1, 1), (arrived, 0, 3)],
        (3, 1): [(relay_b, 1, 1), (full_y_out, 0, 0)],
    }
    backward_steps = {
        (0, 0): [(home, 0, 2), (halves_out, 1, 3), (arrived, 1, 0)],
        (0, 2): [(home, 0, 3), (full_y_out, 1, 2), (full_x_out, 1, 2)],
        (1, 0): [(full_x_out, 0, 0), (full_y_out, 0, 1), (relay_a, 1, 2), (relay_b, 1, 2), (relay_a, 1, 3), (relay_b, 1, 3), (arrived, 1, 1)],
        (1, 1): [(full_x_out, 0, 1), (halves_out, 0, 2)],
        (1, 2): [(halves_out, 0, 3), (home, 0, 0)],
        (2, 0): [(halves_out, 1, 1), (arrived, 1, 2)],
        (2, 2): [(home, 0, 1), (full_y_out, 0, 2), (full_x_out, 0, 2)],
        (3, 0): [(full_y_out, 0, 3), (full_x_out, 0, 3), (halves_out, 1, 2), (arrived, 1, 3)],
        (3, 1): [(full_y_out, 1, 1)],
        (3, 2): [(full_x_out, 1, 1)],
    }
    grad_steps = {
        (1, 0): [(halves_out, 1, 0)],
        (2, 0): [(full_y_out, 1, 3), (full_x_out, 1, 3), (home, 1, 1)],
        (2, 2): [(home, 1, 2)],
        (2, 3): [(full_y_out, 1, 0), (full_x_out, 1, 0)],
        (4, 0): [(home, 1, 3)],
        (4, 2): [(home, 1, 0)],
    }

    own_copy(0).start()
    for k in range(1, group):
        z_copy(0, k).start()
    for r in range(4):
        for copy in w_share(r, core) + w_keep(r):
            copy.start()
    down_share().start()
    down_keep.start()
    own_copy(1).start()

    for k in range(1, group):
        z_copy(1, k).start()

    lax.fori_loop(0, group, forward, 0)
    lax.fori_loop(0, group, backward, 0)
    for event, t, which in grad_steps.get((0, 0), []):
        event(t, which)

    act_t = down_buf.at[:, pl.ds(0, total)]
    rows_t = down_buf.at[pl.ds(0, piece), pl.ds(total, total)]
    send_down = w_buf.at[pl.ds(4 * piece, down_rows), pl.ds(0, width)]

    def send_gate(r):
        return w_buf.at[pl.ds(pl.multiple_of(r * piece, piece), piece), :]

    def turn(j, carry):
        lanes = pl.ds(pl.multiple_of(j * LANES, LANES), LANES)
        act_t[lanes, :] = act_buf[:, lanes].T
        return carry

    lax.fori_loop(0, blocks, turn, 0)

    def pair_span(j):
        return pl.ds(pl.multiple_of(j * 2 * LANES, 2 * LANES), 2 * LANES)

    def down_grad(which, j):
        rows = pl.ds(pl.multiple_of(which * down_rows, down_rows), down_rows)
        return dot_nn(act_t[rows, :], rows_buf[1, :, pair_span(j)])

    def after(steps, number, r):
        turns = {(turn, 0): events for (stage, turn), events in steps.items() if stage == number}
        take(turns, r, 0)

    after(grad_steps, 1, 0)
    def down_for_partner(j, carry):
        send_down[:, pair_span(j)] = down_grad(1 - core, j).astype(jnp.bfloat16)
        return carry

    lax.fori_loop(0, tiles, down_for_partner, 0)
    down_send = remote(
        send_down, other_down, grad_sems.at[0, 4], grad_sems.at[1, 4], partner
    )
    down_send.start()

    def turned_rows(r, which):
        step_y = r // 2
        step_x = r % 2
        chip = (at_y + step_y - 2 * at_y * step_y) * 2 + (at_x + step_x - 2 * at_x * step_x)
        start = pl.multiple_of((chip * 2 + which) * piece, piece)
        rows_t[...] = rows_buf[0, :, pl.ds(start, piece)].T

    def gate_send(r):
        return remote(
            send_gate(r), other_gate.at[r], grad_sems.at[0, r], grad_sems.at[1, r], partner
        )

    def gate_for_partner(r, carry):
        after(grad_steps, 2, r)
        turned_rows(r, 1 - core)
        target = send_gate(r)
        for j in range(blocks):
            cols = span(2 * j, 2)
            target[:, cols] = dot_nn(rows_t[...], gate_buf[:, cols]).astype(jnp.bfloat16)
        gate_send(r).start()
        return carry

    lax.fori_loop(0, 4, gate_for_partner, 0)
    after(grad_steps, 3, 0)
    down_send.wait_recv()

    def down_for_self(j, carry):
        cols = pair_span(j)
        value = down_grad(core, j) + other_down[:, cols].astype(jnp.float32)
        other_down[:, cols] = value.astype(jnp.bfloat16)
        return carry

    lax.fori_loop(0, tiles, down_for_self, 0)
    down_out = pltpu.make_async_copy(other_down, grad_down, grad_sems.at[2, 0])
    down_out.start()

    def gate_out(r):
        return pltpu.make_async_copy(other_gate.at[r], grad_gate_up.at[r], grad_sems.at[2, 2 + r])

    def gate_for_self(r, carry):
        after(grad_steps, 4, r)
        gate_send(r).wait_recv()
        turned_rows(r, core)
        target = other_gate.at[r]
        for j in range(blocks):
            cols = span(2 * j, 2)
            value = dot_nn(rows_t[...], gate_buf[:, cols])
            target[:, cols] = (value + target[:, cols].astype(jnp.float32)).astype(jnp.bfloat16)
        gate_out(r).start()
        return carry

    lax.fori_loop(0, 4, gate_for_self, 0)
    after(grad_steps, 5, 0)

    down_out.wait()
    for r in range(4):
        gate_out(r).wait()
        gate_send(r).wait_send()
        for copy in w_share(r, core):
            copy.wait_send()
    down_share().wait_send()
    down_send.wait_send()
    for t in range(2):
        keep_copy(t).wait()
        for k in range(group):
            x_copy(t, k).wait_send()
            y_copy(t, k).wait_send()
            a_copy(t, k).wait_send()
            b_copy(t, k).wait_send()
            half_x_copy(t, k).wait_send()
            half_y_copy(t, k).wait_send()
            full_x_copy(t, k).wait_send()
            full_y_copy(t, k).wait_send()
            if k > 0:
                z_copy(t, k).wait_send()
                back_copy(t, k).wait_send()
                back_copy(t, k).wait_recv()


def experts_call(sent, d_back, w_gate_up, w_got, w_down):
    group, cap, width = sent.shape
    piece, hidden2 = w_got.shape[1:]
    hidden = hidden2 // 2
    down_rows = w_down.shape[1]
    chunk = 4 * cap
    total = group * chunk
    low = jnp.bfloat16
    anywhere = pl.BlockSpec(memory_space=pl.ANY)
    flops = 2 * total * width * hidden * 9
    moved = 2 * (4 * piece * hidden2 * 2 + down_rows * width * 3)
    return pl.pallas_call(
        functools.partial(experts_kernel, group),
        out_shape=(
            jax.ShapeDtypeStruct((group, cap, width), low),
            jax.ShapeDtypeStruct((group, cap, width), low),
            jax.ShapeDtypeStruct((4, piece, hidden2), low),
            jax.ShapeDtypeStruct((down_rows, width), low),
        ),
        in_specs=[anywhere] * 5,
        out_specs=(anywhere,) * 4,
        scratch_shapes=[
            pltpu.VMEM((width, hidden2), low),
            pltpu.VMEM((hidden, width), low),
            pltpu.VMEM((2, total, width), low),
            pltpu.VMEM((total, hidden2), low),
            pltpu.VMEM((total, hidden), low),
            pltpu.VMEM((2, total, width), low),
            pltpu.VMEM((2, group, cap // 2, width), low),
            pltpu.VMEM((2, group, cap // 2, width), low),
            pltpu.VMEM((2, group, cap, width), low),
            pltpu.VMEM((2, group, cap, width), low),
            pltpu.VMEM((4, piece, hidden2), low),
            pltpu.VMEM((down_rows, width), low),
            pltpu.SemaphoreType.DMA((2, 5, 2, group)),
            pltpu.SemaphoreType.DMA((2, 5, 2, group)),
            pltpu.SemaphoreType.DMA((2, 6)),
            pltpu.SemaphoreType.DMA((10,)),
            pltpu.SemaphoreType.DMA((3, 6)),
        ],
        compiler_params=pltpu.CompilerParams(
            collective_id=1, has_side_effects=True, vmem_limit_bytes=67043328
        ),
        cost_estimate=pl.CostEstimate(flops=flops, bytes_accessed=moved, transcendentals=0),
        name="experts",
    )(sent, d_back, w_gate_up, w_got, w_down)


def rotary_tables(length_total, head_size):
    position = jnp.arange(length_total, dtype=jnp.float32)
    frequency = THETA ** (-(jnp.arange(head_size // 2, dtype=jnp.float32) * 2.0 / head_size))
    angles = position[:, None] * frequency[None, :]
    return (jnp.cos(angles)[:, None, :], jnp.sin(angles)[:, None, :])


def rotate(values, cosine, sine):
    half_size = values.shape[-1] // 2
    first = values[..., :half_size]
    second = values[..., half_size:]
    return jnp.concatenate(
        [first * cosine - second * sine, second * cosine + first * sine], axis=-1
    )


def rotate_back(grad_rows, cosine, sine):
    half_size = grad_rows.shape[-1] // 2
    first = grad_rows[..., :half_size]
    second = grad_rows[..., half_size:]
    return jnp.concatenate(
        [first * cosine + second * sine, second * cosine - first * sine], axis=-1
    )


def slot_table(routes, order, valid, capacity):
    row_count = routes.shape[0]
    top_count = routes.shape[1]
    pair_rank = order[:, None] + row_count * jnp.arange(top_count, dtype=jnp.int32)[None, :]
    flat_rank = pair_rank.reshape(-1)
    flat_expert = routes.reshape(-1)
    flat_valid = jnp.broadcast_to(valid[:, None], routes.shape).reshape(-1)
    earlier = (
        (flat_rank[None, :] < flat_rank[:, None])
        & (flat_expert[None, :] == flat_expert[:, None])
        & flat_valid[None, :]
    )
    slot_index = jnp.sum(earlier.astype(jnp.int32), axis=1).reshape(row_count, top_count)
    kept_pair = valid[:, None] & (slot_index < capacity)
    target = routes * capacity + jnp.minimum(slot_index, capacity - 1)
    return (target, kept_pair)


def masked_scores(query, key_rows, allowed):
    scale = query.shape[-1] ** (-0.5)
    raw = jnp.einsum("qhd,khd->hqk", query, key_rows, preferred_element_type=jnp.float32) * scale
    return jnp.where(allowed[None], raw, NEGATIVE)


def contract_first(left, right):
    return lax.dot_general(
        left, right, (((0,), (0,)), ((), ())), preferred_element_type=jnp.float32
    )


def contract_last(left, right):
    return lax.dot_general(
        left, right, (((1,), (1,)), ((), ())), preferred_element_type=jnp.float32
    )


def normalize(rows):
    inverse = lax.rsqrt(jnp.mean(rows * rows, axis=-1, keepdims=True) + NORM_EPSILON)
    return rows * inverse, inverse


def exchange_experts(blocks):
    return lax.all_to_all(blocks, "expert", split_axis=0, concat_axis=0, tiled=True)


def line_order(place, step):
    upper = place // 2
    low = place * (1 - upper) + (3 - place) * upper
    first = 1 - (step + 1) // 2
    block = step + first * (1 - low) + (1 - first)
    return block * (1 - upper) + (3 - block) * upper


def rotated(grad, cosine, sine):
    return grad * cosine + pltpu.roll(grad, grad.shape[1] // 2, 1) * sine


def attention_back_kernel(
    heads,
    length,
    returned,
    d_sent,
    resid,
    inverse_two,
    gates,
    hits,
    cotangent,
    routes_t,
    small_full,
    tokens_all,
    inverse_all,
    whole,
    w_out,
    w_qkv,
    query,
    key_rows,
    value,
    attended,
    log_total,
    cosine,
    sine,
    gate_grads,
    output,
    grad_tokens,
    grad_weights,
    small_out,
    gate_got,
    returned_buf,
    d_sent_buf,
    resid_buf,
    inverse_two_buf,
    gates_buf,
    hits_buf,
    cotangent_buf,
    rows_buf,
    small_full_buf,
    da_buf,
    tokens_buf,
    inverse_buf,
    whole_buf,
    w_out_buf,
    w_qkv_buf,
    query_buf,
    key_buf,
    value_buf,
    attended_buf,
    log_buf,
    cosine_buf,
    sine_buf,
    d_key_acc,
    d_value_acc,
    d_proj,
    normed_part,
    from_left,
    from_right,
    send_pair,
    recv_pair,
    own_part,
    half_x,
    half_y,
    full_x,
    full_y,
    small_buf,
    small_recv,
    small_z,
    keep_buf,
    sum_buf,
    load_sems,
    line_sems,
    sum_sems,
    pair_sems,
    ring_sems,
    small_sems,
    gate_sems,
):
    tok, width = cotangent.shape
    seq_len = tokens_all.shape[0]
    group = seq_len // tok
    local_width = w_out.shape[0]
    head_size = local_width // heads
    piece = own_part.shape[1]
    half = piece // 2
    scale = head_size**-0.5

    index = lax.axis_index("dp")
    place = lax.axis_index("expert")
    core = index % 2
    at_x = (index // 2) % 2
    at_y = index // 4
    partner = {"dp": at_y * 4 + at_x * 2 + (1 - core)}
    along_x = {"dp": at_y * 4 + (1 - at_x) * 2 + core}
    along_y = {"dp": (1 - at_y) * 4 + at_x * 2 + core}
    over = {"dp": (1 - at_y) * 4 + (1 - at_x) * 2 + core}
    parts = width // piece

    def chip(r):
        step_y = r // 2
        step_x = r % 2
        return (at_y + step_y - 2 * at_y * step_y) * 2 + (at_x + step_x - 2 * at_x * step_x)

    def ring_peer(k):
        return {"dp": (index + k) % parts}

    def line_peer(k):
        return {"expert": (place + k) % group}

    right = {"expert": (place + 1) % group}
    left = {"expert": (place + group - 1) % group}

    loads = [
        pltpu.make_async_copy(source, target, load_sems.at[number])
        for number, (source, target) in enumerate(
            [
                (returned, returned_buf),
                (hits, hits_buf),
                (cotangent, cotangent_buf),
                (resid, resid_buf),
                (inverse_two, inverse_two_buf),
                (gates, gates_buf),
                (routes_t, rows_buf),
                (small_full, small_full_buf),
                (d_sent, d_sent_buf),
                (w_out, w_out_buf),
                (query, query_buf),
                (key_rows, key_buf),
                (value, value_buf),
                (log_total, log_buf),
                (cosine, cosine_buf),
                (sine, sine_buf),
                (w_qkv, w_qkv_buf),
                (tokens_all, tokens_buf),
                (inverse_all, inverse_buf),
                (whole, whole_buf),
                (attended, attended_buf),
                (gate_grads.at[0], keep_buf),
            ]
        )
    ]
    first = 9
    early = first + 7
    for load in loads[:early]:
        load.start()

    greet([ring_peer(k) for k in range(1, parts)] + [line_peer(k) for k in range(1, group)])

    def rows_of(block):
        return pl.ds(pl.multiple_of(block * tok, tok), tok)

    def pass_right(block):
        spot = da_buf.at[rows_of(block)]
        return remote(spot, spot, line_sems.at[0, block], line_sems.at[2, block], right)

    def pass_left(block):
        spot = da_buf.at[rows_of(block)]
        return remote(spot, spot, line_sems.at[1, block], line_sems.at[2, block], left)

    def gate_copy(r, peer):
        return remote(
            gate_grads.at[r], gate_got.at[r], gate_sems.at[0, r], gate_sems.at[1, r], peer
        )

    peers = (None, along_x, along_y, over)
    for r in (3, 1, 2):
        gate_copy(r, peers[r]).start()
    for load in loads[early:]:
        load.start()
    for load in loads[:first]:
        load.wait()

    at = place * tok + lax.broadcasted_iota(jnp.int32, (tok, 1), 0)
    live = jnp.where(at < length[0], 1.0, 0.0)
    d_out = live * cotangent_buf[...].astype(jnp.float32)
    total = resid_buf[...]
    hhat = total * inverse_two_buf[...]
    gate = [gates_buf[:, number : number + 1] for number in range(2)]
    d_gate = []
    for number in range(2):
        picked = dot_nn(hits_buf[number].T, returned_buf[...])
        d_gate.append(jnp.sum(d_out * picked, axis=-1, keepdims=True))
        total = total + gate[number] * picked
    output[...] = (live * total).astype(jnp.bfloat16)
    mixed = gate[0] * d_gate[0] + gate[1] * d_gate[1]
    d_chosen = [gate[number] * (d_gate[number] - mixed) for number in range(2)]
    d_hidden = dot_nn((hits_buf[0] + hits_buf[1]).T, d_sent_buf[...])
    gain_two = small_full_buf[1:2, :]
    hidden_in = (hhat * gain_two).astype(jnp.bfloat16).astype(jnp.float32)
    small_buf[...] = jnp.zeros_like(small_buf)
    square = (tok, tok)
    same = lax.broadcasted_iota(jnp.int32, square, 0) == lax.broadcasted_iota(jnp.int32, square, 1)
    named = []
    for number in range(2):
        row = rows_buf[number : number + 1, :].astype(jnp.float32)
        kept = jnp.where(same, jnp.broadcast_to(row, square), 0.0)
        named.append(jnp.sum(kept, axis=1, keepdims=True).astype(jnp.int32))
    for expert in range(group):
        d_logit = sum(
            jnp.where(named[number] == expert, d_chosen[number], 0.0)
            for number in range(2)
        )
        row = slice(2 + expert, 3 + expert)
        d_hidden = d_hidden + d_logit * small_full_buf[row, :]
        small_buf[row, :] = jnp.sum(d_logit * hidden_in, axis=0, keepdims=True)
    small_buf[1:2, :] = jnp.sum(d_hidden * hhat, axis=0, keepdims=True)
    scaled = d_hidden * gain_two
    shared = jnp.mean(scaled * hhat, axis=-1, keepdims=True)
    d_resid = d_out + inverse_two_buf[...] * (scaled - hhat * shared)
    resid_buf[...] = d_resid
    da_buf[rows_of(place), :] = d_resid.astype(jnp.bfloat16)

    @pl.when(place < group - 1)
    def _():
        pass_right(place).start()

    @pl.when(place > 0)
    def _():
        pass_left(place).start()

    d_key_acc[...] = jnp.zeros_like(d_key_acc)
    d_value_acc[...] = jnp.zeros_like(d_value_acc)

    def attend_back(block):
        rows = rows_of(block)
        d_heads = dot_nt(da_buf[rows, :], w_out_buf[...]).astype(jnp.bfloat16)
        shape = (tok, seq_len)
        at_query = block * tok + lax.broadcasted_iota(jnp.int32, shape, 0)
        at_key = lax.broadcasted_iota(jnp.int32, shape, 1)
        allowed = (at_key <= at_query) & (at_key < length[0])
        for head in range(heads):
            cols = slice(head * head_size, (head + 1) * head_size)
            one_query = query_buf[rows, cols]
            one_key = key_buf[:, cols]
            d_head = d_heads[:, cols]
            scores = jnp.where(allowed, dot_nt(one_query, one_key) * scale, NEGATIVE)
            probs = jnp.exp(scores - log_buf[rows, head : head + 1])
            d_probs = dot_nt(d_head, value_buf[:, cols])
            delta = jnp.sum(probs * d_probs, axis=-1, keepdims=True)
            d_scores = (probs * (d_probs - delta)).astype(jnp.bfloat16)
            d_query = dot_nn(d_scores, one_key) * scale
            d_key_acc[:, cols] += dot_nn(d_scores.T, one_query) * scale
            d_value_acc[:, cols] += dot_nn(probs.astype(jnp.bfloat16).T, d_head)
            d_proj[rows, cols] = rotated(d_query, cosine_buf[rows, :], -sine_buf[rows, :]).astype(
                jnp.bfloat16
            )

    for load in loads[first:early]:
        load.wait()

    def arrive(step, carry):
        later = (step + group - 2) // (group - 1)
        block = place * (1 - later) + line_order(place, step - later) * later

        @pl.when(step > 0)
        def _():
            pass_right(block).wait_recv()

        @pl.when((block < place) & (place < group - 1))
        def _():
            pass_right(block).start()

        @pl.when((block > place) & (place > 0))
        def _():
            pass_left(block).start()

        attend_back(block)
        return carry

    lax.fori_loop(0, group, arrive, 0)
    for load in loads[early:]:
        load.wait()
    keep = pltpu.make_async_copy(keep_buf, gate_got.at[0], load_sems.at[22])
    keep.start()

    for head in range(heads):
        cols = slice(head * head_size, (head + 1) * head_size)
        key_cols = slice(local_width + head * head_size, local_width + (head + 1) * head_size)
        d_proj[:, key_cols] = rotated(d_key_acc[:, cols], cosine_buf[...], -sine_buf[...]).astype(
            jnp.bfloat16
        )
    d_proj[:, 2 * local_width :] = d_value_acc[...].astype(jnp.bfloat16)

    def normed_tile(j, carry):
        cols = pl.ds(pl.multiple_of(j * piece, piece), piece)
        d_normed = jnp.zeros((seq_len, piece), jnp.float32)
        for c in range(3):
            d_normed += dot_nt(
                d_proj[:, c * local_width : (c + 1) * local_width], w_qkv_buf[c, cols, :]
            )
        hat = tokens_buf[:, cols].astype(jnp.float32) * inverse_buf[...]
        small_buf[0:1, cols] = jnp.sum(d_normed * hat, axis=0, keepdims=True)
        normed_part[:, cols] = d_normed.astype(jnp.bfloat16)
        return carry

    lax.fori_loop(0, parts, normed_tile, 0)

    def go_right(block):
        return remote(
            normed_part.at[pl.ds(block * tok, tok)],
            from_left.at[block],
            sum_sems.at[0, block],
            sum_sems.at[1, block],
            right,
        )

    def go_left(block):
        return remote(
            normed_part.at[pl.ds(block * tok, tok)],
            from_right.at[block],
            sum_sems.at[0, block],
            sum_sems.at[2, block],
            left,
        )

    def add_into(target, other):
        value = target[...].astype(jnp.float32) + other[...].astype(jnp.float32)
        target[...] = value.astype(jnp.bfloat16)

    def on_right(block):
        go_right(block).wait_recv()
        add_into(normed_part.at[pl.ds(block * tok, tok)], from_left.at[block])
        go_right(block).start()

    def on_left(block):
        go_left(block).wait_recv()
        add_into(normed_part.at[pl.ds(block * tok, tok)], from_right.at[block])
        go_left(block).start()

    @pl.when(place == 0)
    def _():
        for block in (3, 2, 1):
            go_right(block).start()

    @pl.when(place == 3)
    def _():
        for block in (0, 1, 2):
            go_left(block).start()

    def small_copy(k):
        to = (index + k) % parts
        cols = pl.ds(pl.multiple_of(to * piece, piece), piece)
        return remote(
            small_buf.at[:, cols],
            small_recv.at[k],
            small_sems.at[0, k],
            small_sems.at[1, k],
            ring_peer(k),
        )

    for k in range(1, parts):
        small_copy(k).start()

    def weight_grad(which, r):
        cols = pl.ds(pl.multiple_of((chip(r) * 2 + which) * piece, piece), piece)
        left_side = whole_buf[:, cols].T
        first = dot_nn(left_side, d_proj[...])
        second = dot_nn(da_buf[:, cols].T, attended_buf[...])
        return jnp.concatenate([first, second], axis=1)

    def pair_copy(r):
        return remote(
            send_pair.at[r], recv_pair.at[r], pair_sems.at[0, r], pair_sems.at[1, r], partner
        )

    def for_partner(i, carry):
        r = 3 - i
        send_pair[r] = weight_grad(1 - core, r).astype(jnp.bfloat16)
        pair_copy(r).start()
        return carry

    lax.fori_loop(0, 4, for_partner, 0)

    @pl.when(place == 1)
    def _():
        on_right(3)

    @pl.when(place == 2)
    def _():
        on_left(0)

    def lanes_of(c):
        return pl.ds(c * (2 * local_width), 2 * local_width)

    def ring_copy(number, c, source, target, peer):
        sem = 4 * c + number
        return remote(source, target, ring_sems.at[0, sem], ring_sems.at[1, sem], peer)

    def half_x_copy(c):
        source = own_part.at[3, pl.ds(0, half), lanes_of(c)]
        return ring_copy(0, c, source, half_x.at[:, lanes_of(c)], along_x)

    def half_y_copy(c):
        source = own_part.at[3, pl.ds(half, half), lanes_of(c)]
        return ring_copy(1, c, source, half_y.at[:, lanes_of(c)], along_y)

    def full_x_copy(c):
        return ring_copy(
            2, c, own_part.at[1, :, lanes_of(c)], full_x.at[:, lanes_of(c)], along_x
        )

    def full_y_copy(c):
        return ring_copy(
            3, c, own_part.at[2, :, lanes_of(c)], full_y.at[:, lanes_of(c)], along_y
        )

    def for_self(i, carry):
        r = 3 - i
        pair_copy(r).wait_recv()
        own_part[r] = (weight_grad(core, r) + recv_pair[r].astype(jnp.float32)).astype(
            jnp.bfloat16
        )

        @pl.when(i == 0)
        def _():
            for c in range(2):
                half_x_copy(c).start()
                half_y_copy(c).start()

        return carry

    lax.fori_loop(0, 4, for_self, 0)

    total = small_buf[:, pl.ds(pl.multiple_of(index * piece, piece), piece)]
    for k in range(1, parts):
        small_copy(k).wait_recv()
        total = total + small_recv[k]
    small_z[0] = total

    @pl.when(place == 1)
    def _():
        on_right(2)

    @pl.when(place == 2)
    def _():
        on_left(1)

    def small_line_copy(k):
        return remote(
            small_z.at[0],
            small_z.at[k],
            small_sems.at[0, parts + k],
            small_sems.at[1, parts + k],
            line_peer(k),
        )

    for k in range(1, group):
        small_line_copy(k).start()

    for c in range(2):
        half_x_copy(c).wait_recv()
        add_into(own_part.at[2, pl.ds(0, half), lanes_of(c)], half_x.at[:, lanes_of(c)])
        full_y_copy(c).start()
        half_y_copy(c).wait_recv()
        add_into(own_part.at[1, pl.ds(half, half), lanes_of(c)], half_y.at[:, lanes_of(c)])
        full_x_copy(c).start()

    @pl.when(place == 1)
    def _():
        on_left(0)

    @pl.when(place == 2)
    def _():
        on_right(3)

    total = small_z[0]
    for k in range(1, group):
        small_line_copy(k).wait_recv()
        total = total + small_z[k]
    small_out[...] = total

    sum_buf[...] = normed_part[rows_of(place), :].astype(jnp.float32)

    @pl.when(place > 0)
    def _():
        go_right(place).wait_recv()
        sum_buf[...] += from_left[place].astype(jnp.float32)

    @pl.when(place < group - 1)
    def _():
        go_left(place).wait_recv()
        sum_buf[...] += from_right[place].astype(jnp.float32)

    inverse_one = inverse_buf[rows_of(place), :]
    hat = tokens_buf[rows_of(place), :].astype(jnp.float32) * inverse_one
    scaled = sum_buf[...] * small_full_buf[0:1, :]
    shared = jnp.mean(scaled * hat, axis=-1, keepdims=True)
    grad_tokens[...] = (resid_buf[...] + inverse_one * (scaled - hat * shared)).astype(
        jnp.bfloat16
    )

    for c in range(2):
        full_x_copy(c).wait_recv()
        full_y_copy(c).wait_recv()
        grad_weights[:, lanes_of(c)] = (
            own_part[0, :, lanes_of(c)].astype(jnp.float32)
            + full_x[:, lanes_of(c)].astype(jnp.float32)
            + full_y[:, lanes_of(c)].astype(jnp.float32)
        )

    for r in (1, 2, 3):
        gate_copy(r, peers[r]).wait()
    keep.wait()
    for c in range(2):
        half_x_copy(c).wait_send()
        half_y_copy(c).wait_send()
        full_x_copy(c).wait_send()
        full_y_copy(c).wait_send()
    for r in range(4):
        pair_copy(r).wait_send()
    for k in range(1, parts):
        small_copy(k).wait_send()
    for k in range(1, group):
        small_line_copy(k).wait_send()
    for block in range(group):

        @pl.when(block > place)
        def _():
            go_right(block).wait_send()

        @pl.when(block < place)
        def _():
            go_left(block).wait_send()

        @pl.when((block <= place) & (place < group - 1))
        def _():
            pass_right(block).wait_send()

        @pl.when((block >= place) & (place > 0))
        def _():
            pass_left(block).wait_send()


def attention_back_call(
    lengths,
    returned,
    d_sent,
    resid,
    inverse_two,
    gates,
    hits,
    cotangent,
    routes_t,
    small_full,
    tokens_all,
    inverse_all,
    whole,
    w_out,
    w_qkv,
    query,
    key_rows,
    value,
    attended,
    log_total,
    cosine,
    sine,
    gate_grads,
):
    tok, width = cotangent.shape
    seq_len = tokens_all.shape[0]
    group = seq_len // tok
    local_width = w_out.shape[0]
    heads = log_total.shape[1]
    piece = gate_grads.shape[1]
    half = piece // 2
    parts = width // piece
    small_rows = small_full.shape[0]
    low, full = jnp.bfloat16, jnp.float32
    anywhere = pl.BlockSpec(memory_space=pl.ANY)
    inside = pl.BlockSpec(memory_space=pltpu.VMEM)

    def like(array):
        return pltpu.VMEM(array.shape, array.dtype)

    flops = 2 * seq_len * width * local_width * 8 + 10 * seq_len * seq_len * local_width
    return pl.pallas_call(
        functools.partial(attention_back_kernel, heads),
        out_shape=(
            jax.ShapeDtypeStruct((tok, width), low),
            jax.ShapeDtypeStruct((tok, width), low),
            jax.ShapeDtypeStruct((piece, 4 * local_width), full),
            jax.ShapeDtypeStruct((small_rows, piece), full),
            jax.ShapeDtypeStruct(gate_grads.shape, low),
        ),
        in_specs=[pl.BlockSpec(memory_space=pltpu.SMEM)] + [anywhere] * 22,
        out_specs=(inside, inside, inside, inside, anywhere),
        scratch_shapes=[
            like(returned),
            like(d_sent),
            like(resid),
            like(inverse_two),
            like(gates),
            like(hits),
            like(cotangent),
            like(routes_t),
            like(small_full),
            pltpu.VMEM((seq_len, width), low),
            like(tokens_all),
            like(inverse_all),
            like(whole),
            like(w_out),
            like(w_qkv),
            like(query),
            like(key_rows),
            like(value),
            like(attended),
            like(log_total),
            like(cosine),
            like(sine),
            pltpu.VMEM((seq_len, local_width), full),
            pltpu.VMEM((seq_len, local_width), full),
            pltpu.VMEM((seq_len, 3 * local_width), low),
            pltpu.VMEM((seq_len, width), low),
            pltpu.VMEM((group, tok, width), low),
            pltpu.VMEM((group, tok, width), low),
            pltpu.VMEM((4, piece, 4 * local_width), low),
            pltpu.VMEM((4, piece, 4 * local_width), low),
            pltpu.VMEM((4, piece, 4 * local_width), low),
            pltpu.VMEM((half, 4 * local_width), low),
            pltpu.VMEM((half, 4 * local_width), low),
            pltpu.VMEM((piece, 4 * local_width), low),
            pltpu.VMEM((piece, 4 * local_width), low),
            like(small_full),
            pltpu.VMEM((parts, small_rows, piece), full),
            pltpu.VMEM((group, small_rows, piece), full),
            pltpu.VMEM(gate_grads.shape[1:], low),
            like(resid),
            pltpu.SemaphoreType.DMA((23,)),
            pltpu.SemaphoreType.DMA((3, group)),
            pltpu.SemaphoreType.DMA((3, group)),
            pltpu.SemaphoreType.DMA((2, 4)),
            pltpu.SemaphoreType.DMA((2, 8)),
            pltpu.SemaphoreType.DMA((2, parts + group)),
            pltpu.SemaphoreType.DMA((2, 4)),
        ],
        compiler_params=pltpu.CompilerParams(
            collective_id=2, has_side_effects=True, vmem_limit_bytes=67043328
        ),
        cost_estimate=pl.CostEstimate(flops=flops, bytes_accessed=40000000, transcendentals=0),
        name="attention_back",
    )(
        lengths,
        returned,
        d_sent,
        resid,
        inverse_two,
        gates,
        hits,
        cotangent,
        routes_t,
        small_full,
        tokens_all,
        inverse_all,
        whole,
        w_out,
        w_qkv,
        query,
        key_rows,
        value,
        attended,
        log_total,
        cosine,
        sine,
        gate_grads,
    )


def finish_kernel(
    gate_got,
    grad_down_low,
    grad_tokens_low,
    output_low,
    grad_weights,
    small,
    grad_gate_up,
    grad_down,
    grad_tokens,
    output,
    grad_qkv,
    grad_out,
    gain_one,
    gain_two,
    router,
    got_buf,
    wide_buf,
    low_buf,
    down_buf,
    tokens_buf,
    output_buf,
    weights_buf,
    out_buf,
    small_buf,
    load_sems,
    store_sems,
):
    chips = gate_got.shape[0]
    size = gate_got.shape[2] // 2
    local_width = grad_qkv.shape[2]
    index = lax.axis_index("dp")
    at_x = (index // 2) % 2
    at_y = index // 4

    def load(number, source, target):
        return pltpu.make_async_copy(source, target, load_sems.at[number])

    loads = [load(r, gate_got.at[r], got_buf.at[r]) for r in range(chips)] + [
        load(4, grad_down_low, low_buf),
        load(5, grad_weights, weights_buf),
        load(6, grad_tokens_low, tokens_buf),
        load(7, output_low, output_buf),
        load(8, small, small_buf),
    ]
    for copy in loads:
        copy.start()
    stores = []

    def store(source, target):
        copy = pltpu.make_async_copy(source, target, store_sems.at[len(stores)])
        copy.start()
        stores.append(copy)

    for r in range(chips):
        loads[r].wait()
        step_y = r // 2
        step_x = r % 2
        chip = (at_y + step_y - 2 * at_y * step_y) * 2 + (at_x + step_x - 2 * at_x * step_x)
        for part in range(2):
            wide_buf[2 * r + part] = got_buf[r, :, part * size : (part + 1) * size].astype(
                jnp.float32
            )
            lanes = pl.ds(pl.multiple_of((part * chips + chip) * size, LANES), size)
            store(wide_buf.at[2 * r + part], grad_gate_up.at[0, :, lanes])
    loads[4].wait()
    down_buf[...] = low_buf[...].astype(jnp.float32)
    store(down_buf, grad_down.at[0])
    loads[5].wait()
    out_buf[...] = weights_buf[:, 3 * local_width :].T
    for c in range(3):
        store(weights_buf.at[:, pl.ds(c * local_width, local_width)], grad_qkv.at[c])
    store(out_buf, grad_out)
    loads[6].wait()
    store(tokens_buf, grad_tokens)
    loads[7].wait()
    store(output_buf, output)
    loads[8].wait()
    gain_one[...] = small_buf[0:1, :]
    gain_two[...] = small_buf[1:2, :]
    router[...] = small_buf[2 : 2 + router.shape[0], :]
    for copy in stores:
        copy.wait()


def finish_call(gate_got, grad_down, grad_tokens, output, grad_weights, small, experts):
    chips, rows, hidden2 = gate_got.shape
    local_width = grad_weights.shape[1] // 4
    full = jnp.float32
    anywhere = pl.BlockSpec(memory_space=pl.ANY)
    out_t = (local_width, rows)

    def like(array, kind=None):
        return pltpu.VMEM(array.shape, kind or array.dtype)

    return pl.pallas_call(
        finish_kernel,
        out_shape=(
            jax.ShapeDtypeStruct((1, rows, chips * hidden2), full),
            jax.ShapeDtypeStruct((1,) + grad_down.shape, full),
            jax.ShapeDtypeStruct(grad_tokens.shape, grad_tokens.dtype),
            jax.ShapeDtypeStruct(output.shape, output.dtype),
            jax.ShapeDtypeStruct((3, rows, local_width), full),
            jax.ShapeDtypeStruct(out_t, full),
            jax.ShapeDtypeStruct((1, rows), full),
            jax.ShapeDtypeStruct((1, rows), full),
            jax.ShapeDtypeStruct((experts, rows), full),
        ),
        in_specs=[anywhere] * 6,
        out_specs=(anywhere,) * 6 + (pl.BlockSpec(memory_space=pltpu.VMEM),) * 3,
        scratch_shapes=[
            like(gate_got),
            pltpu.VMEM((2 * chips, rows, hidden2 // 2), full),
            like(grad_down),
            like(grad_down, full),
            like(grad_tokens),
            like(output),
            like(grad_weights),
            pltpu.VMEM(out_t, full),
            like(small),
            pltpu.SemaphoreType.DMA((9,)),
            pltpu.SemaphoreType.DMA((15,)),
        ],
        compiler_params=pltpu.CompilerParams(vmem_limit_bytes=67043328),
        name="finish",
    )(gate_got, grad_down, grad_tokens, output, grad_weights, small)


def rotary_constants(length_total, head_size):
    low = 32
    steps = np.arange(head_size // 2, dtype=np.float32) * np.float32(2.0) / np.float32(head_size)
    frequency = np.power(np.float32(THETA), -steps).astype(np.float32).astype(np.float64)
    position = np.concatenate([np.arange(0, length_total, low), np.arange(low)])
    angles = position[:, None] * np.concatenate([frequency, frequency])[None, :]
    return np.stack([np.cos(angles), np.sin(angles)]).astype(np.float32)


def attention_kernel(
    heads,
    length,
    tokens,
    w_qkv,
    w_out,
    gain_one,
    gain_two,
    router_t,
    w_gate_up,
    routes_t,
    order_row,
    angles,
    cotangent,
    tokens_all,
    whole,
    qkv_full,
    out_full,
    w_got,
    inverse_all,
    query,
    key_rows,
    value,
    attended,
    log_total,
    small_full,
    cosine_buf,
    sine_buf,
    resid,
    inverse_two,
    gates,
    hits,
    sent,
    d_back,
    tokens_buf,
    whole_buf,
    w_qkv_buf,
    w_out_buf,
    part_buf,
    from_left,
    from_right,
    rows_buf,
    order_buf,
    angles_buf,
    cotangent_buf,
    gain_one_buf,
    gain_two_buf,
    router_buf,
    small,
    load_sems,
    line_sems,
    sum_sems,
    gather_sems,
    small_sems,
    slice_sems,
):
    tok, width = tokens.shape
    seq_len = tokens_buf.shape[0]
    group = seq_len // tok
    local_width = w_out.shape[0]
    head_size = local_width // heads
    piece = w_qkv.shape[1]
    parts = width // piece
    ff = w_gate_up.shape[2] // 2
    hidden = ff // 4
    slots = hits.shape[1]
    cap = slots // group
    scale = head_size**-0.5

    index = lax.axis_index("dp")
    place = lax.axis_index("expert")
    core = index % 2
    at_x = (index // 2) % 2
    at_y = index // 4
    other = at_y * 4 + at_x * 2 + (1 - core)
    by_x = at_y * 4 + (1 - at_x) * 2 + core
    by_y = (1 - at_y) * 4 + at_x * 2 + core
    by_both = (1 - at_y) * 4 + (1 - at_x) * 2 + core
    partner = {"dp": other}
    along_x = {"dp": by_x}
    along_y = {"dp": by_y}
    over = {"dp": by_both}
    right = {"expert": (place + 1) % group}
    left = {"expert": (place + group - 1) % group}

    def ring_peer(k):
        return {"dp": (index + k) % parts}

    def rows_of(block):
        return pl.ds(pl.multiple_of(block * tok, tok), tok)

    def piece_of(number):
        return pl.ds(pl.multiple_of(number * piece, piece), piece)

    def qkv_spot(number):
        return w_qkv_buf.at[:, piece_of(number), :]

    def qkv_half(number, which):
        start = pl.multiple_of(number * piece + which * (piece // 2), piece // 2)
        return w_qkv_buf.at[:, pl.ds(start, piece // 2), :]

    def out_spot(number):
        return w_out_buf.at[:, piece_of(number)]

    def out_half(number, which):
        rows = pl.ds(which * (local_width // 2), local_width // 2)
        return w_out_buf.at[rows, piece_of(number)]

    class Gather:
        def __init__(self, number, source, spot, half_spot):
            self.number, self.source, self.spot, self.half_spot = number, source, spot, half_spot

        def copy(self, slot, source, target, peer):
            sems = gather_sems.at[self.number]
            return remote(source, target, sems.at[0, slot], sems.at[1, slot], peer)

        def own(self, slot, peer):
            return self.copy(slot, self.source, self.spot(index), peer)

        def keep(self):
            return pltpu.make_async_copy(
                self.source, self.spot(index), load_sems.at[16 + self.number]
            )

        def relay_x(self):
            spot = self.half_spot(by_y, 0)
            return self.copy(3, spot, spot, along_x)

        def relay_y(self):
            spot = self.half_spot(by_x, 1)
            return self.copy(4, spot, spot, along_y)

        def hand(self, slot):
            spot = (
                self.spot(by_x),
                self.spot(by_y),
                self.half_spot(by_both, 0),
                self.half_spot(by_both, 1),
            )[slot - 5]
            return self.copy(slot, spot, spot, partner)

        def begin(self):
            self.own(0, along_x).start()
            self.own(1, along_y).start()
            self.own(2, partner).start()
            self.keep().start()

        def relay(self):
            self.own(1, along_y).wait_recv()
            self.relay_x().start()
            self.own(0, along_x).wait_recv()
            self.relay_y().start()
            self.hand(5).start()
            self.hand(6).start()

        def finish(self):
            self.relay_x().wait_recv()
            self.hand(7).start()
            self.relay_y().wait_recv()
            self.hand(8).start()
            self.keep().wait()
            self.own(2, partner).wait_recv()
            for slot in (5, 6, 7, 8):
                self.hand(slot).wait_recv()

        def drain(self):
            for slot, peer in ((0, along_x), (1, along_y), (2, partner)):
                self.own(slot, peer).wait_send()
            self.relay_x().wait_send()
            self.relay_y().wait_send()
            for slot in (5, 6, 7, 8):
                self.hand(slot).wait_send()

    gather_qkv = Gather(0, w_qkv, qkv_spot, qkv_half)
    gather_out = Gather(1, w_out, out_spot, out_half)

    loads = [
        pltpu.make_async_copy(source, target, load_sems.at[number])
        for number, (source, target) in enumerate(
            [
                (tokens, tokens_buf.at[rows_of(place)]),
                (gain_one, gain_one_buf),
                (gain_two, gain_two_buf),
                (router_t, router_buf),
                (routes_t, rows_buf),
                (order_row, order_buf),
                (angles, angles_buf),
                (cotangent, cotangent_buf),
            ]
        )
    ]
    for load in loads:
        load.start()

    greet([ring_peer(k) for k in range(1, parts)] + [right, left])

    def own_pass(side, peer):
        return remote(
            tokens,
            tokens_buf.at[rows_of(place)],
            line_sems.at[side, place],
            line_sems.at[2, place],
            peer,
        )

    def pass_on(block, side, peer):
        spot = tokens_buf.at[rows_of(block)]
        return remote(spot, spot, line_sems.at[side, block], line_sems.at[2, block], peer)

    @pl.when(place < group - 1)
    def _():
        own_pass(0, right).start()

    @pl.when(place > 0)
    def _():
        own_pass(1, left).start()

    def small_copy(k):
        return remote(
            small,
            small_full.at[:, piece_of(index)],
            small_sems.at[0, k],
            small_sems.at[1, k],
            ring_peer(k),
        )

    gather_qkv.begin()

    for load in loads:
        load.wait()
    experts = router_t.shape[0]
    small[...] = jnp.zeros_like(small)
    for number in range(piece // LANES):
        lanes = slice(number * LANES, (number + 1) * LANES)
        small[0:1, lanes] = gain_one_buf[number : number + 1, :].astype(jnp.float32)
        small[1:2, lanes] = gain_two_buf[number : number + 1, :].astype(jnp.float32)
    small[2 : 2 + experts, :] = router_buf[...].astype(jnp.float32)
    small_full[:, piece_of(index)] = small[...]
    for k in range(1, parts):
        small_copy(k).start()

    rows = rows_buf[...]
    first_row, second_row, order_at = rows[0:1], rows[1:2], order_buf[...]
    square = (tok, tok)
    same = lax.broadcasted_iota(jnp.int32, square, 0) == lax.broadcasted_iota(jnp.int32, square, 1)

    def as_column(row):
        kept = jnp.where(same, jnp.broadcast_to(row.astype(jnp.float32), square), 0.0)
        return jnp.sum(kept, axis=1, keepdims=True).astype(jnp.int32)

    first_col, second_col, order_col = [as_column(r) for r in (first_row, second_row, order_at)]
    start = place * tok
    live_col = (start + lax.broadcasted_iota(jnp.int32, (tok, 1), 0)) < length[0]
    live_row = (start + lax.broadcasted_iota(jnp.int32, (1, tok), 1)) < length[0]
    before = order_col < order_at

    def count(mask):
        return jnp.sum(jnp.where(mask & live_col, 1.0, 0.0), axis=0, keepdims=True)

    slot_first = count((first_col == first_row) & before)
    slot_second = count(first_col == second_row) + count((second_col == second_row) & before)
    slot_ids = lax.broadcasted_iota(jnp.int32, (slots, tok), 0)
    for number, (named, slot) in enumerate(((first_row, slot_first), (second_row, slot_second))):
        slot = slot.astype(jnp.int32)
        step = named - place
        step = jnp.where(step < 0, step + group, step)
        target = jnp.where(live_row & (slot < cap), step * cap + slot, -1)
        hits[number] = jnp.where(slot_ids == target, 1.0, 0.0).astype(jnp.bfloat16)

    low = 32
    highs = seq_len // low
    sign = jnp.where(
        lax.broadcasted_iota(jnp.int32, (low, head_size), 1) < head_size // 2, -1.0, 1.0
    )
    cosine_low, sine_low = angles_buf[0, highs:, :], angles_buf[1, highs:, :]
    for number in range(highs):
        at = slice(number * low, (number + 1) * low)
        cosine_high = angles_buf[0, number : number + 1, :]
        sine_high = angles_buf[1, number : number + 1, :]
        cosine_buf[at, :] = cosine_high * cosine_low - sine_high * sine_low
        sine_buf[at, :] = sign * (sine_high * cosine_low + cosine_high * sine_low)

    for k in range(1, parts):
        small_copy(k).wait_recv()

    def normalize_block(block):
        at = rows_of(block)
        value = tokens_buf[at, :].astype(jnp.float32)
        inverse = lax.rsqrt(jnp.mean(value * value, axis=-1, keepdims=True) + NORM_EPSILON)
        inverse_all[at, :] = inverse
        whole_buf[at, :] = (value * inverse * small_full[0:1, :]).astype(jnp.bfloat16)

    def arrive(step):
        block = line_order(place, step)
        pass_on(block, 0, right).wait_recv()

        @pl.when((block < place) & (place < group - 1))
        def _():
            pass_on(block, 0, right).start()

        @pl.when((block > place) & (place > 0))
        def _():
            pass_on(block, 1, left).start()

        normalize_block(block)

    early = piece // 4

    def slice_copy(r, turn):
        number = (by_x // 2, by_y // 2, by_both // 2)[r - 1]
        part = turn // 2
        lanes = pl.ds(pl.multiple_of(part * ff + number * hidden, LANES), hidden)
        at = (pl.ds(0, early), pl.ds(early, piece - early), pl.ds(0, piece))[turn]
        return remote(
            w_gate_up.at[0, at, lanes],
            w_got.at[r - 1, at, pl.ds(part * hidden, hidden)],
            slice_sems.at[0, r - 1, turn],
            slice_sems.at[1, r - 1, turn],
            (along_x, along_y, over)[r - 1],
        )

    normalize_block(place)
    arrive(0)
    gather_qkv.relay()
    gather_out.begin()
    for r in (1, 2):
        slice_copy(r, 0).start()
    arrive(1)
    gather_qkv.finish()

    def project(first, size):
        at = pl.ds(pl.multiple_of(first, tok), size)
        source = whole_buf[at, :]

        def two_heads(number, carry):
            lanes = pl.ds(pl.multiple_of(number * 2 * head_size, 2 * head_size), 2 * head_size)
            for c, target in ((0, query), (1, key_rows)):
                plain = dot_nn(source, w_qkv_buf[c, :, lanes])
                turned = [
                    rotated(
                        plain[:, side * head_size : (side + 1) * head_size],
                        cosine_buf[at, :],
                        sine_buf[at, :],
                    )
                    for side in range(2)
                ]
                target[at, lanes] = jnp.concatenate(turned, axis=1).astype(jnp.bfloat16)
            value[at, lanes] = dot_nn(source, w_qkv_buf[2, :, lanes]).astype(jnp.bfloat16)
            return carry

        lax.fori_loop(0, heads // 2, two_heads, 0)

    upper = place // 2
    project(upper * tok, seq_len - tok)
    gather_out.relay()
    for turn in (1, 2):
        for r in (1, 2):
            slice_copy(r, turn).start()
    for turn in range(3):
        slice_copy(3, turn).start()
    arrive(2)
    project((1 - upper) * (seq_len - tok), tok)

    stores = [
        pltpu.make_async_copy(source, target, load_sems.at[10 + number])
        for number, (source, target) in enumerate(
            [
                (w_qkv_buf, qkv_full),
                (tokens_buf, tokens_all),
                (whole_buf, whole),
                (w_out_buf, out_full),
            ]
        )
    ]
    for store in stores[:3]:
        store.start()

    for number in range(group):
        at = slice(number * tok, (number + 1) * tok)
        extent = (number + 1) * tok
        shape = (tok, extent)
        at_query = number * tok + lax.broadcasted_iota(jnp.int32, shape, 0)
        at_key = lax.broadcasted_iota(jnp.int32, shape, 1)
        allowed = (at_key <= at_query) & (at_key < length[0])
        for head in range(heads):
            lanes = slice(head * head_size, (head + 1) * head_size)
            scores = dot_nt(query[at, lanes], key_rows[0:extent, lanes]) * scale
            scores = jnp.where(allowed, scores, NEGATIVE)
            top = jnp.max(scores, axis=-1, keepdims=True)
            exponent = jnp.exp(scores - top)
            row_total = jnp.sum(exponent, axis=-1, keepdims=True)
            probs = (exponent / row_total).astype(jnp.bfloat16)
            attended[at, lanes] = dot_nn(probs, value[0:extent, lanes]).astype(jnp.bfloat16)
            log_total[at, head : head + 1] = top + jnp.log(row_total)

    gather_out.finish()
    stores[3].start()

    def out_tile(j, carry):
        lanes = piece_of(j)
        part_buf[:, lanes] = dot_nn(attended[...], w_out_buf[:, lanes]).astype(jnp.bfloat16)
        return carry

    lax.fori_loop(0, parts, out_tile, 0)

    def go_right(block):
        return remote(
            part_buf.at[rows_of(block)],
            from_left.at[block],
            sum_sems.at[0, block],
            sum_sems.at[1, block],
            right,
        )

    def go_left(block):
        return remote(
            part_buf.at[rows_of(block)],
            from_right.at[block],
            sum_sems.at[0, block],
            sum_sems.at[2, block],
            left,
        )

    def add_into(target, added):
        total = target[...].astype(jnp.float32) + added[...].astype(jnp.float32)
        target[...] = total.astype(jnp.bfloat16)

    def on_right(block):
        go_right(block).wait_recv()
        add_into(part_buf.at[rows_of(block)], from_left.at[block])
        go_right(block).start()

    def on_left(block):
        go_left(block).wait_recv()
        add_into(part_buf.at[rows_of(block)], from_right.at[block])
        go_left(block).start()

    @pl.when(place == 0)
    def _():
        for block in (3, 2, 1):
            go_right(block).start()

    @pl.when(place == 3)
    def _():
        for block in (0, 1, 2):
            go_left(block).start()

    @pl.when(place == 1)
    def _():
        on_right(3)
        on_right(2)
        on_left(0)

    @pl.when(place == 2)
    def _():
        on_left(0)
        on_left(1)
        on_right(3)

    resid[...] = tokens_buf[rows_of(place), :].astype(jnp.float32) + part_buf[
        rows_of(place), :
    ].astype(jnp.float32)

    @pl.when(place > 0)
    def _():
        go_right(place).wait_recv()
        resid[...] += from_left[place].astype(jnp.float32)

    @pl.when(place < group - 1)
    def _():
        go_left(place).wait_recv()
        resid[...] += from_right[place].astype(jnp.float32)

    total = resid[...]
    inverse = lax.rsqrt(jnp.mean(total * total, axis=-1, keepdims=True) + NORM_EPSILON)
    inverse_two[...] = inverse
    hidden_in = (total * inverse * small_full[1:2, :]).astype(jnp.bfloat16)
    logits = dot_nt(hidden_in, small_full[...].astype(jnp.bfloat16))
    lane = lax.broadcasted_iota(jnp.int32, logits.shape, 1)
    chosen = [
        jnp.sum(jnp.where(lane == named + 2, logits, 0.0), axis=1, keepdims=True)
        for named in (first_col, second_col)
    ]
    top = jnp.maximum(chosen[0], chosen[1])
    raised = [jnp.exp(entry - top) for entry in chosen]
    both = raised[0] + raised[1]
    gate = [entry / both for entry in raised]
    for number in range(2):
        gates[:, number : number + 1] = gate[number]
    sent[...] = dot_nn(hits[0] + hits[1], hidden_in).astype(jnp.bfloat16)
    d_out = jnp.where(live_col, 1.0, 0.0) * cotangent_buf[...].astype(jnp.float32)
    d_back[...] = (
        dot_nn(hits[0], (gate[0] * d_out).astype(jnp.bfloat16))
        + dot_nn(hits[1], (gate[1] * d_out).astype(jnp.bfloat16))
    ).astype(jnp.bfloat16)

    for store in stores:
        store.wait()
    gather_qkv.drain()
    gather_out.drain()
    for k in range(1, parts):
        small_copy(k).wait_send()
    for block in range(group):

        @pl.when(block > place)
        def _():
            go_right(block).wait_send()

        @pl.when(block < place)
        def _():
            go_left(block).wait_send()

        @pl.when((block <= place) & (place < group - 1))
        def _():
            pass_on(block, 0, right).wait_send()

        @pl.when((block >= place) & (place > 0))
        def _():
            pass_on(block, 1, left).wait_send()

    for turn in range(3):
        for r in (1, 2, 3):
            slice_copy(r, turn).wait()


def attention_call(
    lengths,
    tokens,
    w_qkv,
    w_out,
    gain_one,
    gain_two,
    router_t,
    w_gate_up,
    routes_t,
    order_row,
    angles,
    cotangent,
    group,
):
    tok, width = tokens.shape
    seq_len = tok * group
    local_width = w_qkv.shape[2]
    heads = local_width // HEAD_DIM
    slots = tok * 2
    piece = w_qkv.shape[1]
    low, full = jnp.bfloat16, jnp.float32
    anywhere = pl.BlockSpec(memory_space=pl.ANY)
    inside = pl.BlockSpec(memory_space=pltpu.VMEM)
    narrow = jax.ShapeDtypeStruct((seq_len, local_width), low)
    flops = 2 * seq_len * width * local_width * 4 + 4 * seq_len * seq_len * local_width
    return pl.pallas_call(
        functools.partial(attention_kernel, heads),
        out_shape=(
            jax.ShapeDtypeStruct((seq_len, width), low),
            jax.ShapeDtypeStruct((seq_len, width), low),
            jax.ShapeDtypeStruct((3, width, local_width), low),
            jax.ShapeDtypeStruct((local_width, width), low),
            jax.ShapeDtypeStruct((3, piece, w_gate_up.shape[2] // 4), low),
            jax.ShapeDtypeStruct((seq_len, 1), full),
            narrow,
            narrow,
            narrow,
            narrow,
            jax.ShapeDtypeStruct((seq_len, heads), full),
            jax.ShapeDtypeStruct((8, width), full),
            jax.ShapeDtypeStruct((seq_len, HEAD_DIM), full),
            jax.ShapeDtypeStruct((seq_len, HEAD_DIM), full),
            jax.ShapeDtypeStruct((tok, width), full),
            jax.ShapeDtypeStruct((tok, 1), full),
            jax.ShapeDtypeStruct((tok, 2), full),
            jax.ShapeDtypeStruct((2, slots, tok), low),
            jax.ShapeDtypeStruct((slots, width), low),
            jax.ShapeDtypeStruct((slots, width), low),
        ),
        in_specs=[pl.BlockSpec(memory_space=pltpu.SMEM)] + [anywhere] * 11,
        out_specs=(anywhere,) * 5 + (inside,) * 15,
        scratch_shapes=[
            pltpu.VMEM((seq_len, width), low),
            pltpu.VMEM((seq_len, width), low),
            pltpu.VMEM((3, width, local_width), low),
            pltpu.VMEM((local_width, width), low),
            pltpu.VMEM((seq_len, width), low),
            pltpu.VMEM((group, tok, width), low),
            pltpu.VMEM((group, tok, width), low),
            pltpu.VMEM(routes_t.shape, jnp.int32),
            pltpu.VMEM(order_row.shape, jnp.int32),
            pltpu.VMEM(angles.shape, full),
            pltpu.VMEM((tok, width), low),
            pltpu.VMEM(gain_one.shape, low),
            pltpu.VMEM(gain_two.shape, low),
            pltpu.VMEM(router_t.shape, low),
            pltpu.VMEM((8, piece), full),
            pltpu.SemaphoreType.DMA((18,)),
            pltpu.SemaphoreType.DMA((3, group)),
            pltpu.SemaphoreType.DMA((3, group)),
            pltpu.SemaphoreType.DMA((2, 2, 9)),
            pltpu.SemaphoreType.DMA((2, width // piece)),
            pltpu.SemaphoreType.DMA((2, 3, 3)),
        ],
        compiler_params=pltpu.CompilerParams(
            collective_id=3, has_side_effects=True, vmem_limit_bytes=67043328
        ),
        cost_estimate=pl.CostEstimate(flops=flops, bytes_accessed=40000000, transcendentals=0),
        name="attention",
    )(
        lengths,
        tokens,
        w_qkv,
        w_out,
        gain_one,
        gain_two,
        router_t,
        w_gate_up,
        routes_t,
        order_row,
        angles,
        cotangent,
    )


def expert_step(gate_up_w, down_w, rows, d_rows_out):
    ff = down_w.shape[0]
    gate_up = jnp.dot(rows, gate_up_w, preferred_element_type=jnp.float32)
    gate = gate_up[:, :ff]
    upward = gate_up[:, ff:]
    sigmoid = jax.nn.sigmoid(gate)
    activated = (gate * sigmoid * upward).astype(jnp.bfloat16)
    out = jnp.dot(activated, down_w, preferred_element_type=jnp.float32).astype(jnp.bfloat16)
    d_activated = contract_last(d_rows_out, down_w)
    grad_down = contract_first(activated, d_rows_out)
    d_gate = d_activated * upward * sigmoid * (1.0 + gate * (1.0 - sigmoid))
    d_up = d_activated * gate * sigmoid
    d_gate_up = jnp.concatenate([d_gate, d_up], axis=1).astype(jnp.bfloat16)
    d_rows = contract_last(d_gate_up, gate_up_w).astype(jnp.bfloat16)
    grad_gate_up = contract_first(rows, d_gate_up)
    return out, d_rows, grad_gate_up, grad_down


def experts_gather_weights(w_gate_up, w_down, rows, d_rows_out):
    gate_up_w = lax.all_gather(w_gate_up, "dp", axis=1, tiled=True)[0]
    down_w = lax.all_gather(w_down, "dp", axis=1, tiled=True)[0]
    shape = rows.shape
    flat = (-1, shape[2])
    rows = exchange_experts(rows).reshape(flat)
    d_rows_out = exchange_experts(d_rows_out).reshape(flat)
    out, d_rows, grad_gate_up, grad_down = expert_step(gate_up_w, down_w, rows, d_rows_out)
    out = exchange_experts(out.reshape(shape))
    d_rows = exchange_experts(d_rows.reshape(shape))
    grad_gate_up = lax.psum_scatter(
        grad_gate_up.astype(jnp.bfloat16), "dp", scatter_dimension=0, tiled=True
    )
    grad_down = lax.psum_scatter(
        grad_down.astype(jnp.bfloat16), "dp", scatter_dimension=0, tiled=True
    )
    return (
        out,
        d_rows,
        grad_gate_up.astype(jnp.float32)[None],
        grad_down.astype(jnp.float32)[None],
    )


def attention_back_plain(
    lengths,
    d_attn,
    hat_all,
    whole,
    out_full,
    qkv_full,
    query,
    key_rows,
    value,
    attended,
    log_total,
    cosine,
    sine,
):
    seq_len, heads_local, head_size = query.shape
    local_width = heads_local * head_size
    position = jnp.arange(seq_len, dtype=jnp.int32)
    allowed = (position[None, :] <= position[:, None]) & (position < lengths[0])[None, :]
    whole_grad = lax.all_gather(d_attn, "expert", axis=0, tiled=True)
    d_attended = contract_last(whole_grad, out_full).astype(jnp.bfloat16)
    out_part = contract_first(attended, whole_grad)
    grad_out = lax.psum_scatter(
        out_part.astype(jnp.bfloat16), "dp", scatter_dimension=1, tiled=True
    ).astype(jnp.float32)
    d_heads = d_attended.reshape(seq_len, heads_local, head_size)
    probs = jnp.exp(masked_scores(query, key_rows, allowed) - log_total)
    probs_low = probs.astype(jnp.bfloat16)
    d_value = jnp.einsum(
        "hqk,qhd->khd", probs_low, d_heads, preferred_element_type=jnp.float32
    ).astype(jnp.bfloat16)
    d_probs = jnp.einsum("qhd,khd->hqk", d_heads, value, preferred_element_type=jnp.float32)
    row_delta = jnp.sum(probs * d_probs, axis=-1, keepdims=True)
    d_scores = (probs * (d_probs - row_delta)).astype(jnp.bfloat16)
    scale = head_size ** (-0.5)
    d_query = (
        jnp.einsum("hqk,khd->qhd", d_scores, key_rows, preferred_element_type=jnp.float32) * scale
    )
    d_key = jnp.einsum("hqk,qhd->khd", d_scores, query, preferred_element_type=jnp.float32) * scale
    d_query_pre = (
        rotate_back(d_query, cosine, sine).reshape(seq_len, local_width).astype(jnp.bfloat16)
    )
    d_key_pre = rotate_back(d_key, cosine, sine).reshape(seq_len, local_width).astype(jnp.bfloat16)
    d_projected = jnp.stack([d_query_pre, d_key_pre, d_value.reshape(seq_len, local_width)])
    d_normed_part = jnp.einsum(
        "cte,cde->td", d_projected, qkv_full, preferred_element_type=jnp.float32
    )
    grad_normalized = lax.psum_scatter(
        d_normed_part.astype(jnp.bfloat16), "expert", scatter_dimension=0, tiled=True
    ).astype(jnp.float32)
    qkv_part = jnp.einsum("td,cte->cde", whole, d_projected, preferred_element_type=jnp.float32)
    grad_qkv = lax.psum_scatter(
        qkv_part.astype(jnp.bfloat16), "dp", scatter_dimension=1, tiled=True
    ).astype(jnp.float32)
    first_gain_part = jnp.sum(d_normed_part * hat_all, axis=0)
    return grad_normalized, grad_qkv, grad_out, first_gain_part


def on_device(
    tokens,
    w_qkv,
    w_out,
    attention_norm_gain,
    gain_ffn,
    w_router,
    w_gate_up,
    w_down,
    lengths,
    routes,
    order,
    cotangent,
):
    group_size = lax.axis_size("expert")
    dp_size = lax.axis_size("dp")
    tok_dev = tokens.shape[0]
    seq_len = tok_dev * group_size
    width = tokens.shape[1]
    top_count = routes.shape[1]
    capacity = tok_dev * top_count // group_size
    slots = group_size * capacity
    head_size = HEAD_DIM
    local_width = w_qkv.shape[2]
    heads_local = local_width // head_size
    tokens_all = lax.all_gather(tokens, "expert", axis=0, tiled=True)
    small = jnp.concatenate(
        [attention_norm_gain[:, None], gain_ffn[:, None], w_router], axis=1
    )
    small_full = lax.all_gather(small, "dp", axis=0, tiled=True)
    qkv_full = lax.all_gather(w_qkv, "dp", axis=1, tiled=True)
    out_full = lax.all_gather(w_out, "dp", axis=1, tiled=True)
    first_norm_gain = small_full[:, 0].astype(jnp.float32)
    gain_two = small_full[:, 1].astype(jnp.float32)
    router_full = small_full[:, 2:]

    own_start = lax.axis_index("expert") * tok_dev
    own_position = own_start + jnp.arange(tok_dev, dtype=jnp.int32)
    live_own = own_position < lengths[0]
    live_rows = live_own.astype(jnp.float32)[:, None]
    target, kept_pair = slot_table(routes, order, live_own, capacity)
    slot_ids = jnp.arange(slots, dtype=jnp.int32)
    pair_hits = (slot_ids[:, None, None] == target[None]) & kept_pair[None]
    select = jnp.sum(pair_hits.astype(jnp.float32), axis=2).astype(jnp.bfloat16)

    inputs_float = tokens.astype(jnp.float32)
    input_normalized_hat, first_inverse_rms = normalize(inputs_float)
    hat_all, _ = normalize(tokens_all.astype(jnp.float32))
    whole = (hat_all * first_norm_gain).astype(jnp.bfloat16)
    cosine, sine = rotary_tables(seq_len, head_size)
    projected = jnp.einsum("td,cde->cte", whole, qkv_full, preferred_element_type=jnp.float32)
    query = rotate(projected[0].reshape(seq_len, heads_local, head_size), cosine, sine).astype(
        jnp.bfloat16
    )
    key_rows = rotate(projected[1].reshape(seq_len, heads_local, head_size), cosine, sine).astype(
        jnp.bfloat16
    )
    value = projected[2].astype(jnp.bfloat16).reshape(seq_len, heads_local, head_size)
    position = jnp.arange(seq_len, dtype=jnp.int32)
    live_all = position < lengths[0]
    allowed = (position[None, :] <= position[:, None]) & live_all[None, :]
    scores = masked_scores(query, key_rows, allowed)
    top_score = jnp.max(scores, axis=-1, keepdims=True)
    exponent = jnp.exp(scores - top_score)
    row_total = jnp.sum(exponent, axis=-1, keepdims=True)
    probs = exponent / row_total
    log_total = top_score + jnp.log(row_total)
    probs_low = probs.astype(jnp.bfloat16)
    attended = jnp.einsum("hqk,khd->qhd", probs_low, value, preferred_element_type=jnp.float32)
    attended = attended.reshape(seq_len, local_width).astype(jnp.bfloat16)
    attn_part = jnp.dot(attended, out_full, preferred_element_type=jnp.float32)
    attn_own = lax.psum_scatter(
        attn_part.astype(jnp.bfloat16), "expert", scatter_dimension=0, tiled=True
    ).astype(jnp.float32)
    resid = inputs_float + attn_own
    hhat, inverse_two = normalize(resid)
    hidden_in = (hhat * gain_two).astype(jnp.bfloat16)
    sent = jnp.dot(select, hidden_in, preferred_element_type=jnp.float32).astype(jnp.bfloat16)

    logits = jnp.dot(hidden_in, router_full, preferred_element_type=jnp.float32)
    chosen = jnp.take_along_axis(logits, routes, axis=1)
    gates = jax.nn.softmax(chosen, axis=1)
    d_out = live_rows * cotangent.astype(jnp.float32)
    d_back = jnp.zeros((slots, width), jnp.float32)
    for index in range(top_count):
        weighted = (gates[:, index : index + 1] * d_out).astype(jnp.bfloat16)
        d_back = d_back + jnp.dot(
            pair_hits[:, :, index].astype(jnp.bfloat16),
            weighted,
            preferred_element_type=jnp.float32,
        )
    d_back = d_back.astype(jnp.bfloat16)
    blocked = (group_size, capacity, width)
    returned, d_sent, grad_gate_up, grad_down = experts_gather_weights(
        w_gate_up, w_down, sent.reshape(blocked), d_back.reshape(blocked)
    )
    returned = returned.reshape(slots, width)
    d_sent = d_sent.reshape(slots, width)

    moe = jnp.zeros_like(resid)
    d_gates_list = []
    for index in range(top_count):
        one_hot = pair_hits[:, :, index].astype(jnp.bfloat16)
        picked = contract_first(one_hot, returned)
        d_gates_list.append(jnp.sum(d_out * picked, axis=-1))
        moe = moe + gates[:, index : index + 1] * picked
    output = (live_rows * (resid + moe)).astype(jnp.bfloat16)
    d_gates = jnp.stack(d_gates_list, axis=1)
    d_hidden = contract_first(select, d_sent)
    d_chosen = gates * (d_gates - jnp.sum(gates * d_gates, axis=1, keepdims=True))
    expert_ids = jnp.arange(group_size, dtype=jnp.int32)
    route_hits = (routes[:, :, None] == expert_ids[None, None, :]).astype(jnp.float32)
    d_logits = jnp.sum(route_hits * d_chosen[:, :, None], axis=1)
    router_f = router_full.astype(jnp.float32)
    d_hidden = d_hidden + jnp.dot(
        d_logits, router_f.T, precision=HIGH, preferred_element_type=jnp.float32
    )
    router_part = jnp.dot(
        hidden_in.astype(jnp.float32).T,
        d_logits,
        precision=HIGH,
        preferred_element_type=jnp.float32,
    )
    gain_two_part = jnp.sum(d_hidden * hhat, axis=0)
    scaled_two = d_hidden * gain_two
    d_resid = d_out + inverse_two * (
        scaled_two - hhat * jnp.mean(scaled_two * hhat, axis=-1, keepdims=True)
    )
    d_attn = d_resid.astype(jnp.bfloat16)
    grad_normalized, grad_qkv, grad_out, first_gain_part = attention_back_plain(
        lengths,
        d_attn,
        hat_all,
        whole,
        out_full,
        qkv_full,
        query,
        key_rows,
        value,
        attended,
        log_total,
        cosine,
        sine,
    )
    small_part = jnp.concatenate(
        [first_gain_part[None], gain_two_part[None], router_part.T], axis=0
    )
    small_sum = lax.psum(small_part, ("dp", "expert"))
    own_rows = width // dp_size
    small_own = lax.dynamic_slice_in_dim(
        small_sum, lax.axis_index("dp") * own_rows, own_rows, axis=1
    )
    first_scaled_input = grad_normalized * first_norm_gain
    grad_tokens = d_resid + first_inverse_rms * (
        first_scaled_input
        - input_normalized_hat
        * jnp.mean(first_scaled_input * input_normalized_hat, axis=-1, keepdims=True)
    )
    return (
        output,
        grad_tokens.astype(jnp.bfloat16),
        grad_qkv,
        grad_out,
        small_own[0],
        small_own[1],
        small_own[2 : 2 + group_size].T,
        grad_gate_up,
        grad_down,
    )


def on_device_split(
    tokens,
    w_qkv,
    w_out,
    attention_norm_gain,
    gain_ffn,
    w_router,
    w_gate_up,
    w_down,
    lengths,
    routes,
    order,
    cotangent,
):
    group = lax.axis_size("expert")
    tok, width = tokens.shape
    piece = w_router.shape[0]
    slots = tok * routes.shape[1]
    angles = rotary_constants(tok * group, HEAD_DIM)
    routes_t = routes.T
    (
        tokens_all,
        whole,
        qkv_full,
        out_full,
        w_got,
        inverse_all,
        query,
        key_rows,
        value,
        attended,
        log_total,
        small_full,
        cosine,
        sine,
        resid,
        inverse_two,
        gates,
        hits,
        sent,
        d_back,
    ) = attention_call(
        lengths,
        tokens,
        w_qkv,
        w_out,
        attention_norm_gain.reshape(-1, LANES),
        gain_ffn.reshape(-1, LANES),
        w_router.T,
        w_gate_up,
        routes_t,
        order.reshape(1, tok),
        angles,
        cotangent,
        group,
    )
    blocked = (group, slots // group, width)
    returned, d_sent, grad_gate_up, grad_down = experts_call(
        sent.reshape(blocked), d_back.reshape(blocked), w_gate_up, w_got, w_down
    )
    output, grad_tokens, grad_weights, small_own, gate_got = attention_back_call(
        lengths,
        returned.reshape(slots, width),
        d_sent.reshape(slots, width),
        resid,
        inverse_two,
        gates,
        hits,
        cotangent,
        routes_t,
        small_full,
        tokens_all,
        inverse_all,
        whole,
        out_full,
        qkv_full,
        query,
        key_rows,
        value,
        attended,
        log_total,
        cosine,
        sine,
        grad_gate_up,
    )
    (
        grad_gate_up,
        grad_down,
        grad_tokens,
        output,
        grad_qkv,
        grad_out,
        gain_one,
        gain_two,
        router,
    ) = finish_call(gate_got, grad_down, grad_tokens, output, grad_weights, small_own, group)
    return (
        output,
        grad_tokens,
        grad_qkv,
        grad_out,
        gain_one.reshape(piece),
        gain_two.reshape(piece),
        router.T,
        grad_gate_up,
        grad_down,
    )


def solution(mesh):
    placed = (
        P(("dp", "expert"), None),
        P(None, "dp", "expert"),
        P("expert", "dp"),
        P("dp"),
        P("dp"),
        P("dp", None),
        P("expert", "dp", None),
        P("expert", "dp", None),
        P("dp"),
        P(("dp", "expert"), None),
        P(("dp", "expert")),
        P(("dp", "expert"), None),
    )
    split = mesh.shape["dp"] == 8 and mesh.shape["expert"] == 4
    return jax.shard_map(
        on_device_split if split else on_device,
        mesh=mesh,
        in_specs=placed,
        out_specs=(
            P(("dp", "expert"), None),
            P(("dp", "expert"), None),
            P(None, "dp", "expert"),
            P("expert", "dp"),
            P("dp"),
            P("dp"),
            P("dp", None),
            P("expert", "dp", None),
            P("expert", "dp", None),
        ),
        check_vma=False,
    )
```

```python
import functools

import jax
import jax.numpy as jnp
import numpy as np
from jax import lax
from jax.experimental import pallas as pl
from jax.experimental.pallas import tpu as pltpu
from jax.sharding import PartitionSpec as P

HEAD_DIM = 128
FF = 5632


NORM_EPSILON = 1e-05
NEGATIVE = -1e30
THETA = 10000.0
HIGH = lax.Precision.HIGHEST
MESH_ID = pl.DeviceIdType.MESH
LANES = 128


def remote(src, dst, send_sem, recv_sem, peer):
    return pltpu.make_async_remote_copy(
        src_ref=src,
        dst_ref=dst,
        send_sem=send_sem,
        recv_sem=recv_sem,
        device_id=peer,
        device_id_type=MESH_ID,
    )


def greet(peers):
    barrier = pltpu.get_barrier_semaphore()
    for peer in peers:
        pl.semaphore_signal(barrier, inc=1, device_id=peer, device_id_type=MESH_ID)
    pl.semaphore_wait(barrier, len(peers))


def dot_nn(left, right):
    return jnp.dot(left, right, preferred_element_type=jnp.float32)


def dot_nt(left, right):
    return lax.dot_general(
        left, right, (((1,), (1,)), ((), ())), preferred_element_type=jnp.float32
    )


def experts_kernel(
    group,
    sent,
    d_back,
    w_gate_up,
    w_got,
    w_down,
    ret,
    d_ret,
    grad_gate_up,
    grad_down,
    w_buf,
    down_buf,
    rows_buf,
    gate_buf,
    act_buf,
    part_buf,
    half_x,
    half_y,
    full_x,
    full_y,
    other_gate,
    other_down,
    ag_sems,
    rs_sems,
    weight_sems,
    local_sems,
    grad_sems,
):
    cap, width = sent.shape[1], sent.shape[2]
    half = cap // 2
    piece, hidden2 = w_got.shape[1:]
    hidden = hidden2 // 2
    down_own = w_down.at[0]
    down_rows = down_own.shape[0]
    chunk = 4 * cap
    total = group * chunk

    index = lax.axis_index("dp")
    place = lax.axis_index("expert")
    core = index % 2
    at_x = (index // 2) % 2
    at_y = index // 4
    partner = {"dp": at_y * 4 + at_x * 2 + (1 - core)}
    along_x = {"dp": at_y * 4 + (1 - at_x) * 2 + core}
    along_y = {"dp": (1 - at_y) * 4 + at_x * 2 + core}
    chips = [
        at_y * 2 + at_x,
        at_y * 2 + (1 - at_x),
        (1 - at_y) * 2 + at_x,
        (1 - at_y) * 2 + (1 - at_x),
    ]

    def ahead(k):
        return {"expert": (place + k) % group}

    def behind(k):
        return {"expert": (place + group - k) % group}

    greet([partner, along_x, along_y] + [ahead(k) for k in range(1, group)])

    def block(t, k, r, start=0, size=None):
        size = cap if size is None else size
        return rows_buf.at[t, pl.ds((k * 4 + r) * cap + start, size), :]

    def part(t, k, r, start=0, size=None):
        size = cap if size is None else size
        return part_buf.at[t, pl.ds((k * 4 + r) * cap + start, size), :]

    def ag(kind, t, k):
        return ag_sems.at[0, kind, t, k], ag_sems.at[1, kind, t, k]

    def rs(kind, t, k):
        return rs_sems.at[0, kind, t, k], rs_sems.at[1, kind, t, k]

    sources = (sent, d_back)
    results = (ret, d_ret)

    def z_copy(t, k):
        return remote(sources[t].at[k], block(t, k, 0), *ag(0, t, k), ahead(k))

    def own_copy(t):
        return pltpu.make_async_copy(sources[t].at[0], block(t, 0, 0), local_sems.at[t])

    def x_copy(t, k):
        return remote(block(t, k, 0), block(t, k, 1), *ag(1, t, k), along_x)

    def y_copy(t, k):
        return remote(block(t, k, 0), block(t, k, 2), *ag(2, t, k), along_y)

    def a_copy(t, k):
        return remote(block(t, k, 2, 0, half), block(t, k, 3, 0, half), *ag(3, t, k), along_x)

    def b_copy(t, k):
        return remote(
            block(t, k, 1, half, half), block(t, k, 3, half, half), *ag(4, t, k), along_y
        )

    def spread(t, k):
        if k == 0:
            own_copy(t).wait()
        else:
            z_copy(t, k).wait_recv()
        x_copy(t, k).start()
        y_copy(t, k).start()

    def relay_a(t, k):
        y_copy(t, k).wait_recv()
        a_copy(t, k).start()

    def relay_b(t, k):
        x_copy(t, k).wait_recv()
        b_copy(t, k).start()

    def arrived(t, k):
        a_copy(t, k).wait_recv()
        b_copy(t, k).wait_recv()
        if t == 0 and k == 0:
            for r in range(4):
                for copy in w_keep(r):
                    copy.wait()
                for copy in w_share(r, 1 - core):
                    copy.wait_recv()
            down_keep.wait()
            down_share().wait_recv()

    def half_x_copy(t, k):
        return remote(part(t, k, 3, 0, half), half_x.at[t, k], *rs(0, t, k), along_x)

    def half_y_copy(t, k):
        return remote(part(t, k, 3, half, half), half_y.at[t, k], *rs(1, t, k), along_y)

    def full_x_copy(t, k):
        return remote(part(t, k, 1), full_x.at[t, k], *rs(2, t, k), along_x)

    def full_y_copy(t, k):
        return remote(part(t, k, 2), full_y.at[t, k], *rs(3, t, k), along_y)

    def back_copy(t, k):
        return remote(part(t, k, 0), results[t].at[k], *rs(4, t, k), behind(k))

    def keep_copy(t):
        return pltpu.make_async_copy(part(t, 0, 0), results[t].at[0], local_sems.at[2 + t])

    def halves_out(t, k):
        half_x_copy(t, k).start()
        half_y_copy(t, k).start()

    def add_into(target, *others):
        value = target[...].astype(jnp.float32)
        for other in others:
            value = value + other[...].astype(jnp.float32)
        target[...] = value.astype(jnp.bfloat16)

    def full_y_out(t, k):
        half_x_copy(t, k).wait_recv()
        add_into(part(t, k, 2, 0, half), half_x.at[t, k])
        full_y_copy(t, k).start()

    def full_x_out(t, k):
        half_y_copy(t, k).wait_recv()
        add_into(part(t, k, 1, half, half), half_y.at[t, k])
        full_x_copy(t, k).start()

    def home(t, k):
        full_x_copy(t, k).wait_recv()
        full_y_copy(t, k).wait_recv()
        add_into(part(t, k, 0), full_x.at[t, k], full_y.at[t, k])
        if k == 0:
            keep_copy(t).start()
        else:
            back_copy(t, k).start()

    def w_rows(r, which):
        return pl.ds(pl.multiple_of((chips[r] * 2 + which) * piece, piece), piece)

    def w_parts(r, which):
        rows = w_rows(r, which)
        if r > 0:
            return [(w_got.at[r - 1], w_buf.at[rows, :], r)]
        return [
            (
                w_gate_up.at[
                    0, :, pl.ds(pl.multiple_of((4 * part + chips[0]) * hidden, LANES), hidden)
                ],
                w_buf.at[rows, pl.ds(part * hidden, hidden)],
                4 * part,
            )
            for part in range(2)
        ]

    def w_share(r, which):
        return [
            remote(source, target, weight_sems.at[0, n], weight_sems.at[1, n], partner)
            for source, target, n in w_parts(r, which)
        ]

    def w_keep(r):
        return [
            pltpu.make_async_copy(source, target, local_sems.at[4 + n])
            for source, target, n in w_parts(r, core)
        ]

    def down_at(which):
        return down_buf.at[pl.ds(pl.multiple_of(which * down_rows, down_rows), down_rows), :]

    def down_share():
        return remote(
            down_own, down_at(core), weight_sems.at[0, 5], weight_sems.at[1, 5], partner
        )

    down_keep = pltpu.make_async_copy(down_own, down_at(core), local_sems.at[9])

    def take(steps, k, number):
        for at in range(group):
            if (at, number) in steps:

                @pl.when(k == at)
                def _(events=steps[at, number]):
                    for event, t, which in events:
                        event(t, which)

    blocks = hidden // LANES
    spans = [(2 * j, min(2, blocks - 2 * j)) for j in range((blocks + 1) // 2)]
    tiles = width // (2 * LANES)

    def span(first, count):
        return pl.ds(first * LANES, count * LANES)

    def forward(k, carry):
        at = pl.ds(pl.multiple_of(k * chunk, chunk), chunk)

        def tile(first, count):
            gate_cols, up_cols = span(first, count), span(blocks + first, count)
            rows = rows_buf[0, at, :]
            if count == 1:
                weights = jnp.concatenate([w_buf[:, gate_cols], w_buf[:, up_cols]], axis=1)
                both = dot_nn(rows, weights)
                gate, up = both[:, :LANES], both[:, LANES:]
            else:
                gate = dot_nn(rows, w_buf[:, gate_cols])
                up = dot_nn(rows, w_buf[:, up_cols])
            sigmoid = 1.0 / (1.0 + jnp.exp(-gate))
            gate_buf[at, gate_cols] = gate.astype(jnp.bfloat16)
            gate_buf[at, up_cols] = up.astype(jnp.bfloat16)
            act_buf[at, gate_cols] = (gate * sigmoid * up).astype(jnp.bfloat16)

        take(forward_steps, k, 0)
        for first, count in spans[:3]:
            tile(first, count)
        take(forward_steps, k, 1)
        for first, count in spans[3:]:
            tile(first, count)
        take(forward_steps, k, 2)
        for j in range(tiles):
            cols = span(2 * j, 2)
            out = dot_nn(act_buf[at, :], down_buf[:, cols])
            part_buf[0, at, cols] = out.astype(jnp.bfloat16)
        return carry

    def backward(turn, carry):
        k = (turn + 1) % group
        at = pl.ds(pl.multiple_of(k * chunk, chunk), chunk)
        take(backward_steps, k, 0)
        for first, count in spans:
            gate_cols, up_cols = span(first, count), span(blocks + first, count)
            d_act = dot_nt(rows_buf[1, at, :], down_buf[gate_cols, :])
            gate = gate_buf[at, gate_cols].astype(jnp.float32)
            up = gate_buf[at, up_cols].astype(jnp.float32)
            sigmoid = 1.0 / (1.0 + jnp.exp(-gate))
            scaled = d_act * sigmoid
            d_gate = scaled * up * (1.0 + gate * (1.0 - sigmoid))
            gate_buf[at, gate_cols] = d_gate.astype(jnp.bfloat16)
            gate_buf[at, up_cols] = (scaled * gate).astype(jnp.bfloat16)
        for side in range(2):
            take(backward_steps, k, 1 + side)
            for j in range(side * (tiles // 2), (side + 1) * (tiles // 2)):
                cols = span(2 * j, 2)
                out = dot_nt(gate_buf[at, :], w_buf[cols, :])
                part_buf[1, at, cols] = out.astype(jnp.bfloat16)
        return carry

    forward_steps = {
        (0, 0): [(spread, 0, 0), (spread, 1, 0), (relay_a, 0, 0), (relay_b, 0, 0), (spread, 0, 1), (relay_a, 1, 0), (relay_b, 1, 0), (arrived, 0, 0)],
        (0, 2): [(spread, 0, 2)],
        (1, 0): [(relay_a, 0, 1), (relay_b, 0, 1), (spread, 0, 3), (halves_out, 0, 0), (relay_a, 0, 2), (relay_b, 0, 2), (spread, 1, 1), (arrived, 0, 1)],
        (2, 0): [(relay_a, 0, 3), (relay_b, 0, 3), (halves_out, 0, 1), (spread, 1, 2), (arrived, 0, 2)],
        (2, 1): [(spread, 1, 3)],
        (3, 0): [(relay_a, 1, 1), (arrived, 0, 3)],
        (3, 1): [(relay_b, 1, 1), (full_y_out, 0, 0)],
    }
    backward_steps = {
        (0, 0): [(home, 0, 2), (halves_out, 1, 3), (arrived, 1, 0)],
        (0, 2): [(home, 0, 3), (full_y_out, 1, 2), (full_x_out, 1, 2)],
        (1, 0): [(full_x_out, 0, 0), (full_y_out, 0, 1), (relay_a, 1, 2), (relay_b, 1, 2), (relay_a, 1, 3), (relay_b, 1, 3), (arrived, 1, 1)],
        (1, 1): [(full_x_out, 0, 1), (halves_out, 0, 2)],
        (1, 2): [(halves_out, 0, 3), (home, 0, 0)],
        (2, 0): [(halves_out, 1, 1), (arrived, 1, 2)],
        (2, 2): [(home, 0, 1), (full_y_out, 0, 2), (full_x_out, 0, 2)],
        (3, 0): [(full_y_out, 0, 3), (full_x_out, 0, 3), (halves_out, 1, 2), (arrived, 1, 3)],
        (3, 1): [(full_y_out, 1, 1)],
        (3, 2): [(full_x_out, 1, 1)],
    }
    grad_steps = {
        (1, 0): [(halves_out, 1, 0)],
        (2, 0): [(full_y_out, 1, 3), (full_x_out, 1, 3), (home, 1, 1)],
        (2, 2): [(home, 1, 2)],
        (2, 3): [(full_y_out, 1, 0), (full_x_out, 1, 0)],
        (4, 0): [(home, 1, 3)],
        (4, 2): [(home, 1, 0)],
    }

    own_copy(0).start()
    for k in range(1, group):
        z_copy(0, k).start()
    for r in range(4):
        for copy in w_share(r, core) + w_keep(r):
            copy.start()
    down_share().start()
    down_keep.start()
    own_copy(1).start()

    for k in range(1, group):
        z_copy(1, k).start()

    lax.fori_loop(0, group, forward, 0)
    lax.fori_loop(0, group, backward, 0)
    for event, t, which in grad_steps.get((0, 0), []):
        event(t, which)

    act_t = down_buf.at[:, pl.ds(0, total)]
    rows_t = down_buf.at[pl.ds(0, piece), pl.ds(total, total)]
    send_down = w_buf.at[pl.ds(4 * piece, down_rows), pl.ds(0, width)]

    def send_gate(r):
        return w_buf.at[pl.ds(pl.multiple_of(r * piece, piece), piece), :]

    def turn(j, carry):
        lanes = pl.ds(pl.multiple_of(j * LANES, LANES), LANES)
        act_t[lanes, :] = act_buf[:, lanes].T
        return carry

    lax.fori_loop(0, blocks, turn, 0)

    def pair_span(j):
        return pl.ds(pl.multiple_of(j * 2 * LANES, 2 * LANES), 2 * LANES)

    def down_grad(which, j):
        rows = pl.ds(pl.multiple_of(which * down_rows, down_rows), down_rows)
        return dot_nn(act_t[rows, :], rows_buf[1, :, pair_span(j)])

    def after(steps, number, r):
        turns = {(turn, 0): events for (stage, turn), events in steps.items() if stage == number}
        take(turns, r, 0)

    after(grad_steps, 1, 0)
    def down_for_partner(j, carry):
        send_down[:, pair_span(j)] = down_grad(1 - core, j).astype(jnp.bfloat16)
        return carry

    lax.fori_loop(0, tiles, down_for_partner, 0, unroll=2)
    down_send = remote(
        send_down, other_down, grad_sems.at[0, 4], grad_sems.at[1, 4], partner
    )
    down_send.start()

    def turned_rows(r, which):
        step_y = r // 2
        step_x = r % 2
        chip = (at_y + step_y - 2 * at_y * step_y) * 2 + (at_x + step_x - 2 * at_x * step_x)
        start = pl.multiple_of((chip * 2 + which) * piece, piece)
        rows_t[...] = rows_buf[0, :, pl.ds(start, piece)].T

    def gate_send(r):
        return remote(
            send_gate(r), other_gate.at[r], grad_sems.at[0, r], grad_sems.at[1, r], partner
        )

    def gate_for_partner(r, carry):
        after(grad_steps, 2, r)
        turned_rows(r, 1 - core)
        target = send_gate(r)
        for j in range(blocks):
            cols = span(2 * j, 2)
            target[:, cols] = dot_nn(rows_t[...], gate_buf[:, cols]).astype(jnp.bfloat16)
        gate_send(r).start()
        return carry

    lax.fori_loop(0, 4, gate_for_partner, 0)
    after(grad_steps, 3, 0)
    down_send.wait_recv()

    def down_for_self(j, carry):
        cols = pair_span(j)
        value = down_grad(core, j) + other_down[:, cols].astype(jnp.float32)
        other_down[:, cols] = value.astype(jnp.bfloat16)
        return carry

    lax.fori_loop(0, tiles, down_for_self, 0, unroll=2)
    down_out = pltpu.make_async_copy(other_down, grad_down, grad_sems.at[2, 0])
    down_out.start()

    def gate_out(r):
        return pltpu.make_async_copy(other_gate.at[r], grad_gate_up.at[r], grad_sems.at[2, 2 + r])

    def gate_for_self(r, carry):
        after(grad_steps, 4, r)
        gate_send(r).wait_recv()
        turned_rows(r, core)
        target = other_gate.at[r]
        for j in range(blocks):
            cols = span(2 * j, 2)
            value = dot_nn(rows_t[...], gate_buf[:, cols])
            target[:, cols] = (value + target[:, cols].astype(jnp.float32)).astype(jnp.bfloat16)
        gate_out(r).start()
        return carry

    lax.fori_loop(0, 4, gate_for_self, 0)
    after(grad_steps, 5, 0)

    down_out.wait()
    for r in range(4):
        gate_out(r).wait()
        gate_send(r).wait_send()
        for copy in w_share(r, core):
            copy.wait_send()
    down_share().wait_send()
    down_send.wait_send()
    for t in range(2):
        keep_copy(t).wait()
        for k in range(group):
            x_copy(t, k).wait_send()
            y_copy(t, k).wait_send()
            a_copy(t, k).wait_send()
            b_copy(t, k).wait_send()
            half_x_copy(t, k).wait_send()
            half_y_copy(t, k).wait_send()
            full_x_copy(t, k).wait_send()
            full_y_copy(t, k).wait_send()
            if k > 0:
                z_copy(t, k).wait_send()
                back_copy(t, k).wait_send()
                back_copy(t, k).wait_recv()


def experts_call(sent, d_back, w_gate_up, w_got, w_down):
    group, cap, width = sent.shape
    piece, hidden2 = w_got.shape[1:]
    hidden = hidden2 // 2
    down_rows = w_down.shape[1]
    chunk = 4 * cap
    total = group * chunk
    low = jnp.bfloat16
    anywhere = pl.BlockSpec(memory_space=pl.ANY)
    flops = 2 * total * width * hidden * 9
    moved = 2 * (4 * piece * hidden2 * 2 + down_rows * width * 3)
    return pl.pallas_call(
        functools.partial(experts_kernel, group),
        out_shape=(
            jax.ShapeDtypeStruct((group, cap, width), low),
            jax.ShapeDtypeStruct((group, cap, width), low),
            jax.ShapeDtypeStruct((4, piece, hidden2), low),
            jax.ShapeDtypeStruct((down_rows, width), low),
        ),
        in_specs=[anywhere] * 5,
        out_specs=(anywhere,) * 4,
        scratch_shapes=[
            pltpu.VMEM((width, hidden2), low),
            pltpu.VMEM((hidden, width), low),
            pltpu.VMEM((2, total, width), low),
            pltpu.VMEM((total, hidden2), low),
            pltpu.VMEM((total, hidden), low),
            pltpu.VMEM((2, total, width), low),
            pltpu.VMEM((2, group, cap // 2, width), low),
            pltpu.VMEM((2, group, cap // 2, width), low),
            pltpu.VMEM((2, group, cap, width), low),
            pltpu.VMEM((2, group, cap, width), low),
            pltpu.VMEM((4, piece, hidden2), low),
            pltpu.VMEM((down_rows, width), low),
            pltpu.SemaphoreType.DMA((2, 5, 2, group)),
            pltpu.SemaphoreType.DMA((2, 5, 2, group)),
            pltpu.SemaphoreType.DMA((2, 6)),
            pltpu.SemaphoreType.DMA((10,)),
            pltpu.SemaphoreType.DMA((3, 6)),
        ],
        compiler_params=pltpu.CompilerParams(
            collective_id=1, has_side_effects=True, vmem_limit_bytes=67043328
        ),
        cost_estimate=pl.CostEstimate(flops=flops, bytes_accessed=moved, transcendentals=0),
        name="experts",
    )(sent, d_back, w_gate_up, w_got, w_down)


def rotary_tables(length_total, head_size):
    position = jnp.arange(length_total, dtype=jnp.float32)
    frequency = THETA ** (-(jnp.arange(head_size // 2, dtype=jnp.float32) * 2.0 / head_size))
    angles = position[:, None] * frequency[None, :]
    return (jnp.cos(angles)[:, None, :], jnp.sin(angles)[:, None, :])


def rotate(values, cosine, sine):
    half_size = values.shape[-1] // 2
    first = values[..., :half_size]
    second = values[..., half_size:]
    return jnp.concatenate(
        [first * cosine - second * sine, second * cosine + first * sine], axis=-1
    )


def rotate_back(grad_rows, cosine, sine):
    half_size = grad_rows.shape[-1] // 2
    first = grad_rows[..., :half_size]
    second = grad_rows[..., half_size:]
    return jnp.concatenate(
        [first * cosine + second * sine, second * cosine - first * sine], axis=-1
    )


def slot_table(routes, order, valid, capacity):
    row_count = routes.shape[0]
    top_count = routes.shape[1]
    pair_rank = order[:, None] + row_count * jnp.arange(top_count, dtype=jnp.int32)[None, :]
    flat_rank = pair_rank.reshape(-1)
    flat_expert = routes.reshape(-1)
    flat_valid = jnp.broadcast_to(valid[:, None], routes.shape).reshape(-1)
    earlier = (
        (flat_rank[None, :] < flat_rank[:, None])
        & (flat_expert[None, :] == flat_expert[:, None])
        & flat_valid[None, :]
    )
    slot_index = jnp.sum(earlier.astype(jnp.int32), axis=1).reshape(row_count, top_count)
    kept_pair = valid[:, None] & (slot_index < capacity)
    target = routes * capacity + jnp.minimum(slot_index, capacity - 1)
    return (target, kept_pair)


def masked_scores(query, key_rows, allowed):
    scale = query.shape[-1] ** (-0.5)
    raw = jnp.einsum("qhd,khd->hqk", query, key_rows, preferred_element_type=jnp.float32) * scale
    return jnp.where(allowed[None], raw, NEGATIVE)


def contract_first(left, right):
    return lax.dot_general(
        left, right, (((0,), (0,)), ((), ())), preferred_element_type=jnp.float32
    )


def contract_last(left, right):
    return lax.dot_general(
        left, right, (((1,), (1,)), ((), ())), preferred_element_type=jnp.float32
    )


def normalize(rows):
    inverse = lax.rsqrt(jnp.mean(rows * rows, axis=-1, keepdims=True) + NORM_EPSILON)
    return rows * inverse, inverse


def exchange_experts(blocks):
    return lax.all_to_all(blocks, "expert", split_axis=0, concat_axis=0, tiled=True)


def line_order(place, step):
    upper = place // 2
    low = place * (1 - upper) + (3 - place) * upper
    first = 1 - (step + 1) // 2
    block = step + first * (1 - low) + (1 - first)
    return block * (1 - upper) + (3 - block) * upper


def rotated(grad, cosine, sine):
    return grad * cosine + pltpu.roll(grad, grad.shape[1] // 2, 1) * sine


def attention_back_kernel(
    heads,
    length,
    returned,
    d_sent,
    resid,
    inverse_two,
    gates,
    hits,
    cotangent,
    routes_t,
    small_full,
    tokens_all,
    inverse_all,
    whole,
    w_out,
    w_qkv,
    query,
    key_rows,
    value,
    attended,
    log_total,
    cosine,
    sine,
    gate_grads,
    output,
    grad_tokens,
    grad_weights,
    small_out,
    gate_got,
    returned_buf,
    d_sent_buf,
    resid_buf,
    inverse_two_buf,
    gates_buf,
    hits_buf,
    cotangent_buf,
    rows_buf,
    small_full_buf,
    da_buf,
    tokens_buf,
    inverse_buf,
    whole_buf,
    w_out_buf,
    w_qkv_buf,
    query_buf,
    key_buf,
    value_buf,
    attended_buf,
    log_buf,
    cosine_buf,
    sine_buf,
    d_key_acc,
    d_value_acc,
    d_proj,
    normed_part,
    from_left,
    from_right,
    send_pair,
    recv_pair,
    own_part,
    half_x,
    half_y,
    full_x,
    full_y,
    small_buf,
    small_recv,
    small_z,
    keep_buf,
    sum_buf,
    load_sems,
    line_sems,
    sum_sems,
    pair_sems,
    ring_sems,
    small_sems,
    gate_sems,
):
    tok, width = cotangent.shape
    seq_len = tokens_all.shape[0]
    group = seq_len // tok
    local_width = w_out.shape[0]
    head_size = local_width // heads
    piece = own_part.shape[1]
    half = piece // 2
    scale = head_size**-0.5

    index = lax.axis_index("dp")
    place = lax.axis_index("expert")
    core = index % 2
    at_x = (index // 2) % 2
    at_y = index // 4
    partner = {"dp": at_y * 4 + at_x * 2 + (1 - core)}
    along_x = {"dp": at_y * 4 + (1 - at_x) * 2 + core}
    along_y = {"dp": (1 - at_y) * 4 + at_x * 2 + core}
    over = {"dp": (1 - at_y) * 4 + (1 - at_x) * 2 + core}
    parts = width // piece

    def chip(r):
        step_y = r // 2
        step_x = r % 2
        return (at_y + step_y - 2 * at_y * step_y) * 2 + (at_x + step_x - 2 * at_x * step_x)

    def ring_peer(k):
        return {"dp": (index + k) % parts}

    def line_peer(k):
        return {"expert": (place + k) % group}

    right = {"expert": (place + 1) % group}
    left = {"expert": (place + group - 1) % group}

    loads = [
        pltpu.make_async_copy(source, target, load_sems.at[number])
        for number, (source, target) in enumerate(
            [
                (returned, returned_buf),
                (hits, hits_buf),
                (cotangent, cotangent_buf),
                (resid, resid_buf),
                (inverse_two, inverse_two_buf),
                (gates, gates_buf),
                (routes_t, rows_buf),
                (small_full, small_full_buf),
                (d_sent, d_sent_buf),
                (w_out, w_out_buf),
                (query, query_buf),
                (key_rows, key_buf),
                (value, value_buf),
                (log_total, log_buf),
                (cosine, cosine_buf),
                (sine, sine_buf),
                (w_qkv, w_qkv_buf),
                (tokens_all, tokens_buf),
                (inverse_all, inverse_buf),
                (whole, whole_buf),
                (attended, attended_buf),
                (gate_grads.at[0], keep_buf),
            ]
        )
    ]
    first = 9
    early = first + 7
    for load in loads[:early]:
        load.start()

    greet([ring_peer(k) for k in range(1, parts)] + [line_peer(k) for k in range(1, group)])

    def rows_of(block):
        return pl.ds(pl.multiple_of(block * tok, tok), tok)

    def pass_right(block):
        spot = da_buf.at[rows_of(block)]
        return remote(spot, spot, line_sems.at[0, block], line_sems.at[2, block], right)

    def pass_left(block):
        spot = da_buf.at[rows_of(block)]
        return remote(spot, spot, line_sems.at[1, block], line_sems.at[2, block], left)

    def gate_copy(r, peer):
        return remote(
            gate_grads.at[r], gate_got.at[r], gate_sems.at[0, r], gate_sems.at[1, r], peer
        )

    peers = (None, along_x, along_y, over)
    for r in (3, 1, 2):
        gate_copy(r, peers[r]).start()
    for load in loads[early:]:
        load.start()
    for load in loads[:first]:
        load.wait()

    at = place * tok + lax.broadcasted_iota(jnp.int32, (tok, 1), 0)
    live = jnp.where(at < length[0], 1.0, 0.0)
    d_out = live * cotangent_buf[...].astype(jnp.float32)
    total = resid_buf[...]
    hhat = total * inverse_two_buf[...]
    gate = [gates_buf[:, number : number + 1] for number in range(2)]
    d_gate = []
    for number in range(2):
        picked = dot_nn(hits_buf[number].T, returned_buf[...])
        d_gate.append(jnp.sum(d_out * picked, axis=-1, keepdims=True))
        total = total + gate[number] * picked
    output[...] = (live * total).astype(jnp.bfloat16)
    mixed = gate[0] * d_gate[0] + gate[1] * d_gate[1]
    d_chosen = [gate[number] * (d_gate[number] - mixed) for number in range(2)]
    d_hidden = dot_nn((hits_buf[0] + hits_buf[1]).T, d_sent_buf[...])
    gain_two = small_full_buf[1:2, :]
    hidden_in = (hhat * gain_two).astype(jnp.bfloat16).astype(jnp.float32)
    small_buf[...] = jnp.zeros_like(small_buf)
    square = (tok, tok)
    same = lax.broadcasted_iota(jnp.int32, square, 0) == lax.broadcasted_iota(jnp.int32, square, 1)
    named = []
    for number in range(2):
        row = rows_buf[number : number + 1, :].astype(jnp.float32)
        kept = jnp.where(same, jnp.broadcast_to(row, square), 0.0)
        named.append(jnp.sum(kept, axis=1, keepdims=True).astype(jnp.int32))
    for expert in range(group):
        d_logit = sum(
            jnp.where(named[number] == expert, d_chosen[number], 0.0)
            for number in range(2)
        )
        row = slice(2 + expert, 3 + expert)
        d_hidden = d_hidden + d_logit * small_full_buf[row, :]
        small_buf[row, :] = jnp.sum(d_logit * hidden_in, axis=0, keepdims=True)
    small_buf[1:2, :] = jnp.sum(d_hidden * hhat, axis=0, keepdims=True)
    scaled = d_hidden * gain_two
    shared = jnp.mean(scaled * hhat, axis=-1, keepdims=True)
    d_resid = d_out + inverse_two_buf[...] * (scaled - hhat * shared)
    resid_buf[...] = d_resid
    da_buf[rows_of(place), :] = d_resid.astype(jnp.bfloat16)

    @pl.when(place < group - 1)
    def _():
        pass_right(place).start()

    @pl.when(place > 0)
    def _():
        pass_left(place).start()

    d_key_acc[...] = jnp.zeros_like(d_key_acc)
    d_value_acc[...] = jnp.zeros_like(d_value_acc)

    def attend_back(block):
        rows = rows_of(block)
        d_heads = dot_nt(da_buf[rows, :], w_out_buf[...]).astype(jnp.bfloat16)
        shape = (tok, seq_len)
        at_query = block * tok + lax.broadcasted_iota(jnp.int32, shape, 0)
        at_key = lax.broadcasted_iota(jnp.int32, shape, 1)
        allowed = (at_key <= at_query) & (at_key < length[0])
        for head in range(heads):
            cols = slice(head * head_size, (head + 1) * head_size)
            one_query = query_buf[rows, cols]
            one_key = key_buf[:, cols]
            d_head = d_heads[:, cols]
            scores = jnp.where(allowed, dot_nt(one_query, one_key) * scale, NEGATIVE)
            probs = jnp.exp(scores - log_buf[rows, head : head + 1])
            d_probs = dot_nt(d_head, value_buf[:, cols])
            delta = jnp.sum(probs * d_probs, axis=-1, keepdims=True)
            d_scores = (probs * (d_probs - delta)).astype(jnp.bfloat16)
            d_query = dot_nn(d_scores, one_key) * scale
            d_key_acc[:, cols] += dot_nn(d_scores.T, one_query) * scale
            d_value_acc[:, cols] += dot_nn(probs.astype(jnp.bfloat16).T, d_head)
            d_proj[rows, cols] = rotated(d_query, cosine_buf[rows, :], -sine_buf[rows, :]).astype(
                jnp.bfloat16
            )

    for load in loads[first:early]:
        load.wait()

    def arrive(step, carry):
        later = (step + group - 2) // (group - 1)
        block = place * (1 - later) + line_order(place, step - later) * later

        @pl.when(step > 0)
        def _():
            pass_right(block).wait_recv()

        @pl.when((block < place) & (place < group - 1))
        def _():
            pass_right(block).start()

        @pl.when((block > place) & (place > 0))
        def _():
            pass_left(block).start()

        attend_back(block)
        return carry

    lax.fori_loop(0, group, arrive, 0)
    for load in loads[early:]:
        load.wait()
    keep = pltpu.make_async_copy(keep_buf, gate_got.at[0], load_sems.at[22])
    keep.start()

    for head in range(heads):
        cols = slice(head * head_size, (head + 1) * head_size)
        key_cols = slice(local_width + head * head_size, local_width + (head + 1) * head_size)
        d_proj[:, key_cols] = rotated(d_key_acc[:, cols], cosine_buf[...], -sine_buf[...]).astype(
            jnp.bfloat16
        )
    d_proj[:, 2 * local_width :] = d_value_acc[...].astype(jnp.bfloat16)

    def normed_tile(j, carry):
        cols = pl.ds(pl.multiple_of(j * piece, piece), piece)
        d_normed = jnp.zeros((seq_len, piece), jnp.float32)
        for c in range(3):
            d_normed += dot_nt(
                d_proj[:, c * local_width : (c + 1) * local_width], w_qkv_buf[c, cols, :]
            )
        hat = tokens_buf[:, cols].astype(jnp.float32) * inverse_buf[...]
        small_buf[0:1, cols] = jnp.sum(d_normed * hat, axis=0, keepdims=True)
        normed_part[:, cols] = d_normed.astype(jnp.bfloat16)
        return carry

    lax.fori_loop(0, parts, normed_tile, 0)

    def go_right(block):
        return remote(
            normed_part.at[pl.ds(block * tok, tok)],
            from_left.at[block],
            sum_sems.at[0, block],
            sum_sems.at[1, block],
            right,
        )

    def go_left(block):
        return remote(
            normed_part.at[pl.ds(block * tok, tok)],
            from_right.at[block],
            sum_sems.at[0, block],
            sum_sems.at[2, block],
            left,
        )

    def add_into(target, other):
        value = target[...].astype(jnp.float32) + other[...].astype(jnp.float32)
        target[...] = value.astype(jnp.bfloat16)

    def on_right(block):
        go_right(block).wait_recv()
        add_into(normed_part.at[pl.ds(block * tok, tok)], from_left.at[block])
        go_right(block).start()

    def on_left(block):
        go_left(block).wait_recv()
        add_into(normed_part.at[pl.ds(block * tok, tok)], from_right.at[block])
        go_left(block).start()

    @pl.when(place == 0)
    def _():
        for block in (3, 2, 1):
            go_right(block).start()

    @pl.when(place == 3)
    def _():
        for block in (0, 1, 2):
            go_left(block).start()

    def small_copy(k):
        to = (index + k) % parts
        cols = pl.ds(pl.multiple_of(to * piece, piece), piece)
        return remote(
            small_buf.at[:, cols],
            small_recv.at[k],
            small_sems.at[0, k],
            small_sems.at[1, k],
            ring_peer(k),
        )

    for k in range(1, parts):
        small_copy(k).start()

    def weight_grad(which, r):
        cols = pl.ds(pl.multiple_of((chip(r) * 2 + which) * piece, piece), piece)
        left_side = whole_buf[:, cols].T
        first = dot_nn(left_side, d_proj[...])
        second = dot_nn(da_buf[:, cols].T, attended_buf[...])
        return jnp.concatenate([first, second], axis=1)

    def pair_copy(r):
        return remote(
            send_pair.at[r], recv_pair.at[r], pair_sems.at[0, r], pair_sems.at[1, r], partner
        )

    def for_partner(i, carry):
        r = 3 - i
        send_pair[r] = weight_grad(1 - core, r).astype(jnp.bfloat16)
        pair_copy(r).start()
        return carry

    lax.fori_loop(0, 4, for_partner, 0)

    @pl.when(place == 1)
    def _():
        on_right(3)

    @pl.when(place == 2)
    def _():
        on_left(0)

    def lanes_of(c):
        return pl.ds(c * (2 * local_width), 2 * local_width)

    def ring_copy(number, c, source, target, peer):
        sem = 4 * c + number
        return remote(source, target, ring_sems.at[0, sem], ring_sems.at[1, sem], peer)

    def half_x_copy(c):
        source = own_part.at[3, pl.ds(0, half), lanes_of(c)]
        return ring_copy(0, c, source, half_x.at[:, lanes_of(c)], along_x)

    def half_y_copy(c):
        source = own_part.at[3, pl.ds(half, half), lanes_of(c)]
        return ring_copy(1, c, source, half_y.at[:, lanes_of(c)], along_y)

    def full_x_copy(c):
        return ring_copy(
            2, c, own_part.at[1, :, lanes_of(c)], full_x.at[:, lanes_of(c)], along_x
        )

    def full_y_copy(c):
        return ring_copy(
            3, c, own_part.at[2, :, lanes_of(c)], full_y.at[:, lanes_of(c)], along_y
        )

    def for_self(i, carry):
        r = 3 - i
        pair_copy(r).wait_recv()
        own_part[r] = (weight_grad(core, r) + recv_pair[r].astype(jnp.float32)).astype(
            jnp.bfloat16
        )

        @pl.when(i == 0)
        def _():
            for c in range(2):
                half_x_copy(c).start()
                half_y_copy(c).start()

        return carry

    lax.fori_loop(0, 4, for_self, 0)

    total = small_buf[:, pl.ds(pl.multiple_of(index * piece, piece), piece)]
    for k in range(1, parts):
        small_copy(k).wait_recv()
        total = total + small_recv[k]
    small_z[0] = total

    @pl.when(place == 1)
    def _():
        on_right(2)

    @pl.when(place == 2)
    def _():
        on_left(1)

    def small_line_copy(k):
        return remote(
            small_z.at[0],
            small_z.at[k],
            small_sems.at[0, parts + k],
            small_sems.at[1, parts + k],
            line_peer(k),
        )

    for k in range(1, group):
        small_line_copy(k).start()

    for c in range(2):
        half_x_copy(c).wait_recv()
        add_into(own_part.at[2, pl.ds(0, half), lanes_of(c)], half_x.at[:, lanes_of(c)])
        full_y_copy(c).start()
        half_y_copy(c).wait_recv()
        add_into(own_part.at[1, pl.ds(half, half), lanes_of(c)], half_y.at[:, lanes_of(c)])
        full_x_copy(c).start()

    @pl.when(place == 1)
    def _():
        on_left(0)

    @pl.when(place == 2)
    def _():
        on_right(3)

    total = small_z[0]
    for k in range(1, group):
        small_line_copy(k).wait_recv()
        total = total + small_z[k]
    small_out[...] = total

    sum_buf[...] = normed_part[rows_of(place), :].astype(jnp.float32)

    @pl.when(place > 0)
    def _():
        go_right(place).wait_recv()
        sum_buf[...] += from_left[place].astype(jnp.float32)

    @pl.when(place < group - 1)
    def _():
        go_left(place).wait_recv()
        sum_buf[...] += from_right[place].astype(jnp.float32)

    inverse_one = inverse_buf[rows_of(place), :]
    hat = tokens_buf[rows_of(place), :].astype(jnp.float32) * inverse_one
    scaled = sum_buf[...] * small_full_buf[0:1, :]
    shared = jnp.mean(scaled * hat, axis=-1, keepdims=True)
    grad_tokens[...] = (resid_buf[...] + inverse_one * (scaled - hat * shared)).astype(
        jnp.bfloat16
    )

    for c in range(2):
        full_x_copy(c).wait_recv()
        full_y_copy(c).wait_recv()
        grad_weights[:, lanes_of(c)] = (
            own_part[0, :, lanes_of(c)].astype(jnp.float32)
            + full_x[:, lanes_of(c)].astype(jnp.float32)
            + full_y[:, lanes_of(c)].astype(jnp.float32)
        )

    for r in (1, 2, 3):
        gate_copy(r, peers[r]).wait()
    keep.wait()
    for c in range(2):
        half_x_copy(c).wait_send()
        half_y_copy(c).wait_send()
        full_x_copy(c).wait_send()
        full_y_copy(c).wait_send()
    for r in range(4):
        pair_copy(r).wait_send()
    for k in range(1, parts):
        small_copy(k).wait_send()
    for k in range(1, group):
        small_line_copy(k).wait_send()
    for block in range(group):

        @pl.when(block > place)
        def _():
            go_right(block).wait_send()

        @pl.when(block < place)
        def _():
            go_left(block).wait_send()

        @pl.when((block <= place) & (place < group - 1))
        def _():
            pass_right(block).wait_send()

        @pl.when((block >= place) & (place > 0))
        def _():
            pass_left(block).wait_send()


def attention_back_call(
    lengths,
    returned,
    d_sent,
    resid,
    inverse_two,
    gates,
    hits,
    cotangent,
    routes_t,
    small_full,
    tokens_all,
    inverse_all,
    whole,
    w_out,
    w_qkv,
    query,
    key_rows,
    value,
    attended,
    log_total,
    cosine,
    sine,
    gate_grads,
):
    tok, width = cotangent.shape
    seq_len = tokens_all.shape[0]
    group = seq_len // tok
    local_width = w_out.shape[0]
    heads = log_total.shape[1]
    piece = gate_grads.shape[1]
    half = piece // 2
    parts = width // piece
    small_rows = small_full.shape[0]
    low, full = jnp.bfloat16, jnp.float32
    anywhere = pl.BlockSpec(memory_space=pl.ANY)
    inside = pl.BlockSpec(memory_space=pltpu.VMEM)

    def like(array):
        return pltpu.VMEM(array.shape, array.dtype)

    flops = 2 * seq_len * width * local_width * 8 + 10 * seq_len * seq_len * local_width
    return pl.pallas_call(
        functools.partial(attention_back_kernel, heads),
        out_shape=(
            jax.ShapeDtypeStruct((tok, width), low),
            jax.ShapeDtypeStruct((tok, width), low),
            jax.ShapeDtypeStruct((piece, 4 * local_width), full),
            jax.ShapeDtypeStruct((small_rows, piece), full),
            jax.ShapeDtypeStruct(gate_grads.shape, low),
        ),
        in_specs=[pl.BlockSpec(memory_space=pltpu.SMEM)] + [anywhere] * 22,
        out_specs=(inside, inside, inside, inside, anywhere),
        scratch_shapes=[
            like(returned),
            like(d_sent),
            like(resid),
            like(inverse_two),
            like(gates),
            like(hits),
            like(cotangent),
            like(routes_t),
            like(small_full),
            pltpu.VMEM((seq_len, width), low),
            like(tokens_all),
            like(inverse_all),
            like(whole),
            like(w_out),
            like(w_qkv),
            like(query),
            like(key_rows),
            like(value),
            like(attended),
            like(log_total),
            like(cosine),
            like(sine),
            pltpu.VMEM((seq_len, local_width), full),
            pltpu.VMEM((seq_len, local_width), full),
            pltpu.VMEM((seq_len, 3 * local_width), low),
            pltpu.VMEM((seq_len, width), low),
            pltpu.VMEM((group, tok, width), low),
            pltpu.VMEM((group, tok, width), low),
            pltpu.VMEM((4, piece, 4 * local_width), low),
            pltpu.VMEM((4, piece, 4 * local_width), low),
            pltpu.VMEM((4, piece, 4 * local_width), low),
            pltpu.VMEM((half, 4 * local_width), low),
            pltpu.VMEM((half, 4 * local_width), low),
            pltpu.VMEM((piece, 4 * local_width), low),
            pltpu.VMEM((piece, 4 * local_width), low),
            like(small_full),
            pltpu.VMEM((parts, small_rows, piece), full),
            pltpu.VMEM((group, small_rows, piece), full),
            pltpu.VMEM(gate_grads.shape[1:], low),
            like(resid),
            pltpu.SemaphoreType.DMA((23,)),
            pltpu.SemaphoreType.DMA((3, group)),
            pltpu.SemaphoreType.DMA((3, group)),
            pltpu.SemaphoreType.DMA((2, 4)),
            pltpu.SemaphoreType.DMA((2, 8)),
            pltpu.SemaphoreType.DMA((2, parts + group)),
            pltpu.SemaphoreType.DMA((2, 4)),
        ],
        compiler_params=pltpu.CompilerParams(
            collective_id=2, has_side_effects=True, vmem_limit_bytes=67043328
        ),
        cost_estimate=pl.CostEstimate(flops=flops, bytes_accessed=40000000, transcendentals=0),
        name="attention_back",
    )(
        lengths,
        returned,
        d_sent,
        resid,
        inverse_two,
        gates,
        hits,
        cotangent,
        routes_t,
        small_full,
        tokens_all,
        inverse_all,
        whole,
        w_out,
        w_qkv,
        query,
        key_rows,
        value,
        attended,
        log_total,
        cosine,
        sine,
        gate_grads,
    )


def finish_kernel(
    gate_got,
    grad_down_low,
    grad_tokens_low,
    output_low,
    grad_weights,
    small,
    grad_gate_up,
    grad_down,
    grad_tokens,
    output,
    grad_qkv,
    grad_out,
    gain_one,
    gain_two,
    router,
    got_buf,
    wide_buf,
    low_buf,
    down_buf,
    tokens_buf,
    output_buf,
    weights_buf,
    out_buf,
    small_buf,
    load_sems,
    store_sems,
):
    chips = gate_got.shape[0]
    size = gate_got.shape[2] // 2
    local_width = grad_qkv.shape[2]
    index = lax.axis_index("dp")
    at_x = (index // 2) % 2
    at_y = index // 4

    def load(number, source, target):
        return pltpu.make_async_copy(source, target, load_sems.at[number])

    loads = [load(r, gate_got.at[r], got_buf.at[r]) for r in range(chips)] + [
        load(4, grad_down_low, low_buf),
        load(5, grad_weights, weights_buf),
        load(6, grad_tokens_low, tokens_buf),
        load(7, output_low, output_buf),
        load(8, small, small_buf),
    ]
    for copy in loads:
        copy.start()
    stores = []

    def store(source, target):
        copy = pltpu.make_async_copy(source, target, store_sems.at[len(stores)])
        copy.start()
        stores.append(copy)

    for r in range(chips):
        loads[r].wait()
        step_y = r // 2
        step_x = r % 2
        chip = (at_y + step_y - 2 * at_y * step_y) * 2 + (at_x + step_x - 2 * at_x * step_x)
        for part in range(2):
            wide_buf[2 * r + part] = got_buf[r, :, part * size : (part + 1) * size].astype(
                jnp.float32
            )
            lanes = pl.ds(pl.multiple_of((part * chips + chip) * size, LANES), size)
            store(wide_buf.at[2 * r + part], grad_gate_up.at[0, :, lanes])
    loads[4].wait()
    down_buf[...] = low_buf[...].astype(jnp.float32)
    store(down_buf, grad_down.at[0])
    loads[5].wait()
    out_buf[...] = weights_buf[:, 3 * local_width :].T
    for c in range(3):
        store(weights_buf.at[:, pl.ds(c * local_width, local_width)], grad_qkv.at[c])
    store(out_buf, grad_out)
    loads[6].wait()
    store(tokens_buf, grad_tokens)
    loads[7].wait()
    store(output_buf, output)
    loads[8].wait()
    gain_one[...] = small_buf[0:1, :]
    gain_two[...] = small_buf[1:2, :]
    router[...] = small_buf[2 : 2 + router.shape[0], :]
    for copy in stores:
        copy.wait()


def finish_call(gate_got, grad_down, grad_tokens, output, grad_weights, small, experts):
    chips, rows, hidden2 = gate_got.shape
    local_width = grad_weights.shape[1] // 4
    full = jnp.float32
    anywhere = pl.BlockSpec(memory_space=pl.ANY)
    out_t = (local_width, rows)

    def like(array, kind=None):
        return pltpu.VMEM(array.shape, kind or array.dtype)

    return pl.pallas_call(
        finish_kernel,
        out_shape=(
            jax.ShapeDtypeStruct((1, rows, chips * hidden2), full),
            jax.ShapeDtypeStruct((1,) + grad_down.shape, full),
            jax.ShapeDtypeStruct(grad_tokens.shape, grad_tokens.dtype),
            jax.ShapeDtypeStruct(output.shape, output.dtype),
            jax.ShapeDtypeStruct((3, rows, local_width), full),
            jax.ShapeDtypeStruct(out_t, full),
            jax.ShapeDtypeStruct((1, rows), full),
            jax.ShapeDtypeStruct((1, rows), full),
            jax.ShapeDtypeStruct((experts, rows), full),
        ),
        in_specs=[anywhere] * 6,
        out_specs=(anywhere,) * 6 + (pl.BlockSpec(memory_space=pltpu.VMEM),) * 3,
        scratch_shapes=[
            like(gate_got),
            pltpu.VMEM((2 * chips, rows, hidden2 // 2), full),
            like(grad_down),
            like(grad_down, full),
            like(grad_tokens),
            like(output),
            like(grad_weights),
            pltpu.VMEM(out_t, full),
            like(small),
            pltpu.SemaphoreType.DMA((9,)),
            pltpu.SemaphoreType.DMA((15,)),
        ],
        compiler_params=pltpu.CompilerParams(vmem_limit_bytes=67043328),
        name="finish",
    )(gate_got, grad_down, grad_tokens, output, grad_weights, small)


def rotary_constants(length_total, head_size):
    low = 32
    steps = np.arange(head_size // 2, dtype=np.float32) * np.float32(2.0) / np.float32(head_size)
    frequency = np.power(np.float32(THETA), -steps).astype(np.float32).astype(np.float64)
    position = np.concatenate([np.arange(0, length_total, low), np.arange(low)])
    angles = position[:, None] * np.concatenate([frequency, frequency])[None, :]
    return np.stack([np.cos(angles), np.sin(angles)]).astype(np.float32)


def attention_kernel(
    heads,
    length,
    tokens,
    w_qkv,
    w_out,
    gain_one,
    gain_two,
    router_t,
    w_gate_up,
    routes_t,
    order_row,
    angles,
    cotangent,
    tokens_all,
    whole,
    qkv_full,
    out_full,
    w_got,
    inverse_all,
    query,
    key_rows,
    value,
    attended,
    log_total,
    small_full,
    cosine_buf,
    sine_buf,
    resid,
    inverse_two,
    gates,
    hits,
    sent,
    d_back,
    tokens_buf,
    whole_buf,
    w_qkv_buf,
    w_out_buf,
    part_buf,
    from_left,
    from_right,
    rows_buf,
    order_buf,
    angles_buf,
    cotangent_buf,
    gain_one_buf,
    gain_two_buf,
    router_buf,
    small,
    load_sems,
    line_sems,
    sum_sems,
    gather_sems,
    small_sems,
    slice_sems,
):
    tok, width = tokens.shape
    seq_len = tokens_buf.shape[0]
    group = seq_len // tok
    local_width = w_out.shape[0]
    head_size = local_width // heads
    piece = w_qkv.shape[1]
    parts = width // piece
    ff = w_gate_up.shape[2] // 2
    hidden = ff // 4
    slots = hits.shape[1]
    cap = slots // group
    scale = head_size**-0.5

    index = lax.axis_index("dp")
    place = lax.axis_index("expert")
    core = index % 2
    at_x = (index // 2) % 2
    at_y = index // 4
    other = at_y * 4 + at_x * 2 + (1 - core)
    by_x = at_y * 4 + (1 - at_x) * 2 + core
    by_y = (1 - at_y) * 4 + at_x * 2 + core
    by_both = (1 - at_y) * 4 + (1 - at_x) * 2 + core
    partner = {"dp": other}
    along_x = {"dp": by_x}
    along_y = {"dp": by_y}
    over = {"dp": by_both}
    right = {"expert": (place + 1) % group}
    left = {"expert": (place + group - 1) % group}

    def ring_peer(k):
        return {"dp": (index + k) % parts}

    def rows_of(block):
        return pl.ds(pl.multiple_of(block * tok, tok), tok)

    def piece_of(number):
        return pl.ds(pl.multiple_of(number * piece, piece), piece)

    def qkv_spot(number):
        return w_qkv_buf.at[:, piece_of(number), :]

    def qkv_half(number, which):
        start = pl.multiple_of(number * piece + which * (piece // 2), piece // 2)
        return w_qkv_buf.at[:, pl.ds(start, piece // 2), :]

    def out_spot(number):
        return w_out_buf.at[:, piece_of(number)]

    def out_half(number, which):
        rows = pl.ds(which * (local_width // 2), local_width // 2)
        return w_out_buf.at[rows, piece_of(number)]

    class Gather:
        def __init__(self, number, source, spot, half_spot):
            self.number, self.source, self.spot, self.half_spot = number, source, spot, half_spot

        def copy(self, slot, source, target, peer):
            sems = gather_sems.at[self.number]
            return remote(source, target, sems.at[0, slot], sems.at[1, slot], peer)

        def own(self, slot, peer):
            return self.copy(slot, self.source, self.spot(index), peer)

        def keep(self):
            return pltpu.make_async_copy(
                self.source, self.spot(index), load_sems.at[16 + self.number]
            )

        def relay_x(self):
            spot = self.half_spot(by_y, 0)
            return self.copy(3, spot, spot, along_x)

        def relay_y(self):
            spot = self.half_spot(by_x, 1)
            return self.copy(4, spot, spot, along_y)

        def hand(self, slot):
            spot = (
                self.spot(by_x),
                self.spot(by_y),
                self.half_spot(by_both, 0),
                self.half_spot(by_both, 1),
            )[slot - 5]
            return self.copy(slot, spot, spot, partner)

        def begin(self):
            self.own(0, along_x).start()
            self.own(1, along_y).start()
            self.own(2, partner).start()
            self.keep().start()

        def relay(self):
            self.own(1, along_y).wait_recv()
            self.relay_x().start()
            self.own(0, along_x).wait_recv()
            self.relay_y().start()
            self.hand(5).start()
            self.hand(6).start()

        def finish(self):
            self.relay_x().wait_recv()
            self.hand(7).start()
            self.relay_y().wait_recv()
            self.hand(8).start()
            self.keep().wait()
            self.own(2, partner).wait_recv()
            for slot in (5, 6, 7, 8):
                self.hand(slot).wait_recv()

        def drain(self):
            for slot, peer in ((0, along_x), (1, along_y), (2, partner)):
                self.own(slot, peer).wait_send()
            self.relay_x().wait_send()
            self.relay_y().wait_send()
            for slot in (5, 6, 7, 8):
                self.hand(slot).wait_send()

    gather_qkv = Gather(0, w_qkv, qkv_spot, qkv_half)
    gather_out = Gather(1, w_out, out_spot, out_half)

    loads = [
        pltpu.make_async_copy(source, target, load_sems.at[number])
        for number, (source, target) in enumerate(
            [
                (tokens, tokens_buf.at[rows_of(place)]),
                (gain_one, gain_one_buf),
                (gain_two, gain_two_buf),
                (router_t, router_buf),
                (routes_t, rows_buf),
                (order_row, order_buf),
                (angles, angles_buf),
                (cotangent, cotangent_buf),
            ]
        )
    ]
    for load in loads:
        load.start()

    greet([ring_peer(k) for k in range(1, parts)] + [right, left])

    def own_pass(side, peer):
        return remote(
            tokens,
            tokens_buf.at[rows_of(place)],
            line_sems.at[side, place],
            line_sems.at[2, place],
            peer,
        )

    def pass_on(block, side, peer):
        spot = tokens_buf.at[rows_of(block)]
        return remote(spot, spot, line_sems.at[side, block], line_sems.at[2, block], peer)

    @pl.when(place < group - 1)
    def _():
        own_pass(0, right).start()

    @pl.when(place > 0)
    def _():
        own_pass(1, left).start()

    def small_copy(k):
        return remote(
            small,
            small_full.at[:, piece_of(index)],
            small_sems.at[0, k],
            small_sems.at[1, k],
            ring_peer(k),
        )

    gather_qkv.begin()

    for load in loads:
        load.wait()
    experts = router_t.shape[0]
    small[...] = jnp.zeros_like(small)
    for number in range(piece // LANES):
        lanes = slice(number * LANES, (number + 1) * LANES)
        small[0:1, lanes] = gain_one_buf[number : number + 1, :].astype(jnp.float32)
        small[1:2, lanes] = gain_two_buf[number : number + 1, :].astype(jnp.float32)
    small[2 : 2 + experts, :] = router_buf[...].astype(jnp.float32)
    small_full[:, piece_of(index)] = small[...]
    for k in range(1, parts):
        small_copy(k).start()

    rows = rows_buf[...]
    first_row, second_row, order_at = rows[0:1], rows[1:2], order_buf[...]
    square = (tok, tok)
    same = lax.broadcasted_iota(jnp.int32, square, 0) == lax.broadcasted_iota(jnp.int32, square, 1)

    def as_column(row):
        kept = jnp.where(same, jnp.broadcast_to(row.astype(jnp.float32), square), 0.0)
        return jnp.sum(kept, axis=1, keepdims=True).astype(jnp.int32)

    first_col, second_col, order_col = [as_column(r) for r in (first_row, second_row, order_at)]
    start = place * tok
    live_col = (start + lax.broadcasted_iota(jnp.int32, (tok, 1), 0)) < length[0]
    live_row = (start + lax.broadcasted_iota(jnp.int32, (1, tok), 1)) < length[0]
    before = order_col < order_at

    def count(mask):
        return jnp.sum(jnp.where(mask & live_col, 1.0, 0.0), axis=0, keepdims=True)

    slot_first = count((first_col == first_row) & before)
    slot_second = count(first_col == second_row) + count((second_col == second_row) & before)
    slot_ids = lax.broadcasted_iota(jnp.int32, (slots, tok), 0)
    for number, (named, slot) in enumerate(((first_row, slot_first), (second_row, slot_second))):
        slot = slot.astype(jnp.int32)
        step = named - place
        step = jnp.where(step < 0, step + group, step)
        target = jnp.where(live_row & (slot < cap), step * cap + slot, -1)
        hits[number] = jnp.where(slot_ids == target, 1.0, 0.0).astype(jnp.bfloat16)

    low = 32
    highs = seq_len // low
    sign = jnp.where(
        lax.broadcasted_iota(jnp.int32, (low, head_size), 1) < head_size // 2, -1.0, 1.0
    )
    cosine_low, sine_low = angles_buf[0, highs:, :], angles_buf[1, highs:, :]
    for number in range(highs):
        at = slice(number * low, (number + 1) * low)
        cosine_high = angles_buf[0, number : number + 1, :]
        sine_high = angles_buf[1, number : number + 1, :]
        cosine_buf[at, :] = cosine_high * cosine_low - sine_high * sine_low
        sine_buf[at, :] = sign * (sine_high * cosine_low + cosine_high * sine_low)

    for k in range(1, parts):
        small_copy(k).wait_recv()

    def normalize_block(block):
        at = rows_of(block)
        value = tokens_buf[at, :].astype(jnp.float32)
        inverse = lax.rsqrt(jnp.mean(value * value, axis=-1, keepdims=True) + NORM_EPSILON)
        inverse_all[at, :] = inverse
        whole_buf[at, :] = (value * inverse * small_full[0:1, :]).astype(jnp.bfloat16)

    def arrive(step):
        block = line_order(place, step)
        pass_on(block, 0, right).wait_recv()

        @pl.when((block < place) & (place < group - 1))
        def _():
            pass_on(block, 0, right).start()

        @pl.when((block > place) & (place > 0))
        def _():
            pass_on(block, 1, left).start()

        normalize_block(block)

    early = piece // 4

    def slice_copy(r, turn):
        number = (by_x // 2, by_y // 2, by_both // 2)[r - 1]
        part = turn // 2
        lanes = pl.ds(pl.multiple_of(part * ff + number * hidden, LANES), hidden)
        at = (pl.ds(0, early), pl.ds(early, piece - early), pl.ds(0, piece))[turn]
        return remote(
            w_gate_up.at[0, at, lanes],
            w_got.at[r - 1, at, pl.ds(part * hidden, hidden)],
            slice_sems.at[0, r - 1, turn],
            slice_sems.at[1, r - 1, turn],
            (along_x, along_y, over)[r - 1],
        )

    normalize_block(place)
    arrive(0)
    gather_qkv.relay()
    gather_out.begin()
    for r in (1, 2):
        slice_copy(r, 0).start()
    arrive(1)
    gather_qkv.finish()

    def project(first, size):
        at = pl.ds(pl.multiple_of(first, tok), size)
        source = whole_buf[at, :]

        def two_heads(number, carry):
            lanes = pl.ds(pl.multiple_of(number * 2 * head_size, 2 * head_size), 2 * head_size)
            for c, target in ((0, query), (1, key_rows)):
                plain = dot_nn(source, w_qkv_buf[c, :, lanes])
                turned = [
                    rotated(
                        plain[:, side * head_size : (side + 1) * head_size],
                        cosine_buf[at, :],
                        sine_buf[at, :],
                    )
                    for side in range(2)
                ]
                target[at, lanes] = jnp.concatenate(turned, axis=1).astype(jnp.bfloat16)
            value[at, lanes] = dot_nn(source, w_qkv_buf[2, :, lanes]).astype(jnp.bfloat16)
            return carry

        lax.fori_loop(0, heads // 2, two_heads, 0)

    upper = place // 2
    project(upper * tok, seq_len - tok)
    gather_out.relay()
    for turn in (1, 2):
        for r in (1, 2):
            slice_copy(r, turn).start()
    for turn in range(3):
        slice_copy(3, turn).start()
    arrive(2)
    project((1 - upper) * (seq_len - tok), tok)

    stores = [
        pltpu.make_async_copy(source, target, load_sems.at[10 + number])
        for number, (source, target) in enumerate(
            [
                (w_qkv_buf, qkv_full),
                (tokens_buf, tokens_all),
                (whole_buf, whole),
                (w_out_buf, out_full),
            ]
        )
    ]
    for store in stores[:3]:
        store.start()

    for number in range(group):
        at = slice(number * tok, (number + 1) * tok)
        extent = (number + 1) * tok
        shape = (tok, extent)
        at_query = number * tok + lax.broadcasted_iota(jnp.int32, shape, 0)
        at_key = lax.broadcasted_iota(jnp.int32, shape, 1)
        allowed = (at_key <= at_query) & (at_key < length[0])
        for head in range(heads):
            lanes = slice(head * head_size, (head + 1) * head_size)
            scores = dot_nt(query[at, lanes], key_rows[0:extent, lanes]) * scale
            scores = jnp.where(allowed, scores, NEGATIVE)
            top = jnp.max(scores, axis=-1, keepdims=True)
            exponent = jnp.exp(scores - top)
            row_total = jnp.sum(exponent, axis=-1, keepdims=True)
            probs = (exponent / row_total).astype(jnp.bfloat16)
            attended[at, lanes] = dot_nn(probs, value[0:extent, lanes]).astype(jnp.bfloat16)
            log_total[at, head : head + 1] = top + jnp.log(row_total)

    gather_out.finish()
    stores[3].start()

    def out_tile(j, carry):
        lanes = piece_of(j)
        part_buf[:, lanes] = dot_nn(attended[...], w_out_buf[:, lanes]).astype(jnp.bfloat16)
        return carry

    lax.fori_loop(0, parts, out_tile, 0)

    def go_right(block):
        return remote(
            part_buf.at[rows_of(block)],
            from_left.at[block],
            sum_sems.at[0, block],
            sum_sems.at[1, block],
            right,
        )

    def go_left(block):
        return remote(
            part_buf.at[rows_of(block)],
            from_right.at[block],
            sum_sems.at[0, block],
            sum_sems.at[2, block],
            left,
        )

    def add_into(target, added):
        total = target[...].astype(jnp.float32) + added[...].astype(jnp.float32)
        target[...] = total.astype(jnp.bfloat16)

    def on_right(block):
        go_right(block).wait_recv()
        add_into(part_buf.at[rows_of(block)], from_left.at[block])
        go_right(block).start()

    def on_left(block):
        go_left(block).wait_recv()
        add_into(part_buf.at[rows_of(block)], from_right.at[block])
        go_left(block).start()

    @pl.when(place == 0)
    def _():
        for block in (3, 2, 1):
            go_right(block).start()

    @pl.when(place == 3)
    def _():
        for block in (0, 1, 2):
            go_left(block).start()

    @pl.when(place == 1)
    def _():
        on_right(3)
        on_right(2)
        on_left(0)

    @pl.when(place == 2)
    def _():
        on_left(0)
        on_left(1)
        on_right(3)

    resid[...] = tokens_buf[rows_of(place), :].astype(jnp.float32) + part_buf[
        rows_of(place), :
    ].astype(jnp.float32)

    @pl.when(place > 0)
    def _():
        go_right(place).wait_recv()
        resid[...] += from_left[place].astype(jnp.float32)

    @pl.when(place < group - 1)
    def _():
        go_left(place).wait_recv()
        resid[...] += from_right[place].astype(jnp.float32)

    total = resid[...]
    inverse = lax.rsqrt(jnp.mean(total * total, axis=-1, keepdims=True) + NORM_EPSILON)
    inverse_two[...] = inverse
    hidden_in = (total * inverse * small_full[1:2, :]).astype(jnp.bfloat16)
    logits = dot_nt(hidden_in, small_full[...].astype(jnp.bfloat16))
    lane = lax.broadcasted_iota(jnp.int32, logits.shape, 1)
    chosen = [
        jnp.sum(jnp.where(lane == named + 2, logits, 0.0), axis=1, keepdims=True)
        for named in (first_col, second_col)
    ]
    top = jnp.maximum(chosen[0], chosen[1])
    raised = [jnp.exp(entry - top) for entry in chosen]
    both = raised[0] + raised[1]
    gate = [entry / both for entry in raised]
    for number in range(2):
        gates[:, number : number + 1] = gate[number]
    sent[...] = dot_nn(hits[0] + hits[1], hidden_in).astype(jnp.bfloat16)
    d_out = jnp.where(live_col, 1.0, 0.0) * cotangent_buf[...].astype(jnp.float32)
    d_back[...] = (
        dot_nn(hits[0], (gate[0] * d_out).astype(jnp.bfloat16))
        + dot_nn(hits[1], (gate[1] * d_out).astype(jnp.bfloat16))
    ).astype(jnp.bfloat16)

    for store in stores:
        store.wait()
    gather_qkv.drain()
    gather_out.drain()
    for k in range(1, parts):
        small_copy(k).wait_send()
    for block in range(group):

        @pl.when(block > place)
        def _():
            go_right(block).wait_send()

        @pl.when(block < place)
        def _():
            go_left(block).wait_send()

        @pl.when((block <= place) & (place < group - 1))
        def _():
            pass_on(block, 0, right).wait_send()

        @pl.when((block >= place) & (place > 0))
        def _():
            pass_on(block, 1, left).wait_send()

    for turn in range(3):
        for r in (1, 2, 3):
            slice_copy(r, turn).wait()


def attention_call(
    lengths,
    tokens,
    w_qkv,
    w_out,
    gain_one,
    gain_two,
    router_t,
    w_gate_up,
    routes_t,
    order_row,
    angles,
    cotangent,
    group,
):
    tok, width = tokens.shape
    seq_len = tok * group
    local_width = w_qkv.shape[2]
    heads = local_width // HEAD_DIM
    slots = tok * 2
    piece = w_qkv.shape[1]
    low, full = jnp.bfloat16, jnp.float32
    anywhere = pl.BlockSpec(memory_space=pl.ANY)
    inside = pl.BlockSpec(memory_space=pltpu.VMEM)
    narrow = jax.ShapeDtypeStruct((seq_len, local_width), low)
    flops = 2 * seq_len * width * local_width * 4 + 4 * seq_len * seq_len * local_width
    return pl.pallas_call(
        functools.partial(attention_kernel, heads),
        out_shape=(
            jax.ShapeDtypeStruct((seq_len, width), low),
            jax.ShapeDtypeStruct((seq_len, width), low),
            jax.ShapeDtypeStruct((3, width, local_width), low),
            jax.ShapeDtypeStruct((local_width, width), low),
            jax.ShapeDtypeStruct((3, piece, w_gate_up.shape[2] // 4), low),
            jax.ShapeDtypeStruct((seq_len, 1), full),
            narrow,
            narrow,
            narrow,
            narrow,
            jax.ShapeDtypeStruct((seq_len, heads), full),
            jax.ShapeDtypeStruct((8, width), full),
            jax.ShapeDtypeStruct((seq_len, HEAD_DIM), full),
            jax.ShapeDtypeStruct((seq_len, HEAD_DIM), full),
            jax.ShapeDtypeStruct((tok, width), full),
            jax.ShapeDtypeStruct((tok, 1), full),
            jax.ShapeDtypeStruct((tok, 2), full),
            jax.ShapeDtypeStruct((2, slots, tok), low),
            jax.ShapeDtypeStruct((slots, width), low),
            jax.ShapeDtypeStruct((slots, width), low),
        ),
        in_specs=[pl.BlockSpec(memory_space=pltpu.SMEM)] + [anywhere] * 11,
        out_specs=(anywhere,) * 5 + (inside,) * 15,
        scratch_shapes=[
            pltpu.VMEM((seq_len, width), low),
            pltpu.VMEM((seq_len, width), low),
            pltpu.VMEM((3, width, local_width), low),
            pltpu.VMEM((local_width, width), low),
            pltpu.VMEM((seq_len, width), low),
            pltpu.VMEM((group, tok, width), low),
            pltpu.VMEM((group, tok, width), low),
            pltpu.VMEM(routes_t.shape, jnp.int32),
            pltpu.VMEM(order_row.shape, jnp.int32),
            pltpu.VMEM(angles.shape, full),
            pltpu.VMEM((tok, width), low),
            pltpu.VMEM(gain_one.shape, low),
            pltpu.VMEM(gain_two.shape, low),
            pltpu.VMEM(router_t.shape, low),
            pltpu.VMEM((8, piece), full),
            pltpu.SemaphoreType.DMA((18,)),
            pltpu.SemaphoreType.DMA((3, group)),
            pltpu.SemaphoreType.DMA((3, group)),
            pltpu.SemaphoreType.DMA((2, 2, 9)),
            pltpu.SemaphoreType.DMA((2, width // piece)),
            pltpu.SemaphoreType.DMA((2, 3, 3)),
        ],
        compiler_params=pltpu.CompilerParams(
            collective_id=3, has_side_effects=True, vmem_limit_bytes=67043328
        ),
        cost_estimate=pl.CostEstimate(flops=flops, bytes_accessed=40000000, transcendentals=0),
        name="attention",
    )(
        lengths,
        tokens,
        w_qkv,
        w_out,
        gain_one,
        gain_two,
        router_t,
        w_gate_up,
        routes_t,
        order_row,
        angles,
        cotangent,
    )


def expert_step(gate_up_w, down_w, rows, d_rows_out):
    ff = down_w.shape[0]
    gate_up = jnp.dot(rows, gate_up_w, preferred_element_type=jnp.float32)
    gate = gate_up[:, :ff]
    upward = gate_up[:, ff:]
    sigmoid = jax.nn.sigmoid(gate)
    activated = (gate * sigmoid * upward).astype(jnp.bfloat16)
    out = jnp.dot(activated, down_w, preferred_element_type=jnp.float32).astype(jnp.bfloat16)
    d_activated = contract_last(d_rows_out, down_w)
    grad_down = contract_first(activated, d_rows_out)
    d_gate = d_activated * upward * sigmoid * (1.0 + gate * (1.0 - sigmoid))
    d_up = d_activated * gate * sigmoid
    d_gate_up = jnp.concatenate([d_gate, d_up], axis=1).astype(jnp.bfloat16)
    d_rows = contract_last(d_gate_up, gate_up_w).astype(jnp.bfloat16)
    grad_gate_up = contract_first(rows, d_gate_up)
    return out, d_rows, grad_gate_up, grad_down


def experts_gather_weights(w_gate_up, w_down, rows, d_rows_out):
    gate_up_w = lax.all_gather(w_gate_up, "dp", axis=1, tiled=True)[0]
    down_w = lax.all_gather(w_down, "dp", axis=1, tiled=True)[0]
    shape = rows.shape
    flat = (-1, shape[2])
    rows = exchange_experts(rows).reshape(flat)
    d_rows_out = exchange_experts(d_rows_out).reshape(flat)
    out, d_rows, grad_gate_up, grad_down = expert_step(gate_up_w, down_w, rows, d_rows_out)
    out = exchange_experts(out.reshape(shape))
    d_rows = exchange_experts(d_rows.reshape(shape))
    grad_gate_up = lax.psum_scatter(
        grad_gate_up.astype(jnp.bfloat16), "dp", scatter_dimension=0, tiled=True
    )
    grad_down = lax.psum_scatter(
        grad_down.astype(jnp.bfloat16), "dp", scatter_dimension=0, tiled=True
    )
    return (
        out,
        d_rows,
        grad_gate_up.astype(jnp.float32)[None],
        grad_down.astype(jnp.float32)[None],
    )


def attention_back_plain(
    lengths,
    d_attn,
    hat_all,
    whole,
    out_full,
    qkv_full,
    query,
    key_rows,
    value,
    attended,
    log_total,
    cosine,
    sine,
):
    seq_len, heads_local, head_size = query.shape
    local_width = heads_local * head_size
    position = jnp.arange(seq_len, dtype=jnp.int32)
    allowed = (position[None, :] <= position[:, None]) & (position < lengths[0])[None, :]
    whole_grad = lax.all_gather(d_attn, "expert", axis=0, tiled=True)
    d_attended = contract_last(whole_grad, out_full).astype(jnp.bfloat16)
    out_part = contract_first(attended, whole_grad)
    grad_out = lax.psum_scatter(
        out_part.astype(jnp.bfloat16), "dp", scatter_dimension=1, tiled=True
    ).astype(jnp.float32)
    d_heads = d_attended.reshape(seq_len, heads_local, head_size)
    probs = jnp.exp(masked_scores(query, key_rows, allowed) - log_total)
    probs_low = probs.astype(jnp.bfloat16)
    d_value = jnp.einsum(
        "hqk,qhd->khd", probs_low, d_heads, preferred_element_type=jnp.float32
    ).astype(jnp.bfloat16)
    d_probs = jnp.einsum("qhd,khd->hqk", d_heads, value, preferred_element_type=jnp.float32)
    row_delta = jnp.sum(probs * d_probs, axis=-1, keepdims=True)
    d_scores = (probs * (d_probs - row_delta)).astype(jnp.bfloat16)
    scale = head_size ** (-0.5)
    d_query = (
        jnp.einsum("hqk,khd->qhd", d_scores, key_rows, preferred_element_type=jnp.float32) * scale
    )
    d_key = jnp.einsum("hqk,qhd->khd", d_scores, query, preferred_element_type=jnp.float32) * scale
    d_query_pre = (
        rotate_back(d_query, cosine, sine).reshape(seq_len, local_width).astype(jnp.bfloat16)
    )
    d_key_pre = rotate_back(d_key, cosine, sine).reshape(seq_len, local_width).astype(jnp.bfloat16)
    d_projected = jnp.stack([d_query_pre, d_key_pre, d_value.reshape(seq_len, local_width)])
    d_normed_part = jnp.einsum(
        "cte,cde->td", d_projected, qkv_full, preferred_element_type=jnp.float32
    )
    grad_normalized = lax.psum_scatter(
        d_normed_part.astype(jnp.bfloat16), "expert", scatter_dimension=0, tiled=True
    ).astype(jnp.float32)
    qkv_part = jnp.einsum("td,cte->cde", whole, d_projected, preferred_element_type=jnp.float32)
    grad_qkv = lax.psum_scatter(
        qkv_part.astype(jnp.bfloat16), "dp", scatter_dimension=1, tiled=True
    ).astype(jnp.float32)
    first_gain_part = jnp.sum(d_normed_part * hat_all, axis=0)
    return grad_normalized, grad_qkv, grad_out, first_gain_part


def on_device(
    tokens,
    w_qkv,
    w_out,
    attention_norm_gain,
    gain_ffn,
    w_router,
    w_gate_up,
    w_down,
    lengths,
    routes,
    order,
    cotangent,
):
    group_size = lax.axis_size("expert")
    dp_size = lax.axis_size("dp")
    tok_dev = tokens.shape[0]
    seq_len = tok_dev * group_size
    width = tokens.shape[1]
    top_count = routes.shape[1]
    capacity = tok_dev * top_count // group_size
    slots = group_size * capacity
    head_size = HEAD_DIM
    local_width = w_qkv.shape[2]
    heads_local = local_width // head_size
    tokens_all = lax.all_gather(tokens, "expert", axis=0, tiled=True)
    small = jnp.concatenate(
        [attention_norm_gain[:, None], gain_ffn[:, None], w_router], axis=1
    )
    small_full = lax.all_gather(small, "dp", axis=0, tiled=True)
    qkv_full = lax.all_gather(w_qkv, "dp", axis=1, tiled=True)
    out_full = lax.all_gather(w_out, "dp", axis=1, tiled=True)
    first_norm_gain = small_full[:, 0].astype(jnp.float32)
    gain_two = small_full[:, 1].astype(jnp.float32)
    router_full = small_full[:, 2:]

    own_start = lax.axis_index("expert") * tok_dev
    own_position = own_start + jnp.arange(tok_dev, dtype=jnp.int32)
    live_own = own_position < lengths[0]
    live_rows = live_own.astype(jnp.float32)[:, None]
    target, kept_pair = slot_table(routes, order, live_own, capacity)
    slot_ids = jnp.arange(slots, dtype=jnp.int32)
    pair_hits = (slot_ids[:, None, None] == target[None]) & kept_pair[None]
    select = jnp.sum(pair_hits.astype(jnp.float32), axis=2).astype(jnp.bfloat16)

    inputs_float = tokens.astype(jnp.float32)
    input_normalized_hat, first_inverse_rms = normalize(inputs_float)
    hat_all, _ = normalize(tokens_all.astype(jnp.float32))
    whole = (hat_all * first_norm_gain).astype(jnp.bfloat16)
    cosine, sine = rotary_tables(seq_len, head_size)
    projected = jnp.einsum("td,cde->cte", whole, qkv_full, preferred_element_type=jnp.float32)
    query = rotate(projected[0].reshape(seq_len, heads_local, head_size), cosine, sine).astype(
        jnp.bfloat16
    )
    key_rows = rotate(projected[1].reshape(seq_len, heads_local, head_size), cosine, sine).astype(
        jnp.bfloat16
    )
    value = projected[2].astype(jnp.bfloat16).reshape(seq_len, heads_local, head_size)
    position = jnp.arange(seq_len, dtype=jnp.int32)
    live_all = position < lengths[0]
    allowed = (position[None, :] <= position[:, None]) & live_all[None, :]
    scores = masked_scores(query, key_rows, allowed)
    top_score = jnp.max(scores, axis=-1, keepdims=True)
    exponent = jnp.exp(scores - top_score)
    row_total = jnp.sum(exponent, axis=-1, keepdims=True)
    probs = exponent / row_total
    log_total = top_score + jnp.log(row_total)
    probs_low = probs.astype(jnp.bfloat16)
    attended = jnp.einsum("hqk,khd->qhd", probs_low, value, preferred_element_type=jnp.float32)
    attended = attended.reshape(seq_len, local_width).astype(jnp.bfloat16)
    attn_part = jnp.dot(attended, out_full, preferred_element_type=jnp.float32)
    attn_own = lax.psum_scatter(
        attn_part.astype(jnp.bfloat16), "expert", scatter_dimension=0, tiled=True
    ).astype(jnp.float32)
    resid = inputs_float + attn_own
    hhat, inverse_two = normalize(resid)
    hidden_in = (hhat * gain_two).astype(jnp.bfloat16)
    sent = jnp.dot(select, hidden_in, preferred_element_type=jnp.float32).astype(jnp.bfloat16)

    logits = jnp.dot(hidden_in, router_full, preferred_element_type=jnp.float32)
    chosen = jnp.take_along_axis(logits, routes, axis=1)
    gates = jax.nn.softmax(chosen, axis=1)
    d_out = live_rows * cotangent.astype(jnp.float32)
    d_back = jnp.zeros((slots, width), jnp.float32)
    for index in range(top_count):
        weighted = (gates[:, index : index + 1] * d_out).astype(jnp.bfloat16)
        d_back = d_back + jnp.dot(
            pair_hits[:, :, index].astype(jnp.bfloat16),
            weighted,
            preferred_element_type=jnp.float32,
        )
    d_back = d_back.astype(jnp.bfloat16)
    blocked = (group_size, capacity, width)
    returned, d_sent, grad_gate_up, grad_down = experts_gather_weights(
        w_gate_up, w_down, sent.reshape(blocked), d_back.reshape(blocked)
    )
    returned = returned.reshape(slots, width)
    d_sent = d_sent.reshape(slots, width)

    moe = jnp.zeros_like(resid)
    d_gates_list = []
    for index in range(top_count):
        one_hot = pair_hits[:, :, index].astype(jnp.bfloat16)
        picked = contract_first(one_hot, returned)
        d_gates_list.append(jnp.sum(d_out * picked, axis=-1))
        moe = moe + gates[:, index : index + 1] * picked
    output = (live_rows * (resid + moe)).astype(jnp.bfloat16)
    d_gates = jnp.stack(d_gates_list, axis=1)
    d_hidden = contract_first(select, d_sent)
    d_chosen = gates * (d_gates - jnp.sum(gates * d_gates, axis=1, keepdims=True))
    expert_ids = jnp.arange(group_size, dtype=jnp.int32)
    route_hits = (routes[:, :, None] == expert_ids[None, None, :]).astype(jnp.float32)
    d_logits = jnp.sum(route_hits * d_chosen[:, :, None], axis=1)
    router_f = router_full.astype(jnp.float32)
    d_hidden = d_hidden + jnp.dot(
        d_logits, router_f.T, precision=HIGH, preferred_element_type=jnp.float32
    )
    router_part = jnp.dot(
        hidden_in.astype(jnp.float32).T,
        d_logits,
        precision=HIGH,
        preferred_element_type=jnp.float32,
    )
    gain_two_part = jnp.sum(d_hidden * hhat, axis=0)
    scaled_two = d_hidden * gain_two
    d_resid = d_out + inverse_two * (
        scaled_two - hhat * jnp.mean(scaled_two * hhat, axis=-1, keepdims=True)
    )
    d_attn = d_resid.astype(jnp.bfloat16)
    grad_normalized, grad_qkv, grad_out, first_gain_part = attention_back_plain(
        lengths,
        d_attn,
        hat_all,
        whole,
        out_full,
        qkv_full,
        query,
        key_rows,
        value,
        attended,
        log_total,
        cosine,
        sine,
    )
    small_part = jnp.concatenate(
        [first_gain_part[None], gain_two_part[None], router_part.T], axis=0
    )
    small_sum = lax.psum(small_part, ("dp", "expert"))
    own_rows = width // dp_size
    small_own = lax.dynamic_slice_in_dim(
        small_sum, lax.axis_index("dp") * own_rows, own_rows, axis=1
    )
    first_scaled_input = grad_normalized * first_norm_gain
    grad_tokens = d_resid + first_inverse_rms * (
        first_scaled_input
        - input_normalized_hat
        * jnp.mean(first_scaled_input * input_normalized_hat, axis=-1, keepdims=True)
    )
    return (
        output,
        grad_tokens.astype(jnp.bfloat16),
        grad_qkv,
        grad_out,
        small_own[0],
        small_own[1],
        small_own[2 : 2 + group_size].T,
        grad_gate_up,
        grad_down,
    )


def on_device_split(
    tokens,
    w_qkv,
    w_out,
    attention_norm_gain,
    gain_ffn,
    w_router,
    w_gate_up,
    w_down,
    lengths,
    routes,
    order,
    cotangent,
):
    group = lax.axis_size("expert")
    tok, width = tokens.shape
    piece = w_router.shape[0]
    slots = tok * routes.shape[1]
    angles = rotary_constants(tok * group, HEAD_DIM)
    routes_t = routes.T
    (
        tokens_all,
        whole,
        qkv_full,
        out_full,
        w_got,
        inverse_all,
        query,
        key_rows,
        value,
        attended,
        log_total,
        small_full,
        cosine,
        sine,
        resid,
        inverse_two,
        gates,
        hits,
        sent,
        d_back,
    ) = attention_call(
        lengths,
        tokens,
        w_qkv,
        w_out,
        attention_norm_gain.reshape(-1, LANES),
        gain_ffn.reshape(-1, LANES),
        w_router.T,
        w_gate_up,
        routes_t,
        order.reshape(1, tok),
        angles,
        cotangent,
        group,
    )
    blocked = (group, slots // group, width)
    returned, d_sent, grad_gate_up, grad_down = experts_call(
        sent.reshape(blocked), d_back.reshape(blocked), w_gate_up, w_got, w_down
    )
    output, grad_tokens, grad_weights, small_own, gate_got = attention_back_call(
        lengths,
        returned.reshape(slots, width),
        d_sent.reshape(slots, width),
        resid,
        inverse_two,
        gates,
        hits,
        cotangent,
        routes_t,
        small_full,
        tokens_all,
        inverse_all,
        whole,
        out_full,
        qkv_full,
        query,
        key_rows,
        value,
        attended,
        log_total,
        cosine,
        sine,
        grad_gate_up,
    )
    (
        grad_gate_up,
        grad_down,
        grad_tokens,
        output,
        grad_qkv,
        grad_out,
        gain_one,
        gain_two,
        router,
    ) = finish_call(gate_got, grad_down, grad_tokens, output, grad_weights, small_own, group)
    return (
        output,
        grad_tokens,
        grad_qkv,
        grad_out,
        gain_one.reshape(piece),
        gain_two.reshape(piece),
        router.T,
        grad_gate_up,
        grad_down,
    )


def solution(mesh):
    placed = (
        P(("dp", "expert"), None),
        P(None, "dp", "expert"),
        P("expert", "dp"),
        P("dp"),
        P("dp"),
        P("dp", None),
        P("expert", "dp", None),
        P("expert", "dp", None),
        P("dp"),
        P(("dp", "expert"), None),
        P(("dp", "expert")),
        P(("dp", "expert"), None),
    )
    split = mesh.shape["dp"] == 8 and mesh.shape["expert"] == 4
    return jax.shard_map(
        on_device_split if split else on_device,
        mesh=mesh,
        in_specs=placed,
        out_specs=(
            P(("dp", "expert"), None),
            P(("dp", "expert"), None),
            P(None, "dp", "expert"),
            P("expert", "dp"),
            P("dp"),
            P("dp"),
            P("dp", None),
            P("expert", "dp", None),
            P("expert", "dp", None),
        ),
        check_vma=False,
    )
```
